32 devices in a mesh: rep: 2 (over core), fsdp: 2 (over y), seq: 8 (over z, x).
Axes of the slice: x: 2, y: 2, z: 4, core: 2. Of those that a mesh axis runs over, the one named last changes fastest.
Arguments:
- hidden_states: bfloat16 [4, 2048, 1024], P(('rep', 'fsdp'), 'seq'), may hold values from -6 to 6
- unit_order: int32 [4, 16], P(('rep', 'fsdp')), may hold values from 0 to 15, each once within a row
- piece_starts: int32 [4, 2], P(('rep', 'fsdp')), may hold values from 0 to 1792, as said below
- first_gain: bfloat16 [1024], P('fsdp'), may hold values from 0.5 to 1.5
- first_shift: bfloat16 [1024], P('fsdp'), may hold values from -1 to 1
- second_gain: bfloat16 [1024], P('fsdp'), may hold values from 0.5 to 1.5
- second_shift: bfloat16 [1024], P('fsdp'), may hold values from -1 to 1
- merged_weight: bfloat16 [1024, 3072], P('fsdp'), may hold values from -0.1875 to 0.1875
- merged_bias: bfloat16 [3072], P('fsdp'), may hold values from -1 to 1
- output_weight: bfloat16 [1024, 1024], P('fsdp'), may hold values from -0.5 to 0.5
- output_bias: bfloat16 [1024], P('fsdp'), may hold values from -1 to 1
- expand_weight: bfloat16 [1024, 4096], P('fsdp'), may hold values from -0.1875 to 0.1875
- expand_bias: bfloat16 [4096], P('fsdp'), may hold values from -1 to 1
- contract_weight: bfloat16 [4096, 1024], P('fsdp'), may hold values from -0.09375 to 0.09375
- contract_bias: bfloat16 [1024], P('fsdp'), may hold values from -1 to 1
- out_cotangent: bfloat16 [4, 2048, 1024], P(('rep', 'fsdp'), 'seq'), may hold values from -6 to 6
Outputs:
- hidden_output: bfloat16 [4, 2048, 1024], P(('rep', 'fsdp'), 'seq')
- input_gradient: float32 [4, 2048, 1024], P(('rep', 'fsdp'), 'seq')
- first_gain_gradient: float32 [1024], P('fsdp')
- first_shift_gradient: float32 [1024], P('fsdp')
- second_gain_gradient: float32 [1024], P('fsdp')
- second_shift_gradient: float32 [1024], P('fsdp')
- merged_weight_gradient: float32 [1024, 3072], P('fsdp')
- merged_bias_gradient: float32 [3072], P('fsdp')
- output_weight_gradient: float32 [1024, 1024], P('fsdp')
- output_bias_gradient: float32 [1024], P('fsdp')
- expand_weight_gradient: float32 [1024, 4096], P('fsdp')
- expand_bias_gradient: float32 [4096], P('fsdp')
- contract_weight_gradient: float32 [4096, 1024], P('fsdp')
- contract_bias_gradient: float32 [1024], P('fsdp')
The draws below stay inside these ranges and needn't reach their ends.
Inputs may be any that keep to these rules, and one draw needn't show every extreme that they name: `piece_starts`: piece p of a sequence starts at (8 p + k) * 128 for some k from 0 to 6, so pieces lie in order and never intersection (two may be adjacent); some sequence's first piece starts at 0 and some sequence's last piece ends at the sequence's end. Each sequence's row of unit_order names every unit of positions once.
All inputs are finite; a program needn't handle non-finite values.
Results may differ from the reference program's by a relative error of at most 0.012.
Values may be sent and summed in bfloat16 or wider, within the bound.
A program may use at most 384 MiB of HBM per device.

```python
import math
import jax
import jax.numpy as jnp
from jax import lax

D = 1024
HEADS = 16
HEAD = 64
ROT = 16
FF = 4096
UNIT = 128
PIECE = 256
LEN = 2048
SEQS = 4
UNITS = 16
PIECES = 2


def draw_piece_starts(key, part):
    offsets = jax.random.randint(jax.random.fold_in(key, 1), (SEQS, PIECES), 0, 7).astype(jnp.int32)
    low_row = jax.random.randint(jax.random.fold_in(key, 2), (), 0, SEQS)
    high_row = jax.random.randint(jax.random.fold_in(key, 3), (), 0, SEQS)
    rows = jnp.arange(SEQS, dtype=jnp.int32)[:, None]
    columns = jnp.arange(PIECES, dtype=jnp.int32)[None, :]
    offsets = jnp.where((rows == low_row) & (columns == 0), 0, offsets)
    offsets = jnp.where((rows == high_row) & (columns == PIECES - 1), 6, offsets)
    slots = columns * 8
    return ((slots + offsets) * UNIT).astype(jnp.int32)


def block_scale(stream_key, dims, pieces, smallest, top_value):
    def one(axis_at, blocks):
        draws = jax.random.uniform(jax.random.fold_in(jax.random.fold_in(stream_key, 6), axis_at), (blocks,), jnp.float32, smallest / len(pieces), top_value / len(pieces))
        return jnp.repeat(jnp.exp(draws), dims[axis_at] // blocks).reshape((-1,) + (1,) * (len(dims) - axis_at - 1))

    loudness = one(*pieces[0])
    for cut in pieces[1:]:
        loudness = loudness * one(*cut)
    return loudness


def bell_draw(rng, extent, width, reach, split=(), held_as=jnp.bfloat16):
    entries = width * jax.random.normal(rng, extent, jnp.float32)
    if split:
        entries = entries * block_scale(rng, extent, split, -0.22, 0.18)
    return jnp.clip(entries, -reach, reach).astype(held_as)


def setup_inputs(seed: int = 0) -> dict:
    streams_of = jax.random.split(jax.random.key(seed), 17)
    return {
        "hidden_states": bell_draw(streams_of[0], (SEQS, LEN, D), 1.0, 6.0, ((0, 4), (1, 8))),
        "unit_order": jax.vmap(lambda own: jax.random.permutation(own, UNITS))(jax.random.split(streams_of[1], SEQS)).reshape((SEQS, UNITS)).astype(jnp.int32),
        "piece_starts": draw_piece_starts(jax.random.fold_in(streams_of[16], 71), 0),
        "first_gain": jnp.clip(1.0 + 0.1 * jax.random.normal(streams_of[3], (D,), jnp.float32), 0.5, 1.5).astype(jnp.bfloat16),
        "first_shift": bell_draw(streams_of[4], (D,), 0.2, 1.0, ((0, 2),)),
        "second_gain": jnp.clip(1.0 + 0.1 * jax.random.normal(streams_of[5], (D,), jnp.float32), 0.5, 1.5).astype(jnp.bfloat16),
        "second_shift": bell_draw(streams_of[6], (D,), 0.2, 1.0, ((0, 2),)),
        "merged_weight": bell_draw(streams_of[7], (D, 3 * D), D ** -0.5, 0.1875, ((0, 2),)),
        "merged_bias": bell_draw(streams_of[8], (3 * D,), 0.2, 1.0, ((0, 2),)),
        "output_weight": bell_draw(streams_of[9], (D, D), (max(8, D * 256 // LEN)) ** -0.5, 0.5, ((0, 2),)),
        "output_bias": bell_draw(streams_of[10], (D,), 0.2, 1.0, ((0, 2),)),
        "expand_weight": bell_draw(streams_of[11], (D, FF), D ** -0.5, 0.1875, ((0, 2),)),
        "expand_bias": bell_draw(streams_of[12], (FF,), 0.2, 1.0, ((0, 2),)),
        "contract_weight": bell_draw(streams_of[13], (FF, D), FF ** -0.5, 0.09375, ((0, 2),)),
        "contract_bias": bell_draw(streams_of[14], (D,), 0.2, 1.0, ((0, 2),)),
        "out_cotangent": bell_draw(streams_of[15], (SEQS, LEN, D), 1.0, 6.0, ((0, 4), (1, 8))),
    }


@jax.custom_vjp
def low(v):
    return lax.optimization_barrier(v.astype(jnp.bfloat16)).astype(jnp.float32)

@jax.custom_vjp
def low_back(v):
    return v

def low_keep(v):
    return (low(v), None)

def low_pass(kept, grad):
    return (grad,)

def back_keep(v):
    return (v, None)

def back_low(kept, grad):
    return (low(grad),)
low.defvjp(low_keep, low_pass)
low_back.defvjp(back_keep, back_low)
EPS = 1e-05
NEGATIVE = -1e+30

def norm_rows(values, gain, shift):
    mean = lax.optimization_barrier(jnp.mean(values, axis=-1, keepdims=True))
    centred = values - mean
    spread = lax.optimization_barrier(jnp.mean(centred * centred, axis=-1, keepdims=True))
    return centred * lax.rsqrt(spread + EPS) * gain + shift

def rotary_tables(positions):
    index = jnp.arange(ROT // 2, dtype=jnp.float32)
    inverse = jnp.exp(index * (-2.0 * math.log(10000.0) / ROT))
    angles = positions.astype(jnp.float32)[:, None] * inverse[None, :]
    angles = jnp.concatenate([angles, angles], axis=1)
    return (jnp.cos(angles), jnp.sin(angles))

def rotate(values, cosine, sine):
    part = values[..., :ROT]
    turned = jnp.concatenate([-part[..., ROT // 2:], part[..., :ROT // 2]], axis=-1)
    moved = part * cosine[:, None, :] + turned * sine[:, None, :]
    return jnp.concatenate([moved, values[..., ROT:]], axis=-1)

def unit_positions(order):
    offsets = jnp.arange(UNIT, dtype=jnp.int32)
    return (order[:, None] * UNIT + offsets[None, :]).reshape(-1).astype(jnp.int32)

def piece_labels(positions, starts):
    inside = (positions[:, None] >= starts[None, :]) & (positions[:, None] < starts[None, :] + PIECE)
    labels = jnp.arange(1, starts.shape[0] + 1, dtype=jnp.int32)
    return (lax.optimization_barrier(jnp.sum(jnp.where(inside, labels[None, :], 0), axis=1)) - 1).astype(jnp.int32)

def visible(row_pos, row_lab, col_pos, col_lab):
    earlier = col_pos[None, :] <= row_pos[:, None]
    same = (row_lab[:, None] == col_lab[None, :]) & (row_lab[:, None] >= 0)
    return earlier | same

def sequence_forward(hidden, params, positions, labels):
    first_gain, first_shift, second_gain, second_shift, merged_weight, merged_bias, output_weight, output_bias, expand_weight, expand_bias, contract_weight, contract_bias = params
    high = lax.Precision.HIGHEST
    scale = 1.0 / math.sqrt(HEAD)
    first = low(norm_rows(hidden, first_gain, first_shift))
    merged = low_back(jnp.dot(first, merged_weight, precision=high) + merged_bias)
    cosine, sine = rotary_tables(positions)
    queries = low(rotate(merged[:, :D].reshape(LEN, HEADS, HEAD), cosine, sine))
    keys = low(rotate(merged[:, D:2 * D].reshape(LEN, HEADS, HEAD), cosine, sine))
    values = low(merged[:, 2 * D:].reshape(LEN, HEADS, HEAD))
    block = min(LEN, 512)

    def attend(index):
        start = (index * block).astype(jnp.int32)
        rows = lax.dynamic_slice_in_dim(queries, start, block, 0)
        row_pos = lax.dynamic_slice_in_dim(positions, start, block, 0)
        row_lab = lax.dynamic_slice_in_dim(labels, start, block, 0)
        scores = low_back(jnp.einsum('qhd,khd->hqk', rows, keys, precision=high) * scale)
        allowed = visible(row_pos, row_lab, positions, labels)
        scores = jnp.where(allowed[None], scores, NEGATIVE)
        weights = low(jax.nn.softmax(scores, axis=-1))
        return jnp.einsum('hqk,khd->qhd', weights, values, precision=high)
    mixed = lax.map(jax.checkpoint(attend), jnp.arange(LEN // block, dtype=jnp.int32))
    mixed = low(low_back(mixed.reshape(LEN, D)))
    attention = jnp.dot(mixed, output_weight, precision=high) + output_bias
    second = low(norm_rows(hidden, second_gain, second_shift))
    expanded = low_back(jnp.dot(second, expand_weight, precision=high) + expand_bias)
    active = low(jax.nn.gelu(expanded, approximate=False))
    feed = jnp.dot(active, contract_weight, precision=high) + contract_bias
    return hidden + attention + feed

def reference(hidden_states, unit_order, piece_starts, first_gain, first_shift, second_gain, second_shift, merged_weight, merged_bias, output_weight, output_bias, expand_weight, expand_bias, contract_weight, contract_bias, out_cotangent):
    params = tuple((p.astype(jnp.float32) for p in (first_gain, first_shift, second_gain, second_shift, merged_weight, merged_bias, output_weight, output_bias, expand_weight, expand_bias, contract_weight, contract_bias)))

    def one(carry, item):
        hidden, order, starts, cotangent = item
        positions = unit_positions(order)
        labels = piece_labels(positions, starts)

        def forward(inputs, weights):
            return sequence_forward(inputs, weights, positions, labels)
        result, pullback = jax.vjp(forward, hidden.astype(jnp.float32), params)
        grad_hidden, grad_params = pullback(cotangent.astype(jnp.float32))
        carry = jax.tree.map(jnp.add, carry, grad_params)
        return (carry, (result.astype(jnp.bfloat16), grad_hidden))
    zeros = tuple((jnp.zeros(p.shape, jnp.float32) for p in params))
    totals, (outputs, gradients) = lax.scan(one, zeros, (hidden_states, unit_order, piece_starts, out_cotangent))
    return (outputs, gradients, totals[0], totals[1], totals[2], totals[3], totals[4], totals[5], totals[6], totals[7], totals[8], totals[9], totals[10], totals[11])
```

```python
import functools
import math

import jax
import jax.numpy as jnp
from jax import lax
from jax.experimental import pallas as pl
from jax.experimental.pallas import tpu as pltpu
from jax.sharding import PartitionSpec as P

HEAD = 64
ROT = 16
UNIT = 128
PIECE = 256


EPS = 1e-05
NEGATIVE = -1e30


def norm_rows(values, gain, shift):
    mean = jnp.mean(values, axis=-1, keepdims=True)
    centred = values - mean
    spread = jnp.mean(centred * centred, axis=-1, keepdims=True)
    return centred * lax.rsqrt(spread + EPS) * gain + shift


def gelu_exact(values):
    return jax.nn.gelu(values, approximate=False)


def rotary_tables(positions):
    index = jnp.arange(ROT // 2, dtype=jnp.float32)
    inverse = jnp.exp(index * (-2.0 * math.log(10000.0) / ROT))
    angles = positions.astype(jnp.float32)[:, None] * inverse[None, :]
    angles = jnp.concatenate([angles, angles], axis=1)
    return (jnp.cos(angles), jnp.sin(angles))


def rotate(values, cosine, sine):
    part = values[..., :ROT]
    turned = jnp.concatenate([-part[..., ROT // 2 :], part[..., : ROT // 2]], axis=-1)
    moved = part * cosine[:, None, :] + turned * sine[:, None, :]
    return jnp.concatenate([moved, values[..., ROT:]], axis=-1)


def unit_positions(order):
    offsets = jnp.arange(UNIT, dtype=jnp.int32)
    return (order[:, None] * UNIT + offsets[None, :]).reshape(-1)


def piece_labels(positions, starts):
    inside = (positions[:, None] >= starts[None, :]) & (
        positions[:, None] < starts[None, :] + PIECE
    )
    labels = jnp.arange(1, starts.shape[0] + 1, dtype=jnp.int32)
    return jnp.sum(jnp.where(inside, labels[None, :], 0), axis=1) - 1


def visible(row_pos, row_lab, col_pos, col_lab):
    earlier = col_pos[None, :] <= row_pos[:, None]
    same = (row_lab[:, None] == col_lab[None, :]) & (row_lab[:, None] >= 0)
    return earlier | same


def merged_parts(first, merged_weight, merged_bias, cosine, sine):
    tokens = first.shape[0]
    width = first.shape[1]
    heads = width // HEAD
    merged = jnp.dot(first, merged_weight, preferred_element_type=jnp.float32) + merged_bias.astype(
        jnp.float32
    )
    queries = rotate(merged[:, :width].reshape(tokens, heads, HEAD), cosine, sine).astype(
        jnp.bfloat16
    )
    keys = rotate(merged[:, width : 2 * width].reshape(tokens, heads, HEAD), cosine, sine)
    keys = keys.reshape(tokens, width).astype(jnp.bfloat16)
    values = merged[:, 2 * width :].astype(jnp.bfloat16)
    return (queries, keys, values)


def block_view(queries, keys_all, values_all, row_pos, row_lab, col_pos, col_lab, span):
    heads = queries.shape[1]
    scale = 1.0 / math.sqrt(HEAD)

    def view(index):
        start = index * span
        key_rows = lax.dynamic_slice_in_dim(keys_all, start, span, 0).reshape(span, heads, HEAD)
        value_rows = lax.dynamic_slice_in_dim(values_all, start, span, 0).reshape(span, heads, HEAD)
        scores = (
            jnp.einsum("thd,khd->htk", queries, key_rows, preferred_element_type=jnp.float32)
            * scale
        )
        allowed = visible(
            row_pos,
            row_lab,
            lax.dynamic_slice_in_dim(col_pos, start, span, 0),
            lax.dynamic_slice_in_dim(col_lab, start, span, 0),
        )[None]
        return (scores, allowed, key_rows, value_rows)

    return view


def log_sums(view, count, heads, tokens):

    def log_step(carry, index):
        top, total = carry
        scores, allowed, key_rows, value_rows = view(index)
        masked = jnp.where(allowed, scores, NEGATIVE)
        newer = jnp.maximum(top, jnp.max(masked, axis=-1))
        terms = jnp.where(allowed, jnp.exp(masked - newer[..., None]), 0.0)
        total = total * jnp.exp(top - newer) + jnp.sum(terms, axis=-1)
        return ((newer, total), None)

    begin = (
        jnp.full((heads, tokens), NEGATIVE, jnp.float32),
        jnp.zeros((heads, tokens), jnp.float32),
    )
    (top, total), unused = lax.scan(log_step, begin, jnp.arange(count, dtype=jnp.int32))
    return top + jnp.log(total)


def mix_values(view, count, logsum, heads, tokens, grad_rows):

    def mix_step(carry, index):
        mixed, delta = carry
        scores, allowed, key_rows, value_rows = view(index)
        weights = jnp.where(allowed, jnp.exp(scores - logsum[..., None]), 0.0)
        mixed = mixed + jnp.einsum(
            "htk,khd->thd",
            weights.astype(jnp.bfloat16),
            value_rows,
            preferred_element_type=jnp.float32,
        )
        if grad_rows is not None:
            slopes = jnp.einsum(
                "thd,khd->htk", grad_rows, value_rows, preferred_element_type=jnp.float32
            )
            delta = delta + jnp.sum(weights * slopes, axis=-1)
        return ((mixed, delta), None)

    begin = (jnp.zeros((tokens, heads, HEAD), jnp.float32), jnp.zeros((heads, tokens), jnp.float32))
    (mixed, delta), unused = lax.scan(mix_step, begin, jnp.arange(count, dtype=jnp.int32))
    return (mixed, delta)


def attend_back(view, count, logsum, delta, grad_rows, queries):
    scale = 1.0 / math.sqrt(HEAD)

    def attend_step(carry, index):
        scores, allowed, key_rows, value_rows = view(index)
        weights = jnp.where(allowed, jnp.exp(scores - logsum[..., None]), 0.0)
        slopes = jnp.einsum(
            "thd,khd->htk", grad_rows, value_rows, preferred_element_type=jnp.float32
        )
        grad_scores = (weights * (slopes - delta[..., None])).astype(jnp.bfloat16)
        carry = carry + jnp.einsum(
            "htk,khd->thd", grad_scores, key_rows, preferred_element_type=jnp.float32
        )
        key_grad = jnp.einsum(
            "htk,thd->khd", grad_scores, queries, preferred_element_type=jnp.float32
        )
        value_grad = jnp.einsum(
            "htk,thd->khd",
            weights.astype(jnp.bfloat16),
            grad_rows,
            preferred_element_type=jnp.float32,
        )
        span = key_rows.shape[0]
        joined = jnp.concatenate(
            [key_grad.reshape(span, -1) * scale, value_grad.reshape(span, -1)], axis=1
        )
        return (carry, joined)

    begin = jnp.zeros(queries.shape, jnp.float32)
    grad_query, parts = lax.scan(attend_step, begin, jnp.arange(count, dtype=jnp.int32))
    return (grad_query * scale, parts)


def body(
    hidden_states,
    unit_order,
    piece_starts,
    first_gain,
    first_shift,
    second_gain,
    second_shift,
    merged_weight,
    merged_bias,
    output_weight,
    output_bias,
    expand_weight,
    expand_bias,
    contract_weight,
    contract_bias,
    out_cotangent,
):
    shards = (
        first_gain,
        first_shift,
        second_gain,
        second_shift,
        merged_weight,
        merged_bias,
        output_weight,
        output_bias,
        expand_weight,
        expand_bias,
        contract_weight,
        contract_bias,
    )
    gathered = (
        lax.all_gather(shards[0], "fsdp", axis=0, tiled=True),
        lax.all_gather(shards[1], "fsdp", axis=0, tiled=True),
        lax.all_gather(shards[2], "fsdp", axis=0, tiled=True),
        lax.all_gather(shards[3], "fsdp", axis=0, tiled=True),
        lax.all_gather(shards[4], "fsdp", axis=0, tiled=True),
        lax.all_gather(shards[5], "fsdp", axis=0, tiled=True),
        lax.all_gather(shards[6], "fsdp", axis=0, tiled=True),
        lax.all_gather(shards[7], "fsdp", axis=0, tiled=True),
        lax.all_gather(shards[8], "fsdp", axis=0, tiled=True),
        lax.all_gather(shards[9], "fsdp", axis=0, tiled=True),
        lax.all_gather(shards[10], "fsdp", axis=0, tiled=True),
        lax.all_gather(shards[11], "fsdp", axis=0, tiled=True),
    )
    hidden = hidden_states[0].astype(jnp.float32)
    tokens = hidden.shape[0]
    width = hidden.shape[1]
    heads = width // HEAD
    length = tokens * lax.axis_size("seq")
    span = min(length, 512)
    count = length // span
    col_pos = unit_positions(unit_order[0])
    col_lab = piece_labels(col_pos, piece_starts[0])
    offset = lax.axis_index("seq") * tokens
    row_pos = lax.dynamic_slice_in_dim(col_pos, offset, tokens, 0)
    row_lab = lax.dynamic_slice_in_dim(col_lab, offset, tokens, 0)
    cosine, sine = rotary_tables(row_pos)
    first = norm_rows(
        hidden, gathered[0].astype(jnp.float32), gathered[1].astype(jnp.float32)
    ).astype(jnp.bfloat16)
    queries, keys, values = merged_parts(first, gathered[4], gathered[5], cosine, sine)
    keys_all, values_all = (
        lax.all_gather(keys, "seq", axis=0, tiled=True),
        lax.all_gather(values, "seq", axis=0, tiled=True),
    )
    view = block_view(queries, keys_all, values_all, row_pos, row_lab, col_pos, col_lab, span)
    logsum = log_sums(view, count, heads, tokens)
    mixed, unused = mix_values(view, count, logsum, heads, tokens, None)
    mixed = mixed.reshape(tokens, width).astype(jnp.bfloat16)
    attention = jnp.dot(mixed, gathered[6], preferred_element_type=jnp.float32) + gathered[
        7
    ].astype(jnp.float32)
    second = norm_rows(
        hidden, gathered[2].astype(jnp.float32), gathered[3].astype(jnp.float32)
    ).astype(jnp.bfloat16)
    expanded = jnp.dot(second, gathered[8], preferred_element_type=jnp.float32) + gathered[
        9
    ].astype(jnp.float32)
    active = gelu_exact(expanded).astype(jnp.bfloat16)
    feed = jnp.dot(active, gathered[10], preferred_element_type=jnp.float32) + gathered[11].astype(
        jnp.float32
    )
    output = (hidden + attention + feed).astype(jnp.bfloat16)
    weights = (
        lax.all_gather(shards[0], "fsdp", axis=0, tiled=True),
        lax.all_gather(shards[1], "fsdp", axis=0, tiled=True),
        lax.all_gather(shards[2], "fsdp", axis=0, tiled=True),
        lax.all_gather(shards[3], "fsdp", axis=0, tiled=True),
        lax.all_gather(shards[4], "fsdp", axis=0, tiled=True),
        lax.all_gather(shards[5], "fsdp", axis=0, tiled=True),
        lax.all_gather(shards[6], "fsdp", axis=0, tiled=True),
        lax.all_gather(shards[7], "fsdp", axis=0, tiled=True),
        lax.all_gather(shards[8], "fsdp", axis=0, tiled=True),
        lax.all_gather(shards[9], "fsdp", axis=0, tiled=True),
        lax.all_gather(shards[10], "fsdp", axis=0, tiled=True),
        lax.all_gather(shards[11], "fsdp", axis=0, tiled=True),
    )
    cotangent = out_cotangent[0]
    upstream = cotangent.astype(jnp.float32)
    normed_one, first_pull = jax.vjp(
        norm_rows, hidden, weights[0].astype(jnp.float32), weights[1].astype(jnp.float32)
    )
    first = normed_one.astype(jnp.bfloat16)
    queries, keys, values = merged_parts(first, weights[4], weights[5], cosine, sine)
    keys_back, values_back = (
        lax.all_gather(keys, "seq", axis=0, tiled=True),
        lax.all_gather(values, "seq", axis=0, tiled=True),
    )
    view = block_view(queries, keys_back, values_back, row_pos, row_lab, col_pos, col_lab, span)
    grad_mixed = jnp.einsum(
        "te,de->td", cotangent, weights[6], preferred_element_type=jnp.float32
    ).astype(jnp.bfloat16)
    grad_rows = grad_mixed.reshape(tokens, heads, HEAD)
    mixed, delta = mix_values(view, count, logsum, heads, tokens, grad_rows)
    mixed = mixed.reshape(tokens, width).astype(jnp.bfloat16)
    grad_query, parts = attend_back(view, count, logsum, delta, grad_rows, queries)
    term = parts.reshape(length, 2 * width)
    own_grads = lax.psum_scatter(
        term.astype(jnp.bfloat16), "seq", scatter_dimension=0, tiled=True
    ).astype(jnp.float32)
    normed_two, second_pull = jax.vjp(
        norm_rows, hidden, weights[2].astype(jnp.float32), weights[3].astype(jnp.float32)
    )
    second = normed_two.astype(jnp.bfloat16)
    expanded = jnp.dot(second, weights[8], preferred_element_type=jnp.float32) + weights[9].astype(
        jnp.float32
    )
    activated, gelu_pull = jax.vjp(gelu_exact, expanded)
    active = activated.astype(jnp.bfloat16)
    grad_active = jnp.einsum(
        "te,fe->tf", cotangent, weights[10], preferred_element_type=jnp.float32
    )
    grad_expanded = gelu_pull(grad_active)[0].astype(jnp.bfloat16)
    grad_second = jnp.einsum(
        "tf,df->td", grad_expanded, weights[8], preferred_element_type=jnp.float32
    )
    unused, turn_pull = jax.vjp(rotate, grad_query, cosine, sine)
    query_back = turn_pull(grad_query)[0].reshape(tokens, width)
    key_back = turn_pull(own_grads[:, :width].reshape(tokens, heads, HEAD))[0].reshape(
        tokens, width
    )
    grad_merged = jnp.concatenate([query_back, key_back, own_grads[:, width:]], axis=1).astype(
        jnp.bfloat16
    )
    grad_first = jnp.einsum(
        "tc,dc->td", grad_merged, weights[4], preferred_element_type=jnp.float32
    )
    first_term, first_gain_grad, first_shift_grad = first_pull(grad_first)
    second_term, second_gain_grad, second_shift_grad = second_pull(grad_second)
    input_gradient = upstream + first_term + second_term
    row_total = jnp.sum(upstream, axis=0)
    local_grads = (
        first_gain_grad,
        first_shift_grad,
        second_gain_grad,
        second_shift_grad,
        jnp.einsum("td,tc->dc", first, grad_merged, preferred_element_type=jnp.float32),
        jnp.sum(grad_merged.astype(jnp.float32), axis=0),
        jnp.einsum("td,te->de", mixed, cotangent, preferred_element_type=jnp.float32),
        row_total,
        jnp.einsum("td,tf->df", second, grad_expanded, preferred_element_type=jnp.float32),
        jnp.sum(grad_expanded.astype(jnp.float32), axis=0),
        jnp.einsum("tf,te->fe", active, cotangent, preferred_element_type=jnp.float32),
        row_total,
    )
    owned = (
        lax.psum_scatter(
            local_grads[0].astype(jnp.bfloat16), "fsdp", scatter_dimension=0, tiled=True
        ).astype(jnp.float32),
        lax.psum_scatter(
            local_grads[1].astype(jnp.bfloat16), "fsdp", scatter_dimension=0, tiled=True
        ).astype(jnp.float32),
        lax.psum_scatter(
            local_grads[2].astype(jnp.bfloat16), "fsdp", scatter_dimension=0, tiled=True
        ).astype(jnp.float32),
        lax.psum_scatter(
            local_grads[3].astype(jnp.bfloat16), "fsdp", scatter_dimension=0, tiled=True
        ).astype(jnp.float32),
        lax.psum_scatter(
            local_grads[4].astype(jnp.bfloat16), "fsdp", scatter_dimension=0, tiled=True
        ).astype(jnp.float32),
        lax.psum_scatter(
            local_grads[5].astype(jnp.bfloat16), "fsdp", scatter_dimension=0, tiled=True
        ).astype(jnp.float32),
        lax.psum_scatter(
            local_grads[6].astype(jnp.bfloat16), "fsdp", scatter_dimension=0, tiled=True
        ).astype(jnp.float32),
        lax.psum_scatter(
            local_grads[7].astype(jnp.bfloat16), "fsdp", scatter_dimension=0, tiled=True
        ).astype(jnp.float32),
        lax.psum_scatter(
            local_grads[8].astype(jnp.bfloat16), "fsdp", scatter_dimension=0, tiled=True
        ).astype(jnp.float32),
        lax.psum_scatter(
            local_grads[9].astype(jnp.bfloat16), "fsdp", scatter_dimension=0, tiled=True
        ).astype(jnp.float32),
        lax.psum_scatter(
            local_grads[10].astype(jnp.bfloat16), "fsdp", scatter_dimension=0, tiled=True
        ).astype(jnp.float32),
        lax.psum_scatter(
            local_grads[11].astype(jnp.bfloat16), "fsdp", scatter_dimension=0, tiled=True
        ).astype(jnp.float32),
    )
    summed = lax.psum(
        (
            owned[0],
            owned[1],
            owned[2],
            owned[3],
            owned[4],
            owned[5],
            owned[6],
            owned[7],
            owned[8],
            owned[9],
            owned[10],
            owned[11],
        ),
        ("rep", "seq"),
    )
    return (
        output[None],
        input_gradient[None],
        summed[0],
        summed[1],
        summed[2],
        summed[3],
        summed[4],
        summed[5],
        summed[6],
        summed[7],
        summed[8],
        summed[9],
        summed[10],
        summed[11],
    )


MESH = pl.DeviceIdType.MESH
GROUP = 4
HALF = ROT // 2
SPAN = 512


def position_here():
    return (lax.axis_index("rep"), lax.axis_index("fsdp"), lax.axis_index("seq"))


def greet(partners):
    barrier = pltpu.get_barrier_semaphore()
    for partner in partners:
        pl.semaphore_signal(barrier, inc=1, device_id=partner, device_id_type=MESH)
    pl.semaphore_wait(barrier, len(partners))


def exchange_kernel(
    hid, cot, ints, vec, wm, we, hid_all, cot_all, ints_all, vec_all, wm_all, we_all, send, recv, local
):
    c, y, s = position_here()
    me = 2 * c + y
    core = (1 - c, y, s)
    across = (c, 1 - y, s)
    greet((core, across))
    head_cols = wm_all.shape[2] // 3
    width = wm.shape[1] // 3
    ff = we_all.shape[2]
    other = 2 * (1 - y) + c
    own = 2 * y + c

    def remote(index, src, dst, target):
        copy = pltpu.make_async_remote_copy(
            src_ref=src,
            dst_ref=dst,
            send_sem=send.at[index],
            recv_sem=recv.at[index],
            device_id=target,
            device_id_type=MESH,
        )
        copy.start()
        return copy

    first = [
        remote(0, hid, hid_all.at[me], across),
        remote(1, cot, cot_all.at[me], across),
        remote(2, ints, ints_all.at[me], across),
    ]
    rest = [remote(3, vec, vec_all.at[y], across)]
    for j in range(3):
        cols = pl.ds(pl.multiple_of(j * width + other * head_cols, head_cols), head_cols)
        rest.append(
            remote(
                4 + j, wm.at[:, cols], wm_all.at[y, :, pl.ds(j * head_cols, head_cols)], across
            )
        )
    cols = pl.ds(pl.multiple_of(other * ff, ff), ff)
    rest.append(remote(7, we.at[:, cols], we_all.at[y], across))
    rest += [
        remote(8, hid, hid_all.at[me], core),
        remote(9, cot, cot_all.at[me], core),
        remote(10, ints, ints_all.at[me], core),
    ]
    moves = [(hid, hid_all.at[me]), (cot, cot_all.at[me]), (ints, ints_all.at[me]), (vec, vec_all.at[y])]
    for j in range(3):
        cols = pl.ds(pl.multiple_of(j * width + own * head_cols, head_cols), head_cols)
        moves.append((wm.at[:, cols], wm_all.at[y, :, pl.ds(j * head_cols, head_cols)]))
    cols = pl.ds(pl.multiple_of(own * ff, ff), ff)
    moves.append((we.at[:, cols], we_all.at[y]))
    locals_ = []
    for index, (src, dst) in enumerate(moves):
        copy = pltpu.make_async_copy(src, dst, local.at[index])
        copy.start()
        locals_.append(copy)
    beside = 2 * c + 1 - y
    for index, (copy, full) in enumerate(zip(first, (hid_all, cot_all, ints_all))):
        copy.wait_recv()
        rest.append(remote(11 + index, full.at[beside], full.at[beside], core))
    for copy in first:
        copy.wait_send()
    for copy in rest:
        copy.wait()
    for copy in locals_:
        copy.wait()


def exchange(hid, cot, ints, vec, wm, we):
    tokens, width = hid.shape
    rows = wm.shape[0]
    any_spec = pl.BlockSpec(memory_space=pl.ANY)
    shapes = (
        jax.ShapeDtypeStruct((GROUP,) + hid.shape, hid.dtype),
        jax.ShapeDtypeStruct((GROUP,) + cot.shape, cot.dtype),
        jax.ShapeDtypeStruct((GROUP,) + ints.shape, ints.dtype),
        jax.ShapeDtypeStruct((2,) + vec.shape, vec.dtype),
        jax.ShapeDtypeStruct((2, rows, wm.shape[1] // GROUP), wm.dtype),
        jax.ShapeDtypeStruct((2, rows, we.shape[1] // GROUP), we.dtype),
    )
    return pl.pallas_call(
        exchange_kernel,
        out_shape=shapes,
        in_specs=[any_spec] * 6,
        out_specs=[any_spec] * 6,
        scratch_shapes=[
            pltpu.SemaphoreType.DMA((14,)),
            pltpu.SemaphoreType.DMA((14,)),
            pltpu.SemaphoreType.DMA((8,)),
        ],
        compiler_params=pltpu.CompilerParams(collective_id=0, has_side_effects=True),
        name="exchange",
    )(hid, cot, ints, vec, wm, we)


def scatter_kernel(count, src, dst, send, recv, local):
    c, y, s = position_here()
    rows, lanes = dst.shape[2], dst.shape[3]
    peers = [(c, y, lax.rem(s + d, count)) for d in range(1, count)]
    greet(peers)

    def part(target):
        return src.at[
            :,
            pl.ds(pl.multiple_of((target // 2) * rows, rows), rows),
            pl.ds(pl.multiple_of(lax.rem(target, 2) * lanes, lanes), lanes),
        ]

    copies = []
    for d in range(1, count):
        target = lax.rem(s + d, count)
        copy = pltpu.make_async_remote_copy(
            src_ref=part(target),
            dst_ref=dst.at[:, s],
            send_sem=send.at[d],
            recv_sem=recv.at[d],
            device_id=(c, y, target),
            device_id_type=MESH,
        )
        copy.start()
        copies.append(copy)
    own = pltpu.make_async_copy(part(s), dst.at[:, s], local)
    own.start()
    own.wait()
    for copy in copies:
        copy.wait()


def gather_kernel(count, src, dst, send, recv, local):
    c, y, s = position_here()
    rows, lanes = src.shape[2], src.shape[3]
    peers = [(c, y, lax.rem(s + d, count)) for d in range(1, count)]
    greet(peers)
    place = dst.at[
        :,
        pl.ds(pl.multiple_of((s // 2) * rows, rows), rows),
        pl.ds(pl.multiple_of(lax.rem(s, 2) * lanes, lanes), lanes),
    ]
    copies = []
    for d in range(1, count):
        target = lax.rem(s + d, count)
        copy = pltpu.make_async_remote_copy(
            src_ref=src.at[:, target],
            dst_ref=place,
            send_sem=send.at[d],
            recv_sem=recv.at[d],
            device_id=(c, y, target),
            device_id_type=MESH,
        )
        copy.start()
        copies.append(copy)
    own = pltpu.make_async_copy(src.at[:, s], place, local)
    own.start()
    own.wait()
    for copy in copies:
        copy.wait()


def swap_tokens(kernel, identity, name, array, shape, count):
    any_spec = pl.BlockSpec(memory_space=pl.ANY)
    return pl.pallas_call(
        functools.partial(kernel, count),
        out_shape=jax.ShapeDtypeStruct(shape, array.dtype),
        in_specs=[any_spec],
        out_specs=any_spec,
        scratch_shapes=[
            pltpu.SemaphoreType.DMA((count,)),
            pltpu.SemaphoreType.DMA((count,)),
            pltpu.SemaphoreType.DMA,
        ],
        compiler_params=pltpu.CompilerParams(collective_id=identity, has_side_effects=True),
        name=name,
    )(array)


def attention_kernel(
    ints,
    parts,
    cosine,
    sine_up,
    sine_down,
    out,
    masked,
    flat,
    scores,
    slopes,
    key_sum,
    value_sum,
    mixed_sum,
    query_sum,
    units,
    pieces,
):
    length = parts.shape[1]
    scale = 1.0 / math.sqrt(HEAD)
    blocks = length // SPAN
    lanes = lax.broadcasted_iota(jnp.int32, (UNIT, 2 * HEAD), 1)
    lower = lanes < HEAD

    def arrange(index, carry):
        here = pl.multiple_of(index * UNIT, UNIT)
        place = pl.multiple_of(ints[0, index] * UNIT, UNIT)
        for which in range(4):
            rows = parts[which, pl.ds(here, UNIT), :].astype(jnp.float32)
            if which == 0:
                rows = rows * scale
            masked[which, 0, pl.ds(place, UNIT), :] = jnp.where(lower, rows, 0.0).astype(
                jnp.bfloat16
            )
            masked[which, 1, pl.ds(place, UNIT), :] = jnp.where(lower, 0.0, rows).astype(
                jnp.bfloat16
            )
            flat[which, :, pl.ds(place, UNIT)] = rows.T.astype(jnp.bfloat16)
        return carry

    lax.fori_loop(0, units, arrange, 0)
    key_sum[...] = jnp.zeros_like(key_sum)
    value_sum[...] = jnp.zeros_like(value_sum)

    def labels(positions):
        found = jnp.full(positions.shape, -1, jnp.int32)
        for piece in range(pieces):
            start = ints[0, units + piece]
            found = jnp.where(
                (positions >= start) & (positions < start + PIECE), piece, found
            )
        return found

    def dot(a, b):
        return jnp.dot(a, b, preferred_element_type=jnp.float32)

    for block in range(blocks):
        begin = block * SPAN
        last = SPAN + (UNIT if block + 1 < blocks else 0)
        columns = pl.ds(begin, SPAN)
        row_at = begin + lax.broadcasted_iota(jnp.int32, (1, SPAN), 1)
        col_at = begin + lax.broadcasted_iota(jnp.int32, (last, 1), 0)
        row_lab = labels(row_at)
        col_lab = labels(col_at)
        allowed = (col_at <= row_at) | (
            (col_lab == row_lab) & (row_lab >= 0)
        )

        def one_head(head, carry):
            queries = flat[0, :, columns]
            grads = flat[3, :, columns]
            side = pl.ds(pl.multiple_of(head * HEAD, HEAD), HEAD)

            def score_tile(start, size, top, mask):
                rows = pl.ds(start, size)
                tile = dot(masked[1, head, rows, :], queries)
                if mask is not None:
                    tile = jnp.where(mask, tile, NEGATIVE)
                scores[rows, :] = tile
                return jnp.maximum(top, jnp.max(tile, axis=0, keepdims=True))

            top = lax.fori_loop(
                0,
                block,
                lambda j, top: score_tile(pl.multiple_of(j * SPAN, SPAN), SPAN, top, None),
                jnp.full((1, SPAN), NEGATIVE, jnp.float32),
            )
            top = score_tile(begin, last, top, allowed)

            def weight_tile(start, size, sums):
                total, delta = sums
                rows = pl.ds(start, size)
                weights = jnp.exp(scores[rows, :] - top)
                slope = dot(masked[2, head, rows, :], grads)
                scores[rows, :] = weights
                slopes[rows, :] = slope
                return (
                    total + jnp.sum(weights, axis=0, keepdims=True),
                    delta + jnp.sum(weights * slope, axis=0, keepdims=True),
                )

            zero = jnp.zeros((1, SPAN), jnp.float32)
            sums = lax.fori_loop(
                0,
                block,
                lambda j, sums: weight_tile(pl.multiple_of(j * SPAN, SPAN), SPAN, sums),
                (zero, zero),
            )
            total, delta = weight_tile(begin, last, sums)
            inverse = 1.0 / total
            delta = delta * inverse

            def grad_tile(start, size, sums):
                mixed, query = sums
                rows = pl.ds(start, size)
                probs = scores[rows, :] * inverse
                grad = (probs * (slopes[rows, :] - delta)).astype(jnp.bfloat16)
                probs = probs.astype(jnp.bfloat16)
                value_sum[rows, :] += dot(probs, masked[3, head, columns, :])
                key_sum[rows, :] += dot(grad, masked[0, head, columns, :])
                mixed = mixed + dot(flat[2, side, rows], probs)
                query = query + dot(flat[1, side, rows], grad)
                return (mixed, query)

            none = jnp.zeros((HEAD, SPAN), jnp.float32)
            sums = lax.fori_loop(
                0,
                block,
                lambda j, sums: grad_tile(pl.multiple_of(j * SPAN, SPAN), SPAN, sums),
                (none, none),
            )
            mixed, query = grad_tile(begin, last, sums)
            mixed_sum[side, columns] = mixed
            query_sum[side, columns] = query * scale
            return carry

        lax.fori_loop(0, 2, one_head, 0)

    def turn_back(rows, at):
        up = pltpu.roll(rows, 2 * HEAD - HALF, 1)
        down = pltpu.roll(rows, HALF, 1)
        return (
            rows * cosine[at, :] + up * sine_up[at, :] - down * sine_down[at, :]
        )

    def finish(index, carry):
        at = pl.ds(pl.multiple_of(index * UNIT, UNIT), UNIT)
        key_sum[at, :] = turn_back(key_sum[at, :], at)
        masked[0, 0, at, :] = mixed_sum[:, at].T.astype(jnp.bfloat16)
        masked[1, 0, at, :] = turn_back(query_sum[:, at].T, at).astype(jnp.bfloat16)
        return carry

    lax.fori_loop(0, units, finish, 0)

    def restore(index, carry):
        here = pl.ds(pl.multiple_of(index * UNIT, UNIT), UNIT)
        place = pl.ds(pl.multiple_of(ints[0, index] * UNIT, UNIT), UNIT)
        out[0, here, :] = masked[0, 0, place, :]
        out[1, here, :] = masked[1, 0, place, :]
        out[2, here, :] = key_sum[place, :].astype(jnp.bfloat16)
        out[3, here, :] = value_sum[place, :].astype(jnp.bfloat16)
        return carry

    lax.fori_loop(0, units, restore, 0)


def attend(ints, parts, cosine, sine_up, sine_down, units, pieces):
    length = parts.shape[1]
    vmem = pl.BlockSpec(memory_space=pltpu.VMEM)
    flops = 6 * 2 * 2 * HEAD * length * length // 2
    return pl.pallas_call(
        functools.partial(attention_kernel, units=units, pieces=pieces),
        out_shape=jax.ShapeDtypeStruct(parts.shape, parts.dtype),
        in_specs=[pl.BlockSpec(memory_space=pltpu.SMEM)] + [vmem] * 4,
        out_specs=vmem,
        scratch_shapes=[
            pltpu.VMEM((4, 2, length, 2 * HEAD), jnp.bfloat16),
            pltpu.VMEM((4, 2 * HEAD, length), jnp.bfloat16),
            pltpu.VMEM((length, SPAN), jnp.float32),
            pltpu.VMEM((length, SPAN), jnp.float32),
            pltpu.VMEM((length, 2 * HEAD), jnp.float32),
            pltpu.VMEM((length, 2 * HEAD), jnp.float32),
            pltpu.VMEM((2 * HEAD, length), jnp.float32),
            pltpu.VMEM((2 * HEAD, length), jnp.float32),
        ],
        compiler_params=pltpu.CompilerParams(vmem_limit_bytes=48 << 20),
        cost_estimate=pl.CostEstimate(
            flops=flops * 4, bytes_accessed=8 << 20, transcendentals=length * length
        ),
        name="attend",
    )(ints, parts, cosine, sine_up, sine_down)


def total_kernel(outs, terms, out_sum, term_sum, near, far, pair, send, recv):
    c, y, s = position_here()
    core = (1 - c, y, s)
    across = (c, 1 - y, s)
    greet((core, across))
    copies = []
    for index, src in enumerate((outs, terms)):
        copy = pltpu.make_async_remote_copy(
            src_ref=src.at[pl.ds(2 * (1 - c), 2)],
            dst_ref=near.at[index],
            send_sem=send.at[index],
            recv_sem=recv.at[index],
            device_id=core,
            device_id_type=MESH,
        )
        copy.start()
        copies.append(copy)
    later = []
    for index, src in enumerate((outs, terms)):
        copies[index].wait()
        pair[index] = (
            src[2 * c + 1 - y].astype(jnp.float32) + near[index, 1 - y].astype(jnp.float32)
        ).astype(jnp.bfloat16)
        copy = pltpu.make_async_remote_copy(
            src_ref=pair.at[index],
            dst_ref=far.at[index],
            send_sem=send.at[2 + index],
            recv_sem=recv.at[2 + index],
            device_id=across,
            device_id_type=MESH,
        )
        copy.start()
        later.append(copy)
    for index, (src, dst) in enumerate(((outs, out_sum), (terms, term_sum))):
        dst[...] = src[2 * c + y].astype(jnp.float32) + near[index, y].astype(jnp.float32)
    for index, dst in enumerate((out_sum, term_sum)):
        later[index].wait()
        dst[...] += far[index].astype(jnp.float32)


def total_group(outs, terms):
    shape = outs.shape[1:]
    vmem = pl.BlockSpec(memory_space=pltpu.VMEM)
    return pl.pallas_call(
        total_kernel,
        out_shape=(jax.ShapeDtypeStruct(shape, jnp.float32),) * 2,
        in_specs=[vmem] * 2,
        out_specs=[vmem] * 2,
        scratch_shapes=[
            pltpu.VMEM((2, 2) + shape, jnp.bfloat16),
            pltpu.VMEM((2,) + shape, jnp.bfloat16),
            pltpu.VMEM((2,) + shape, jnp.bfloat16),
            pltpu.SemaphoreType.DMA((4,)),
            pltpu.SemaphoreType.DMA((4,)),
        ],
        compiler_params=pltpu.CompilerParams(
            collective_id=3, has_side_effects=True, vmem_limit_bytes=32 << 20
        ),
        name="total_group",
    )(outs, terms)


def lane_tables(positions, lanes):
    lane = jnp.arange(lanes, dtype=jnp.int32) % HEAD
    inverse = jnp.exp((lane % HALF).astype(jnp.float32) * (-2.0 * math.log(10000.0) / ROT))
    angles = positions.astype(jnp.float32)[:, None] * inverse[None, :]
    cosine = jnp.where(lane[None, :] < ROT, jnp.cos(angles), 1.0)
    sine = jnp.sin(angles)
    up = jnp.where(lane[None, :] < HALF, sine, 0.0)
    down = jnp.where((lane[None, :] >= HALF) & (lane[None, :] < ROT), sine, 0.0)
    return (cosine, up, down)


def turn_lanes(values, tables):
    cosine, up, down = tables
    return (
        values * cosine
        - jnp.roll(values, -HALF, axis=1) * up
        + jnp.roll(values, HALF, axis=1) * down
    )


def group_body(
    hidden_states,
    unit_order,
    piece_starts,
    first_gain,
    first_shift,
    second_gain,
    second_shift,
    merged_weight,
    merged_bias,
    output_weight,
    output_bias,
    expand_weight,
    expand_bias,
    contract_weight,
    contract_bias,
    out_cotangent,
):
    c, y, s = position_here()
    quarter = 2 * y + c
    count = lax.axis_size("seq")
    tokens, width = hidden_states.shape[1:]
    length = tokens * count
    units = unit_order.shape[1]
    pieces = piece_starts.shape[1]
    rows = GROUP * tokens
    part = width // GROUP
    ff_part = expand_weight.shape[1] // GROUP
    vectors = (
        first_gain,
        first_shift,
        second_gain,
        second_shift,
        merged_bias,
        output_bias,
        expand_bias,
        contract_bias,
    )
    sizes = [v.shape[0] for v in vectors]
    packed = jnp.concatenate(vectors).reshape(-1, 128)
    ints = jnp.concatenate([unit_order[0], piece_starts[0]])
    ints = jnp.broadcast_to(jnp.pad(ints, (0, 128 - ints.shape[0]))[None], (8, 128))
    hid_all, cot_all, ints_all, vec_all, wm_all, we_all = exchange(
        hidden_states[0], out_cotangent[0], ints, packed, merged_weight, expand_weight
    )
    vec_all = vec_all.reshape(2, -1)
    whole = []
    at = 0
    for size in sizes:
        whole.append(vec_all[:, at : at + size].reshape(-1).astype(jnp.float32))
        at += size
    gain_one, shift_one, gain_two, shift_two, bias_merged, bias_out, bias_expand, bias_contract = whole
    wm = wm_all.reshape(width, 3 * part)
    we = we_all.reshape(width, ff_part)
    wo = lax.dynamic_slice_in_dim(output_weight, c * part, part, 0)
    wc = lax.dynamic_slice_in_dim(contract_weight, c * ff_part, ff_part, 0)
    cots = cot_all.reshape(rows, width)
    hidden = hid_all.reshape(rows, width).astype(jnp.float32)
    mean = jnp.mean(hidden, axis=1, keepdims=True)
    centred = hidden - mean
    rstd = lax.rsqrt(jnp.mean(centred * centred, axis=1, keepdims=True) + EPS)
    xhat = centred * rstd
    first = (xhat * gain_one + shift_one).astype(jnp.bfloat16)
    second = (xhat * gain_two + shift_two).astype(jnp.bfloat16)
    own_bias = lax.dynamic_slice_in_dim(
        bias_merged.reshape(3, GROUP, part), quarter, 1, 1
    ).reshape(3 * part)
    merged = jnp.dot(first, wm, preferred_element_type=jnp.float32) + own_bias
    own_units = tokens // UNIT
    local_units = lax.dynamic_slice_in_dim(ints_all[:, 0, :], s * own_units, own_units, 1)
    positions = (
        local_units.reshape(-1)[:, None] * UNIT + jnp.arange(UNIT, dtype=jnp.int32)[None, :]
    ).reshape(-1)
    tables = lane_tables(positions, part)
    queries = turn_lanes(merged[:, :part], tables).astype(jnp.bfloat16)
    keys = turn_lanes(merged[:, part : 2 * part], tables).astype(jnp.bfloat16)
    values = merged[:, 2 * part :].astype(jnp.bfloat16)
    grad_mixed = lax.dot_general(
        cots, wo, (((1,), (1,)), ((), ())), preferred_element_type=jnp.float32
    ).astype(jnp.bfloat16)
    sent = jnp.stack([queries, keys, values, grad_mixed])
    got = swap_tokens(
        scatter_kernel, 1, "scatter", sent, (4, count, tokens, 2 * HEAD), count
    ).reshape(4, length, 2 * HEAD)
    own_ints = lax.dynamic_index_in_dim(ints_all[:, 0, :], s // 2, 0, keepdims=True)
    sorted_tables = lane_tables(jnp.arange(length, dtype=jnp.int32), 2 * HEAD)
    done = attend(own_ints, got, *sorted_tables, units, pieces)
    back = swap_tokens(
        gather_kernel,
        2,
        "gather",
        done.reshape(4, count, tokens, 2 * HEAD),
        (4, rows, part),
        count,
    )
    mixed = back[0]
    grad_merged = jnp.concatenate([back[1], back[2], back[3]], axis=1)

    own_expand = lax.dynamic_slice_in_dim(bias_expand, quarter * ff_part, ff_part, 0)
    expanded = jnp.dot(second, we, preferred_element_type=jnp.float32) + own_expand
    activated, gelu_pull = jax.vjp(gelu_exact, expanded)
    active = activated.astype(jnp.bfloat16)
    grad_active = lax.dot_general(
        cots, wc, (((1,), (1,)), ((), ())), preferred_element_type=jnp.float32
    )
    grad_expanded = gelu_pull(grad_active)[0].astype(jnp.bfloat16)

    def against(a, b):
        return lax.dot_general(a, b, (((0,), (0,)), ((), ())), preferred_element_type=jnp.float32)

    def swap_halves(own, other):
        got = lax.ppermute(other, "fsdp", [(0, 1), (1, 0)])
        return jnp.where(y == 0, jnp.stack([own, got]), jnp.stack([got, own]))

    half = width // 2
    d_expand = against(second, grad_expanded).astype(jnp.bfloat16)
    d_contract = against(active, cots).astype(jnp.bfloat16)
    feed_part = jnp.concatenate(
        [d_expand[:half], d_expand[half:], d_contract[:half], d_contract[half:]], axis=1
    )
    feed_part = lax.psum_scatter(feed_part, "seq", scatter_dimension=0, tiled=True)
    d_merged = against(first, grad_merged).astype(jnp.bfloat16)
    d_output = against(mixed, cots).astype(jnp.bfloat16)
    d_output = jnp.concatenate([d_output[:, :half], d_output[:, half:]], axis=0)
    attn_part = jnp.concatenate([d_merged[:half], d_merged[half:], d_output], axis=1)
    attn_part = lax.psum_scatter(attn_part, "seq", scatter_dimension=0, tiled=True)

    def spread(piece, cols):
        parts = piece[:, : 2 * cols].reshape(-1, 2, cols)
        own = lax.dynamic_index_in_dim(parts, y, 1, keepdims=False)
        other = lax.dynamic_index_in_dim(parts, 1 - y, 1, keepdims=False)
        pair = swap_halves(own, other)
        piece = jnp.concatenate([pair[0], pair[1], piece[:, 2 * cols :]], axis=1)
        piece = lax.all_gather(piece, "seq", axis=0, tiled=True)
        return lax.all_gather(piece, "rep", axis=0)

    feed_all = spread(feed_part, ff_part)
    attn_all = spread(attn_part, 3 * part)
    expand_out = feed_all[:, :, : 2 * ff_part].reshape(2, half, 2, ff_part)
    expand_out = expand_out.transpose(1, 2, 0, 3).reshape(half, GROUP * ff_part)
    contract_out = feed_all[:, :, 2 * ff_part :].reshape(2, half, 2, width)
    contract_out = contract_out.transpose(0, 2, 1, 3).reshape(2 * ff_part, width)
    merged_out = attn_all[:, :, : 6 * part].reshape(2, half, 2, 3, part)
    merged_out = merged_out.transpose(1, 3, 2, 0, 4).reshape(half, 3 * width)
    output_out = attn_all[:, :, 6 * part :].reshape(2, 2, part, half)
    output_out = output_out.transpose(0, 2, 1, 3).reshape(2 * part, width)

    out_partial = jnp.dot(mixed, wo, preferred_element_type=jnp.float32) + jnp.dot(
        active, wc, preferred_element_type=jnp.float32
    )
    grad_first = lax.dot_general(
        grad_merged, wm, (((1,), (1,)), ((), ())), preferred_element_type=jnp.float32
    )
    grad_second = lax.dot_general(
        grad_expanded, we, (((1,), (1,)), ((), ())), preferred_element_type=jnp.float32
    )
    term_partial = grad_first * gain_one + grad_second * gain_two
    shape = (GROUP, tokens, width)
    out_sum, term_sum = total_group(
        out_partial.astype(jnp.bfloat16).reshape(shape),
        term_partial.astype(jnp.bfloat16).reshape(shape),
    )
    own_hidden = hidden_states[0].astype(jnp.float32)
    own_mean = jnp.mean(own_hidden, axis=1, keepdims=True)
    own_centred = own_hidden - own_mean
    own_rstd = lax.rsqrt(jnp.mean(own_centred * own_centred, axis=1, keepdims=True) + EPS)
    own_xhat = own_centred * own_rstd
    output = (own_hidden + out_sum + bias_out + bias_contract).astype(jnp.bfloat16)
    upstream = out_cotangent[0].astype(jnp.float32)
    input_gradient = upstream + own_rstd * (
        term_sum
        - jnp.mean(term_sum, axis=1, keepdims=True)
        - own_xhat * jnp.mean(term_sum * own_xhat, axis=1, keepdims=True)
    )
    merged_bias_part = jnp.sum(grad_merged.astype(jnp.float32), axis=0).reshape(3, 1, part)
    slot = (jnp.arange(GROUP, dtype=jnp.int32) == quarter).astype(jnp.float32)
    merged_bias_part = (merged_bias_part * slot[None, :, None]).reshape(-1)
    expand_bias_part = jnp.sum(grad_expanded.astype(jnp.float32), axis=0)
    expand_bias_part = (expand_bias_part[None, :] * slot[:, None]).reshape(-1)
    small = jnp.concatenate(
        [
            jnp.sum(grad_first * xhat, axis=0),
            jnp.sum(grad_first, axis=0),
            jnp.sum(grad_second * xhat, axis=0),
            jnp.sum(grad_second, axis=0),
            jnp.sum(upstream, axis=0),
            merged_bias_part,
            expand_bias_part,
        ]
    )
    small = lax.psum(small, ("rep", "fsdp", "seq"))

    def own_half(begin, size):
        return lax.dynamic_slice_in_dim(small, begin + y * (size // 2), size // 2, 0)

    row_total = own_half(4 * width, width)
    return (
        output[None],
        input_gradient[None],
        own_half(0, width),
        own_half(width, width),
        own_half(2 * width, width),
        own_half(3 * width, width),
        merged_out.astype(jnp.float32),
        own_half(5 * width, 3 * width),
        output_out.astype(jnp.float32),
        row_total,
        expand_out.astype(jnp.float32),
        own_half(8 * width, GROUP * ff_part),
        contract_out.astype(jnp.float32),
        row_total,
    )


def fits_groups(mesh, args):
    hidden, order = args[0], args[1]
    count = mesh.shape["seq"]
    tokens = hidden.shape[1] // count
    heads = hidden.shape[2] // HEAD
    return (
        mesh.shape["rep"] == 2
        and mesh.shape["fsdp"] == 2
        and hidden.shape[0] == GROUP
        and count == heads // 2
        and tokens % UNIT == 0
        and hidden.shape[1] % SPAN == 0
        and order.shape[1] + args[2].shape[1] <= 128
    )


def solution(mesh):
    in_specs = (
        P(("rep", "fsdp"), "seq", None),
        P(("rep", "fsdp"), None),
        P(("rep", "fsdp"), None),
        P("fsdp"),
        P("fsdp"),
        P("fsdp"),
        P("fsdp"),
        P("fsdp", None),
        P("fsdp"),
        P("fsdp", None),
        P("fsdp"),
        P("fsdp", None),
        P("fsdp"),
        P("fsdp", None),
        P("fsdp"),
        P(("rep", "fsdp"), "seq", None),
    )
    out_specs = (
        P(("rep", "fsdp"), "seq", None),
        P(("rep", "fsdp"), "seq", None),
        P("fsdp"),
        P("fsdp"),
        P("fsdp"),
        P("fsdp"),
        P("fsdp", None),
        P("fsdp"),
        P("fsdp", None),
        P("fsdp"),
        P("fsdp", None),
        P("fsdp"),
        P("fsdp", None),
        P("fsdp"),
    )

    def run(*args):
        chosen = group_body if fits_groups(mesh, args) else body
        mapped = jax.shard_map(
            chosen, mesh=mesh, in_specs=in_specs, out_specs=out_specs, check_vma=False
        )
        return mapped(*args)

    return run
```

```python
import functools
import math

import jax
import jax.numpy as jnp
from jax import lax
from jax.experimental import pallas as pl
from jax.experimental.pallas import tpu as pltpu
from jax.sharding import PartitionSpec as P

HEAD = 64
ROT = 16
UNIT = 128
PIECE = 256


EPS = 1e-05
NEGATIVE = -1e30


def norm_rows(values, gain, shift):
    mean = jnp.mean(values, axis=-1, keepdims=True)
    centred = values - mean
    spread = jnp.mean(centred * centred, axis=-1, keepdims=True)
    return centred * lax.rsqrt(spread + EPS) * gain + shift


def gelu_exact(values):
    return jax.nn.gelu(values, approximate=False)


def rotary_tables(positions):
    index = jnp.arange(ROT // 2, dtype=jnp.float32)
    inverse = jnp.exp(index * (-2.0 * math.log(10000.0) / ROT))
    angles = positions.astype(jnp.float32)[:, None] * inverse[None, :]
    angles = jnp.concatenate([angles, angles], axis=1)
    return (jnp.cos(angles), jnp.sin(angles))


def rotate(values, cosine, sine):
    part = values[..., :ROT]
    turned = jnp.concatenate([-part[..., ROT // 2 :], part[..., : ROT // 2]], axis=-1)
    moved = part * cosine[:, None, :] + turned * sine[:, None, :]
    return jnp.concatenate([moved, values[..., ROT:]], axis=-1)


def unit_positions(order):
    offsets = jnp.arange(UNIT, dtype=jnp.int32)
    return (order[:, None] * UNIT + offsets[None, :]).reshape(-1)


def piece_labels(positions, starts):
    inside = (positions[:, None] >= starts[None, :]) & (
        positions[:, None] < starts[None, :] + PIECE
    )
    labels = jnp.arange(1, starts.shape[0] + 1, dtype=jnp.int32)
    return jnp.sum(jnp.where(inside, labels[None, :], 0), axis=1) - 1


def visible(row_pos, row_lab, col_pos, col_lab):
    earlier = col_pos[None, :] <= row_pos[:, None]
    same = (row_lab[:, None] == col_lab[None, :]) & (row_lab[:, None] >= 0)
    return earlier | same


def merged_parts(first, merged_weight, merged_bias, cosine, sine):
    tokens = first.shape[0]
    width = first.shape[1]
    heads = width // HEAD
    merged = jnp.dot(first, merged_weight, preferred_element_type=jnp.float32) + merged_bias.astype(
        jnp.float32
    )
    queries = rotate(merged[:, :width].reshape(tokens, heads, HEAD), cosine, sine).astype(
        jnp.bfloat16
    )
    keys = rotate(merged[:, width : 2 * width].reshape(tokens, heads, HEAD), cosine, sine)
    keys = keys.reshape(tokens, width).astype(jnp.bfloat16)
    values = merged[:, 2 * width :].astype(jnp.bfloat16)
    return (queries, keys, values)


def block_view(queries, keys_all, values_all, row_pos, row_lab, col_pos, col_lab, span):
    heads = queries.shape[1]
    scale = 1.0 / math.sqrt(HEAD)

    def view(index):
        start = index * span
        key_rows = lax.dynamic_slice_in_dim(keys_all, start, span, 0).reshape(span, heads, HEAD)
        value_rows = lax.dynamic_slice_in_dim(values_all, start, span, 0).reshape(span, heads, HEAD)
        scores = (
            jnp.einsum("thd,khd->htk", queries, key_rows, preferred_element_type=jnp.float32)
            * scale
        )
        allowed = visible(
            row_pos,
            row_lab,
            lax.dynamic_slice_in_dim(col_pos, start, span, 0),
            lax.dynamic_slice_in_dim(col_lab, start, span, 0),
        )[None]
        return (scores, allowed, key_rows, value_rows)

    return view


def log_sums(view, count, heads, tokens):

    def log_step(carry, index):
        top, total = carry
        scores, allowed, key_rows, value_rows = view(index)
        masked = jnp.where(allowed, scores, NEGATIVE)
        newer = jnp.maximum(top, jnp.max(masked, axis=-1))
        terms = jnp.where(allowed, jnp.exp(masked - newer[..., None]), 0.0)
        total = total * jnp.exp(top - newer) + jnp.sum(terms, axis=-1)
        return ((newer, total), None)

    begin = (
        jnp.full((heads, tokens), NEGATIVE, jnp.float32),
        jnp.zeros((heads, tokens), jnp.float32),
    )
    (top, total), unused = lax.scan(log_step, begin, jnp.arange(count, dtype=jnp.int32))
    return top + jnp.log(total)


def mix_values(view, count, logsum, heads, tokens, grad_rows):

    def mix_step(carry, index):
        mixed, delta = carry
        scores, allowed, key_rows, value_rows = view(index)
        weights = jnp.where(allowed, jnp.exp(scores - logsum[..., None]), 0.0)
        mixed = mixed + jnp.einsum(
            "htk,khd->thd",
            weights.astype(jnp.bfloat16),
            value_rows,
            preferred_element_type=jnp.float32,
        )
        if grad_rows is not None:
            slopes = jnp.einsum(
                "thd,khd->htk", grad_rows, value_rows, preferred_element_type=jnp.float32
            )
            delta = delta + jnp.sum(weights * slopes, axis=-1)
        return ((mixed, delta), None)

    begin = (jnp.zeros((tokens, heads, HEAD), jnp.float32), jnp.zeros((heads, tokens), jnp.float32))
    (mixed, delta), unused = lax.scan(mix_step, begin, jnp.arange(count, dtype=jnp.int32))
    return (mixed, delta)


def attend_back(view, count, logsum, delta, grad_rows, queries):
    scale = 1.0 / math.sqrt(HEAD)

    def attend_step(carry, index):
        scores, allowed, key_rows, value_rows = view(index)
        weights = jnp.where(allowed, jnp.exp(scores - logsum[..., None]), 0.0)
        slopes = jnp.einsum(
            "thd,khd->htk", grad_rows, value_rows, preferred_element_type=jnp.float32
        )
        grad_scores = (weights * (slopes - delta[..., None])).astype(jnp.bfloat16)
        carry = carry + jnp.einsum(
            "htk,khd->thd", grad_scores, key_rows, preferred_element_type=jnp.float32
        )
        key_grad = jnp.einsum(
            "htk,thd->khd", grad_scores, queries, preferred_element_type=jnp.float32
        )
        value_grad = jnp.einsum(
            "htk,thd->khd",
            weights.astype(jnp.bfloat16),
            grad_rows,
            preferred_element_type=jnp.float32,
        )
        span = key_rows.shape[0]
        joined = jnp.concatenate(
            [key_grad.reshape(span, -1) * scale, value_grad.reshape(span, -1)], axis=1
        )
        return (carry, joined)

    begin = jnp.zeros(queries.shape, jnp.float32)
    grad_query, parts = lax.scan(attend_step, begin, jnp.arange(count, dtype=jnp.int32))
    return (grad_query * scale, parts)


def body(
    hidden_states,
    unit_order,
    piece_starts,
    first_gain,
    first_shift,
    second_gain,
    second_shift,
    merged_weight,
    merged_bias,
    output_weight,
    output_bias,
    expand_weight,
    expand_bias,
    contract_weight,
    contract_bias,
    out_cotangent,
):
    shards = (
        first_gain,
        first_shift,
        second_gain,
        second_shift,
        merged_weight,
        merged_bias,
        output_weight,
        output_bias,
        expand_weight,
        expand_bias,
        contract_weight,
        contract_bias,
    )
    gathered = (
        lax.all_gather(shards[0], "fsdp", axis=0, tiled=True),
        lax.all_gather(shards[1], "fsdp", axis=0, tiled=True),
        lax.all_gather(shards[2], "fsdp", axis=0, tiled=True),
        lax.all_gather(shards[3], "fsdp", axis=0, tiled=True),
        lax.all_gather(shards[4], "fsdp", axis=0, tiled=True),
        lax.all_gather(shards[5], "fsdp", axis=0, tiled=True),
        lax.all_gather(shards[6], "fsdp", axis=0, tiled=True),
        lax.all_gather(shards[7], "fsdp", axis=0, tiled=True),
        lax.all_gather(shards[8], "fsdp", axis=0, tiled=True),
        lax.all_gather(shards[9], "fsdp", axis=0, tiled=True),
        lax.all_gather(shards[10], "fsdp", axis=0, tiled=True),
        lax.all_gather(shards[11], "fsdp", axis=0, tiled=True),
    )
    hidden = hidden_states[0].astype(jnp.float32)
    tokens = hidden.shape[0]
    width = hidden.shape[1]
    heads = width // HEAD
    length = tokens * lax.axis_size("seq")
    span = min(length, 512)
    count = length // span
    col_pos = unit_positions(unit_order[0])
    col_lab = piece_labels(col_pos, piece_starts[0])
    offset = lax.axis_index("seq") * tokens
    row_pos = lax.dynamic_slice_in_dim(col_pos, offset, tokens, 0)
    row_lab = lax.dynamic_slice_in_dim(col_lab, offset, tokens, 0)
    cosine, sine = rotary_tables(row_pos)
    first = norm_rows(
        hidden, gathered[0].astype(jnp.float32), gathered[1].astype(jnp.float32)
    ).astype(jnp.bfloat16)
    queries, keys, values = merged_parts(first, gathered[4], gathered[5], cosine, sine)
    keys_all, values_all = (
        lax.all_gather(keys, "seq", axis=0, tiled=True),
        lax.all_gather(values, "seq", axis=0, tiled=True),
    )
    view = block_view(queries, keys_all, values_all, row_pos, row_lab, col_pos, col_lab, span)
    logsum = log_sums(view, count, heads, tokens)
    mixed, unused = mix_values(view, count, logsum, heads, tokens, None)
    mixed = mixed.reshape(tokens, width).astype(jnp.bfloat16)
    attention = jnp.dot(mixed, gathered[6], preferred_element_type=jnp.float32) + gathered[
        7
    ].astype(jnp.float32)
    second = norm_rows(
        hidden, gathered[2].astype(jnp.float32), gathered[3].astype(jnp.float32)
    ).astype(jnp.bfloat16)
    expanded = jnp.dot(second, gathered[8], preferred_element_type=jnp.float32) + gathered[
        9
    ].astype(jnp.float32)
    active = gelu_exact(expanded).astype(jnp.bfloat16)
    feed = jnp.dot(active, gathered[10], preferred_element_type=jnp.float32) + gathered[11].astype(
        jnp.float32
    )
    output = (hidden + attention + feed).astype(jnp.bfloat16)
    weights = (
        lax.all_gather(shards[0], "fsdp", axis=0, tiled=True),
        lax.all_gather(shards[1], "fsdp", axis=0, tiled=True),
        lax.all_gather(shards[2], "fsdp", axis=0, tiled=True),
        lax.all_gather(shards[3], "fsdp", axis=0, tiled=True),
        lax.all_gather(shards[4], "fsdp", axis=0, tiled=True),
        lax.all_gather(shards[5], "fsdp", axis=0, tiled=True),
        lax.all_gather(shards[6], "fsdp", axis=0, tiled=True),
        lax.all_gather(shards[7], "fsdp", axis=0, tiled=True),
        lax.all_gather(shards[8], "fsdp", axis=0, tiled=True),
        lax.all_gather(shards[9], "fsdp", axis=0, tiled=True),
        lax.all_gather(shards[10], "fsdp", axis=0, tiled=True),
        lax.all_gather(shards[11], "fsdp", axis=0, tiled=True),
    )
    cotangent = out_cotangent[0]
    upstream = cotangent.astype(jnp.float32)
    normed_one, first_pull = jax.vjp(
        norm_rows, hidden, weights[0].astype(jnp.float32), weights[1].astype(jnp.float32)
    )
    first = normed_one.astype(jnp.bfloat16)
    queries, keys, values = merged_parts(first, weights[4], weights[5], cosine, sine)
    keys_back, values_back = (
        lax.all_gather(keys, "seq", axis=0, tiled=True),
        lax.all_gather(values, "seq", axis=0, tiled=True),
    )
    view = block_view(queries, keys_back, values_back, row_pos, row_lab, col_pos, col_lab, span)
    grad_mixed = jnp.einsum(
        "te,de->td", cotangent, weights[6], preferred_element_type=jnp.float32
    ).astype(jnp.bfloat16)
    grad_rows = grad_mixed.reshape(tokens, heads, HEAD)
    mixed, delta = mix_values(view, count, logsum, heads, tokens, grad_rows)
    mixed = mixed.reshape(tokens, width).astype(jnp.bfloat16)
    grad_query, parts = attend_back(view, count, logsum, delta, grad_rows, queries)
    term = parts.reshape(length, 2 * width)
    own_grads = lax.psum_scatter(
        term.astype(jnp.bfloat16), "seq", scatter_dimension=0, tiled=True
    ).astype(jnp.float32)
    normed_two, second_pull = jax.vjp(
        norm_rows, hidden, weights[2].astype(jnp.float32), weights[3].astype(jnp.float32)
    )
    second = normed_two.astype(jnp.bfloat16)
    expanded = jnp.dot(second, weights[8], preferred_element_type=jnp.float32) + weights[9].astype(
        jnp.float32
    )
    activated, gelu_pull = jax.vjp(gelu_exact, expanded)
    active = activated.astype(jnp.bfloat16)
    grad_active = jnp.einsum(
        "te,fe->tf", cotangent, weights[10], preferred_element_type=jnp.float32
    )
    grad_expanded = gelu_pull(grad_active)[0].astype(jnp.bfloat16)
    grad_second = jnp.einsum(
        "tf,df->td", grad_expanded, weights[8], preferred_element_type=jnp.float32
    )
    unused, turn_pull = jax.vjp(rotate, grad_query, cosine, sine)
    query_back = turn_pull(grad_query)[0].reshape(tokens, width)
    key_back = turn_pull(own_grads[:, :width].reshape(tokens, heads, HEAD))[0].reshape(
        tokens, width
    )
    grad_merged = jnp.concatenate([query_back, key_back, own_grads[:, width:]], axis=1).astype(
        jnp.bfloat16
    )
    grad_first = jnp.einsum(
        "tc,dc->td", grad_merged, weights[4], preferred_element_type=jnp.float32
    )
    first_term, first_gain_grad, first_shift_grad = first_pull(grad_first)
    second_term, second_gain_grad, second_shift_grad = second_pull(grad_second)
    input_gradient = upstream + first_term + second_term
    row_total = jnp.sum(upstream, axis=0)
    local_grads = (
        first_gain_grad,
        first_shift_grad,
        second_gain_grad,
        second_shift_grad,
        jnp.einsum("td,tc->dc", first, grad_merged, preferred_element_type=jnp.float32),
        jnp.sum(grad_merged.astype(jnp.float32), axis=0),
        jnp.einsum("td,te->de", mixed, cotangent, preferred_element_type=jnp.float32),
        row_total,
        jnp.einsum("td,tf->df", second, grad_expanded, preferred_element_type=jnp.float32),
        jnp.sum(grad_expanded.astype(jnp.float32), axis=0),
        jnp.einsum("tf,te->fe", active, cotangent, preferred_element_type=jnp.float32),
        row_total,
    )
    owned = (
        lax.psum_scatter(
            local_grads[0].astype(jnp.bfloat16), "fsdp", scatter_dimension=0, tiled=True
        ).astype(jnp.float32),
        lax.psum_scatter(
            local_grads[1].astype(jnp.bfloat16), "fsdp", scatter_dimension=0, tiled=True
        ).astype(jnp.float32),
        lax.psum_scatter(
            local_grads[2].astype(jnp.bfloat16), "fsdp", scatter_dimension=0, tiled=True
        ).astype(jnp.float32),
        lax.psum_scatter(
            local_grads[3].astype(jnp.bfloat16), "fsdp", scatter_dimension=0, tiled=True
        ).astype(jnp.float32),
        lax.psum_scatter(
            local_grads[4].astype(jnp.bfloat16), "fsdp", scatter_dimension=0, tiled=True
        ).astype(jnp.float32),
        lax.psum_scatter(
            local_grads[5].astype(jnp.bfloat16), "fsdp", scatter_dimension=0, tiled=True
        ).astype(jnp.float32),
        lax.psum_scatter(
            local_grads[6].astype(jnp.bfloat16), "fsdp", scatter_dimension=0, tiled=True
        ).astype(jnp.float32),
        lax.psum_scatter(
            local_grads[7].astype(jnp.bfloat16), "fsdp", scatter_dimension=0, tiled=True
        ).astype(jnp.float32),
        lax.psum_scatter(
            local_grads[8].astype(jnp.bfloat16), "fsdp", scatter_dimension=0, tiled=True
        ).astype(jnp.float32),
        lax.psum_scatter(
            local_grads[9].astype(jnp.bfloat16), "fsdp", scatter_dimension=0, tiled=True
        ).astype(jnp.float32),
        lax.psum_scatter(
            local_grads[10].astype(jnp.bfloat16), "fsdp", scatter_dimension=0, tiled=True
        ).astype(jnp.float32),
        lax.psum_scatter(
            local_grads[11].astype(jnp.bfloat16), "fsdp", scatter_dimension=0, tiled=True
        ).astype(jnp.float32),
    )
    summed = lax.psum(
        (
            owned[0],
            owned[1],
            owned[2],
            owned[3],
            owned[4],
            owned[5],
            owned[6],
            owned[7],
            owned[8],
            owned[9],
            owned[10],
            owned[11],
        ),
        ("rep", "seq"),
    )
    return (
        output[None],
        input_gradient[None],
        summed[0],
        summed[1],
        summed[2],
        summed[3],
        summed[4],
        summed[5],
        summed[6],
        summed[7],
        summed[8],
        summed[9],
        summed[10],
        summed[11],
    )


MESH = pl.DeviceIdType.MESH
GROUP = 8
LINE = 4
HALF = ROT // 2
SPAN = 512
CHUNK = 32


def place_here():
    c, y, s = (lax.axis_index("rep"), lax.axis_index("fsdp"), lax.axis_index("seq"))
    x = lax.rem(s, 2)
    return (c, y, x, s // 2)


def device_at(c, y, x, z):
    return (c, y, 2 * z + x)


def greet(partners):
    barrier = pltpu.get_barrier_semaphore()
    for partner in partners:
        pl.semaphore_signal(barrier, inc=1, device_id=partner, device_id_type=MESH)
    pl.semaphore_wait(barrier, len(partners))


def remote(src, dst, send, recv, target):
    return pltpu.make_async_remote_copy(
        src_ref=src,
        dst_ref=dst,
        send_sem=send,
        recv_sem=recv,
        device_id=target,
        device_id_type=MESH,
    )


def exchange_kernel(
    hid, cot, ints, vec, wm, we, hid_all, cot_all, ints_all, vec_all, wm_all, we_all, send, recv, local
):
    c, y, x, z = place_here()
    core = device_at(1 - c, y, x, z)
    over_x = device_at(c, y, 1 - x, z)
    over_y = device_at(c, 1 - y, x, z)
    greet((core, over_x, over_y))

    def block(cc, yy, xx):
        return (2 * cc + yy) * 2 + xx

    me = block(c, y, x)
    lanes = wm_all.shape[2] // 3
    width = wm.shape[1] // 3
    ff = we_all.shape[2]
    own = 4 * y + 2 * x + c
    other = 4 * (1 - y) + 2 * x + c
    half = hid.shape[0] // 2
    started = []
    count = [0]

    def go(src, dst, target):
        index = count[0]
        count[0] += 1
        copy = remote(src, dst, send.at[index], recv.at[index], target)
        copy.start()
        started.append(copy)
        return copy

    moved = []

    def keep(src, dst):
        copy = pltpu.make_async_copy(src, dst, local.at[len(moved)])
        copy.start()
        moved.append(copy)

    def columns(part, at):
        return pl.ds(pl.multiple_of(at, part), part)

    pairs = ((hid, hid_all), (cot, cot_all))
    from_y = [go(src, dst.at[me], over_y) for src, dst in pairs]
    from_x = [go(src, dst.at[me], over_x) for src, dst in pairs]
    ints_y = go(ints, ints_all.at[2 * c + y], over_y)
    go(vec, vec_all.at[y], over_y)
    for j in range(3):
        go(
            wm.at[:, columns(lanes, j * width + other * lanes)],
            wm_all.at[y, :, pl.ds(j * lanes, lanes)],
            over_y,
        )
    go(we.at[:, columns(ff, other * ff)], we_all.at[y], over_y)
    for src, dst in pairs:
        go(src, dst.at[me], core)
    go(ints, ints_all.at[2 * c + y], core)
    for src, dst in pairs:
        keep(src, dst.at[me])
    keep(ints, ints_all.at[2 * c + y])
    keep(vec, vec_all.at[y])
    for j in range(3):
        keep(
            wm.at[:, columns(lanes, j * width + own * lanes)],
            wm_all.at[y, :, pl.ds(j * lanes, lanes)],
        )
    keep(we.at[:, columns(ff, own * ff)], we_all.at[y])
    ints_y.wait_recv()
    go(ints_all.at[2 * c + 1 - y], ints_all.at[2 * c + 1 - y], core)
    upper, lower = pl.ds(0, half), pl.ds(half, half)
    diagonal = []
    for index, (src, full) in enumerate(pairs):
        near_y, near_x = block(c, 1 - y, x), block(c, y, 1 - x)
        from_y[index].wait_recv()
        first = go(full.at[near_y, upper], full.at[near_y, upper], over_x)
        go(full.at[near_y], full.at[near_y], core)
        from_x[index].wait_recv()
        second = go(full.at[near_x, lower], full.at[near_x, lower], over_y)
        go(full.at[near_x], full.at[near_x], core)
        diagonal.append((first, second))
    for index, (src, full) in enumerate(pairs):
        far = block(c, 1 - y, 1 - x)
        first, second = diagonal[index]
        first.wait_recv()
        second.wait_recv()
        go(full.at[far], full.at[far], core)
    early = from_y + from_x + [ints_y] + [copy for pair in diagonal for copy in pair]
    for copy in started:
        if any(copy is other for other in early):
            copy.wait_send()
        else:
            copy.wait()
    for copy in moved:
        copy.wait()


def exchange(hid, cot, ints, vec, wm, we):
    rows = wm.shape[0]
    any_spec = pl.BlockSpec(memory_space=pl.ANY)
    shapes = (
        jax.ShapeDtypeStruct((GROUP,) + hid.shape, hid.dtype),
        jax.ShapeDtypeStruct((GROUP,) + cot.shape, cot.dtype),
        jax.ShapeDtypeStruct((4,) + ints.shape, ints.dtype),
        jax.ShapeDtypeStruct((2,) + vec.shape, vec.dtype),
        jax.ShapeDtypeStruct((2, rows, wm.shape[1] // GROUP), wm.dtype),
        jax.ShapeDtypeStruct((2, rows, we.shape[1] // GROUP), we.dtype),
    )
    return pl.pallas_call(
        exchange_kernel,
        out_shape=shapes,
        in_specs=[any_spec] * 6,
        out_specs=[any_spec] * 6,
        scratch_shapes=[
            pltpu.SemaphoreType.DMA((24,)),
            pltpu.SemaphoreType.DMA((24,)),
            pltpu.SemaphoreType.DMA((8,)),
        ],
        compiler_params=pltpu.CompilerParams(collective_id=0, has_side_effects=True),
        name="exchange",
    )(hid, cot, ints, vec, wm, we)


def scatter_kernel(src, dst, send, recv, local):
    c, y, x, z = place_here()
    rows = dst.shape[2]
    peers = [lax.rem(z + d, LINE) for d in range(1, LINE)]
    greet([device_at(c, y, x, peer) for peer in peers])
    copies = []
    for index, peer in enumerate(peers):
        copy = remote(
            src.at[:, pl.ds(pl.multiple_of(peer * rows, rows), rows)],
            dst.at[:, z],
            send.at[index],
            recv.at[index],
            device_at(c, y, x, peer),
        )
        copy.start()
        copies.append(copy)
    own = pltpu.make_async_copy(
        src.at[:, pl.ds(pl.multiple_of(z * rows, rows), rows)], dst.at[:, z], local
    )
    own.start()
    own.wait()
    for copy in copies:
        copy.wait()


def gather_kernel(src, dst, send, recv, local):
    c, y, x, z = place_here()
    rows = src.shape[2]
    peers = [lax.rem(z + d, LINE) for d in range(1, LINE)]
    greet([device_at(c, y, x, peer) for peer in peers])
    place = dst.at[:, pl.ds(pl.multiple_of(z * rows, rows), rows)]
    copies = []
    for index, peer in enumerate(peers):
        copy = remote(
            src.at[:, peer], place, send.at[index], recv.at[index], device_at(c, y, x, peer)
        )
        copy.start()
        copies.append(copy)
    own = pltpu.make_async_copy(src.at[:, z], place, local)
    own.start()
    own.wait()
    for copy in copies:
        copy.wait()


def swap_tokens(kernel, identity, name, array, shape):
    any_spec = pl.BlockSpec(memory_space=pl.ANY)
    return pl.pallas_call(
        kernel,
        out_shape=jax.ShapeDtypeStruct(shape, array.dtype),
        in_specs=[any_spec],
        out_specs=any_spec,
        scratch_shapes=[
            pltpu.SemaphoreType.DMA((LINE - 1,)),
            pltpu.SemaphoreType.DMA((LINE - 1,)),
            pltpu.SemaphoreType.DMA,
        ],
        compiler_params=pltpu.CompilerParams(collective_id=identity, has_side_effects=True),
        name=name,
    )(array)


def attention_kernel(
    ints,
    parts,
    cosine,
    sine_up,
    sine_down,
    out,
    masked,
    flat,
    scores,
    slopes,
    key_sum,
    value_sum,
    mixed_sum,
    query_sum,
    units,
    pieces,
):
    length = parts.shape[1]
    scale = 1.0 / math.sqrt(HEAD)
    blocks = length // SPAN
    lanes = lax.broadcasted_iota(jnp.int32, (UNIT, 2 * HEAD), 1)
    lower = lanes < HEAD

    def arrange(index, carry):
        here = pl.multiple_of(index * UNIT, UNIT)
        place = pl.multiple_of(ints[0, index] * UNIT, UNIT)
        for which in range(4):
            rows = parts[which, pl.ds(here, UNIT), :].astype(jnp.float32)
            if which == 0:
                rows = rows * scale
            masked[which, 0, pl.ds(place, UNIT), :] = jnp.where(lower, rows, 0.0).astype(
                jnp.bfloat16
            )
            masked[which, 1, pl.ds(place, UNIT), :] = jnp.where(lower, 0.0, rows).astype(
                jnp.bfloat16
            )
            flat[which, :, pl.ds(place, UNIT)] = rows.T.astype(jnp.bfloat16)
        return carry

    lax.fori_loop(0, units, arrange, 0)
    key_sum[...] = jnp.zeros_like(key_sum)
    value_sum[...] = jnp.zeros_like(value_sum)

    def labels(positions):
        found = jnp.full(positions.shape, -1, jnp.int32)
        for piece in range(pieces):
            start = ints[0, units + piece]
            found = jnp.where(
                (positions >= start) & (positions < start + PIECE), piece, found
            )
        return found

    def dot(a, b):
        return jnp.dot(a, b, preferred_element_type=jnp.float32)

    for block in range(blocks):
        begin = block * SPAN
        last = SPAN + (UNIT if block + 1 < blocks else 0)
        columns = pl.ds(begin, SPAN)
        row_at = begin + lax.broadcasted_iota(jnp.int32, (1, SPAN), 1)
        col_at = begin + lax.broadcasted_iota(jnp.int32, (last, 1), 0)
        row_lab = labels(row_at)
        col_lab = labels(col_at)
        allowed = (col_at <= row_at) | (
            (col_lab == row_lab) & (row_lab >= 0)
        )

        def one_head(head, carry):
            queries = flat[0, :, columns]
            grads = flat[3, :, columns]
            side = pl.ds(pl.multiple_of(head * HEAD, HEAD), HEAD)

            def score_tile(start, size, top, mask):
                rows = pl.ds(start, size)
                tile = dot(masked[1, head, rows, :], queries)
                if mask is not None:
                    tile = jnp.where(mask, tile, NEGATIVE)
                scores[rows, :] = tile
                return jnp.maximum(top, jnp.max(tile, axis=0, keepdims=True))

            top = lax.fori_loop(
                0,
                block,
                lambda j, top: score_tile(pl.multiple_of(j * SPAN, SPAN), SPAN, top, None),
                jnp.full((1, SPAN), NEGATIVE, jnp.float32),
            )
            top = score_tile(begin, last, top, allowed)

            def weight_tile(start, size, sums):
                total, delta = sums
                rows = pl.ds(start, size)
                weights = jnp.exp(scores[rows, :] - top)
                slope = dot(masked[2, head, rows, :], grads)
                scores[rows, :] = weights
                slopes[rows, :] = slope
                return (
                    total + jnp.sum(weights, axis=0, keepdims=True),
                    delta + jnp.sum(weights * slope, axis=0, keepdims=True),
                )

            zero = jnp.zeros((1, SPAN), jnp.float32)
            sums = lax.fori_loop(
                0,
                block,
                lambda j, sums: weight_tile(pl.multiple_of(j * SPAN, SPAN), SPAN, sums),
                (zero, zero),
            )
            total, delta = weight_tile(begin, last, sums)
            inverse = 1.0 / total
            delta = delta * inverse

            def grad_tile(start, size, sums):
                mixed, query = sums
                rows = pl.ds(start, size)
                probs = scores[rows, :] * inverse
                grad = (probs * (slopes[rows, :] - delta)).astype(jnp.bfloat16)
                probs = probs.astype(jnp.bfloat16)
                value_sum[rows, :] += dot(probs, masked[3, head, columns, :])
                key_sum[rows, :] += dot(grad, masked[0, head, columns, :])
                mixed = mixed + dot(flat[2, side, rows], probs)
                query = query + dot(flat[1, side, rows], grad)
                return (mixed, query)

            none = jnp.zeros((HEAD, SPAN), jnp.float32)
            sums = lax.fori_loop(
                0,
                block,
                lambda j, sums: grad_tile(pl.multiple_of(j * SPAN, SPAN), SPAN, sums),
                (none, none),
            )
            mixed, query = grad_tile(begin, last, sums)
            mixed_sum[side, columns] = mixed
            query_sum[side, columns] = query * scale
            return carry

        lax.fori_loop(0, 2, one_head, 0)

    def turn_back(rows, at):
        up = pltpu.roll(rows, 2 * HEAD - HALF, 1)
        down = pltpu.roll(rows, HALF, 1)
        return (
            rows * cosine[at, :] + up * sine_up[at, :] - down * sine_down[at, :]
        )

    def finish(index, carry):
        at = pl.ds(pl.multiple_of(index * UNIT, UNIT), UNIT)
        key_sum[at, :] = turn_back(key_sum[at, :], at)
        masked[0, 0, at, :] = mixed_sum[:, at].T.astype(jnp.bfloat16)
        masked[1, 0, at, :] = turn_back(query_sum[:, at].T, at).astype(jnp.bfloat16)
        return carry

    lax.fori_loop(0, units, finish, 0)

    def restore(index, carry):
        here = pl.ds(pl.multiple_of(index * UNIT, UNIT), UNIT)
        place = pl.ds(pl.multiple_of(ints[0, index] * UNIT, UNIT), UNIT)
        out[0, here, :] = masked[0, 0, place, :]
        out[1, here, :] = masked[1, 0, place, :]
        out[2, here, :] = key_sum[place, :].astype(jnp.bfloat16)
        out[3, here, :] = value_sum[place, :].astype(jnp.bfloat16)
        return carry

    lax.fori_loop(0, units, restore, 0)


def attend(ints, parts, cosine, sine_up, sine_down, units, pieces):
    length = parts.shape[1]
    vmem = pl.BlockSpec(memory_space=pltpu.VMEM)
    flops = 6 * 2 * 2 * HEAD * length * length // 2
    return pl.pallas_call(
        functools.partial(attention_kernel, units=units, pieces=pieces),
        out_shape=jax.ShapeDtypeStruct(parts.shape, parts.dtype),
        in_specs=[pl.BlockSpec(memory_space=pltpu.SMEM)] + [vmem] * 4,
        out_specs=vmem,
        scratch_shapes=[
            pltpu.VMEM((4, 2, length, 2 * HEAD), jnp.bfloat16),
            pltpu.VMEM((4, 2 * HEAD, length), jnp.bfloat16),
            pltpu.VMEM((length, SPAN), jnp.float32),
            pltpu.VMEM((length, SPAN), jnp.float32),
            pltpu.VMEM((length, 2 * HEAD), jnp.float32),
            pltpu.VMEM((length, 2 * HEAD), jnp.float32),
            pltpu.VMEM((2 * HEAD, length), jnp.float32),
            pltpu.VMEM((2 * HEAD, length), jnp.float32),
        ],
        compiler_params=pltpu.CompilerParams(vmem_limit_bytes=48 << 20),
        cost_estimate=pl.CostEstimate(
            flops=flops * 4, bytes_accessed=8 << 20, transcendentals=length * length
        ),
        name="attend",
    )(ints, parts, cosine, sine_up, sine_down)


class LineSum:
    def __init__(self, grad, result, inbox, sems, swap, place):
        self.grad, self.result, self.inbox, self.sems, self.swap = grad, result, inbox, sems, swap
        self.c, self.y, self.x, self.z = place
        self.count = grad.shape[0] // CHUNK
        self.split = (self.count + 1) // 2
        self.slots = self.split + 9

    def rows(self, chunk):
        return pl.ds(pl.multiple_of(chunk * CHUNK, CHUNK), CHUNK)

    def copy(self, kind, chunk, src, dst, target):
        return remote(src, dst, self.sems.at[2 * kind, chunk], self.sems.at[2 * kind + 1, chunk], target)

    def pieces(self, chunk, line):
        c, y, x, z = self.c, self.y, self.x, self.z
        ahead, behind = (z + 1, z - 1) if line == 0 else (z - 1, z + 1)
        rows = self.rows(chunk)
        grad, result = self.grad, self.result
        swap = self.swap
        mine = result.at[c, x, rows]
        beside = result.at[c, 1 - x, rows]

        def lanes(which):
            return pl.ds(pl.multiple_of(which * swap, swap), swap)

        makers = {
            "reduce": lambda: self.copy(
                0, chunk, grad.at[rows], self.inbox.at[rows], device_at(c, y, x, ahead)
            ),
            "swap": lambda: self.copy(
                1,
                chunk,
                grad.at[rows, lanes(1 - y)],
                result.at[c, x, rows, lanes(y)],
                device_at(c, 1 - y, x, z),
            ),
            "back": lambda: self.copy(2, chunk, mine, mine, device_at(c, y, x, behind)),
            "side": lambda: self.copy(3, chunk, mine, mine, device_at(c, y, 1 - x, z)),
            "core": lambda: self.copy(4, chunk, mine, mine, device_at(1 - c, y, x, z)),
            "late": lambda: self.copy(5, chunk, beside, beside, device_at(1 - c, y, x, z)),
        }
        return lambda name: makers[name]()

    def slot(self, t):
        for line in range(2):
            self.line_slot(t, line)

    def line_slot(self, t, line):
        size = self.split if line == 0 else self.count - self.split
        base = 0 if line == 0 else self.split
        away = self.z if line == 0 else LINE - 1 - self.z
        swap = self.swap

        chunk = t - away
        index = jnp.clip(chunk, 0, size - 1) + base

        @pl.when((chunk >= 0) & (chunk < size))
        def _():
            moves = self.pieces(index, line)
            rows = self.rows(index)

            @pl.when(away > 0)
            def _():
                moves("reduce").wait_recv()
                total = self.grad[rows].astype(jnp.float32) + self.inbox[rows].astype(jnp.float32)
                self.grad[rows] = total.astype(jnp.bfloat16)

            @pl.when(away < LINE - 1)
            def _():
                moves("reduce").start()

            @pl.when(away == LINE - 1)
            def _():
                moves("swap").start()
                own = pl.ds(pl.multiple_of(self.y * swap, swap), swap)
                plain = pl.ds(2 * swap, self.grad.shape[1] - 2 * swap)
                self.result[self.c, self.x, rows, own] = self.grad[rows, own]
                self.result[self.c, self.x, rows, plain] = self.grad[rows, plain]

        chunk2 = t - 7 + away
        index2 = jnp.clip(chunk2, 0, size - 1) + base

        @pl.when((chunk2 >= 0) & (chunk2 < size))
        def _():
            moves = self.pieces(index2, line)

            @pl.when(away == LINE - 1)
            def _():
                moves("swap").wait_recv()

            @pl.when(away < LINE - 1)
            def _():
                moves("back").wait_recv()

            @pl.when(away > 0)
            def _():
                moves("back").start()

            moves("side").start()
            moves("core").start()

        chunk3 = t - 8 + away
        index3 = jnp.clip(chunk3, 0, size - 1) + base

        @pl.when((chunk3 >= 0) & (chunk3 < size))
        def _():
            moves = self.pieces(index3, line)
            moves("side").wait_recv()
            moves("late").start()

    def drain(self):
        for line in range(2):
            size = self.split if line == 0 else self.count - self.split
            base = 0 if line == 0 else self.split
            away = self.z if line == 0 else LINE - 1 - self.z

            def finish(chunk, carry):
                moves = self.pieces(chunk + base, line)

                @pl.when(away < LINE - 1)
                def _():
                    moves("reduce").wait_send()

                @pl.when(away == LINE - 1)
                def _():
                    moves("swap").wait_send()

                @pl.when(away > 0)
                def _():
                    moves("back").wait_send()

                moves("side").wait_send()
                moves("core").wait()
                moves("late").wait()
                return carry

            lax.fori_loop(0, size, finish, 0)


def finish_kernel(
    feed_grad,
    attn_grad,
    outs,
    terms,
    feed_all,
    attn_all,
    out_sum,
    term_sum,
    feed_own,
    attn_own,
    feed_inbox,
    attn_inbox,
    near,
    four,
    mid,
    two,
    far,
    feed_sems,
    attn_sems,
    sems,
    local,
    *,
    feed_swap,
    attn_swap,
):
    place = place_here()
    c, y, x, z = place
    core = device_at(1 - c, y, x, z)
    over_x = device_at(c, y, 1 - x, z)
    over_y = device_at(c, 1 - y, x, z)
    barrier = pltpu.get_barrier_semaphore()
    for partner in (core, over_x, over_y):
        pl.semaphore_signal(barrier, inc=1, device_id=partner, device_id_type=MESH)

    @pl.when(z > 0)
    def _():
        pl.semaphore_signal(barrier, inc=1, device_id=device_at(c, y, x, z - 1), device_id_type=MESH)

    @pl.when(z < LINE - 1)
    def _():
        pl.semaphore_signal(barrier, inc=1, device_id=device_at(c, y, x, z + 1), device_id_type=MESH)

    @pl.when((z > 0) & (z < LINE - 1))
    def _():
        pl.semaphore_wait(barrier, 5)

    @pl.when((z == 0) | (z == LINE - 1))
    def _():
        pl.semaphore_wait(barrier, 4)

    def load(which, src, dst):
        copy = pltpu.make_async_copy(src, dst, local.at[which])
        copy.start()
        return copy

    loads = [load(0, feed_grad, feed_own), load(1, attn_grad, attn_own)]
    arrays = (outs, terms)
    nears = []
    for a in range(2):
        copy = remote(
            arrays[a].at[pl.ds(pl.multiple_of(4 * (1 - c), 4), 4)],
            near.at[a],
            sems.at[0, a],
            sems.at[1, a],
            core,
        )
        copy.start()
        nears.append(copy)
    for copy in loads:
        copy.wait()
    feed = LineSum(feed_own, feed_all, feed_inbox, feed_sems, feed_swap, place)
    attn = LineSum(attn_own, attn_all, attn_inbox, attn_sems, attn_swap, place)
    slots = max(feed.slots, attn.slots)

    def step(t, carry):
        attn.slot(t)
        feed.slot(t)
        return carry

    lax.fori_loop(0, 2, step, 0)
    mids = []
    for a in range(2):
        nears[a].wait()
        for j in range(4):
            total = arrays[a][4 * c + j].astype(jnp.float32) + near[a, j].astype(jnp.float32)
            if a == 0:
                four[a, j % 2, j // 2] = total.astype(jnp.bfloat16)
            else:
                four[a, j // 2, j % 2] = total.astype(jnp.bfloat16)
        copy = remote(
            four.at[a, 1 - x if a == 0 else 1 - y],
            mid.at[a],
            sems.at[0, 2 + a],
            sems.at[1, 2 + a],
            over_x if a == 0 else over_y,
        )
        copy.start()
        mids.append(copy)
    lax.fori_loop(2, 7, step, 0)
    fars = []
    for a in range(2):
        mids[a].wait()
        mine, away = (x, y) if a == 0 else (y, x)
        two[a] = (
            four[a, mine, 1 - away].astype(jnp.float32) + mid[a, 1 - away].astype(jnp.float32)
        ).astype(jnp.bfloat16)
        copy = remote(
            two.at[a],
            far.at[a],
            sems.at[0, 4 + a],
            sems.at[1, 4 + a],
            over_y if a == 0 else over_x,
        )
        copy.start()
        fars.append(copy)
    lax.fori_loop(7, slots, step, 0)
    for a, dst in enumerate((out_sum, term_sum)):
        fars[a].wait()
        mine, away = (x, y) if a == 0 else (y, x)
        dst[...] = (
            four[a, mine, away].astype(jnp.float32)
            + mid[a, away].astype(jnp.float32)
            + far[a].astype(jnp.float32)
        )
    feed.drain()
    attn.drain()


def finish(feed_grad, attn_grad, outs, terms, feed_swap, attn_swap):
    block = outs.shape[1:]
    vmem = pl.BlockSpec(memory_space=pltpu.VMEM)
    any_spec = pl.BlockSpec(memory_space=pl.ANY)

    def chunks(grad):
        return grad.shape[0] // CHUNK

    return pl.pallas_call(
        functools.partial(finish_kernel, feed_swap=feed_swap, attn_swap=attn_swap),
        out_shape=(
            jax.ShapeDtypeStruct((2, 2) + feed_grad.shape, jnp.bfloat16),
            jax.ShapeDtypeStruct((2, 2) + attn_grad.shape, jnp.bfloat16),
            jax.ShapeDtypeStruct(block, jnp.float32),
            jax.ShapeDtypeStruct(block, jnp.float32),
        ),
        in_specs=[any_spec, any_spec, vmem, vmem],
        out_specs=[vmem] * 4,
        scratch_shapes=[
            pltpu.VMEM(feed_grad.shape, jnp.bfloat16),
            pltpu.VMEM(attn_grad.shape, jnp.bfloat16),
            pltpu.VMEM(feed_grad.shape, jnp.bfloat16),
            pltpu.VMEM(attn_grad.shape, jnp.bfloat16),
            pltpu.VMEM((2, 4) + block, jnp.bfloat16),
            pltpu.VMEM((2, 2, 2) + block, jnp.bfloat16),
            pltpu.VMEM((2, 2) + block, jnp.bfloat16),
            pltpu.VMEM((2,) + block, jnp.bfloat16),
            pltpu.VMEM((2,) + block, jnp.bfloat16),
            pltpu.SemaphoreType.DMA((12, chunks(feed_grad))),
            pltpu.SemaphoreType.DMA((12, chunks(attn_grad))),
            pltpu.SemaphoreType.DMA((2, 6)),
            pltpu.SemaphoreType.DMA((2,)),
        ],
        compiler_params=pltpu.CompilerParams(
            collective_id=3, has_side_effects=True, vmem_limit_bytes=58 << 20
        ),
        name="finish",
    )(feed_grad, attn_grad, outs, terms)


def widen(src, dst):
    dst[...] = src[...].reshape(dst.shape).astype(jnp.float32)


def place_columns(array, lane_block, offset, groups, rows, row_block):
    total = lane_block * groups * 8

    def source(j, o):
        return (o % 2, (o // 2) % 2, 0, offset // lane_block + (o // 4) * groups + j)

    return pl.pallas_call(
        widen,
        grid=(groups, 8),
        out_shape=jax.ShapeDtypeStruct((rows, total), jnp.float32),
        in_specs=[pl.BlockSpec((1, 1, rows, lane_block), source)],
        out_specs=pl.BlockSpec((rows, lane_block), lambda j, o: (0, j * 8 + o)),
        name="place_columns",
    )(array)


def place_rows(array, lane_block, offset, groups, row_block):
    def source(o, g):
        return (o % 2, o // 2, g, offset // lane_block)

    return pl.pallas_call(
        widen,
        grid=(4, groups),
        out_shape=jax.ShapeDtypeStruct((4 * row_block, groups * lane_block), jnp.float32),
        in_specs=[pl.BlockSpec((1, 1, row_block, lane_block), source)],
        out_specs=pl.BlockSpec((row_block, lane_block), lambda o, g: (o, g)),
        name="place_rows",
    )(array)


def lane_tables(positions, lanes):
    lane = jnp.arange(lanes, dtype=jnp.int32) % HEAD
    inverse = jnp.exp((lane % HALF).astype(jnp.float32) * (-2.0 * math.log(10000.0) / ROT))
    angles = positions.astype(jnp.float32)[:, None] * inverse[None, :]
    cosine = jnp.where(lane[None, :] < ROT, jnp.cos(angles), 1.0)
    sine = jnp.sin(angles)
    up = jnp.where(lane[None, :] < HALF, sine, 0.0)
    down = jnp.where((lane[None, :] >= HALF) & (lane[None, :] < ROT), sine, 0.0)
    return (cosine, up, down)


def turn_lanes(values, tables):
    cosine, up, down = tables
    return (
        values * cosine
        - jnp.roll(values, -HALF, axis=1) * up
        + jnp.roll(values, HALF, axis=1) * down
    )


def group_body(
    hidden_states,
    unit_order,
    piece_starts,
    first_gain,
    first_shift,
    second_gain,
    second_shift,
    merged_weight,
    merged_bias,
    output_weight,
    output_bias,
    expand_weight,
    expand_bias,
    contract_weight,
    contract_bias,
    out_cotangent,
):
    c, y, x, z = place_here()
    octant = 4 * y + 2 * x + c
    tokens, width = hidden_states.shape[1:]
    length = tokens * 2 * LINE
    units = unit_order.shape[1]
    pieces = piece_starts.shape[1]
    rows = GROUP * tokens
    part = width // GROUP
    ff_part = expand_weight.shape[1] // GROUP
    half = width // 2
    vectors = (
        first_gain,
        first_shift,
        second_gain,
        second_shift,
        merged_bias,
        output_bias,
        expand_bias,
        contract_bias,
    )
    sizes = [v.shape[0] for v in vectors]
    packed = jnp.concatenate(vectors).reshape(-1, 128)
    ints = jnp.concatenate([unit_order[0], piece_starts[0]])
    ints = jnp.broadcast_to(jnp.pad(ints, (0, 128 - ints.shape[0]))[None], (8, 128))
    hid_all, cot_all, ints_all, vec_all, wm_all, we_all = exchange(
        hidden_states[0], out_cotangent[0], ints, packed, merged_weight, expand_weight
    )
    vec_all = vec_all.reshape(2, -1)
    whole = []
    at = 0
    for size in sizes:
        whole.append(vec_all[:, at : at + size].reshape(-1).astype(jnp.float32))
        at += size
    gain_one, shift_one, gain_two, shift_two, bias_merged, bias_out, bias_expand, bias_contract = whole
    wm = wm_all.reshape(width, 3 * part)
    we = we_all.reshape(width, ff_part)
    inner = 2 * x + c
    wo = lax.dynamic_slice_in_dim(output_weight, inner * part, part, 0)
    wc = lax.dynamic_slice_in_dim(contract_weight, inner * ff_part, ff_part, 0)
    cots = cot_all.reshape(rows, width)
    hidden = hid_all.reshape(rows, width).astype(jnp.float32)
    mean = jnp.mean(hidden, axis=1, keepdims=True)
    centred = hidden - mean
    rstd = lax.rsqrt(jnp.mean(centred * centred, axis=1, keepdims=True) + EPS)
    xhat = centred * rstd
    first = (xhat * gain_one + shift_one).astype(jnp.bfloat16)
    second = (xhat * gain_two + shift_two).astype(jnp.bfloat16)
    own_bias = lax.dynamic_slice_in_dim(
        bias_merged.reshape(3, GROUP, part), octant, 1, 1
    ).reshape(3 * part)
    merged = jnp.dot(first, wm, preferred_element_type=jnp.float32) + own_bias
    near_units = 2 * tokens // UNIT
    local_units = lax.dynamic_slice_in_dim(ints_all[:, 0, :], z * near_units, near_units, 1)
    positions = (
        local_units.reshape(-1)[:, None] * UNIT + jnp.arange(UNIT, dtype=jnp.int32)[None, :]
    ).reshape(-1)
    tables = lane_tables(positions, part)
    queries = turn_lanes(merged[:, :part], tables).astype(jnp.bfloat16)
    keys = turn_lanes(merged[:, part : 2 * part], tables).astype(jnp.bfloat16)
    values = merged[:, 2 * part :].astype(jnp.bfloat16)
    grad_mixed = lax.dot_general(
        cots, wo, (((1,), (1,)), ((), ())), preferred_element_type=jnp.float32
    ).astype(jnp.bfloat16)
    sent = jnp.stack([queries, keys, values, grad_mixed])
    got = swap_tokens(scatter_kernel, 1, "scatter", sent, (4, LINE, 2 * tokens, part))
    own_ints = lax.dynamic_index_in_dim(ints_all[:, 0, :], z, 0, keepdims=True)
    sorted_tables = lane_tables(jnp.arange(length, dtype=jnp.int32), part)
    done = attend(own_ints, got.reshape(4, length, part), *sorted_tables, units, pieces)
    back = swap_tokens(
        gather_kernel, 2, "gather", done.reshape(4, LINE, 2 * tokens, part), (4, rows, part)
    )
    mixed = back[0]
    grad_merged = jnp.concatenate([back[1], back[2], back[3]], axis=1)

    own_expand = lax.dynamic_slice_in_dim(bias_expand, octant * ff_part, ff_part, 0)
    expanded = jnp.dot(second, we, preferred_element_type=jnp.float32) + own_expand
    activated, gelu_pull = jax.vjp(gelu_exact, expanded)
    active = activated.astype(jnp.bfloat16)
    grad_active = lax.dot_general(
        cots, wc, (((1,), (1,)), ((), ())), preferred_element_type=jnp.float32
    )
    grad_expanded = gelu_pull(grad_active)[0].astype(jnp.bfloat16)

    def against(a, b):
        return lax.dot_general(a, b, (((0,), (0,)), ((), ())), preferred_element_type=jnp.float32)

    d_expand = against(second, grad_expanded).astype(jnp.bfloat16)
    d_contract = against(active, cots).astype(jnp.bfloat16)
    feed_grad = jnp.concatenate([d_expand[:half], d_expand[half:], d_contract], axis=1)
    d_merged = against(first, grad_merged).astype(jnp.bfloat16)
    d_output = against(mixed, cots).astype(jnp.bfloat16)
    lane = 2 * part
    d_output = jnp.concatenate(
        [d_output[:, k * lane : (k + 1) * lane] for k in range(width // lane)], axis=0
    )
    out_partial = jnp.dot(mixed, wo, preferred_element_type=jnp.float32) + jnp.dot(
        active, wc, preferred_element_type=jnp.float32
    )
    grad_first = lax.dot_general(
        grad_merged, wm, (((1,), (1,)), ((), ())), preferred_element_type=jnp.float32
    )
    grad_second = lax.dot_general(
        grad_expanded, we, (((1,), (1,)), ((), ())), preferred_element_type=jnp.float32
    )
    term_partial = grad_first * gain_one + grad_second * gain_two
    small = jnp.concatenate(
        [
            jnp.sum(grad_first * xhat, axis=0),
            jnp.sum(grad_first, axis=0),
            jnp.sum(grad_second * xhat, axis=0),
            jnp.sum(grad_second, axis=0),
            jnp.sum(cots.astype(jnp.float32), axis=0),
            jnp.sum(grad_merged.astype(jnp.float32), axis=0),
            jnp.sum(grad_expanded.astype(jnp.float32), axis=0),
        ]
    )
    swap = 3 * part
    lines = CHUNK * -(-small.shape[0] // (swap * CHUNK))
    small = jnp.pad(small, (0, lines * swap - small.shape[0])).reshape(lines, swap)
    small = small.astype(jnp.bfloat16)
    attn_grad = jnp.concatenate(
        [
            jnp.concatenate([d_merged[:half], d_merged[half:], d_output], axis=1),
            jnp.concatenate([small, small, jnp.zeros((lines, lane), jnp.bfloat16)], axis=1),
        ],
        axis=0,
    )
    shape = (GROUP, tokens, width)
    feed_all, attn_all, out_sum, term_sum = finish(
        feed_grad,
        attn_grad,
        out_partial.astype(jnp.bfloat16).reshape(shape),
        term_partial.astype(jnp.bfloat16).reshape(shape),
        ff_part,
        swap,
    )
    expand_out = place_columns(feed_all, ff_part, 0, 1, half, 0)
    contract_out = place_rows(feed_all, width, 2 * ff_part, 1, ff_part)
    merged_out = place_columns(attn_all, part, 0, 3, half, 0)
    output_out = place_rows(attn_all, lane, 2 * swap, width // lane, part)

    own_hidden = hidden_states[0].astype(jnp.float32)
    own_mean = jnp.mean(own_hidden, axis=1, keepdims=True)
    own_centred = own_hidden - own_mean
    own_rstd = lax.rsqrt(jnp.mean(own_centred * own_centred, axis=1, keepdims=True) + EPS)
    own_xhat = own_centred * own_rstd
    output = (own_hidden + out_sum + bias_out + bias_contract).astype(jnp.bfloat16)
    upstream = out_cotangent[0].astype(jnp.float32)
    input_gradient = upstream + own_rstd * (
        term_sum
        - jnp.mean(term_sum, axis=1, keepdims=True)
        - own_xhat * jnp.mean(term_sum * own_xhat, axis=1, keepdims=True)
    )

    sums = attn_all[:, :, half : half + lines, : 2 * swap].astype(jnp.float32)
    sums = sums.reshape(2, 2, lines, 2, swap).transpose(3, 1, 0, 2, 4).reshape(GROUP, lines * swap)
    shared = jnp.sum(sums[:, : 4 * width], axis=0)
    row_total = sums[0, 4 * width : 5 * width]
    begin = 5 * width
    merged_sums = sums[:, begin : begin + swap].reshape(GROUP, 3, part)
    merged_sums = merged_sums.transpose(1, 0, 2).reshape(-1)
    expand_sums = sums[:, begin + swap : begin + swap + ff_part].reshape(-1)

    def own_half(vector):
        size = vector.shape[0] // 2
        return lax.dynamic_slice_in_dim(vector, y * size, size, 0)

    row_total = own_half(row_total)
    return (
        output[None],
        input_gradient[None],
        own_half(shared[:width]),
        own_half(shared[width : 2 * width]),
        own_half(shared[2 * width : 3 * width]),
        own_half(shared[3 * width :]),
        merged_out,
        own_half(merged_sums),
        output_out,
        row_total,
        expand_out,
        own_half(expand_sums),
        contract_out,
        row_total,
    )


def fits_groups(mesh, args):
    hidden, order = args[0], args[1]
    count = mesh.shape["seq"]
    tokens = hidden.shape[1] // count
    return (
        mesh.shape["rep"] == 2
        and mesh.shape["fsdp"] == 2
        and count == 2 * LINE
        and hidden.shape[0] == LINE
        and hidden.shape[2] == GROUP * 2 * HEAD
        and tokens % UNIT == 0
        and hidden.shape[1] % SPAN == 0
        and order.shape[1] + args[2].shape[1] <= 128
    )


def solution(mesh):
    in_specs = (
        P(("rep", "fsdp"), "seq", None),
        P(("rep", "fsdp"), None),
        P(("rep", "fsdp"), None),
        P("fsdp"),
        P("fsdp"),
        P("fsdp"),
        P("fsdp"),
        P("fsdp", None),
        P("fsdp"),
        P("fsdp", None),
        P("fsdp"),
        P("fsdp", None),
        P("fsdp"),
        P("fsdp", None),
        P("fsdp"),
        P(("rep", "fsdp"), "seq", None),
    )
    out_specs = (
        P(("rep", "fsdp"), "seq", None),
        P(("rep", "fsdp"), "seq", None),
        P("fsdp"),
        P("fsdp"),
        P("fsdp"),
        P("fsdp"),
        P("fsdp", None),
        P("fsdp"),
        P("fsdp", None),
        P("fsdp"),
        P("fsdp", None),
        P("fsdp"),
        P("fsdp", None),
        P("fsdp"),
    )

    def run(*args):
        chosen = group_body if fits_groups(mesh, args) else body
        mapped = jax.shard_map(
            chosen, mesh=mesh, in_specs=in_specs, out_specs=out_specs, check_vma=False
        )
        return mapped(*args)

    return run
```

```python
import functools
import math

import jax
import jax.numpy as jnp
from jax import lax
from jax.experimental import pallas as pl
from jax.experimental.pallas import tpu as pltpu
from jax.sharding import PartitionSpec as P

HEAD = 64
ROT = 16
UNIT = 128
PIECE = 256


EPS = 1e-05
NEGATIVE = -1e30


def norm_rows(values, gain, shift):
    mean = jnp.mean(values, axis=-1, keepdims=True)
    centred = values - mean
    spread = jnp.mean(centred * centred, axis=-1, keepdims=True)
    return centred * lax.rsqrt(spread + EPS) * gain + shift


def gelu_exact(values):
    return jax.nn.gelu(values, approximate=False)


def rotary_tables(positions):
    index = jnp.arange(ROT // 2, dtype=jnp.float32)
    inverse = jnp.exp(index * (-2.0 * math.log(10000.0) / ROT))
    angles = positions.astype(jnp.float32)[:, None] * inverse[None, :]
    angles = jnp.concatenate([angles, angles], axis=1)
    return (jnp.cos(angles), jnp.sin(angles))


def rotate(values, cosine, sine):
    part = values[..., :ROT]
    turned = jnp.concatenate([-part[..., ROT // 2 :], part[..., : ROT // 2]], axis=-1)
    moved = part * cosine[:, None, :] + turned * sine[:, None, :]
    return jnp.concatenate([moved, values[..., ROT:]], axis=-1)


def unit_positions(order):
    offsets = jnp.arange(UNIT, dtype=jnp.int32)
    return (order[:, None] * UNIT + offsets[None, :]).reshape(-1)


def piece_labels(positions, starts):
    inside = (positions[:, None] >= starts[None, :]) & (
        positions[:, None] < starts[None, :] + PIECE
    )
    labels = jnp.arange(1, starts.shape[0] + 1, dtype=jnp.int32)
    return jnp.sum(jnp.where(inside, labels[None, :], 0), axis=1) - 1


def visible(row_pos, row_lab, col_pos, col_lab):
    earlier = col_pos[None, :] <= row_pos[:, None]
    same = (row_lab[:, None] == col_lab[None, :]) & (row_lab[:, None] >= 0)
    return earlier | same


def merged_parts(first, merged_weight, merged_bias, cosine, sine):
    tokens = first.shape[0]
    width = first.shape[1]
    heads = width // HEAD
    merged = jnp.dot(first, merged_weight, preferred_element_type=jnp.float32) + merged_bias.astype(
        jnp.float32
    )
    queries = rotate(merged[:, :width].reshape(tokens, heads, HEAD), cosine, sine).astype(
        jnp.bfloat16
    )
    keys = rotate(merged[:, width : 2 * width].reshape(tokens, heads, HEAD), cosine, sine)
    keys = keys.reshape(tokens, width).astype(jnp.bfloat16)
    values = merged[:, 2 * width :].astype(jnp.bfloat16)
    return (queries, keys, values)


def block_view(queries, keys_all, values_all, row_pos, row_lab, col_pos, col_lab, span):
    heads = queries.shape[1]
    scale = 1.0 / math.sqrt(HEAD)

    def view(index):
        start = index * span
        key_rows = lax.dynamic_slice_in_dim(keys_all, start, span, 0).reshape(span, heads, HEAD)
        value_rows = lax.dynamic_slice_in_dim(values_all, start, span, 0).reshape(span, heads, HEAD)
        scores = (
            jnp.einsum("thd,khd->htk", queries, key_rows, preferred_element_type=jnp.float32)
            * scale
        )
        allowed = visible(
            row_pos,
            row_lab,
            lax.dynamic_slice_in_dim(col_pos, start, span, 0),
            lax.dynamic_slice_in_dim(col_lab, start, span, 0),
        )[None]
        return (scores, allowed, key_rows, value_rows)

    return view


def log_sums(view, count, heads, tokens):

    def log_step(carry, index):
        top, total = carry
        scores, allowed, key_rows, value_rows = view(index)
        masked = jnp.where(allowed, scores, NEGATIVE)
        newer = jnp.maximum(top, jnp.max(masked, axis=-1))
        terms = jnp.where(allowed, jnp.exp(masked - newer[..., None]), 0.0)
        total = total * jnp.exp(top - newer) + jnp.sum(terms, axis=-1)
        return ((newer, total), None)

    begin = (
        jnp.full((heads, tokens), NEGATIVE, jnp.float32),
        jnp.zeros((heads, tokens), jnp.float32),
    )
    (top, total), unused = lax.scan(log_step, begin, jnp.arange(count, dtype=jnp.int32))
    return top + jnp.log(total)


def mix_values(view, count, logsum, heads, tokens, grad_rows):

    def mix_step(carry, index):
        mixed, delta = carry
        scores, allowed, key_rows, value_rows = view(index)
        weights = jnp.where(allowed, jnp.exp(scores - logsum[..., None]), 0.0)
        mixed = mixed + jnp.einsum(
            "htk,khd->thd",
            weights.astype(jnp.bfloat16),
            value_rows,
            preferred_element_type=jnp.float32,
        )
        if grad_rows is not None:
            slopes = jnp.einsum(
                "thd,khd->htk", grad_rows, value_rows, preferred_element_type=jnp.float32
            )
            delta = delta + jnp.sum(weights * slopes, axis=-1)
        return ((mixed, delta), None)

    begin = (jnp.zeros((tokens, heads, HEAD), jnp.float32), jnp.zeros((heads, tokens), jnp.float32))
    (mixed, delta), unused = lax.scan(mix_step, begin, jnp.arange(count, dtype=jnp.int32))
    return (mixed, delta)


def attend_back(view, count, logsum, delta, grad_rows, queries):
    scale = 1.0 / math.sqrt(HEAD)

    def attend_step(carry, index):
        scores, allowed, key_rows, value_rows = view(index)
        weights = jnp.where(allowed, jnp.exp(scores - logsum[..., None]), 0.0)
        slopes = jnp.einsum(
            "thd,khd->htk", grad_rows, value_rows, preferred_element_type=jnp.float32
        )
        grad_scores = (weights * (slopes - delta[..., None])).astype(jnp.bfloat16)
        carry = carry + jnp.einsum(
            "htk,khd->thd", grad_scores, key_rows, preferred_element_type=jnp.float32
        )
        key_grad = jnp.einsum(
            "htk,thd->khd", grad_scores, queries, preferred_element_type=jnp.float32
        )
        value_grad = jnp.einsum(
            "htk,thd->khd",
            weights.astype(jnp.bfloat16),
            grad_rows,
            preferred_element_type=jnp.float32,
        )
        span = key_rows.shape[0]
        joined = jnp.concatenate(
            [key_grad.reshape(span, -1) * scale, value_grad.reshape(span, -1)], axis=1
        )
        return (carry, joined)

    begin = jnp.zeros(queries.shape, jnp.float32)
    grad_query, parts = lax.scan(attend_step, begin, jnp.arange(count, dtype=jnp.int32))
    return (grad_query * scale, parts)


def body(
    hidden_states,
    unit_order,
    piece_starts,
    first_gain,
    first_shift,
    second_gain,
    second_shift,
    merged_weight,
    merged_bias,
    output_weight,
    output_bias,
    expand_weight,
    expand_bias,
    contract_weight,
    contract_bias,
    out_cotangent,
):
    shards = (
        first_gain,
        first_shift,
        second_gain,
        second_shift,
        merged_weight,
        merged_bias,
        output_weight,
        output_bias,
        expand_weight,
        expand_bias,
        contract_weight,
        contract_bias,
    )
    gathered = (
        lax.all_gather(shards[0], "fsdp", axis=0, tiled=True),
        lax.all_gather(shards[1], "fsdp", axis=0, tiled=True),
        lax.all_gather(shards[2], "fsdp", axis=0, tiled=True),
        lax.all_gather(shards[3], "fsdp", axis=0, tiled=True),
        lax.all_gather(shards[4], "fsdp", axis=0, tiled=True),
        lax.all_gather(shards[5], "fsdp", axis=0, tiled=True),
        lax.all_gather(shards[6], "fsdp", axis=0, tiled=True),
        lax.all_gather(shards[7], "fsdp", axis=0, tiled=True),
        lax.all_gather(shards[8], "fsdp", axis=0, tiled=True),
        lax.all_gather(shards[9], "fsdp", axis=0, tiled=True),
        lax.all_gather(shards[10], "fsdp", axis=0, tiled=True),
        lax.all_gather(shards[11], "fsdp", axis=0, tiled=True),
    )
    hidden = hidden_states[0].astype(jnp.float32)
    tokens = hidden.shape[0]
    width = hidden.shape[1]
    heads = width // HEAD
    length = tokens * lax.axis_size("seq")
    span = min(length, 512)
    count = length // span
    col_pos = unit_positions(unit_order[0])
    col_lab = piece_labels(col_pos, piece_starts[0])
    offset = lax.axis_index("seq") * tokens
    row_pos = lax.dynamic_slice_in_dim(col_pos, offset, tokens, 0)
    row_lab = lax.dynamic_slice_in_dim(col_lab, offset, tokens, 0)
    cosine, sine = rotary_tables(row_pos)
    first = norm_rows(
        hidden, gathered[0].astype(jnp.float32), gathered[1].astype(jnp.float32)
    ).astype(jnp.bfloat16)
    queries, keys, values = merged_parts(first, gathered[4], gathered[5], cosine, sine)
    keys_all, values_all = (
        lax.all_gather(keys, "seq", axis=0, tiled=True),
        lax.all_gather(values, "seq", axis=0, tiled=True),
    )
    view = block_view(queries, keys_all, values_all, row_pos, row_lab, col_pos, col_lab, span)
    logsum = log_sums(view, count, heads, tokens)
    mixed, unused = mix_values(view, count, logsum, heads, tokens, None)
    mixed = mixed.reshape(tokens, width).astype(jnp.bfloat16)
    attention = jnp.dot(mixed, gathered[6], preferred_element_type=jnp.float32) + gathered[
        7
    ].astype(jnp.float32)
    second = norm_rows(
        hidden, gathered[2].astype(jnp.float32), gathered[3].astype(jnp.float32)
    ).astype(jnp.bfloat16)
    expanded = jnp.dot(second, gathered[8], preferred_element_type=jnp.float32) + gathered[
        9
    ].astype(jnp.float32)
    active = gelu_exact(expanded).astype(jnp.bfloat16)
    feed = jnp.dot(active, gathered[10], preferred_element_type=jnp.float32) + gathered[11].astype(
        jnp.float32
    )
    output = (hidden + attention + feed).astype(jnp.bfloat16)
    weights = (
        lax.all_gather(shards[0], "fsdp", axis=0, tiled=True),
        lax.all_gather(shards[1], "fsdp", axis=0, tiled=True),
        lax.all_gather(shards[2], "fsdp", axis=0, tiled=True),
        lax.all_gather(shards[3], "fsdp", axis=0, tiled=True),
        lax.all_gather(shards[4], "fsdp", axis=0, tiled=True),
        lax.all_gather(shards[5], "fsdp", axis=0, tiled=True),
        lax.all_gather(shards[6], "fsdp", axis=0, tiled=True),
        lax.all_gather(shards[7], "fsdp", axis=0, tiled=True),
        lax.all_gather(shards[8], "fsdp", axis=0, tiled=True),
        lax.all_gather(shards[9], "fsdp", axis=0, tiled=True),
        lax.all_gather(shards[10], "fsdp", axis=0, tiled=True),
        lax.all_gather(shards[11], "fsdp", axis=0, tiled=True),
    )
    cotangent = out_cotangent[0]
    upstream = cotangent.astype(jnp.float32)
    normed_one, first_pull = jax.vjp(
        norm_rows, hidden, weights[0].astype(jnp.float32), weights[1].astype(jnp.float32)
    )
    first = normed_one.astype(jnp.bfloat16)
    queries, keys, values = merged_parts(first, weights[4], weights[5], cosine, sine)
    keys_back, values_back = (
        lax.all_gather(keys, "seq", axis=0, tiled=True),
        lax.all_gather(values, "seq", axis=0, tiled=True),
    )
    view = block_view(queries, keys_back, values_back, row_pos, row_lab, col_pos, col_lab, span)
    grad_mixed = jnp.einsum(
        "te,de->td", cotangent, weights[6], preferred_element_type=jnp.float32
    ).astype(jnp.bfloat16)
    grad_rows = grad_mixed.reshape(tokens, heads, HEAD)
    mixed, delta = mix_values(view, count, logsum, heads, tokens, grad_rows)
    mixed = mixed.reshape(tokens, width).astype(jnp.bfloat16)
    grad_query, parts = attend_back(view, count, logsum, delta, grad_rows, queries)
    term = parts.reshape(length, 2 * width)
    own_grads = lax.psum_scatter(
        term.astype(jnp.bfloat16), "seq", scatter_dimension=0, tiled=True
    ).astype(jnp.float32)
    normed_two, second_pull = jax.vjp(
        norm_rows, hidden, weights[2].astype(jnp.float32), weights[3].astype(jnp.float32)
    )
    second = normed_two.astype(jnp.bfloat16)
    expanded = jnp.dot(second, weights[8], preferred_element_type=jnp.float32) + weights[9].astype(
        jnp.float32
    )
    activated, gelu_pull = jax.vjp(gelu_exact, expanded)
    active = activated.astype(jnp.bfloat16)
    grad_active = jnp.einsum(
        "te,fe->tf", cotangent, weights[10], preferred_element_type=jnp.float32
    )
    grad_expanded = gelu_pull(grad_active)[0].astype(jnp.bfloat16)
    grad_second = jnp.einsum(
        "tf,df->td", grad_expanded, weights[8], preferred_element_type=jnp.float32
    )
    unused, turn_pull = jax.vjp(rotate, grad_query, cosine, sine)
    query_back = turn_pull(grad_query)[0].reshape(tokens, width)
    key_back = turn_pull(own_grads[:, :width].reshape(tokens, heads, HEAD))[0].reshape(
        tokens, width
    )
    grad_merged = jnp.concatenate([query_back, key_back, own_grads[:, width:]], axis=1).astype(
        jnp.bfloat16
    )
    grad_first = jnp.einsum(
        "tc,dc->td", grad_merged, weights[4], preferred_element_type=jnp.float32
    )
    first_term, first_gain_grad, first_shift_grad = first_pull(grad_first)
    second_term, second_gain_grad, second_shift_grad = second_pull(grad_second)
    input_gradient = upstream + first_term + second_term
    row_total = jnp.sum(upstream, axis=0)
    local_grads = (
        first_gain_grad,
        first_shift_grad,
        second_gain_grad,
        second_shift_grad,
        jnp.einsum("td,tc->dc", first, grad_merged, preferred_element_type=jnp.float32),
        jnp.sum(grad_merged.astype(jnp.float32), axis=0),
        jnp.einsum("td,te->de", mixed, cotangent, preferred_element_type=jnp.float32),
        row_total,
        jnp.einsum("td,tf->df", second, grad_expanded, preferred_element_type=jnp.float32),
        jnp.sum(grad_expanded.astype(jnp.float32), axis=0),
        jnp.einsum("tf,te->fe", active, cotangent, preferred_element_type=jnp.float32),
        row_total,
    )
    owned = (
        lax.psum_scatter(
            local_grads[0].astype(jnp.bfloat16), "fsdp", scatter_dimension=0, tiled=True
        ).astype(jnp.float32),
        lax.psum_scatter(
            local_grads[1].astype(jnp.bfloat16), "fsdp", scatter_dimension=0, tiled=True
        ).astype(jnp.float32),
        lax.psum_scatter(
            local_grads[2].astype(jnp.bfloat16), "fsdp", scatter_dimension=0, tiled=True
        ).astype(jnp.float32),
        lax.psum_scatter(
            local_grads[3].astype(jnp.bfloat16), "fsdp", scatter_dimension=0, tiled=True
        ).astype(jnp.float32),
        lax.psum_scatter(
            local_grads[4].astype(jnp.bfloat16), "fsdp", scatter_dimension=0, tiled=True
        ).astype(jnp.float32),
        lax.psum_scatter(
            local_grads[5].astype(jnp.bfloat16), "fsdp", scatter_dimension=0, tiled=True
        ).astype(jnp.float32),
        lax.psum_scatter(
            local_grads[6].astype(jnp.bfloat16), "fsdp", scatter_dimension=0, tiled=True
        ).astype(jnp.float32),
        lax.psum_scatter(
            local_grads[7].astype(jnp.bfloat16), "fsdp", scatter_dimension=0, tiled=True
        ).astype(jnp.float32),
        lax.psum_scatter(
            local_grads[8].astype(jnp.bfloat16), "fsdp", scatter_dimension=0, tiled=True
        ).astype(jnp.float32),
        lax.psum_scatter(
            local_grads[9].astype(jnp.bfloat16), "fsdp", scatter_dimension=0, tiled=True
        ).astype(jnp.float32),
        lax.psum_scatter(
            local_grads[10].astype(jnp.bfloat16), "fsdp", scatter_dimension=0, tiled=True
        ).astype(jnp.float32),
        lax.psum_scatter(
            local_grads[11].astype(jnp.bfloat16), "fsdp", scatter_dimension=0, tiled=True
        ).astype(jnp.float32),
    )
    summed = lax.psum(
        (
            owned[0],
            owned[1],
            owned[2],
            owned[3],
            owned[4],
            owned[5],
            owned[6],
            owned[7],
            owned[8],
            owned[9],
            owned[10],
            owned[11],
        ),
        ("rep", "seq"),
    )
    return (
        output[None],
        input_gradient[None],
        summed[0],
        summed[1],
        summed[2],
        summed[3],
        summed[4],
        summed[5],
        summed[6],
        summed[7],
        summed[8],
        summed[9],
        summed[10],
        summed[11],
    )


MESH = pl.DeviceIdType.MESH
GROUP = 8
LINE = 4
HALF = ROT // 2
SPAN = 512
CHUNK = 32
FEED_CHUNK = 16


def place_here():
    c, y, s = (lax.axis_index("rep"), lax.axis_index("fsdp"), lax.axis_index("seq"))
    x = lax.rem(s, 2)
    return (c, y, x, s // 2)


def device_at(c, y, x, z):
    return (c, y, 2 * z + x)


def greet(partners):
    barrier = pltpu.get_barrier_semaphore()
    for partner in partners:
        pl.semaphore_signal(barrier, inc=1, device_id=partner, device_id_type=MESH)
    pl.semaphore_wait(barrier, len(partners))


def remote(src, dst, send, recv, target):
    return pltpu.make_async_remote_copy(
        src_ref=src,
        dst_ref=dst,
        send_sem=send,
        recv_sem=recv,
        device_id=target,
        device_id_type=MESH,
    )


def dot_rows(a, b):
    return lax.dot_general(a, b, (((1,), (1,)), ((), ())), preferred_element_type=jnp.float32)


def dot_tokens(a, b):
    return lax.dot_general(a, b, (((0,), (0,)), ((), ())), preferred_element_type=jnp.float32)


def dot_plain(a, b):
    return jnp.dot(a, b, preferred_element_type=jnp.float32)


class TokenExchange:
    def __init__(self, place, send, recv):
        self.place, self.send, self.recv = place, send, recv
        self.count = 0
        self.sends = []

    def go(self, src, dst, target):
        copy = remote(src, dst, self.send.at[self.count], self.recv.at[self.count], target)
        self.count += 1
        copy.start()
        self.sends.append(copy)
        return copy

    def blocks(self, cc):
        c, y, x, z = self.place

        def block(yy, xx):
            return (2 * cc + yy) * 2 + xx

        return (block(y, x), block(y, 1 - x), block(1 - y, x), block(1 - y, 1 - x))

    def start(self, src, full):
        c, y, x, z = self.place
        self.full = full
        me = self.blocks(c)[0]
        self.from_x = self.go(src, full.at[me], device_at(c, y, 1 - x, z))
        self.from_y = self.go(src, full.at[me], device_at(c, 1 - y, x, z))
        self.from_core = [self.go(src, full.at[me], device_at(1 - c, y, x, z))]

    def relay(self):
        c, y, x, z = self.place
        full = self.full
        me, near_x, near_y, far = self.blocks(c)
        half = full.shape[1] // 2
        core = device_at(1 - c, y, x, z)
        upper, lower = pl.ds(0, half), pl.ds(half, half)
        self.from_x.wait_recv()
        second = self.go(
            full.at[near_x, lower], full.at[near_x, lower], device_at(c, 1 - y, x, z)
        )
        self.from_core.append(self.go(full.at[near_x], full.at[near_x], core))
        self.from_y.wait_recv()
        first = self.go(full.at[near_y, upper], full.at[near_y, upper], device_at(c, y, 1 - x, z))
        self.from_core.append(self.go(full.at[near_y], full.at[near_y], core))
        self.corner = (first, second)

    def relay_corner(self):
        c, y, x, z = self.place
        far = self.blocks(c)[3]
        for copy in self.corner:
            copy.wait_recv()
        self.from_core.append(
            self.go(self.full.at[far], self.full.at[far], device_at(1 - c, y, x, z))
        )

    def wait_core(self, index):
        self.from_core[index].wait_recv()

    def finish(self):
        for copy in self.sends:
            copy.wait_send()


def column_block(part, at):
    return pl.ds(pl.multiple_of(at, part), part)


def enter_kernel(
    hid,
    ints,
    vec,
    wm,
    unit_cos,
    unit_sin,
    row_cos,
    row_sin,
    hid_all,
    ints_all,
    vec_all,
    wm_all,
    heads,
    second,
    units,
    rotated,
    send,
    recv,
    local,
):
    place = place_here()
    c, y, x, z = place
    core = device_at(1 - c, y, x, z)
    over_x = device_at(c, y, 1 - x, z)
    over_y = device_at(c, 1 - y, x, z)
    lanes = wm_all.shape[2] // 3
    width = wm.shape[1] // 3
    tokens = hid.shape[0]
    own = 4 * y + 2 * x + c
    other = 4 * (1 - y) + 2 * x + c
    moved = []

    def keep(src, dst):
        copy = pltpu.make_async_copy(src, dst, local.at[len(moved)])
        copy.start()
        moved.append(copy)
        return copy

    me = (2 * c + y) * 2 + x
    own_block = keep(hid, hid_all.at[me])
    keep(ints, ints_all.at[2 * c + y])
    keep(vec, vec_all.at[y])
    for j in range(3):
        keep(
            wm.at[:, column_block(lanes, j * width + own * lanes)],
            wm_all.at[y, :, pl.ds(j * lanes, lanes)],
        )
    greet((core, over_x, over_y))
    tokens_move = TokenExchange(place, send, recv)
    go = tokens_move.go
    ints_y = go(ints, ints_all.at[2 * c + y], over_y)
    vec_y = go(vec, vec_all.at[y], over_y)
    ints_core = [go(ints, ints_all.at[2 * c + y], core)]
    tokens_move.start(hid, hid_all)
    weights = [
        go(
            wm.at[:, column_block(lanes, j * width + other * lanes)],
            wm_all.at[y, :, pl.ds(j * lanes, lanes)],
            over_y,
        )
        for j in range(3)
    ]
    ints_y.wait_recv()
    ints_core.append(go(ints_all.at[2 * c + 1 - y], ints_all.at[2 * c + 1 - y], core))
    vec_y.wait_recv()
    for copy in moved:
        copy.wait()
    for copy in ints_core:
        copy.wait_recv()
    to_units = pltpu.make_async_copy(ints_all, units, local.at[0])
    to_units.start()
    to_units.wait()

    def vector(row):
        return jnp.concatenate(
            [vec_all[h, row + i : row + i + 1, :] for h in range(2) for i in range(4)], axis=1
        )

    gain_one, shift_one, gain_two, shift_two = [vector(4 * i) for i in range(4)]
    bias = []
    for j in range(3):
        at = j * GROUP + own
        bias.append(vec_all[at // 12, pl.ds(16 + lax.rem(at, 12), 1), :])
    bias = jnp.concatenate(bias, axis=1)

    def normal(block):
        raw = hid_all[block].astype(jnp.float32)
        mean = jnp.mean(raw, axis=1, keepdims=True)
        centred = raw - mean
        rstd = lax.rsqrt(jnp.mean(centred * centred, axis=1, keepdims=True) + EPS)
        xhat = centred * rstd
        rows = pl.ds(pl.multiple_of(block * tokens, tokens), tokens)
        second[rows, :] = (xhat * gain_two + shift_two).astype(jnp.bfloat16)
        return (xhat * gain_one + shift_one).astype(jnp.bfloat16)

    unit_index = lax.broadcasted_iota(jnp.int32, unit_cos.shape, 0)
    lane = lax.rem(lax.broadcasted_iota(jnp.int32, row_cos.shape, 1), HEAD)

    def project(block):
        rows = pl.ds(pl.multiple_of(block * tokens, tokens), tokens)
        sequence, side = block // 2, lax.rem(block, 2)
        normed = normal(block)
        half = wm.shape[0]
        merged = (
            dot_plain(normed[:, :half], wm_all[0])
            + dot_plain(normed[:, half:], wm_all[1])
            + bias
        )
        count = tokens // UNIT
        for u in range(count):
            unit = units[sequence, 0, (2 * z + side) * count + u]
            here = pl.ds(u * UNIT, UNIT)
            chosen = unit_index == unit
            base_cos = jnp.sum(jnp.where(chosen, unit_cos[...], 0.0), axis=0, keepdims=True)
            base_sin = jnp.sum(jnp.where(chosen, unit_sin[...], 0.0), axis=0, keepdims=True)
            sine = base_sin * row_cos[...] + base_cos * row_sin[...]
            rotated[0, here, :] = base_cos * row_cos[...] - base_sin * row_sin[...]
            rotated[1, here, :] = jnp.where(lane < HALF, sine, 0.0)
            rotated[2, here, :] = jnp.where(lane < HALF, 0.0, sine)
        for j in range(2):
            values = merged[:, j * lanes : (j + 1) * lanes]
            turned = (
                values * rotated[0]
                - pltpu.roll(values, lanes - HALF, 1) * rotated[1]
                + pltpu.roll(values, HALF, 1) * rotated[2]
            )
            heads[j, rows, :] = turned.astype(jnp.bfloat16)
        heads[2, rows, :] = merged[:, 2 * lanes :].astype(jnp.bfloat16)

    tokens_move.relay()
    for copy in weights:
        copy.wait_recv()
    mine, theirs = tokens_move.blocks(c), tokens_move.blocks(1 - c)
    for index in range(3):
        project(mine[index])
    tokens_move.relay_corner()
    for index in range(3):
        tokens_move.wait_core(index)
        project(theirs[index])
    project(mine[3])
    tokens_move.wait_core(3)
    project(theirs[3])
    tokens_move.finish()


def enter(hid, ints, vec, wm, tables):
    tokens, width = hid.shape
    rows = wm.shape[0]
    lanes = width // GROUP
    vmem = pl.BlockSpec(memory_space=pltpu.VMEM)
    any_spec = pl.BlockSpec(memory_space=pl.ANY)
    return pl.pallas_call(
        enter_kernel,
        out_shape=(
            jax.ShapeDtypeStruct((GROUP,) + hid.shape, hid.dtype),
            jax.ShapeDtypeStruct((4,) + ints.shape, ints.dtype),
            jax.ShapeDtypeStruct((2,) + vec.shape, vec.dtype),
            jax.ShapeDtypeStruct((2, rows, 3 * lanes), wm.dtype),
            jax.ShapeDtypeStruct((3, GROUP * tokens, lanes), jnp.bfloat16),
            jax.ShapeDtypeStruct((GROUP * tokens, width), jnp.bfloat16),
        ),
        in_specs=[any_spec] * 4 + [vmem] * 4,
        out_specs=[vmem, any_spec, vmem, vmem, vmem, vmem],
        scratch_shapes=[
            pltpu.SMEM((4,) + ints.shape, jnp.int32),
            pltpu.VMEM((3, tokens, lanes), jnp.float32),
            pltpu.SemaphoreType.DMA((20,)),
            pltpu.SemaphoreType.DMA((20,)),
            pltpu.SemaphoreType.DMA((8,)),
        ],
        compiler_params=pltpu.CompilerParams(
            collective_id=0, has_side_effects=True, vmem_limit_bytes=48 << 20
        ),
        name="enter",
    )(hid, ints, vec, wm, *tables)


def greet_line(place, more=()):
    c, y, x, z = place
    barrier = pltpu.get_barrier_semaphore()
    partners = (device_at(1 - c, y, x, z), device_at(c, y, 1 - x, z), device_at(c, 1 - y, x, z))
    for partner in partners:
        pl.semaphore_signal(barrier, inc=1, device_id=partner, device_id_type=MESH)

    @pl.when(z > 0)
    def _():
        pl.semaphore_signal(barrier, inc=1, device_id=device_at(c, y, x, z - 1), device_id_type=MESH)

    @pl.when(z < LINE - 1)
    def _():
        pl.semaphore_signal(barrier, inc=1, device_id=device_at(c, y, x, z + 1), device_id_type=MESH)

    @pl.when((z > 0) & (z < LINE - 1))
    def _():
        pl.semaphore_wait(barrier, 5)

    @pl.when((z == 0) | (z == LINE - 1))
    def _():
        pl.semaphore_wait(barrier, 4)


TILE = 256


def feed_kernel(
    heads,
    second,
    cot,
    we,
    wo,
    wc,
    bias,
    got,
    cot_all,
    we_all,
    active,
    grad_expanded,
    feed_grad,
    sums,
    slope,
    grad_heads,
    send,
    recv,
    token_send,
    token_recv,
    local,
):
    place = place_here()
    c, y, x, z = place
    rows = got.shape[2]
    tokens = cot.shape[0]
    ff = we_all.shape[2]
    half = we.shape[0]
    own = 4 * y + 2 * x + c
    other = 4 * (1 - y) + 2 * x + c
    core = device_at(1 - c, y, x, z)
    over_x = device_at(c, y, 1 - x, z)
    over_y = device_at(c, 1 - y, x, z)
    peers = [lax.rem(z + d, LINE) for d in range(1, LINE)]
    mine = pl.ds(pl.multiple_of(z * rows, rows), rows)
    me = (2 * c + y) * 2 + x
    keeps = [
        pltpu.make_async_copy(we.at[:, column_block(ff, own * ff)], we_all.at[y], local.at[0]),
        pltpu.make_async_copy(cot, cot_all.at[me], local.at[1]),
        pltpu.make_async_copy(heads.at[:, mine], got.at[pl.ds(0, 3), z], local.at[2]),
    ]
    for copy in keeps:
        copy.start()
    greet([device_at(c, y, x, peer) for peer in peers] + [core, over_x, over_y])
    tokens_move = TokenExchange(place, token_send, token_recv)
    weight = tokens_move.go(we.at[:, column_block(ff, other * ff)], we_all.at[y], over_y)
    tokens_move.start(cot, cot_all)
    copies = []
    for index, peer in enumerate(peers):
        copy = remote(
            heads.at[:, pl.ds(pl.multiple_of(peer * rows, rows), rows)],
            got.at[pl.ds(0, 3), z],
            send.at[0, index],
            recv.at[0, index],
            device_at(c, y, x, peer),
        )
        copy.start()
        copies.append(copy)
    for copy in keeps[:2]:
        copy.wait()
    weight.wait_recv()
    sums[...] = jnp.zeros_like(sums)

    def forward(index, carry):
        at = pl.ds(pl.multiple_of(index * TILE, TILE), TILE)
        normed = second[at, :]
        expanded = (
            dot_plain(normed[:, :half], we_all[0])
            + dot_plain(normed[:, half:], we_all[1])
            + bias[...]
        )
        below = 0.5 * (1.0 + lax.erf(expanded * math.sqrt(0.5)))
        density = jnp.exp(expanded * expanded * -0.5) * (1.0 / math.sqrt(2.0 * math.pi))
        active[at, :] = (expanded * below).astype(jnp.bfloat16)
        slope[at, :] = below + expanded * density
        return carry

    tiles = second.shape[0] // TILE
    lax.fori_loop(0, tiles // 2, forward, 0)
    tokens_move.relay()
    lax.fori_loop(tiles // 2, tiles, forward, 0)
    tokens_move.relay_corner()

    def backward(block):
        at = pl.ds(pl.multiple_of(block * tokens, tokens), tokens)
        cots = cot_all[block]
        grad_heads[at, :] = dot_rows(cots, wo[...]).astype(jnp.bfloat16)
        grad = (dot_rows(cots, wc[...]) * slope[at, :]).astype(jnp.bfloat16)
        grad_expanded[at, :] = grad
        sums[...] += jnp.sum(grad.astype(jnp.float32), axis=0, keepdims=True)

    ours, theirs = tokens_move.blocks(c), tokens_move.blocks(1 - c)
    for index in range(4):
        backward(ours[index])
    for index in range(4):
        tokens_move.wait_core(index)
        backward(theirs[index])
    for index, peer in enumerate(peers):
        copy = remote(
            grad_heads.at[pl.ds(pl.multiple_of(peer * rows, rows), rows)],
            got.at[3, z],
            send.at[1, index],
            recv.at[1, index],
            device_at(c, y, x, peer),
        )
        copy.start()
        copies.append(copy)
    last = pltpu.make_async_copy(grad_heads.at[mine], got.at[3, z], local.at[0])
    last.start()
    for index in range(2 * half // TILE):
        block = dot_tokens(second[:, pl.ds(index * TILE, TILE)], grad_expanded[...])
        side, row = divmod(index * TILE, half)
        feed_grad[pl.ds(row, TILE), pl.ds(side * ff, ff)] = block.astype(jnp.bfloat16)
    cots = cot_all[...].reshape(GROUP * tokens, 2 * half)
    for index in range(ff // TILE):
        block = dot_tokens(active[:, pl.ds(index * TILE, TILE)], cots)
        feed_grad[pl.ds(index * TILE, TILE), pl.ds(2 * ff, 2 * half)] = block.astype(jnp.bfloat16)
    keeps[2].wait()
    last.wait()
    for copy in copies:
        copy.wait()
    tokens_move.finish()


def feed_forward(heads, second, cot, we, wo, wc, bias):
    rows, width = second.shape
    ff = we.shape[1] // GROUP
    lanes = heads.shape[2]
    vmem = pl.BlockSpec(memory_space=pltpu.VMEM)
    any_spec = pl.BlockSpec(memory_space=pl.ANY)
    return pl.pallas_call(
        feed_kernel,
        out_shape=(
            jax.ShapeDtypeStruct((4, LINE, rows // LINE, lanes), heads.dtype),
            jax.ShapeDtypeStruct((GROUP,) + cot.shape, cot.dtype),
            jax.ShapeDtypeStruct((2, we.shape[0], ff), we.dtype),
            jax.ShapeDtypeStruct((rows, ff), jnp.bfloat16),
            jax.ShapeDtypeStruct((rows, ff), jnp.bfloat16),
            jax.ShapeDtypeStruct((width // 2, 2 * ff + width), jnp.bfloat16),
            jax.ShapeDtypeStruct((1, ff), jnp.float32),
        ),
        in_specs=[any_spec, vmem, any_spec, any_spec, vmem, vmem, vmem],
        out_specs=[any_spec] + [vmem] * 6,
        scratch_shapes=[
            pltpu.VMEM((rows, ff), jnp.float32),
            pltpu.VMEM((rows, lanes), jnp.bfloat16),
            pltpu.SemaphoreType.DMA((2, LINE - 1)),
            pltpu.SemaphoreType.DMA((2, LINE - 1)),
            pltpu.SemaphoreType.DMA((12,)),
            pltpu.SemaphoreType.DMA((12,)),
            pltpu.SemaphoreType.DMA((3,)),
        ],
        compiler_params=pltpu.CompilerParams(
            collective_id=1, has_side_effects=True, vmem_limit_bytes=56 << 20
        ),
        name="feed_forward",
    )(heads, second, cot, we, wo, wc, bias)


class LineReduce:
    LAG = 2

    def __init__(self, grad, result, inbox, sems, swap, size, place):
        self.grad, self.result, self.inbox, self.sems, self.swap = grad, result, inbox, sems, swap
        self.c, self.y, self.x, self.z = place
        self.size = size
        self.each = grad.shape[0] // size // 2
        self.slots = self.each + (LINE - 1) * self.LAG

    def rows(self, chunk):
        return pl.ds(pl.multiple_of(chunk * self.size, self.size), self.size)

    def lanes(self, which):
        return pl.ds(pl.multiple_of(which * self.swap, self.swap), self.swap)

    def ahead(self, chunk, half):
        up = 1 if half == 0 else -1
        rows = self.rows(chunk)
        return remote(
            self.grad.at[rows],
            self.inbox.at[rows],
            self.sems.at[0, chunk],
            self.sems.at[1, chunk],
            device_at(self.c, self.y, self.x, self.z + up),
        )

    def across(self, chunk):
        rows = self.rows(chunk)
        return remote(
            self.grad.at[rows, self.lanes(1 - self.y)],
            self.result.at[rows, self.lanes(self.y)],
            self.sems.at[2, chunk],
            self.sems.at[3, chunk],
            device_at(self.c, 1 - self.y, self.x, self.z),
        )

    def slot(self, t):
        for half in range(2):
            at = self.z if half == 0 else LINE - 1 - self.z
            step = t - self.LAG * at
            chunk = jnp.clip(step, 0, self.each - 1) + half * self.each

            @pl.when((step >= 0) & (step < self.each))
            def _():
                rows = self.rows(chunk)

                @pl.when(at > 0)
                def _():
                    self.ahead(chunk, half).wait_recv()
                    total = self.grad[rows].astype(jnp.float32) + self.inbox[rows].astype(
                        jnp.float32
                    )
                    self.grad[rows] = total.astype(jnp.bfloat16)

                @pl.when(at < LINE - 1)
                def _():
                    self.ahead(chunk, half).start()

                @pl.when(at == LINE - 1)
                def _():
                    self.across(chunk).start()
                    own = self.lanes(self.y)
                    plain = pl.ds(2 * self.swap, self.grad.shape[1] - 2 * self.swap)
                    self.result[rows, own] = self.grad[rows, own]
                    self.result[rows, plain] = self.grad[rows, plain]

    def drain(self):
        for half in range(2):
            at = self.z if half == 0 else LINE - 1 - self.z

            def finish(step, carry):
                chunk = step + half * self.each

                @pl.when(at < LINE - 1)
                def _():
                    self.ahead(chunk, half).wait_send()

                @pl.when(at == LINE - 1)
                def _():
                    self.across(chunk).wait()

                return carry

            lax.fori_loop(0, self.each, finish, 0)


class LineSpread:
    def __init__(self, result, sems, size, place):
        self.result, self.sems = result, sems
        self.c, self.y, self.x, self.z = place
        self.size = size
        self.each = result.shape[2] // size // 2
        self.slots = self.each + LINE

    def move(self, kind, chunk, half):
        c, y, x, z = self.c, self.y, self.x, self.z
        up = 1 if half == 0 else -1
        rows = pl.ds(pl.multiple_of(chunk * self.size, self.size), self.size)
        side = 1 - x if kind == 3 else x
        target = (
            device_at(c, y, x, z - up),
            device_at(c, y, 1 - x, z),
            device_at(1 - c, y, x, z),
            device_at(1 - c, y, x, z),
        )[kind]
        part = self.result.at[c, side, rows]
        return remote(
            part, part, self.sems.at[2 * kind, chunk], self.sems.at[2 * kind + 1, chunk], target
        )

    def slot(self, t):
        for half in range(2):
            at = self.z if half == 0 else LINE - 1 - self.z

            def event(delay, run):
                step = t - delay
                chunk = jnp.clip(step, 0, self.each - 1) + half * self.each

                @pl.when((step >= 0) & (step < self.each))
                def _():
                    run(chunk)

            def spread(chunk):
                @pl.when(at < LINE - 1)
                def _():
                    self.move(0, chunk, half).wait_recv()

                @pl.when(at > 0)
                def _():
                    self.move(0, chunk, half).start()

                self.move(1, chunk, half).start()
                self.move(2, chunk, half).start()

            def late(chunk):
                self.move(1, chunk, half).wait_recv()
                self.move(3, chunk, half).start()

            event(LINE - 1 - at, spread)
            event(LINE - at, late)

    def drain(self):
        for half in range(2):
            at = self.z if half == 0 else LINE - 1 - self.z

            def finish(step, carry):
                chunk = step + half * self.each

                @pl.when(at > 0)
                def _():
                    self.move(0, chunk, half).wait_send()

                self.move(1, chunk, half).wait_send()
                self.move(2, chunk, half).wait()
                self.move(3, chunk, half).wait()
                return carry

            lax.fori_loop(0, self.each, finish, 0)


class LineSum:
    LAG = 1
    KINDS = 8

    def __init__(self, grad, result, inbox, sems, swap, size, place):
        self.grad, self.result, self.inbox, self.sems, self.swap = grad, result, inbox, sems, swap
        self.c, self.y, self.x, self.z = place
        self.size = size
        self.count = grad.shape[0] // size
        self.split = (self.count + 1) // 2
        self.slots = self.split + 6 * self.LAG

    def rows(self, chunk):
        return pl.ds(pl.multiple_of(chunk * self.size, self.size), self.size)

    def moves(self, chunk, half):
        c, y, x, z = self.c, self.y, self.x, self.z
        up = 1 if half == 0 else -1
        rows = self.rows(chunk)
        grad, result, swap = self.grad, self.result, self.swap
        mine = result.at[c, x, rows]
        beside = result.at[c, 1 - x, rows]
        lower, upper = device_at(c, y, x, z - up), device_at(c, y, x, z + up)

        def lanes(which):
            return pl.ds(pl.multiple_of(which * swap, swap), swap)

        makers = {
            "near": (0, lambda: (grad.at[rows], self.inbox.at[0, rows], upper)),
            "far": (1, lambda: (grad.at[rows], self.inbox.at[1, rows], lower)),
            "swap": (
                2,
                lambda: (
                    grad.at[rows, lanes(1 - y)],
                    result.at[c, x, rows, lanes(y)],
                    device_at(c, 1 - y, x, z),
                ),
            ),
            "down": (3, lambda: (mine, mine, lower)),
            "out": (4, lambda: (mine, mine, upper)),
            "side": (5, lambda: (mine, mine, device_at(c, y, 1 - x, z))),
            "core": (6, lambda: (mine, mine, device_at(1 - c, y, x, z))),
            "late": (7, lambda: (beside, beside, device_at(1 - c, y, x, z))),
        }

        def make(name):
            kind, parts = makers[name]
            src, dst, target = parts()
            return remote(
                src, dst, self.sems.at[2 * kind, chunk], self.sems.at[2 * kind + 1, chunk], target
            )

        return make

    def slot(self, t):
        for half in range(2):
            self.half_slot(t, half)

    def extent(self, half):
        size = self.split if half == 0 else self.count - self.split
        base = 0 if half == 0 else self.split
        at = self.z if half == 0 else LINE - 1 - self.z
        return (size, base, at)

    def half_slot(self, t, half):
        size, base, at = self.extent(half)
        lag = self.LAG
        swap = self.swap
        owner = at == 1

        def event(delay, run):
            chunk = t - delay
            index = jnp.clip(chunk, 0, size - 1) + base

            @pl.when((chunk >= 0) & (chunk < size))
            def _():
                run(index, self.moves(index, half))

        def reduce(index, moves):
            rows = self.rows(index)

            @pl.when(at == 0)
            def _():
                moves("near").start()

            @pl.when(at == 2)
            def _():
                moves("far").wait_recv()
                total = self.grad[rows].astype(jnp.float32) + self.inbox[1, rows].astype(
                    jnp.float32
                )
                self.grad[rows] = total.astype(jnp.bfloat16)

            @pl.when(at >= 2)
            def _():
                moves("far").start()

            @pl.when(owner)
            def _():
                moves("near").wait_recv()
                moves("far").wait_recv()
                total = (
                    self.grad[rows].astype(jnp.float32)
                    + self.inbox[0, rows].astype(jnp.float32)
                    + self.inbox[1, rows].astype(jnp.float32)
                )
                self.grad[rows] = total.astype(jnp.bfloat16)
                moves("swap").start()
                own = pl.ds(pl.multiple_of(self.y * swap, swap), swap)
                plain = pl.ds(2 * swap, self.grad.shape[1] - 2 * swap)
                self.result[self.c, self.x, rows, own] = self.grad[rows, own]
                self.result[self.c, self.x, rows, plain] = self.grad[rows, plain]

        event(jnp.where(owner, 2 * lag, jnp.where(at == 2, lag, 0)), reduce)

        def spread(index, moves):
            @pl.when(owner)
            def _():
                moves("swap").wait_recv()
                moves("down").start()

            @pl.when(at == 0)
            def _():
                moves("down").wait_recv()

            @pl.when(at >= 2)
            def _():
                moves("out").wait_recv()

            @pl.when((at == 1) | (at == 2))
            def _():
                moves("out").start()

            moves("side").start()
            moves("core").start()

        wait = jnp.where(owner, 3 * lag, jnp.where(at == 3, 5 * lag, 4 * lag))
        event(wait, spread)

        def late(index, moves):
            moves("side").wait_recv()
            moves("late").start()

        event(wait + lag, late)

    def drain(self):
        for half in range(2):
            size, base, at = self.extent(half)

            def finish(chunk, carry):
                moves = self.moves(chunk + base, half)

                @pl.when(at == 0)
                def _():
                    moves("near").wait_send()

                @pl.when(at >= 2)
                def _():
                    moves("far").wait_send()

                @pl.when(at == 1)
                def _():
                    moves("swap").wait_send()
                    moves("down").wait_send()

                @pl.when((at == 1) | (at == 2))
                def _():
                    moves("out").wait_send()

                moves("side").wait_send()
                moves("core").wait()
                moves("late").wait()
                return carry

            lax.fori_loop(0, size, finish, 0)


def attention_kernel(
    ints,
    parts,
    unit_cos,
    unit_sin,
    row_cos,
    row_sin,
    feed_grad,
    out,
    feed_sum,
    masked,
    flat,
    scores,
    slopes,
    key_sum,
    value_sum,
    mixed_sum,
    query_sum,
    feed_own,
    feed_inbox,
    feed_sems,
    local,
    *,
    units,
    pieces,
    swap,
):
    here = place_here()
    greet_line(here)
    load = pltpu.make_async_copy(feed_grad, feed_own, local)
    load.start()
    line = LineReduce(feed_own, feed_sum, feed_inbox, feed_sems, swap, FEED_CHUNK, here)
    length = parts.shape[1]
    scale = 1.0 / math.sqrt(HEAD)
    blocks = length // SPAN
    lanes = lax.broadcasted_iota(jnp.int32, (UNIT, 2 * HEAD), 1)
    lower = lanes < HEAD

    def arrange(index, carry):
        at = pl.ds(pl.multiple_of(index * UNIT, UNIT), UNIT)
        for which in range(4):
            rows = jnp.zeros((UNIT, 2 * HEAD), jnp.bfloat16)
            for unit in range(units):
                rows = jnp.where(
                    ints[0, unit] == index, parts[which, pl.ds(unit * UNIT, UNIT), :], rows
                )
            rows = rows.astype(jnp.float32)
            if which == 0:
                rows = rows * scale
            masked[which, 0, at, :] = jnp.where(lower, rows, 0.0).astype(jnp.bfloat16)
            masked[which, 1, at, :] = jnp.where(lower, 0.0, rows).astype(jnp.bfloat16)
            flat[which, :, at] = rows.T.astype(jnp.bfloat16)
        return carry

    lax.fori_loop(0, units, arrange, 0)
    load.wait()
    key_sum[...] = jnp.zeros_like(key_sum)
    value_sum[...] = jnp.zeros_like(value_sum)

    def labels(positions):
        found = jnp.full(positions.shape, -1, jnp.int32)
        for piece in range(pieces):
            start = ints[0, units + piece]
            found = jnp.where(
                (positions >= start) & (positions < start + PIECE), piece, found
            )
        return found

    def dot(a, b):
        return jnp.dot(a, b, preferred_element_type=jnp.float32)

    for block in range(blocks):
        begin = block * SPAN
        last = SPAN + (UNIT if block + 1 < blocks else 0)
        columns = pl.ds(begin, SPAN)
        row_at = begin + lax.broadcasted_iota(jnp.int32, (1, SPAN), 1)
        col_at = begin + lax.broadcasted_iota(jnp.int32, (last, 1), 0)
        row_lab = labels(row_at)
        col_lab = labels(col_at)
        allowed = (col_at <= row_at) | (
            (col_lab == row_lab) & (row_lab >= 0)
        )

        def one_head(head, carry):
            slot = 3 * (2 * block + head)
            line.slot(slot)
            queries = flat[0, :, columns]
            grads = flat[3, :, columns]
            side = pl.ds(pl.multiple_of(head * HEAD, HEAD), HEAD)

            def score_tile(start, size, top, mask):
                rows = pl.ds(start, size)
                tile = dot(masked[1, head, rows, :], queries)
                if mask is not None:
                    tile = jnp.where(mask, tile, NEGATIVE)
                scores[rows, :] = tile
                return jnp.maximum(top, jnp.max(tile, axis=0, keepdims=True))

            top = lax.fori_loop(
                0,
                block,
                lambda j, top: score_tile(pl.multiple_of(j * SPAN, SPAN), SPAN, top, None),
                jnp.full((1, SPAN), NEGATIVE, jnp.float32),
            )
            top = score_tile(begin, last, top, allowed)

            def weight_tile(start, size, sums):
                total, delta = sums
                rows = pl.ds(start, size)
                weights = jnp.exp(scores[rows, :] - top)
                slope = dot(masked[2, head, rows, :], grads)
                scores[rows, :] = weights
                slopes[rows, :] = slope
                return (
                    total + jnp.sum(weights, axis=0, keepdims=True),
                    delta + jnp.sum(weights * slope, axis=0, keepdims=True),
                )

            line.slot(slot + 1)
            zero = jnp.zeros((1, SPAN), jnp.float32)
            sums = lax.fori_loop(
                0,
                block,
                lambda j, sums: weight_tile(pl.multiple_of(j * SPAN, SPAN), SPAN, sums),
                (zero, zero),
            )
            total, delta = weight_tile(begin, last, sums)
            inverse = 1.0 / total
            delta = delta * inverse

            def grad_tile(start, size, sums):
                mixed, query = sums
                rows = pl.ds(start, size)
                probs = scores[rows, :] * inverse
                grad = (probs * (slopes[rows, :] - delta)).astype(jnp.bfloat16)
                probs = probs.astype(jnp.bfloat16)
                value_sum[rows, :] += dot(probs, masked[3, head, columns, :])
                key_sum[rows, :] += dot(grad, masked[0, head, columns, :])
                mixed = mixed + dot(flat[2, side, rows], probs)
                query = query + dot(flat[1, side, rows], grad)
                return (mixed, query)

            line.slot(slot + 2)
            none = jnp.zeros((HEAD, SPAN), jnp.float32)
            sums = lax.fori_loop(
                0,
                block,
                lambda j, sums: grad_tile(pl.multiple_of(j * SPAN, SPAN), SPAN, sums),
                (none, none),
            )
            mixed, query = grad_tile(begin, last, sums)
            mixed_sum[side, columns] = mixed
            query_sum[side, columns] = query * scale
            return carry

        lax.fori_loop(0, 2, one_head, 0)

    lane = lax.rem(lax.broadcasted_iota(jnp.int32, row_cos.shape, 1), HEAD)

    def finish(index, carry):
        at = pl.ds(pl.multiple_of(index * UNIT, UNIT), UNIT)
        base_cos, base_sin = unit_cos[pl.ds(index, 1), :], unit_sin[pl.ds(index, 1), :]
        cosine = base_cos * row_cos[...] - base_sin * row_sin[...]
        sine = base_sin * row_cos[...] + base_cos * row_sin[...]
        sine_up = jnp.where(lane < HALF, sine, 0.0)
        sine_down = jnp.where(lane < HALF, 0.0, sine)

        def turn_back(rows):
            up = pltpu.roll(rows, 2 * HEAD - HALF, 1)
            down = pltpu.roll(rows, HALF, 1)
            return rows * cosine + up * sine_up - down * sine_down

        masked[0, 0, at, :] = mixed_sum[:, at].T.astype(jnp.bfloat16)
        masked[1, 0, at, :] = turn_back(query_sum[:, at].T).astype(jnp.bfloat16)
        masked[2, 0, at, :] = turn_back(key_sum[at, :]).astype(jnp.bfloat16)
        masked[3, 0, at, :] = value_sum[at, :].astype(jnp.bfloat16)
        return carry

    lax.fori_loop(0, units, finish, 0)

    def restore(index, carry):
        here = pl.ds(pl.multiple_of(index * UNIT, UNIT), UNIT)
        for which in range(4):
            rows = jnp.zeros((UNIT, 2 * HEAD), jnp.bfloat16)
            for unit in range(units):
                rows = jnp.where(
                    ints[0, index] == unit, masked[which, 0, pl.ds(unit * UNIT, UNIT), :], rows
                )
            out[which, here, :] = rows
        return carry

    lax.fori_loop(0, units, restore, 0)

    def more(slot, carry):
        line.slot(slot)
        return carry

    lax.fori_loop(6 * blocks, max(line.slots, 6 * blocks), more, 0)
    line.drain()


def attend(ints, parts, tables, feed_grad, units, pieces, swap):
    length = parts.shape[1]
    vmem = pl.BlockSpec(memory_space=pltpu.VMEM)
    return pl.pallas_call(
        functools.partial(attention_kernel, units=units, pieces=pieces, swap=swap),
        out_shape=(
            jax.ShapeDtypeStruct(parts.shape, parts.dtype),
            jax.ShapeDtypeStruct(feed_grad.shape, feed_grad.dtype),
        ),
        in_specs=[pl.BlockSpec(memory_space=pltpu.SMEM)]
        + [vmem] * 5
        + [pl.BlockSpec(memory_space=pl.ANY)],
        out_specs=[vmem, vmem],
        scratch_shapes=[
            pltpu.VMEM((4, 2, length, 2 * HEAD), jnp.bfloat16),
            pltpu.VMEM((4, 2 * HEAD, length), jnp.bfloat16),
            pltpu.VMEM((length, SPAN), jnp.float32),
            pltpu.VMEM((length, SPAN), jnp.float32),
            pltpu.VMEM((length, 2 * HEAD), jnp.float32),
            pltpu.VMEM((length, 2 * HEAD), jnp.float32),
            pltpu.VMEM((2 * HEAD, length), jnp.float32),
            pltpu.VMEM((2 * HEAD, length), jnp.float32),
            pltpu.VMEM(feed_grad.shape, jnp.bfloat16),
            pltpu.VMEM(feed_grad.shape, jnp.bfloat16),
            pltpu.SemaphoreType.DMA((4, feed_grad.shape[0] // FEED_CHUNK)),
            pltpu.SemaphoreType.DMA,
        ],
        compiler_params=pltpu.CompilerParams(
            collective_id=2, has_side_effects=True, vmem_limit_bytes=56 << 20
        ),
        name="attend",
    )(ints, parts, *tables, feed_grad)


def close_kernel(
    done,
    active,
    grad_expanded,
    we,
    wc,
    wm,
    wo,
    hidden,
    cots,
    vectors,
    feed_sums,
    feed_sum,
    attn_all,
    feed_all,
    out_sum,
    term_sum,
    parts,
    first,
    stats,
    outs,
    terms,
    attn_own,
    attn_inbox,
    near,
    four,
    mid,
    two,
    far,
    totals,
    send,
    recv,
    attn_sems,
    feed_sems,
    sems,
    local,
    *,
    swap,
):
    place = place_here()
    c, y, x, z = place
    core = device_at(1 - c, y, x, z)
    over_x = device_at(c, y, 1 - x, z)
    over_y = device_at(c, 1 - y, x, z)
    barrier = pltpu.get_barrier_semaphore()
    peers = [lax.rem(z + d, LINE) for d in range(1, LINE)]
    partners = [device_at(c, y, x, peer) for peer in peers] + [core, over_x, over_y]
    for partner in partners:
        pl.semaphore_signal(barrier, inc=1, device_id=partner, device_id_type=MESH)
    pl.semaphore_wait(barrier, len(partners))
    rows = done.shape[2]
    lanes = done.shape[3]
    mine = pl.ds(pl.multiple_of(z * rows, rows), rows)
    copies = []
    for index, peer in enumerate(peers):
        for which in (1, 2, 3, 0):
            copy = remote(
                done.at[which, peer],
                parts.at[mine, pl.ds(which * lanes, lanes)],
                send.at[index, which],
                recv.at[index, which],
                device_at(c, y, x, peer),
            )
            copy.start()
            copies.append(copy)
    owns = []
    for which in range(4):
        copy = pltpu.make_async_copy(
            done.at[which, z], parts.at[mine, pl.ds(which * lanes, lanes)], local.at[which]
        )
        copy.start()
        owns.append(copy)
    spread = LineSpread(feed_all, feed_sems, CHUNK, place)
    own_half = CHUNK * spread.each

    @pl.when((z == 0) | (z == LINE - 1))
    def _():
        at = pl.ds(pl.multiple_of(jnp.where(z == 0, own_half, 0), own_half), own_half)
        copy = pltpu.make_async_copy(feed_sum.at[at], feed_all.at[c, x, at], local.at[4])
        copy.start()
        copy.wait()

    gain_one, shift_one, gain_two = vectors[0:1, :], vectors[1:2, :], vectors[2:3, :]
    width = hidden.shape[1]
    half = width // 2
    tokens = outs.shape[1]
    totals[...] = jnp.zeros_like(totals)

    def normed(at, mean, rstd):
        return (hidden[at, :].astype(jnp.float32) - mean) * rstd

    def before(index, carry):
        spread.slot(index)
        at = pl.ds(pl.multiple_of(index * TILE, TILE), TILE)
        raw = hidden[at, :].astype(jnp.float32)
        mean = jnp.mean(raw, axis=1, keepdims=True)
        centred = raw - mean
        rstd = lax.rsqrt(jnp.mean(centred * centred, axis=1, keepdims=True) + EPS)
        stats[0, at, :] = jnp.broadcast_to(mean, (TILE, stats.shape[2]))
        stats[1, at, :] = jnp.broadcast_to(rstd, (TILE, stats.shape[2]))
        xhat = centred * rstd
        first[at, :] = (xhat * gain_one + shift_one).astype(jnp.bfloat16)
        grad_second = dot_rows(grad_expanded[at, :], we[...])
        terms[index] = (grad_second * gain_two).astype(jnp.bfloat16)
        outs[index] = dot_plain(active[at, :], wc[...]).astype(jnp.bfloat16)
        totals[2:3, :] += jnp.sum(grad_second * xhat, axis=0, keepdims=True)
        totals[3:4, :] += jnp.sum(grad_second, axis=0, keepdims=True)
        totals[4:5, :] += jnp.sum(cots[at, :].astype(jnp.float32), axis=0, keepdims=True)
        return carry

    shown = hidden.shape[0] // TILE
    lax.fori_loop(0, shown, before, 0)

    def spread_rest(t, carry):
        spread.slot(t)
        return carry

    lax.fori_loop(shown, spread.slots, spread_rest, 0)
    for copy in owns:
        copy.wait()
    for copy in copies:
        copy.wait()

    def after(index, carry):
        at = pl.ds(pl.multiple_of(index * TILE, TILE), TILE)
        grads = parts[at, pl.ds(lanes, 3 * lanes)]
        grad_first = dot_rows(grads, wm[...])
        xhat = normed(at, stats[0, at, 0:1], stats[1, at, 0:1])
        terms[index] = (terms[index].astype(jnp.float32) + grad_first * gain_one).astype(
            jnp.bfloat16
        )
        outs[index] = (
            outs[index].astype(jnp.float32) + dot_plain(parts[at, pl.ds(0, lanes)], wo[...])
        ).astype(jnp.bfloat16)
        totals[0:1, :] += jnp.sum(grad_first * xhat, axis=0, keepdims=True)
        totals[1:2, :] += jnp.sum(grad_first, axis=0, keepdims=True)
        totals[5:6, pl.ds(0, 3 * lanes)] += jnp.sum(
            grads.astype(jnp.float32), axis=0, keepdims=True
        )
        return carry

    lax.fori_loop(0, hidden.shape[0] // TILE, after, 0)
    arrays = (outs, terms)
    nears = []
    for a in range(2):
        copy = remote(
            arrays[a].at[pl.ds(pl.multiple_of(4 * (1 - c), 4), 4)],
            near.at[a],
            sems.at[0, a],
            sems.at[1, a],
            core,
        )
        copy.start()
        nears.append(copy)
    for index in range(width // TILE):
        block = dot_tokens(first[:, pl.ds(index * TILE, TILE)], parts[:, pl.ds(lanes, 3 * lanes)])
        side, row = divmod(index * TILE, half)
        attn_own[pl.ds(row, TILE), pl.ds(side * swap, swap)] = block.astype(jnp.bfloat16)
    block = dot_tokens(parts[:, pl.ds(0, lanes)], cots[...]).astype(jnp.bfloat16)
    wide = 2 * lanes
    for index in range(width // wide):
        attn_own[pl.ds(index * lanes, lanes), pl.ds(2 * swap, wide)] = block[
            :, index * wide : (index + 1) * wide
        ]
    lines = []
    fill = jnp.zeros((1, swap), jnp.float32)
    for index in range(5):
        for begin in range(0, width, swap):
            stop = min(begin + swap, width)
            line = totals[index : index + 1, begin:stop]
            if stop - begin < swap:
                line = jnp.concatenate([line, fill[:, : swap - (stop - begin)]], axis=1)
            lines.append(line)
    lines.append(totals[5:6, 0:swap])
    ff = feed_sums.shape[1]
    for begin in range(0, ff, swap):
        stop = min(begin + swap, ff)
        line = feed_sums[:, begin:stop]
        if stop - begin < swap:
            line = jnp.concatenate([line, fill[:, : swap - (stop - begin)]], axis=1)
        lines.append(line)
    lines += [fill] * (attn_own.shape[0] - half - len(lines))
    small = jnp.concatenate(lines, axis=0).astype(jnp.bfloat16)
    tail = pl.ds(half, attn_own.shape[0] - half)
    attn_own[tail, pl.ds(0, swap)] = small
    attn_own[tail, pl.ds(swap, swap)] = small
    attn_own[tail, pl.ds(2 * swap, wide)] = jnp.zeros((small.shape[0], wide), jnp.bfloat16)

    attn = LineSum(attn_own, attn_all, attn_inbox, attn_sems, swap, CHUNK, place)

    def step(t, carry):
        attn.slot(t)
        return carry

    lax.fori_loop(0, 2, step, 0)
    mids = []
    for a in range(2):
        nears[a].wait()
        for j in range(4):
            total = arrays[a][4 * c + j].astype(jnp.float32) + near[a, j].astype(jnp.float32)
            if a == 0:
                four[a, j % 2, j // 2] = total.astype(jnp.bfloat16)
            else:
                four[a, j // 2, j % 2] = total.astype(jnp.bfloat16)
        copy = remote(
            four.at[a, 1 - x if a == 0 else 1 - y],
            mid.at[a],
            sems.at[0, 2 + a],
            sems.at[1, 2 + a],
            over_x if a == 0 else over_y,
        )
        copy.start()
        mids.append(copy)
    lax.fori_loop(2, 9, step, 0)
    fars = []
    for a in range(2):
        mids[a].wait()
        mine_at, away = (x, y) if a == 0 else (y, x)
        two[a] = (
            four[a, mine_at, 1 - away].astype(jnp.float32) + mid[a, 1 - away].astype(jnp.float32)
        ).astype(jnp.bfloat16)
        copy = remote(
            two.at[a],
            far.at[a],
            sems.at[0, 4 + a],
            sems.at[1, 4 + a],
            over_y if a == 0 else over_x,
        )
        copy.start()
        fars.append(copy)
    lax.fori_loop(9, attn.slots, step, 0)
    for a, dst in enumerate((out_sum, term_sum)):
        fars[a].wait()
        mine_at, away = (x, y) if a == 0 else (y, x)
        dst[...] = (
            four[a, mine_at, away].astype(jnp.float32)
            + mid[a, away].astype(jnp.float32)
            + far[a].astype(jnp.float32)
        )
    attn.drain()
    spread.drain()


def close(
    done,
    active,
    grad_expanded,
    we,
    wc,
    wm,
    wo,
    hidden,
    cots,
    vectors,
    feed_sums,
    feed_sum,
    tokens,
):
    rows, width = hidden.shape
    lanes = done.shape[3]
    swap = 3 * lanes
    block = (tokens, width)
    vmem = pl.BlockSpec(memory_space=pltpu.VMEM)
    any_spec = pl.BlockSpec(memory_space=pl.ANY)
    grad_shape = (width // 2 + CHUNK, 2 * swap + 2 * lanes)
    scratch = [
        pltpu.VMEM((rows, 4 * lanes), jnp.bfloat16),
        pltpu.VMEM((rows, width), jnp.bfloat16),
        pltpu.VMEM((2, rows, 128), jnp.float32),
        pltpu.VMEM((GROUP,) + block, jnp.bfloat16),
        pltpu.VMEM((GROUP,) + block, jnp.bfloat16),
        pltpu.VMEM(grad_shape, jnp.bfloat16),
        pltpu.VMEM((2,) + grad_shape, jnp.bfloat16),
        pltpu.VMEM((2, 4) + block, jnp.bfloat16),
        pltpu.VMEM((2, 2, 2) + block, jnp.bfloat16),
        pltpu.VMEM((2, 2) + block, jnp.bfloat16),
        pltpu.VMEM((2,) + block, jnp.bfloat16),
        pltpu.VMEM((2,) + block, jnp.bfloat16),
        pltpu.VMEM((8, width), jnp.float32),
        pltpu.SemaphoreType.DMA((LINE - 1, 4)),
        pltpu.SemaphoreType.DMA((LINE - 1, 4)),
        pltpu.SemaphoreType.DMA((2 * LineSum.KINDS, grad_shape[0] // CHUNK)),
        pltpu.SemaphoreType.DMA((8, feed_sum.shape[0] // CHUNK)),
        pltpu.SemaphoreType.DMA((2, 6)),
        pltpu.SemaphoreType.DMA((5,)),
    ]
    return pl.pallas_call(
        functools.partial(close_kernel, swap=swap),
        out_shape=(
            jax.ShapeDtypeStruct((2, 2) + grad_shape, jnp.bfloat16),
            jax.ShapeDtypeStruct((2, 2) + feed_sum.shape, jnp.bfloat16),
            jax.ShapeDtypeStruct(block, jnp.float32),
            jax.ShapeDtypeStruct(block, jnp.float32),
        ),
        in_specs=[any_spec] + [vmem] * 10 + [any_spec],
        out_specs=[vmem, any_spec, vmem, vmem],
        scratch_shapes=scratch,
        compiler_params=pltpu.CompilerParams(
            collective_id=3, has_side_effects=True, vmem_limit_bytes=60 << 20
        ),
        name="close",
    )(
        done, active, grad_expanded, we, wc, wm, wo, hidden, cots, vectors, feed_sums, feed_sum
    )


def widen_kernel(
    feed_all,
    attn_all,
    expand,
    contract,
    merged,
    output,
    feed,
    attn,
    expand_wide,
    contract_wide,
    merged_wide,
    output_wide,
    loads,
    stores,
    *,
    swap,
    lanes,
    ff,
):
    half = feed.shape[2]
    gets = []
    for index, (src, dst) in enumerate(((feed_all, feed), (attn_all, attn))):
        for part in range(4):
            copy = pltpu.make_async_copy(
                src.at[part // 2, part % 2], dst.at[part // 2, part % 2], loads.at[index, part]
            )
            copy.start()
            gets.append(copy)
    puts = []

    def put(src, dst):
        copy = pltpu.make_async_copy(src, dst, stores.at[len(puts)])
        copy.start()
        puts.append(copy)

    for part in range(4):
        c, x = part // 2, part % 2
        gets[part].wait()
        for y in range(2):
            at = pl.ds((4 * y + 2 * x + c) * ff, ff)
            expand_wide[:, at] = feed[c, x, :, pl.ds(y * ff, ff)].astype(jnp.float32)
            put(expand_wide.at[:, at], expand.at[:, at])
        at = pl.ds((2 * x + c) * ff, ff)
        contract_wide[at, :] = feed[c, x, :, pl.ds(2 * ff, 2 * half)].astype(jnp.float32)
        put(contract_wide.at[at], contract.at[at])
    for copy in gets[4:]:
        copy.wait()
    width = 2 * half
    for j in range(3):
        for octant in range(GROUP):
            c, x, y = octant % 2, octant // 2 % 2, octant // 4
            at = pl.ds(j * width + octant * lanes, lanes)
            merged_wide[:, at] = attn[
                c, x, pl.ds(0, half), pl.ds(y * swap + j * lanes, lanes)
            ].astype(jnp.float32)
        at = pl.ds(j * width, width)
        put(merged_wide.at[:, at], merged.at[:, at])
    for part in range(4):
        c, x = part % 2, part // 2
        for index in range(half // lanes):
            output_wide[pl.ds(part * lanes, lanes), pl.ds(2 * lanes * index, 2 * lanes)] = attn[
                c, x, pl.ds(index * lanes, lanes), pl.ds(2 * swap, 2 * lanes)
            ].astype(jnp.float32)
    put(output_wide, output)
    for copy in puts:
        copy.wait()


def widen(feed_all, attn_all, swap, lanes, ff):
    half = feed_all.shape[2]
    width = 2 * half
    shapes = ((half, GROUP * ff), (4 * ff, width), (half, 3 * width), (4 * lanes, width))
    any_spec = pl.BlockSpec(memory_space=pl.ANY)
    return pl.pallas_call(
        functools.partial(widen_kernel, swap=swap, lanes=lanes, ff=ff),
        out_shape=tuple(jax.ShapeDtypeStruct(shape, jnp.float32) for shape in shapes),
        in_specs=[any_spec] * 2,
        out_specs=[any_spec] * 4,
        scratch_shapes=[
            pltpu.VMEM(feed_all.shape, jnp.bfloat16),
            pltpu.VMEM(attn_all.shape, jnp.bfloat16),
        ]
        + [pltpu.VMEM(shape, jnp.float32) for shape in shapes]
        + [pltpu.SemaphoreType.DMA((2, 4)), pltpu.SemaphoreType.DMA((16,))],
        compiler_params=pltpu.CompilerParams(vmem_limit_bytes=48 << 20),
        name="widen",
    )(feed_all, attn_all)


def turn_tables(positions, lanes):
    lane = jnp.arange(lanes, dtype=jnp.int32) % HEAD
    inverse = jnp.exp((lane % HALF).astype(jnp.float32) * (-2.0 * math.log(10000.0) / ROT))
    angles = positions.astype(jnp.float32)[:, None] * inverse[None, :]
    turned = lane[None, :] < ROT
    return (jnp.where(turned, jnp.cos(angles), 1.0), jnp.where(turned, jnp.sin(angles), 0.0))


def group_body(
    hidden_states,
    unit_order,
    piece_starts,
    first_gain,
    first_shift,
    second_gain,
    second_shift,
    merged_weight,
    merged_bias,
    output_weight,
    output_bias,
    expand_weight,
    expand_bias,
    contract_weight,
    contract_bias,
    out_cotangent,
):
    c, y, x, z = place_here()
    tokens, width = hidden_states.shape[1:]
    length = tokens * 2 * LINE
    units = unit_order.shape[1]
    pieces = piece_starts.shape[1]
    rows = GROUP * tokens
    part = width // GROUP
    ff_part = expand_weight.shape[1] // GROUP
    half = width // 2
    vectors = (
        first_gain,
        first_shift,
        second_gain,
        second_shift,
        merged_bias,
        output_bias,
        expand_bias,
        contract_bias,
    )
    sizes = [v.shape[0] for v in vectors]
    packed = jnp.concatenate(vectors).astype(jnp.float32).reshape(-1, 128)
    ints = jnp.concatenate([unit_order[0], piece_starts[0]])
    ints = jnp.broadcast_to(jnp.pad(ints, (0, 128 - ints.shape[0]))[None], (8, 128))
    tables = turn_tables(jnp.arange(units, dtype=jnp.int32) * UNIT, part) + turn_tables(
        jnp.arange(UNIT, dtype=jnp.int32), part
    )
    hid_all, ints_all, vec_all, wm_all, heads, second = enter(
        hidden_states[0], ints, packed, merged_weight, tables
    )
    inner = 2 * x + c
    wo = lax.dynamic_slice_in_dim(output_weight, inner * part, part, 0)
    wc = lax.dynamic_slice_in_dim(contract_weight, inner * ff_part, ff_part, 0)
    own_expand = lax.dynamic_slice_in_dim(expand_bias, inner * ff_part, ff_part, 0)
    got, cot_all, we_all, active, grad_expanded, feed_grad, feed_sums = feed_forward(
        heads,
        second,
        out_cotangent[0],
        expand_weight,
        wo,
        wc,
        own_expand.astype(jnp.float32)[None],
    )
    vec_all = vec_all.reshape(2, -1)
    whole = []
    at = 0
    for size in sizes:
        whole.append(vec_all[:, at : at + size].reshape(-1))
        at += size
    gain_one, shift_one, gain_two, shift_two, bias_merged, bias_out, bias_expand, bias_contract = whole
    wm = wm_all.reshape(width, 3 * part)
    we = we_all.reshape(width, ff_part)
    cots = cot_all.reshape(rows, width)
    own_ints = lax.dynamic_index_in_dim(ints_all[:, 0], z, 0, keepdims=True)
    done, feed_sum = attend(
        own_ints,
        got.reshape(4, length, part),
        tables,
        feed_grad,
        units,
        pieces,
        ff_part,
    )
    swap = 3 * part
    lines = CHUNK
    attn_all, feed_all, out_sum, term_sum = close(
        done.reshape(4, LINE, 2 * tokens, part),
        active,
        grad_expanded,
        we,
        wc,
        wm,
        wo,
        hid_all.reshape(rows, width),
        cots,
        jnp.stack([gain_one, shift_one, gain_two]),
        feed_sums,
        feed_sum,
        tokens,
    )
    expand_out, contract_out, merged_out, output_out = widen(
        feed_all, attn_all, swap, part, ff_part
    )
    own_hidden = hidden_states[0].astype(jnp.float32)
    own_mean = jnp.mean(own_hidden, axis=1, keepdims=True)
    own_centred = own_hidden - own_mean
    own_rstd = lax.rsqrt(jnp.mean(own_centred * own_centred, axis=1, keepdims=True) + EPS)
    own_xhat = own_centred * own_rstd
    output = (own_hidden + out_sum + bias_out + bias_contract).astype(jnp.bfloat16)
    upstream = out_cotangent[0].astype(jnp.float32)
    input_gradient = upstream + own_rstd * (
        term_sum
        - jnp.mean(term_sum, axis=1, keepdims=True)
        - own_xhat * jnp.mean(term_sum * own_xhat, axis=1, keepdims=True)
    )

    sums = attn_all[:, :, half : half + lines, : 2 * swap].astype(jnp.float32)
    sums = sums.reshape(2, 2, lines, 2, swap).transpose(3, 1, 0, 2, 4).reshape(GROUP, lines, swap)
    per = -(-width // swap)
    shared = jnp.sum(sums[:, : 4 * per], axis=0).reshape(4, per * swap)[:, :width]
    row_total = sums[0, 4 * per : 5 * per].reshape(-1)[:width]
    merged_sums = sums[:, 5 * per].reshape(GROUP, 3, part).transpose(1, 0, 2).reshape(-1)
    expand_sums = sums[:, 5 * per + 1 : 5 * per + 1 - (-ff_part // swap)]
    expand_sums = expand_sums.reshape(GROUP, -1)[:, :ff_part].reshape(-1)

    def own_half(vector):
        size = vector.shape[0] // 2
        return lax.dynamic_slice_in_dim(vector, y * size, size, 0)

    row_total = own_half(row_total)
    return (
        output[None],
        input_gradient[None],
        own_half(shared[0]),
        own_half(shared[1]),
        own_half(shared[2]),
        own_half(shared[3]),
        merged_out,
        own_half(merged_sums),
        output_out,
        row_total,
        expand_out,
        own_half(expand_sums),
        contract_out,
        row_total,
    )


def fits_groups(mesh, args):
    hidden, order = args[0], args[1]
    count = mesh.shape["seq"]
    tokens = hidden.shape[1] // count
    return (
        mesh.shape["rep"] == 2
        and mesh.shape["fsdp"] == 2
        and count == 2 * LINE
        and hidden.shape[0] == LINE
        and hidden.shape[2] == GROUP * 2 * HEAD
        and tokens % UNIT == 0
        and hidden.shape[1] % SPAN == 0
        and order.shape[1] + args[2].shape[1] <= 128
    )


def solution(mesh):
    in_specs = (
        P(("rep", "fsdp"), "seq", None),
        P(("rep", "fsdp"), None),
        P(("rep", "fsdp"), None),
        P("fsdp"),
        P("fsdp"),
        P("fsdp"),
        P("fsdp"),
        P("fsdp", None),
        P("fsdp"),
        P("fsdp", None),
        P("fsdp"),
        P("fsdp", None),
        P("fsdp"),
        P("fsdp", None),
        P("fsdp"),
        P(("rep", "fsdp"), "seq", None),
    )
    out_specs = (
        P(("rep", "fsdp"), "seq", None),
        P(("rep", "fsdp"), "seq", None),
        P("fsdp"),
        P("fsdp"),
        P("fsdp"),
        P("fsdp"),
        P("fsdp", None),
        P("fsdp"),
        P("fsdp", None),
        P("fsdp"),
        P("fsdp", None),
        P("fsdp"),
        P("fsdp", None),
        P("fsdp"),
    )

    def run(*args):
        chosen = group_body if fits_groups(mesh, args) else body
        mapped = jax.shard_map(
            chosen, mesh=mesh, in_specs=in_specs, out_specs=out_specs, check_vma=False
        )
        return mapped(*args)

    return run
```

```python
import functools
import math

import jax
import jax.numpy as jnp
from jax import lax
from jax.experimental import pallas as pl
from jax.experimental.pallas import tpu as pltpu
from jax.sharding import PartitionSpec as P

HEAD = 64
ROT = 16
UNIT = 128
PIECE = 256


EPS = 1e-05
NEGATIVE = -1e30


def norm_rows(values, gain, shift):
    mean = jnp.mean(values, axis=-1, keepdims=True)
    centred = values - mean
    spread = jnp.mean(centred * centred, axis=-1, keepdims=True)
    return centred * lax.rsqrt(spread + EPS) * gain + shift


def gelu_exact(values):
    return jax.nn.gelu(values, approximate=False)


def rotary_tables(positions):
    index = jnp.arange(ROT // 2, dtype=jnp.float32)
    inverse = jnp.exp(index * (-2.0 * math.log(10000.0) / ROT))
    angles = positions.astype(jnp.float32)[:, None] * inverse[None, :]
    angles = jnp.concatenate([angles, angles], axis=1)
    return (jnp.cos(angles), jnp.sin(angles))


def rotate(values, cosine, sine):
    part = values[..., :ROT]
    turned = jnp.concatenate([-part[..., ROT // 2 :], part[..., : ROT // 2]], axis=-1)
    moved = part * cosine[:, None, :] + turned * sine[:, None, :]
    return jnp.concatenate([moved, values[..., ROT:]], axis=-1)


def unit_positions(order):
    offsets = jnp.arange(UNIT, dtype=jnp.int32)
    return (order[:, None] * UNIT + offsets[None, :]).reshape(-1)


def piece_labels(positions, starts):
    inside = (positions[:, None] >= starts[None, :]) & (
        positions[:, None] < starts[None, :] + PIECE
    )
    labels = jnp.arange(1, starts.shape[0] + 1, dtype=jnp.int32)
    return jnp.sum(jnp.where(inside, labels[None, :], 0), axis=1) - 1


def visible(row_pos, row_lab, col_pos, col_lab):
    earlier = col_pos[None, :] <= row_pos[:, None]
    same = (row_lab[:, None] == col_lab[None, :]) & (row_lab[:, None] >= 0)
    return earlier | same


def merged_parts(first, merged_weight, merged_bias, cosine, sine):
    tokens = first.shape[0]
    width = first.shape[1]
    heads = width // HEAD
    merged = jnp.dot(first, merged_weight, preferred_element_type=jnp.float32) + merged_bias.astype(
        jnp.float32
    )
    queries = rotate(merged[:, :width].reshape(tokens, heads, HEAD), cosine, sine).astype(
        jnp.bfloat16
    )
    keys = rotate(merged[:, width : 2 * width].reshape(tokens, heads, HEAD), cosine, sine)
    keys = keys.reshape(tokens, width).astype(jnp.bfloat16)
    values = merged[:, 2 * width :].astype(jnp.bfloat16)
    return (queries, keys, values)


def block_view(queries, keys_all, values_all, row_pos, row_lab, col_pos, col_lab, span):
    heads = queries.shape[1]
    scale = 1.0 / math.sqrt(HEAD)

    def view(index):
        start = index * span
        key_rows = lax.dynamic_slice_in_dim(keys_all, start, span, 0).reshape(span, heads, HEAD)
        value_rows = lax.dynamic_slice_in_dim(values_all, start, span, 0).reshape(span, heads, HEAD)
        scores = (
            jnp.einsum("thd,khd->htk", queries, key_rows, preferred_element_type=jnp.float32)
            * scale
        )
        allowed = visible(
            row_pos,
            row_lab,
            lax.dynamic_slice_in_dim(col_pos, start, span, 0),
            lax.dynamic_slice_in_dim(col_lab, start, span, 0),
        )[None]
        return (scores, allowed, key_rows, value_rows)

    return view


def log_sums(view, count, heads, tokens):

    def log_step(carry, index):
        top, total = carry
        scores, allowed, key_rows, value_rows = view(index)
        masked = jnp.where(allowed, scores, NEGATIVE)
        newer = jnp.maximum(top, jnp.max(masked, axis=-1))
        terms = jnp.where(allowed, jnp.exp(masked - newer[..., None]), 0.0)
        total = total * jnp.exp(top - newer) + jnp.sum(terms, axis=-1)
        return ((newer, total), None)

    begin = (
        jnp.full((heads, tokens), NEGATIVE, jnp.float32),
        jnp.zeros((heads, tokens), jnp.float32),
    )
    (top, total), unused = lax.scan(log_step, begin, jnp.arange(count, dtype=jnp.int32))
    return top + jnp.log(total)


def mix_values(view, count, logsum, heads, tokens, grad_rows):

    def mix_step(carry, index):
        mixed, delta = carry
        scores, allowed, key_rows, value_rows = view(index)
        weights = jnp.where(allowed, jnp.exp(scores - logsum[..., None]), 0.0)
        mixed = mixed + jnp.einsum(
            "htk,khd->thd",
            weights.astype(jnp.bfloat16),
            value_rows,
            preferred_element_type=jnp.float32,
        )
        if grad_rows is not None:
            slopes = jnp.einsum(
                "thd,khd->htk", grad_rows, value_rows, preferred_element_type=jnp.float32
            )
            delta = delta + jnp.sum(weights * slopes, axis=-1)
        return ((mixed, delta), None)

    begin = (jnp.zeros((tokens, heads, HEAD), jnp.float32), jnp.zeros((heads, tokens), jnp.float32))
    (mixed, delta), unused = lax.scan(mix_step, begin, jnp.arange(count, dtype=jnp.int32))
    return (mixed, delta)


def attend_back(view, count, logsum, delta, grad_rows, queries):
    scale = 1.0 / math.sqrt(HEAD)

    def attend_step(carry, index):
        scores, allowed, key_rows, value_rows = view(index)
        weights = jnp.where(allowed, jnp.exp(scores - logsum[..., None]), 0.0)
        slopes = jnp.einsum(
            "thd,khd->htk", grad_rows, value_rows, preferred_element_type=jnp.float32
        )
        grad_scores = (weights * (slopes - delta[..., None])).astype(jnp.bfloat16)
        carry = carry + jnp.einsum(
            "htk,khd->thd", grad_scores, key_rows, preferred_element_type=jnp.float32
        )
        key_grad = jnp.einsum(
            "htk,thd->khd", grad_scores, queries, preferred_element_type=jnp.float32
        )
        value_grad = jnp.einsum(
            "htk,thd->khd",
            weights.astype(jnp.bfloat16),
            grad_rows,
            preferred_element_type=jnp.float32,
        )
        span = key_rows.shape[0]
        joined = jnp.concatenate(
            [key_grad.reshape(span, -1) * scale, value_grad.reshape(span, -1)], axis=1
        )
        return (carry, joined)

    begin = jnp.zeros(queries.shape, jnp.float32)
    grad_query, parts = lax.scan(attend_step, begin, jnp.arange(count, dtype=jnp.int32))
    return (grad_query * scale, parts)


def body(
    hidden_states,
    unit_order,
    piece_starts,
    first_gain,
    first_shift,
    second_gain,
    second_shift,
    merged_weight,
    merged_bias,
    output_weight,
    output_bias,
    expand_weight,
    expand_bias,
    contract_weight,
    contract_bias,
    out_cotangent,
):
    shards = (
        first_gain,
        first_shift,
        second_gain,
        second_shift,
        merged_weight,
        merged_bias,
        output_weight,
        output_bias,
        expand_weight,
        expand_bias,
        contract_weight,
        contract_bias,
    )
    gathered = (
        lax.all_gather(shards[0], "fsdp", axis=0, tiled=True),
        lax.all_gather(shards[1], "fsdp", axis=0, tiled=True),
        lax.all_gather(shards[2], "fsdp", axis=0, tiled=True),
        lax.all_gather(shards[3], "fsdp", axis=0, tiled=True),
        lax.all_gather(shards[4], "fsdp", axis=0, tiled=True),
        lax.all_gather(shards[5], "fsdp", axis=0, tiled=True),
        lax.all_gather(shards[6], "fsdp", axis=0, tiled=True),
        lax.all_gather(shards[7], "fsdp", axis=0, tiled=True),
        lax.all_gather(shards[8], "fsdp", axis=0, tiled=True),
        lax.all_gather(shards[9], "fsdp", axis=0, tiled=True),
        lax.all_gather(shards[10], "fsdp", axis=0, tiled=True),
        lax.all_gather(shards[11], "fsdp", axis=0, tiled=True),
    )
    hidden = hidden_states[0].astype(jnp.float32)
    tokens = hidden.shape[0]
    width = hidden.shape[1]
    heads = width // HEAD
    length = tokens * lax.axis_size("seq")
    span = min(length, 512)
    count = length // span
    col_pos = unit_positions(unit_order[0])
    col_lab = piece_labels(col_pos, piece_starts[0])
    offset = lax.axis_index("seq") * tokens
    row_pos = lax.dynamic_slice_in_dim(col_pos, offset, tokens, 0)
    row_lab = lax.dynamic_slice_in_dim(col_lab, offset, tokens, 0)
    cosine, sine = rotary_tables(row_pos)
    first = norm_rows(
        hidden, gathered[0].astype(jnp.float32), gathered[1].astype(jnp.float32)
    ).astype(jnp.bfloat16)
    queries, keys, values = merged_parts(first, gathered[4], gathered[5], cosine, sine)
    keys_all, values_all = (
        lax.all_gather(keys, "seq", axis=0, tiled=True),
        lax.all_gather(values, "seq", axis=0, tiled=True),
    )
    view = block_view(queries, keys_all, values_all, row_pos, row_lab, col_pos, col_lab, span)
    logsum = log_sums(view, count, heads, tokens)
    mixed, unused = mix_values(view, count, logsum, heads, tokens, None)
    mixed = mixed.reshape(tokens, width).astype(jnp.bfloat16)
    attention = jnp.dot(mixed, gathered[6], preferred_element_type=jnp.float32) + gathered[
        7
    ].astype(jnp.float32)
    second = norm_rows(
        hidden, gathered[2].astype(jnp.float32), gathered[3].astype(jnp.float32)
    ).astype(jnp.bfloat16)
    expanded = jnp.dot(second, gathered[8], preferred_element_type=jnp.float32) + gathered[
        9
    ].astype(jnp.float32)
    active = gelu_exact(expanded).astype(jnp.bfloat16)
    feed = jnp.dot(active, gathered[10], preferred_element_type=jnp.float32) + gathered[11].astype(
        jnp.float32
    )
    output = (hidden + attention + feed).astype(jnp.bfloat16)
    weights = (
        lax.all_gather(shards[0], "fsdp", axis=0, tiled=True),
        lax.all_gather(shards[1], "fsdp", axis=0, tiled=True),
        lax.all_gather(shards[2], "fsdp", axis=0, tiled=True),
        lax.all_gather(shards[3], "fsdp", axis=0, tiled=True),
        lax.all_gather(shards[4], "fsdp", axis=0, tiled=True),
        lax.all_gather(shards[5], "fsdp", axis=0, tiled=True),
        lax.all_gather(shards[6], "fsdp", axis=0, tiled=True),
        lax.all_gather(shards[7], "fsdp", axis=0, tiled=True),
        lax.all_gather(shards[8], "fsdp", axis=0, tiled=True),
        lax.all_gather(shards[9], "fsdp", axis=0, tiled=True),
        lax.all_gather(shards[10], "fsdp", axis=0, tiled=True),
        lax.all_gather(shards[11], "fsdp", axis=0, tiled=True),
    )
    cotangent = out_cotangent[0]
    upstream = cotangent.astype(jnp.float32)
    normed_one, first_pull = jax.vjp(
        norm_rows, hidden, weights[0].astype(jnp.float32), weights[1].astype(jnp.float32)
    )
    first = normed_one.astype(jnp.bfloat16)
    queries, keys, values = merged_parts(first, weights[4], weights[5], cosine, sine)
    keys_back, values_back = (
        lax.all_gather(keys, "seq", axis=0, tiled=True),
        lax.all_gather(values, "seq", axis=0, tiled=True),
    )
    view = block_view(queries, keys_back, values_back, row_pos, row_lab, col_pos, col_lab, span)
    grad_mixed = jnp.einsum(
        "te,de->td", cotangent, weights[6], preferred_element_type=jnp.float32
    ).astype(jnp.bfloat16)
    grad_rows = grad_mixed.reshape(tokens, heads, HEAD)
    mixed, delta = mix_values(view, count, logsum, heads, tokens, grad_rows)
    mixed = mixed.reshape(tokens, width).astype(jnp.bfloat16)
    grad_query, parts = attend_back(view, count, logsum, delta, grad_rows, queries)
    term = parts.reshape(length, 2 * width)
    own_grads = lax.psum_scatter(
        term.astype(jnp.bfloat16), "seq", scatter_dimension=0, tiled=True
    ).astype(jnp.float32)
    normed_two, second_pull = jax.vjp(
        norm_rows, hidden, weights[2].astype(jnp.float32), weights[3].astype(jnp.float32)
    )
    second = normed_two.astype(jnp.bfloat16)
    expanded = jnp.dot(second, weights[8], preferred_element_type=jnp.float32) + weights[9].astype(
        jnp.float32
    )
    activated, gelu_pull = jax.vjp(gelu_exact, expanded)
    active = activated.astype(jnp.bfloat16)
    grad_active = jnp.einsum(
        "te,fe->tf", cotangent, weights[10], preferred_element_type=jnp.float32
    )
    grad_expanded = gelu_pull(grad_active)[0].astype(jnp.bfloat16)
    grad_second = jnp.einsum(
        "tf,df->td", grad_expanded, weights[8], preferred_element_type=jnp.float32
    )
    unused, turn_pull = jax.vjp(rotate, grad_query, cosine, sine)
    query_back = turn_pull(grad_query)[0].reshape(tokens, width)
    key_back = turn_pull(own_grads[:, :width].reshape(tokens, heads, HEAD))[0].reshape(
        tokens, width
    )
    grad_merged = jnp.concatenate([query_back, key_back, own_grads[:, width:]], axis=1).astype(
        jnp.bfloat16
    )
    grad_first = jnp.einsum(
        "tc,dc->td", grad_merged, weights[4], preferred_element_type=jnp.float32
    )
    first_term, first_gain_grad, first_shift_grad = first_pull(grad_first)
    second_term, second_gain_grad, second_shift_grad = second_pull(grad_second)
    input_gradient = upstream + first_term + second_term
    row_total = jnp.sum(upstream, axis=0)
    local_grads = (
        first_gain_grad,
        first_shift_grad,
        second_gain_grad,
        second_shift_grad,
        jnp.einsum("td,tc->dc", first, grad_merged, preferred_element_type=jnp.float32),
        jnp.sum(grad_merged.astype(jnp.float32), axis=0),
        jnp.einsum("td,te->de", mixed, cotangent, preferred_element_type=jnp.float32),
        row_total,
        jnp.einsum("td,tf->df", second, grad_expanded, preferred_element_type=jnp.float32),
        jnp.sum(grad_expanded.astype(jnp.float32), axis=0),
        jnp.einsum("tf,te->fe", active, cotangent, preferred_element_type=jnp.float32),
        row_total,
    )
    owned = (
        lax.psum_scatter(
            local_grads[0].astype(jnp.bfloat16), "fsdp", scatter_dimension=0, tiled=True
        ).astype(jnp.float32),
        lax.psum_scatter(
            local_grads[1].astype(jnp.bfloat16), "fsdp", scatter_dimension=0, tiled=True
        ).astype(jnp.float32),
        lax.psum_scatter(
            local_grads[2].astype(jnp.bfloat16), "fsdp", scatter_dimension=0, tiled=True
        ).astype(jnp.float32),
        lax.psum_scatter(
            local_grads[3].astype(jnp.bfloat16), "fsdp", scatter_dimension=0, tiled=True
        ).astype(jnp.float32),
        lax.psum_scatter(
            local_grads[4].astype(jnp.bfloat16), "fsdp", scatter_dimension=0, tiled=True
        ).astype(jnp.float32),
        lax.psum_scatter(
            local_grads[5].astype(jnp.bfloat16), "fsdp", scatter_dimension=0, tiled=True
        ).astype(jnp.float32),
        lax.psum_scatter(
            local_grads[6].astype(jnp.bfloat16), "fsdp", scatter_dimension=0, tiled=True
        ).astype(jnp.float32),
        lax.psum_scatter(
            local_grads[7].astype(jnp.bfloat16), "fsdp", scatter_dimension=0, tiled=True
        ).astype(jnp.float32),
        lax.psum_scatter(
            local_grads[8].astype(jnp.bfloat16), "fsdp", scatter_dimension=0, tiled=True
        ).astype(jnp.float32),
        lax.psum_scatter(
            local_grads[9].astype(jnp.bfloat16), "fsdp", scatter_dimension=0, tiled=True
        ).astype(jnp.float32),
        lax.psum_scatter(
            local_grads[10].astype(jnp.bfloat16), "fsdp", scatter_dimension=0, tiled=True
        ).astype(jnp.float32),
        lax.psum_scatter(
            local_grads[11].astype(jnp.bfloat16), "fsdp", scatter_dimension=0, tiled=True
        ).astype(jnp.float32),
    )
    summed = lax.psum(
        (
            owned[0],
            owned[1],
            owned[2],
            owned[3],
            owned[4],
            owned[5],
            owned[6],
            owned[7],
            owned[8],
            owned[9],
            owned[10],
            owned[11],
        ),
        ("rep", "seq"),
    )
    return (
        output[None],
        input_gradient[None],
        summed[0],
        summed[1],
        summed[2],
        summed[3],
        summed[4],
        summed[5],
        summed[6],
        summed[7],
        summed[8],
        summed[9],
        summed[10],
        summed[11],
    )


MESH = pl.DeviceIdType.MESH
GROUP = 8
LINE = 4
HALF = ROT // 2
SPAN = 512
CHUNK = 32
FEED_CHUNK = 16


def place_here():
    c, y, s = (lax.axis_index("rep"), lax.axis_index("fsdp"), lax.axis_index("seq"))
    x = lax.rem(s, 2)
    return (c, y, x, s // 2)


def device_at(c, y, x, z):
    return (c, y, 2 * z + x)


def greet(partners):
    barrier = pltpu.get_barrier_semaphore()
    for partner in partners:
        pl.semaphore_signal(barrier, inc=1, device_id=partner, device_id_type=MESH)
    pl.semaphore_wait(barrier, len(partners))


def remote(src, dst, send, recv, target):
    return pltpu.make_async_remote_copy(
        src_ref=src,
        dst_ref=dst,
        send_sem=send,
        recv_sem=recv,
        device_id=target,
        device_id_type=MESH,
    )


def dot_rows(a, b):
    return lax.dot_general(a, b, (((1,), (1,)), ((), ())), preferred_element_type=jnp.float32)


def dot_tokens(a, b):
    return lax.dot_general(a, b, (((0,), (0,)), ((), ())), preferred_element_type=jnp.float32)


def dot_plain(a, b):
    return jnp.dot(a, b, preferred_element_type=jnp.float32)


class TokenExchange:
    def __init__(self, place, send, recv):
        self.place, self.send, self.recv = place, send, recv
        self.count = 0
        self.sends = []

    def go(self, src, dst, target):
        copy = remote(src, dst, self.send.at[self.count], self.recv.at[self.count], target)
        self.count += 1
        copy.start()
        self.sends.append(copy)
        return copy

    def blocks(self, cc):
        c, y, x, z = self.place

        def block(yy, xx):
            return (2 * cc + yy) * 2 + xx

        return (block(y, x), block(y, 1 - x), block(1 - y, x), block(1 - y, 1 - x))

    def start(self, src, full):
        c, y, x, z = self.place
        self.full = full
        me = self.blocks(c)[0]
        self.from_x = self.go(src, full.at[me], device_at(c, y, 1 - x, z))
        self.from_y = self.go(src, full.at[me], device_at(c, 1 - y, x, z))
        self.from_core = [self.go(src, full.at[me], device_at(1 - c, y, x, z))]

    def relay(self):
        c, y, x, z = self.place
        full = self.full
        me, near_x, near_y, far = self.blocks(c)
        half = full.shape[1] // 2
        core = device_at(1 - c, y, x, z)
        upper, lower = pl.ds(0, half), pl.ds(half, half)
        self.from_x.wait_recv()
        second = self.go(
            full.at[near_x, lower], full.at[near_x, lower], device_at(c, 1 - y, x, z)
        )
        self.from_core.append(self.go(full.at[near_x], full.at[near_x], core))
        self.from_y.wait_recv()
        first = self.go(full.at[near_y, upper], full.at[near_y, upper], device_at(c, y, 1 - x, z))
        self.from_core.append(self.go(full.at[near_y], full.at[near_y], core))
        self.corner = (first, second)

    def relay_corner(self):
        c, y, x, z = self.place
        far = self.blocks(c)[3]
        for copy in self.corner:
            copy.wait_recv()
        self.from_core.append(
            self.go(self.full.at[far], self.full.at[far], device_at(1 - c, y, x, z))
        )

    def wait_core(self, index):
        self.from_core[index].wait_recv()

    def finish(self):
        for copy in self.sends:
            copy.wait_send()


def column_block(part, at):
    return pl.ds(pl.multiple_of(at, part), part)


def enter_kernel(
    hid,
    ints,
    vec,
    wm,
    unit_cos,
    unit_sin,
    row_cos,
    row_sin,
    hid_all,
    ints_all,
    vec_all,
    wm_all,
    heads,
    second,
    units,
    rotated,
    send,
    recv,
    local,
):
    place = place_here()
    c, y, x, z = place
    core = device_at(1 - c, y, x, z)
    over_x = device_at(c, y, 1 - x, z)
    over_y = device_at(c, 1 - y, x, z)
    lanes = wm_all.shape[2] // 3
    width = wm.shape[1] // 3
    tokens = hid.shape[0]
    own = 4 * y + 2 * x + c
    other = 4 * (1 - y) + 2 * x + c
    moved = []

    def keep(src, dst):
        copy = pltpu.make_async_copy(src, dst, local.at[len(moved)])
        copy.start()
        moved.append(copy)
        return copy

    me = (2 * c + y) * 2 + x
    own_block = keep(hid, hid_all.at[me])
    keep(ints, ints_all.at[2 * c + y])
    keep(vec, vec_all.at[y])
    for j in range(3):
        keep(
            wm.at[:, column_block(lanes, j * width + own * lanes)],
            wm_all.at[y, :, pl.ds(j * lanes, lanes)],
        )
    greet((core, over_x, over_y))
    tokens_move = TokenExchange(place, send, recv)
    go = tokens_move.go
    ints_y = go(ints, ints_all.at[2 * c + y], over_y)
    vec_y = go(vec, vec_all.at[y], over_y)
    ints_core = [go(ints, ints_all.at[2 * c + y], core)]
    tokens_move.start(hid, hid_all)
    weights = [
        go(
            wm.at[:, column_block(lanes, j * width + other * lanes)],
            wm_all.at[y, :, pl.ds(j * lanes, lanes)],
            over_y,
        )
        for j in range(3)
    ]
    ints_y.wait_recv()
    ints_core.append(go(ints_all.at[2 * c + 1 - y], ints_all.at[2 * c + 1 - y], core))
    vec_y.wait_recv()
    for copy in moved:
        copy.wait()
    for copy in ints_core:
        copy.wait_recv()
    to_units = pltpu.make_async_copy(ints_all, units, local.at[0])
    to_units.start()
    to_units.wait()

    def vector(row):
        return jnp.concatenate(
            [vec_all[h, row + i : row + i + 1, :] for h in range(2) for i in range(4)], axis=1
        )

    gain_one, shift_one, gain_two, shift_two = [vector(4 * i) for i in range(4)]
    bias = []
    for j in range(3):
        at = j * GROUP + own
        bias.append(vec_all[at // 12, pl.ds(16 + lax.rem(at, 12), 1), :])
    bias = jnp.concatenate(bias, axis=1)

    def normal(block):
        raw = hid_all[block].astype(jnp.float32)
        mean = jnp.mean(raw, axis=1, keepdims=True)
        centred = raw - mean
        rstd = lax.rsqrt(jnp.mean(centred * centred, axis=1, keepdims=True) + EPS)
        xhat = centred * rstd
        rows = pl.ds(pl.multiple_of(block * tokens, tokens), tokens)
        second[rows, :] = (xhat * gain_two + shift_two).astype(jnp.bfloat16)
        return (xhat * gain_one + shift_one).astype(jnp.bfloat16)

    unit_index = lax.broadcasted_iota(jnp.int32, unit_cos.shape, 0)
    lane = lax.rem(lax.broadcasted_iota(jnp.int32, row_cos.shape, 1), HEAD)

    def project(block):
        rows = pl.ds(pl.multiple_of(block * tokens, tokens), tokens)
        sequence, side = block // 2, lax.rem(block, 2)
        normed = normal(block)
        half = wm.shape[0]
        merged = (
            dot_plain(normed[:, :half], wm_all[0])
            + dot_plain(normed[:, half:], wm_all[1])
            + bias
        )
        count = tokens // UNIT
        for u in range(count):
            unit = units[sequence, 0, (2 * z + side) * count + u]
            here = pl.ds(u * UNIT, UNIT)
            chosen = unit_index == unit
            base_cos = jnp.sum(jnp.where(chosen, unit_cos[...], 0.0), axis=0, keepdims=True)
            base_sin = jnp.sum(jnp.where(chosen, unit_sin[...], 0.0), axis=0, keepdims=True)
            sine = base_sin * row_cos[...] + base_cos * row_sin[...]
            rotated[0, here, :] = base_cos * row_cos[...] - base_sin * row_sin[...]
            rotated[1, here, :] = jnp.where(lane < HALF, sine, 0.0)
            rotated[2, here, :] = jnp.where(lane < HALF, 0.0, sine)
        for j in range(2):
            values = merged[:, j * lanes : (j + 1) * lanes]
            turned = (
                values * rotated[0]
                - pltpu.roll(values, lanes - HALF, 1) * rotated[1]
                + pltpu.roll(values, HALF, 1) * rotated[2]
            )
            heads[j, rows, :] = turned.astype(jnp.bfloat16)
        heads[2, rows, :] = merged[:, 2 * lanes :].astype(jnp.bfloat16)

    tokens_move.relay()
    for copy in weights:
        copy.wait_recv()
    mine, theirs = tokens_move.blocks(c), tokens_move.blocks(1 - c)
    for index in range(3):
        project(mine[index])
    tokens_move.relay_corner()
    for index in range(3):
        tokens_move.wait_core(index)
        project(theirs[index])
    project(mine[3])
    tokens_move.wait_core(3)
    project(theirs[3])
    tokens_move.finish()


def enter(hid, ints, vec, wm, tables):
    tokens, width = hid.shape
    rows = wm.shape[0]
    lanes = width // GROUP
    vmem = pl.BlockSpec(memory_space=pltpu.VMEM)
    any_spec = pl.BlockSpec(memory_space=pl.ANY)
    return pl.pallas_call(
        enter_kernel,
        out_shape=(
            jax.ShapeDtypeStruct((GROUP,) + hid.shape, hid.dtype),
            jax.ShapeDtypeStruct((4,) + ints.shape, ints.dtype),
            jax.ShapeDtypeStruct((2,) + vec.shape, vec.dtype),
            jax.ShapeDtypeStruct((2, rows, 3 * lanes), wm.dtype),
            jax.ShapeDtypeStruct((3, GROUP * tokens, lanes), jnp.bfloat16),
            jax.ShapeDtypeStruct((GROUP * tokens, width), jnp.bfloat16),
        ),
        in_specs=[any_spec] * 4 + [vmem] * 4,
        out_specs=[vmem, any_spec, vmem, vmem, vmem, vmem],
        scratch_shapes=[
            pltpu.SMEM((4,) + ints.shape, jnp.int32),
            pltpu.VMEM((3, tokens, lanes), jnp.float32),
            pltpu.SemaphoreType.DMA((20,)),
            pltpu.SemaphoreType.DMA((20,)),
            pltpu.SemaphoreType.DMA((8,)),
        ],
        compiler_params=pltpu.CompilerParams(
            collective_id=0, has_side_effects=True, vmem_limit_bytes=48 << 20
        ),
        name="enter",
    )(hid, ints, vec, wm, *tables)


def greet_line(place, more=()):
    c, y, x, z = place
    barrier = pltpu.get_barrier_semaphore()
    partners = (device_at(1 - c, y, x, z), device_at(c, y, 1 - x, z), device_at(c, 1 - y, x, z))
    for partner in partners:
        pl.semaphore_signal(barrier, inc=1, device_id=partner, device_id_type=MESH)

    @pl.when(z > 0)
    def _():
        pl.semaphore_signal(barrier, inc=1, device_id=device_at(c, y, x, z - 1), device_id_type=MESH)

    @pl.when(z < LINE - 1)
    def _():
        pl.semaphore_signal(barrier, inc=1, device_id=device_at(c, y, x, z + 1), device_id_type=MESH)

    @pl.when((z > 0) & (z < LINE - 1))
    def _():
        pl.semaphore_wait(barrier, 5)

    @pl.when((z == 0) | (z == LINE - 1))
    def _():
        pl.semaphore_wait(barrier, 4)


TILE = 256


def feed_kernel(
    heads,
    second,
    cot,
    we,
    wo_src,
    wc_src,
    bias,
    got,
    cot_all,
    we_all,
    active,
    grad_expanded,
    feed_grad,
    sums,
    slope,
    grad_heads,
    wo,
    wc,
    send,
    recv,
    token_send,
    token_recv,
    local,
):
    place = place_here()
    c, y, x, z = place
    rows = got.shape[2]
    tokens = cot.shape[0]
    ff = we_all.shape[2]
    half = we.shape[0]
    own = 4 * y + 2 * x + c
    other = 4 * (1 - y) + 2 * x + c
    core = device_at(1 - c, y, x, z)
    over_x = device_at(c, y, 1 - x, z)
    over_y = device_at(c, 1 - y, x, z)
    peers = [lax.rem(z + d, LINE) for d in range(1, LINE)]
    mine = pl.ds(pl.multiple_of(z * rows, rows), rows)
    me = (2 * c + y) * 2 + x
    inner = 2 * x + c

    def rows_of(src, dst):
        count = dst.shape[0]
        return src.at[pl.ds(pl.multiple_of(inner * count, count), count)]

    keeps = [
        pltpu.make_async_copy(we.at[:, column_block(ff, own * ff)], we_all.at[y], local.at[0]),
        pltpu.make_async_copy(cot, cot_all.at[me], local.at[1]),
        pltpu.make_async_copy(rows_of(wo_src, wo), wo, local.at[2]),
        pltpu.make_async_copy(rows_of(wc_src, wc), wc, local.at[3]),
        pltpu.make_async_copy(heads.at[:, mine], got.at[pl.ds(0, 3), z], local.at[4]),
    ]
    for copy in keeps:
        copy.start()
    greet([device_at(c, y, x, peer) for peer in peers] + [core, over_x, over_y])
    tokens_move = TokenExchange(place, token_send, token_recv)
    weight = tokens_move.go(we.at[:, column_block(ff, other * ff)], we_all.at[y], over_y)
    tokens_move.start(cot, cot_all)
    copies = []
    for index, peer in enumerate(peers):
        copy = remote(
            heads.at[:, pl.ds(pl.multiple_of(peer * rows, rows), rows)],
            got.at[pl.ds(0, 3), z],
            send.at[0, index],
            recv.at[0, index],
            device_at(c, y, x, peer),
        )
        copy.start()
        copies.append(copy)
    for copy in keeps[:4]:
        copy.wait()
    weight.wait_recv()
    sums[...] = jnp.zeros_like(sums)

    def forward(index, carry):
        at = pl.ds(pl.multiple_of(index * TILE, TILE), TILE)
        normed = second[at, :]
        expanded = (
            dot_plain(normed[:, :half], we_all[0])
            + dot_plain(normed[:, half:], we_all[1])
            + bias[...]
        )
        below = 0.5 * (1.0 + lax.erf(expanded * math.sqrt(0.5)))
        density = jnp.exp(expanded * expanded * -0.5) * (1.0 / math.sqrt(2.0 * math.pi))
        active[at, :] = (expanded * below).astype(jnp.bfloat16)
        slope[at, :] = below + expanded * density
        return carry

    tiles = second.shape[0] // TILE
    lax.fori_loop(0, tiles // 2, forward, 0)
    tokens_move.relay()
    lax.fori_loop(tiles // 2, tiles, forward, 0)
    tokens_move.relay_corner()

    def backward(block):
        at = pl.ds(pl.multiple_of(block * tokens, tokens), tokens)
        cots = cot_all[block]
        grad_heads[at, :] = dot_rows(cots, wo[...]).astype(jnp.bfloat16)
        grad = (dot_rows(cots, wc[...]) * slope[at, :]).astype(jnp.bfloat16)
        grad_expanded[at, :] = grad
        sums[...] += jnp.sum(grad.astype(jnp.float32), axis=0, keepdims=True)

    ours, theirs = tokens_move.blocks(c), tokens_move.blocks(1 - c)
    for index in range(4):
        backward(ours[index])
    for index in range(4):
        tokens_move.wait_core(index)
        backward(theirs[index])
    for index, peer in enumerate(peers):
        copy = remote(
            grad_heads.at[pl.ds(pl.multiple_of(peer * rows, rows), rows)],
            got.at[3, z],
            send.at[1, index],
            recv.at[1, index],
            device_at(c, y, x, peer),
        )
        copy.start()
        copies.append(copy)
    last = pltpu.make_async_copy(grad_heads.at[mine], got.at[3, z], local.at[0])
    last.start()
    for index in range(2 * half // TILE):
        block = dot_tokens(second[:, pl.ds(index * TILE, TILE)], grad_expanded[...])
        side, row = divmod(index * TILE, half)
        feed_grad[pl.ds(row, TILE), pl.ds(side * ff, ff)] = block.astype(jnp.bfloat16)
    cots = cot_all[...].reshape(GROUP * tokens, 2 * half)
    for index in range(ff // TILE):
        block = dot_tokens(active[:, pl.ds(index * TILE, TILE)], cots)
        feed_grad[pl.ds(index * TILE, TILE), pl.ds(2 * ff, 2 * half)] = block.astype(jnp.bfloat16)
    keeps[4].wait()
    last.wait()
    for copy in copies:
        copy.wait()
    tokens_move.finish()


def feed_forward(heads, second, cot, we, wo, wc, bias):
    rows, width = second.shape
    ff = we.shape[1] // GROUP
    lanes = heads.shape[2]
    vmem = pl.BlockSpec(memory_space=pltpu.VMEM)
    any_spec = pl.BlockSpec(memory_space=pl.ANY)
    return pl.pallas_call(
        feed_kernel,
        out_shape=(
            jax.ShapeDtypeStruct((4, LINE, rows // LINE, lanes), heads.dtype),
            jax.ShapeDtypeStruct((GROUP,) + cot.shape, cot.dtype),
            jax.ShapeDtypeStruct((2, we.shape[0], ff), we.dtype),
            jax.ShapeDtypeStruct((rows, ff), jnp.bfloat16),
            jax.ShapeDtypeStruct((rows, ff), jnp.bfloat16),
            jax.ShapeDtypeStruct((width // 2, 2 * ff + width), jnp.bfloat16),
            jax.ShapeDtypeStruct((1, ff), jnp.float32),
        ),
        in_specs=[any_spec, vmem] + [any_spec] * 4 + [vmem],
        out_specs=[any_spec] + [vmem] * 6,
        scratch_shapes=[
            pltpu.VMEM((rows, ff), jnp.float32),
            pltpu.VMEM((rows, lanes), jnp.bfloat16),
            pltpu.VMEM((lanes, width), jnp.bfloat16),
            pltpu.VMEM((ff, width), jnp.bfloat16),
            pltpu.SemaphoreType.DMA((2, LINE - 1)),
            pltpu.SemaphoreType.DMA((2, LINE - 1)),
            pltpu.SemaphoreType.DMA((12,)),
            pltpu.SemaphoreType.DMA((12,)),
            pltpu.SemaphoreType.DMA((5,)),
        ],
        compiler_params=pltpu.CompilerParams(
            collective_id=1, has_side_effects=True, vmem_limit_bytes=56 << 20
        ),
        name="feed_forward",
    )(heads, second, cot, we, wo, wc, bias)


class LineSum:
    KINDS = 8

    def __init__(self, grad, result, inbox, sems, swap, size, lag, place):
        self.grad, self.result, self.inbox, self.sems, self.swap = grad, result, inbox, sems, swap
        self.c, self.y, self.x, self.z = place
        self.size = size
        self.count = grad.shape[0] // size
        self.split = (self.count + 1) // 2
        self.lag = lag
        self.slots = self.split + 6 * lag

    def rows(self, chunk):
        return pl.ds(pl.multiple_of(chunk * self.size, self.size), self.size)

    def moves(self, chunk, half):
        c, y, x, z = self.c, self.y, self.x, self.z
        up = 1 if half == 0 else -1
        rows = self.rows(chunk)
        grad, result, swap = self.grad, self.result, self.swap
        mine = result.at[c, x, rows]
        beside = result.at[c, 1 - x, rows]
        lower, upper = device_at(c, y, x, z - up), device_at(c, y, x, z + up)

        def lanes(which):
            return pl.ds(pl.multiple_of(which * swap, swap), swap)

        makers = {
            "near": (0, lambda: (grad.at[rows], self.inbox.at[0, rows], upper)),
            "far": (1, lambda: (grad.at[rows], self.inbox.at[1, rows], lower)),
            "swap": (
                2,
                lambda: (
                    grad.at[rows, lanes(1 - y)],
                    result.at[c, x, rows, lanes(y)],
                    device_at(c, 1 - y, x, z),
                ),
            ),
            "down": (3, lambda: (mine, mine, lower)),
            "out": (4, lambda: (mine, mine, upper)),
            "side": (5, lambda: (mine, mine, device_at(c, y, 1 - x, z))),
            "core": (6, lambda: (mine, mine, device_at(1 - c, y, x, z))),
            "late": (7, lambda: (beside, beside, device_at(1 - c, y, x, z))),
        }

        def make(name):
            kind, parts = makers[name]
            src, dst, target = parts()
            return remote(
                src, dst, self.sems.at[2 * kind, chunk], self.sems.at[2 * kind + 1, chunk], target
            )

        return make

    def slot(self, t):
        for half in range(2):
            self.half_slot(t, half)

    def extent(self, half):
        size = self.split if half == 0 else self.count - self.split
        base = 0 if half == 0 else self.split
        at = self.z if half == 0 else LINE - 1 - self.z
        return (size, base, at)

    def half_slot(self, t, half):
        size, base, at = self.extent(half)
        lag = self.lag
        swap = self.swap
        owner = at == 1

        def event(delay, run):
            chunk = t - delay
            index = jnp.clip(chunk, 0, size - 1) + base

            @pl.when((chunk >= 0) & (chunk < size))
            def _():
                run(index, self.moves(index, half))

        def reduce(index, moves):
            rows = self.rows(index)

            @pl.when(at == 0)
            def _():
                moves("near").start()

            @pl.when(at == 2)
            def _():
                moves("far").wait_recv()
                total = self.grad[rows].astype(jnp.float32) + self.inbox[1, rows].astype(
                    jnp.float32
                )
                self.grad[rows] = total.astype(jnp.bfloat16)

            @pl.when(at >= 2)
            def _():
                moves("far").start()

            @pl.when(owner)
            def _():
                moves("near").wait_recv()
                moves("far").wait_recv()
                total = (
                    self.grad[rows].astype(jnp.float32)
                    + self.inbox[0, rows].astype(jnp.float32)
                    + self.inbox[1, rows].astype(jnp.float32)
                )
                self.grad[rows] = total.astype(jnp.bfloat16)
                moves("swap").start()
                own = pl.ds(pl.multiple_of(self.y * swap, swap), swap)
                plain = pl.ds(2 * swap, self.grad.shape[1] - 2 * swap)
                self.result[self.c, self.x, rows, own] = self.grad[rows, own]
                self.result[self.c, self.x, rows, plain] = self.grad[rows, plain]

        event(jnp.where(owner, 2 * lag, jnp.where(at == 2, lag, 0)), reduce)

        def spread(index, moves):
            @pl.when(owner)
            def _():
                moves("swap").wait_recv()
                moves("down").start()

            @pl.when(at == 0)
            def _():
                moves("down").wait_recv()

            @pl.when(at >= 2)
            def _():
                moves("out").wait_recv()

            @pl.when((at == 1) | (at == 2))
            def _():
                moves("out").start()

            moves("side").start()
            moves("core").start()

        wait = jnp.where(owner, 3 * lag, jnp.where(at == 3, 5 * lag, 4 * lag))
        event(wait, spread)

        def late(index, moves):
            moves("side").wait_recv()
            moves("late").start()

        event(wait + lag, late)

    def drain(self):
        for half in range(2):
            size, base, at = self.extent(half)

            def finish(chunk, carry):
                moves = self.moves(chunk + base, half)

                @pl.when(at == 0)
                def _():
                    moves("near").wait_send()

                @pl.when(at >= 2)
                def _():
                    moves("far").wait_send()

                @pl.when(at == 1)
                def _():
                    moves("swap").wait_send()
                    moves("down").wait_send()

                @pl.when((at == 1) | (at == 2))
                def _():
                    moves("out").wait_send()

                moves("side").wait_send()
                moves("core").wait()
                moves("late").wait()
                return carry

            lax.fori_loop(0, size, finish, 0)


def sort_kernel(order, src, dst, *, units, back):
    for unit in range(units):
        place = order[0, unit]
        if back:
            dst[:, unit] = src[:, place]
        else:
            dst[:, place] = src[:, unit]


def sort_units(order, array, units, back):
    shape = array.shape
    vmem = pl.BlockSpec(memory_space=pltpu.VMEM)
    view = (shape[0], units, UNIT, shape[-1])
    return pl.pallas_call(
        functools.partial(sort_kernel, units=units, back=back),
        out_shape=jax.ShapeDtypeStruct(view, array.dtype),
        in_specs=[pl.BlockSpec(memory_space=pltpu.SMEM), vmem],
        out_specs=vmem,
        compiler_params=pltpu.CompilerParams(vmem_limit_bytes=16 << 20),
        name="restore_units" if back else "sort_units",
    )(order, array.reshape(view))


def attention_kernel(
    ints,
    parts,
    unit_cos,
    unit_sin,
    row_cos,
    row_sin,
    feed_grad,
    out,
    feed_all,
    masked,
    flat,
    scores,
    slopes,
    key_sum,
    value_sum,
    mixed_sum,
    query_sum,
    feed_own,
    feed_inbox,
    feed_sems,
    local,
    *,
    units,
    pieces,
    swap,
):
    here = place_here()
    greet_line(here)
    load = pltpu.make_async_copy(feed_grad, feed_own, local)
    load.start()
    load.wait()
    line = LineSum(feed_own, feed_all, feed_inbox, feed_sems, swap, FEED_CHUNK, 2, here)
    length = parts.shape[1]
    scale = 1.0 / math.sqrt(HEAD)
    blocks = length // SPAN
    lanes = lax.broadcasted_iota(jnp.int32, (UNIT, 2 * HEAD), 1)
    lower = lanes < HEAD

    def arrange(index, carry):
        @pl.when(lax.rem(index, 4) == 0)
        def _():
            line.slot(lax.div(index, 4))

        at = pl.ds(pl.multiple_of(index * UNIT, UNIT), UNIT)
        for which in range(4):
            rows = parts[which, at, :].astype(jnp.float32)
            if which == 0:
                rows = rows * scale
            masked[which, 0, at, :] = jnp.where(lower, rows, 0.0).astype(jnp.bfloat16)
            masked[which, 1, at, :] = jnp.where(lower, 0.0, rows).astype(jnp.bfloat16)
            flat[which, :, at] = rows.T.astype(jnp.bfloat16)
        return carry

    lax.fori_loop(0, units, arrange, 0)
    early = -(-units // 4)
    key_sum[...] = jnp.zeros_like(key_sum)
    value_sum[...] = jnp.zeros_like(value_sum)

    def labels(positions):
        found = jnp.full(positions.shape, -1, jnp.int32)
        for piece in range(pieces):
            start = ints[0, units + piece]
            found = jnp.where(
                (positions >= start) & (positions < start + PIECE), piece, found
            )
        return found

    def dot(a, b):
        return jnp.dot(a, b, preferred_element_type=jnp.float32)

    for block in range(blocks):
        begin = block * SPAN
        last = SPAN + (UNIT if block + 1 < blocks else 0)
        columns = pl.ds(begin, SPAN)
        row_at = begin + lax.broadcasted_iota(jnp.int32, (1, SPAN), 1)
        col_at = begin + lax.broadcasted_iota(jnp.int32, (last, 1), 0)
        row_lab = labels(row_at)
        col_lab = labels(col_at)
        allowed = (col_at <= row_at) | (
            (col_lab == row_lab) & (row_lab >= 0)
        )

        def one_head(head, carry):
            start_tick = 3 * block * (block + 1) + head * 3 * (block + 1)

            def tick(index):
                at = start_tick + index

                @pl.when(lax.rem(at, 2) == 0)
                def _():
                    line.slot(early + lax.div(at, 2))

            queries = flat[0, :, columns]
            grads = flat[3, :, columns]
            side = pl.ds(pl.multiple_of(head * HEAD, HEAD), HEAD)

            def score_tile(start, size, top, mask=None):
                rows = pl.ds(start, size)
                tile = dot(masked[1, head, rows, :], queries)
                if mask is not None:
                    tile = jnp.where(mask, tile, NEGATIVE)
                scores[rows, :] = tile
                return jnp.maximum(top, jnp.max(tile, axis=0, keepdims=True))

            def tile_step(step, run, j, carry):
                tick(step * (block + 1) + j)
                start = pl.multiple_of(j * SPAN, SPAN)
                return run(start, SPAN, carry)

            top = lax.fori_loop(
                0,
                block,
                functools.partial(tile_step, 0, score_tile),
                jnp.full((1, SPAN), NEGATIVE, jnp.float32),
            )
            tick(block)
            top = score_tile(begin, last, top, allowed)

            def weight_tile(start, size, sums):
                total, delta = sums
                rows = pl.ds(start, size)
                weights = jnp.exp(scores[rows, :] - top)
                slope = dot(masked[2, head, rows, :], grads)
                scores[rows, :] = weights
                slopes[rows, :] = slope
                return (
                    total + jnp.sum(weights, axis=0, keepdims=True),
                    delta + jnp.sum(weights * slope, axis=0, keepdims=True),
                )

            zero = jnp.zeros((1, SPAN), jnp.float32)
            sums = lax.fori_loop(
                0,
                block,
                functools.partial(tile_step, 1, weight_tile),
                (zero, zero),
            )
            tick(2 * block + 1)
            total, delta = weight_tile(begin, last, sums)
            inverse = 1.0 / total
            delta = delta * inverse

            def grad_tile(start, size, sums):
                mixed, query = sums
                rows = pl.ds(start, size)
                probs = scores[rows, :] * inverse
                grad = (probs * (slopes[rows, :] - delta)).astype(jnp.bfloat16)
                probs = probs.astype(jnp.bfloat16)
                value_sum[rows, :] += dot(probs, masked[3, head, columns, :])
                key_sum[rows, :] += dot(grad, masked[0, head, columns, :])
                mixed = mixed + dot(flat[2, side, rows], probs)
                query = query + dot(flat[1, side, rows], grad)
                return (mixed, query)

            none = jnp.zeros((HEAD, SPAN), jnp.float32)
            sums = lax.fori_loop(
                0,
                block,
                functools.partial(tile_step, 2, grad_tile),
                (none, none),
            )
            tick(3 * block + 2)
            mixed, query = grad_tile(begin, last, sums)
            mixed_sum[side, columns] = mixed
            query_sum[side, columns] = query * scale
            return carry

        lax.fori_loop(0, 2, one_head, 0)

    lane = lax.rem(lax.broadcasted_iota(jnp.int32, row_cos.shape, 1), HEAD)

    def finish(index, carry):
        at = pl.ds(pl.multiple_of(index * UNIT, UNIT), UNIT)
        base_cos, base_sin = unit_cos[pl.ds(index, 1), :], unit_sin[pl.ds(index, 1), :]
        cosine = base_cos * row_cos[...] - base_sin * row_sin[...]
        sine = base_sin * row_cos[...] + base_cos * row_sin[...]
        sine_up = jnp.where(lane < HALF, sine, 0.0)
        sine_down = jnp.where(lane < HALF, 0.0, sine)

        def turn_back(rows):
            up = pltpu.roll(rows, 2 * HEAD - HALF, 1)
            down = pltpu.roll(rows, HALF, 1)
            return rows * cosine + up * sine_up - down * sine_down

        out[0, at, :] = mixed_sum[:, at].T.astype(jnp.bfloat16)
        out[1, at, :] = turn_back(query_sum[:, at].T).astype(jnp.bfloat16)
        out[2, at, :] = turn_back(key_sum[at, :]).astype(jnp.bfloat16)
        out[3, at, :] = value_sum[at, :].astype(jnp.bfloat16)
        return carry

    lax.fori_loop(0, units, finish, 0)

    def more(slot, carry):
        line.slot(slot)
        return carry

    ticked = early + (3 * blocks * (blocks + 1) + 1) // 2
    lax.fori_loop(ticked, max(line.slots, ticked), more, 0)
    line.drain()


def attend(ints, parts, tables, feed_grad, units, pieces, swap):
    length = parts.shape[1]
    vmem = pl.BlockSpec(memory_space=pltpu.VMEM)
    return pl.pallas_call(
        functools.partial(attention_kernel, units=units, pieces=pieces, swap=swap),
        out_shape=(
            jax.ShapeDtypeStruct(parts.shape, parts.dtype),
            jax.ShapeDtypeStruct((2, 2) + feed_grad.shape, feed_grad.dtype),
        ),
        in_specs=[pl.BlockSpec(memory_space=pltpu.SMEM)]
        + [vmem] * 5
        + [pl.BlockSpec(memory_space=pl.ANY)],
        out_specs=[vmem, vmem],
        scratch_shapes=[
            pltpu.VMEM((4, 2, length, 2 * HEAD), jnp.bfloat16),
            pltpu.VMEM((4, 2 * HEAD, length), jnp.bfloat16),
            pltpu.VMEM((length, SPAN), jnp.float32),
            pltpu.VMEM((length, SPAN), jnp.float32),
            pltpu.VMEM((length, 2 * HEAD), jnp.float32),
            pltpu.VMEM((length, 2 * HEAD), jnp.float32),
            pltpu.VMEM((2 * HEAD, length), jnp.float32),
            pltpu.VMEM((2 * HEAD, length), jnp.float32),
            pltpu.VMEM(feed_grad.shape, jnp.bfloat16),
            pltpu.VMEM((2,) + feed_grad.shape, jnp.bfloat16),
            pltpu.SemaphoreType.DMA((2 * LineSum.KINDS, feed_grad.shape[0] // FEED_CHUNK)),
            pltpu.SemaphoreType.DMA,
        ],
        compiler_params=pltpu.CompilerParams(
            collective_id=2, has_side_effects=True, vmem_limit_bytes=56 << 20
        ),
        name="attend",
    )(ints, parts, *tables, feed_grad)


def close_kernel(
    done,
    active_src,
    grad_expanded_src,
    we_src,
    wc_src,
    wm_src,
    wo_src,
    hidden_src,
    cots_src,
    vectors,
    feed_sums,
    attn_all,
    out_sum,
    term_sum,
    parts,
    first,
    stats,
    outs,
    terms,
    attn_own,
    attn_inbox,
    near,
    pair,
    beside,
    single,
    far,
    totals,
    active,
    grad_expanded,
    we,
    wc,
    wm,
    wo,
    hidden,
    cots,
    send,
    recv,
    attn_sems,
    near_sems,
    beside_sems,
    far_sems,
    local,
    loads,
    *,
    swap,
):
    place = place_here()
    c, y, x, z = place
    core = device_at(1 - c, y, x, z)
    over_x = device_at(c, y, 1 - x, z)
    over_y = device_at(c, 1 - y, x, z)
    inner = 2 * x + c

    def rows_of(src, dst):
        count = dst.shape[0]
        return src.at[pl.ds(pl.multiple_of(inner * count, count), count)]

    sources = (
        (hidden_src, hidden),
        (grad_expanded_src, grad_expanded),
        (we_src, we),
        (active_src, active),
        (rows_of(wc_src, wc), wc),
        (cots_src, cots),
        (wm_src, wm),
        (rows_of(wo_src, wo), wo),
    )
    fetched = []
    for index, (src, dst) in enumerate(sources):
        copy = pltpu.make_async_copy(src, dst, loads.at[index])
        copy.start()
        fetched.append(copy)
    barrier = pltpu.get_barrier_semaphore()
    peers = [lax.rem(z + d, LINE) for d in range(1, LINE)]
    partners = [device_at(c, y, x, peer) for peer in peers] + [core, over_x, over_y]
    for partner in partners:
        pl.semaphore_signal(barrier, inc=1, device_id=partner, device_id_type=MESH)
    pl.semaphore_wait(barrier, len(partners))
    rows = done.shape[2]
    lanes = done.shape[3]
    mine = pl.ds(pl.multiple_of(z * rows, rows), rows)
    copies = []
    for index, peer in enumerate(peers):
        for which in (1, 2, 3, 0):
            copy = remote(
                done.at[which, peer],
                parts.at[mine, pl.ds(which * lanes, lanes)],
                send.at[index, which],
                recv.at[index, which],
                device_at(c, y, x, peer),
            )
            copy.start()
            copies.append(copy)
    owns = []
    for which in range(4):
        copy = pltpu.make_async_copy(
            done.at[which, z], parts.at[mine, pl.ds(which * lanes, lanes)], local.at[which]
        )
        copy.start()
        owns.append(copy)
    gain_one, shift_one, gain_two = vectors[0:1, :], vectors[1:2, :], vectors[2:3, :]
    width = hidden.shape[1]
    half = width // 2
    totals[...] = jnp.zeros_like(totals)
    for copy in fetched:
        copy.wait()

    def before(index, carry):
        at = pl.ds(pl.multiple_of(index * TILE, TILE), TILE)
        raw = hidden[at, :].astype(jnp.float32)
        mean = jnp.mean(raw, axis=1, keepdims=True)
        centred = raw - mean
        rstd = lax.rsqrt(jnp.mean(centred * centred, axis=1, keepdims=True) + EPS)
        stats[0, at, :] = jnp.broadcast_to(mean, (TILE, stats.shape[2]))
        stats[1, at, :] = jnp.broadcast_to(rstd, (TILE, stats.shape[2]))
        xhat = centred * rstd
        first[at, :] = (xhat * gain_one + shift_one).astype(jnp.bfloat16)
        grad_second = dot_rows(grad_expanded[at, :], we[...])
        terms[index] = (grad_second * gain_two).astype(jnp.bfloat16)
        outs[index] = dot_plain(active[at, :], wc[...]).astype(jnp.bfloat16)
        totals[2:3, :] += jnp.sum(grad_second * xhat, axis=0, keepdims=True)
        totals[3:4, :] += jnp.sum(grad_second, axis=0, keepdims=True)
        totals[4:5, :] += jnp.sum(cots[at, :].astype(jnp.float32), axis=0, keepdims=True)
        return carry

    lax.fori_loop(0, hidden.shape[0] // TILE, before, 0)
    for copy in owns:
        copy.wait()
    for copy in copies:
        copy.wait()

    arrays = (outs, terms)

    def block_at(cc, yy, xx):
        return (2 * cc + yy) * 2 + xx

    def to_core(a, yy, xx):
        block = block_at(1 - c, yy, xx)
        return remote(
            arrays[a].at[block],
            near.at[a, yy, xx],
            near_sems.at[0, a, yy, xx],
            near_sems.at[1, a, yy, xx],
            core,
        )

    ways = ((y, x, over_y, over_x), (x, y, over_x, over_y))

    def hop_one(a, index):
        near_axis, far_axis, target, beyond = ways[a]
        return remote(
            pair.at[a, 1 - near_axis, index],
            beside.at[a, index],
            beside_sems.at[0, a, index],
            beside_sems.at[1, a, index],
            target,
        )

    def hop_two(a):
        return remote(
            single.at[a], far.at[a], far_sems.at[0, a], far_sems.at[1, a], ways[a][3]
        )

    def after(index):
        at = pl.ds(pl.multiple_of(index * TILE, TILE), TILE)
        grads = parts[at, pl.ds(lanes, 3 * lanes)]
        grad_first = dot_rows(grads, wm[...])
        xhat = (hidden[at, :].astype(jnp.float32) - stats[0, at, 0:1]) * stats[1, at, 0:1]
        terms[index] = (terms[index].astype(jnp.float32) + grad_first * gain_one).astype(
            jnp.bfloat16
        )
        outs[index] = (
            outs[index].astype(jnp.float32) + dot_plain(parts[at, pl.ds(0, lanes)], wo[...])
        ).astype(jnp.bfloat16)
        totals[0:1, :] += jnp.sum(grad_first * xhat, axis=0, keepdims=True)
        totals[1:2, :] += jnp.sum(grad_first, axis=0, keepdims=True)
        totals[5:6, pl.ds(0, 3 * lanes)] += jnp.sum(
            grads.astype(jnp.float32), axis=0, keepdims=True
        )

    def others(step, carry):
        yy, xx = lax.rem(1 - y + step // 2, 2), lax.rem(step, 2)
        after(block_at(1 - c, yy, xx))
        for a in range(2):
            to_core(a, yy, xx).start()
        return carry

    lax.fori_loop(0, 4, others, 0)

    def ours(step, carry):
        yy, xx = lax.rem(1 - y + step // 2, 2), lax.rem(step, 2)
        after(block_at(c, yy, xx))
        for a in range(2):
            to_core(a, yy, xx).wait_recv()
            total = arrays[a][block_at(c, yy, xx)].astype(jnp.float32) + near[a, yy, xx].astype(
                jnp.float32
            )
            near_at, far_at = (yy, xx) if a == 0 else (xx, yy)
            pair[a, near_at, far_at] = total.astype(jnp.bfloat16)

            @pl.when(near_at != ways[a][0])
            def _():
                hop_one(a, far_at).start()

        return carry

    lax.fori_loop(0, 4, ours, 0)
    for index in range(width // TILE):
        block = dot_tokens(first[:, pl.ds(index * TILE, TILE)], parts[:, pl.ds(lanes, 3 * lanes)])
        side, row = divmod(index * TILE, half)
        attn_own[pl.ds(row, TILE), pl.ds(side * swap, swap)] = block.astype(jnp.bfloat16)
    block = dot_tokens(parts[:, pl.ds(0, lanes)], cots[...]).astype(jnp.bfloat16)
    wide = 2 * lanes
    for index in range(width // wide):
        attn_own[pl.ds(index * lanes, lanes), pl.ds(2 * swap, wide)] = block[
            :, index * wide : (index + 1) * wide
        ]
    lines = []
    fill = jnp.zeros((1, swap), jnp.float32)
    for index in range(5):
        for begin in range(0, width, swap):
            stop = min(begin + swap, width)
            line = totals[index : index + 1, begin:stop]
            if stop - begin < swap:
                line = jnp.concatenate([line, fill[:, : swap - (stop - begin)]], axis=1)
            lines.append(line)
    lines.append(totals[5:6, 0:swap])
    ff = feed_sums.shape[1]
    for begin in range(0, ff, swap):
        stop = min(begin + swap, ff)
        line = feed_sums[:, begin:stop]
        if stop - begin < swap:
            line = jnp.concatenate([line, fill[:, : swap - (stop - begin)]], axis=1)
        lines.append(line)
    lines += [fill] * (attn_own.shape[0] - half - len(lines))
    small = jnp.concatenate(lines, axis=0).astype(jnp.bfloat16)
    tail = pl.ds(half, attn_own.shape[0] - half)
    attn_own[tail, pl.ds(0, swap)] = small
    attn_own[tail, pl.ds(swap, swap)] = small
    attn_own[tail, pl.ds(2 * swap, wide)] = jnp.zeros((small.shape[0], wide), jnp.bfloat16)

    attn = LineSum(attn_own, attn_all, attn_inbox, attn_sems, swap, CHUNK, 1, place)

    def step(t, carry):
        attn.slot(t)
        return carry

    def pass_on(a):
        near_axis, far_axis = ways[a][:2]
        for index in range(2):
            hop_one(a, index).wait()
        single[a] = (
            pair[a, near_axis, 1 - far_axis].astype(jnp.float32)
            + beside[a, 1 - far_axis].astype(jnp.float32)
        ).astype(jnp.bfloat16)
        hop_two(a).start()

    middle = attn.slots - 6
    lax.fori_loop(0, middle, step, 0)
    pass_on(0)
    pass_on(1)
    lax.fori_loop(middle, attn.slots, step, 0)
    for a, dst in enumerate((out_sum, term_sum)):
        hop_two(a).wait()
        near_axis, far_axis = ways[a][:2]
        dst[...] = (
            pair[a, near_axis, far_axis].astype(jnp.float32)
            + beside[a, far_axis].astype(jnp.float32)
            + far[a].astype(jnp.float32)
        )

    def sent(step, carry):
        for a in range(2):
            to_core(a, step // 2, lax.rem(step, 2)).wait_send()
        return carry

    lax.fori_loop(0, 4, sent, 0)
    attn.drain()


def close(done, active, grad_expanded, we, wc, wm, wo, hidden, cots, vectors, feed_sums, tokens):
    rows, width = hidden.shape
    lanes = done.shape[3]
    ff = active.shape[1]
    swap = 3 * lanes
    block = (tokens, width)
    vmem = pl.BlockSpec(memory_space=pltpu.VMEM)
    any_spec = pl.BlockSpec(memory_space=pl.ANY)
    grad_shape = (width // 2 + CHUNK, 2 * swap + 2 * lanes)
    scratch = [
        pltpu.VMEM((rows, 4 * lanes), jnp.bfloat16),
        pltpu.VMEM((rows, width), jnp.bfloat16),
        pltpu.VMEM((2, rows, 128), jnp.float32),
        pltpu.VMEM((GROUP,) + block, jnp.bfloat16),
        pltpu.VMEM((GROUP,) + block, jnp.bfloat16),
        pltpu.VMEM(grad_shape, jnp.bfloat16),
        pltpu.VMEM((2,) + grad_shape, jnp.bfloat16),
        pltpu.VMEM((2, 2, 2) + block, jnp.bfloat16),
        pltpu.VMEM((2, 2, 2) + block, jnp.bfloat16),
        pltpu.VMEM((2, 2) + block, jnp.bfloat16),
        pltpu.VMEM((2,) + block, jnp.bfloat16),
        pltpu.VMEM((2,) + block, jnp.bfloat16),
        pltpu.VMEM((8, width), jnp.float32),
        pltpu.VMEM((rows, ff), jnp.bfloat16),
        pltpu.VMEM((rows, ff), jnp.bfloat16),
        pltpu.VMEM((width, ff), jnp.bfloat16),
        pltpu.VMEM((ff, width), jnp.bfloat16),
        pltpu.VMEM((width, 3 * lanes), jnp.bfloat16),
        pltpu.VMEM((lanes, width), jnp.bfloat16),
        pltpu.VMEM((rows, width), jnp.bfloat16),
        pltpu.VMEM((rows, width), jnp.bfloat16),
        pltpu.SemaphoreType.DMA((LINE - 1, 4)),
        pltpu.SemaphoreType.DMA((LINE - 1, 4)),
        pltpu.SemaphoreType.DMA((2 * LineSum.KINDS, grad_shape[0] // CHUNK)),
        pltpu.SemaphoreType.DMA((2, 2, 2, 2)),
        pltpu.SemaphoreType.DMA((2, 2, 2)),
        pltpu.SemaphoreType.DMA((2, 2)),
        pltpu.SemaphoreType.DMA((4,)),
        pltpu.SemaphoreType.DMA((8,)),
    ]
    return pl.pallas_call(
        functools.partial(close_kernel, swap=swap),
        out_shape=(
            jax.ShapeDtypeStruct((2, 2) + grad_shape, jnp.bfloat16),
            jax.ShapeDtypeStruct(block, jnp.float32),
            jax.ShapeDtypeStruct(block, jnp.float32),
        ),
        in_specs=[any_spec] * 9 + [vmem] * 2,
        out_specs=[vmem] * 3,
        scratch_shapes=scratch,
        compiler_params=pltpu.CompilerParams(
            collective_id=3, has_side_effects=True, vmem_limit_bytes=60 << 20
        ),
        name="close",
    )(done, active, grad_expanded, we, wc, wm, wo, hidden, cots, vectors, feed_sums)


def widen_kernel(
    feed_all,
    attn_all,
    expand,
    contract,
    merged,
    output,
    feed,
    attn,
    expand_wide,
    contract_wide,
    merged_wide,
    output_wide,
    loads,
    stores,
    *,
    swap,
    lanes,
    ff,
):
    half = feed.shape[2]
    gets = []
    for index, (src, dst) in enumerate(((feed_all, feed), (attn_all, attn))):
        for part in range(4):
            copy = pltpu.make_async_copy(
                src.at[part // 2, part % 2], dst.at[part // 2, part % 2], loads.at[index, part]
            )
            copy.start()
            gets.append(copy)
    puts = []

    def put(src, dst):
        copy = pltpu.make_async_copy(src, dst, stores.at[len(puts)])
        copy.start()
        puts.append(copy)

    for part in range(4):
        c, x = part // 2, part % 2
        gets[part].wait()
        for y in range(2):
            at = pl.ds((4 * y + 2 * x + c) * ff, ff)
            expand_wide[:, at] = feed[c, x, :, pl.ds(y * ff, ff)].astype(jnp.float32)
            put(expand_wide.at[:, at], expand.at[:, at])
        at = pl.ds((2 * x + c) * ff, ff)
        contract_wide[at, :] = feed[c, x, :, pl.ds(2 * ff, 2 * half)].astype(jnp.float32)
        put(contract_wide.at[at], contract.at[at])
    for copy in gets[4:]:
        copy.wait()
    width = 2 * half
    for j in range(3):
        for octant in range(GROUP):
            c, x, y = octant % 2, octant // 2 % 2, octant // 4
            at = pl.ds(j * width + octant * lanes, lanes)
            merged_wide[:, at] = attn[
                c, x, pl.ds(0, half), pl.ds(y * swap + j * lanes, lanes)
            ].astype(jnp.float32)
        at = pl.ds(j * width, width)
        put(merged_wide.at[:, at], merged.at[:, at])
    for part in range(4):
        c, x = part % 2, part // 2
        for index in range(half // lanes):
            output_wide[pl.ds(part * lanes, lanes), pl.ds(2 * lanes * index, 2 * lanes)] = attn[
                c, x, pl.ds(index * lanes, lanes), pl.ds(2 * swap, 2 * lanes)
            ].astype(jnp.float32)
    put(output_wide, output)
    for copy in puts:
        copy.wait()


def widen(feed_all, attn_all, swap, lanes, ff):
    half = feed_all.shape[2]
    width = 2 * half
    shapes = ((half, GROUP * ff), (4 * ff, width), (half, 3 * width), (4 * lanes, width))
    any_spec = pl.BlockSpec(memory_space=pl.ANY)
    return pl.pallas_call(
        functools.partial(widen_kernel, swap=swap, lanes=lanes, ff=ff),
        out_shape=tuple(jax.ShapeDtypeStruct(shape, jnp.float32) for shape in shapes),
        in_specs=[any_spec] * 2,
        out_specs=[any_spec] * 4,
        scratch_shapes=[
            pltpu.VMEM(feed_all.shape, jnp.bfloat16),
            pltpu.VMEM(attn_all.shape, jnp.bfloat16),
        ]
        + [pltpu.VMEM(shape, jnp.float32) for shape in shapes]
        + [pltpu.SemaphoreType.DMA((2, 4)), pltpu.SemaphoreType.DMA((16,))],
        compiler_params=pltpu.CompilerParams(vmem_limit_bytes=48 << 20),
        name="widen",
    )(feed_all, attn_all)


def turn_tables(positions, lanes):
    lane = jnp.arange(lanes, dtype=jnp.int32) % HEAD
    inverse = jnp.exp((lane % HALF).astype(jnp.float32) * (-2.0 * math.log(10000.0) / ROT))
    angles = positions.astype(jnp.float32)[:, None] * inverse[None, :]
    turned = lane[None, :] < ROT
    return (jnp.where(turned, jnp.cos(angles), 1.0), jnp.where(turned, jnp.sin(angles), 0.0))


def group_body(
    hidden_states,
    unit_order,
    piece_starts,
    first_gain,
    first_shift,
    second_gain,
    second_shift,
    merged_weight,
    merged_bias,
    output_weight,
    output_bias,
    expand_weight,
    expand_bias,
    contract_weight,
    contract_bias,
    out_cotangent,
):
    c, y, x, z = place_here()
    tokens, width = hidden_states.shape[1:]
    length = tokens * 2 * LINE
    units = unit_order.shape[1]
    pieces = piece_starts.shape[1]
    rows = GROUP * tokens
    part = width // GROUP
    ff_part = expand_weight.shape[1] // GROUP
    half = width // 2
    vectors = (
        first_gain,
        first_shift,
        second_gain,
        second_shift,
        merged_bias,
        output_bias,
        expand_bias,
        contract_bias,
    )
    sizes = [v.shape[0] for v in vectors]
    packed = jnp.concatenate([v.astype(jnp.float32).reshape(-1, 128) for v in vectors])
    ints = jnp.concatenate([unit_order[0], piece_starts[0]])
    ints = jnp.broadcast_to(jnp.pad(ints, (0, 128 - ints.shape[0]))[None], (8, 128))
    tables = turn_tables(jnp.arange(units, dtype=jnp.int32) * UNIT, part) + turn_tables(
        jnp.arange(UNIT, dtype=jnp.int32), part
    )
    hid_all, ints_all, vec_all, wm_all, heads, second = enter(
        hidden_states[0], ints, packed, merged_weight, tables
    )
    inner = 2 * x + c
    own_expand = lax.dynamic_slice_in_dim(expand_bias, inner * ff_part, ff_part, 0)
    got, cot_all, we_all, active, grad_expanded, feed_grad, feed_sums = feed_forward(
        heads,
        second,
        out_cotangent[0],
        expand_weight,
        output_weight,
        contract_weight,
        own_expand.astype(jnp.float32)[None],
    )
    vec_all = vec_all.reshape(2, -1)
    whole = []
    at = 0
    for size in sizes:
        whole.append(vec_all[:, at : at + size].reshape(-1))
        at += size
    gain_one, shift_one, gain_two, shift_two, bias_merged, bias_out, bias_expand, bias_contract = whole
    wm = wm_all.reshape(width, 3 * part)
    we = we_all.reshape(width, ff_part)
    cots = cot_all.reshape(rows, width)
    own_ints = lax.dynamic_index_in_dim(ints_all[:, 0], z, 0, keepdims=True)
    sorted_parts = sort_units(own_ints, got, units, False)
    done, feed_all = attend(
        own_ints,
        sorted_parts.reshape(4, length, part),
        tables,
        feed_grad,
        units,
        pieces,
        ff_part,
    )
    swap = 3 * part
    lines = CHUNK
    attn_all, out_sum, term_sum = close(
        sort_units(own_ints, done, units, True).reshape(4, LINE, 2 * tokens, part),
        active,
        grad_expanded,
        we,
        contract_weight,
        wm,
        output_weight,
        hid_all.reshape(rows, width),
        cots,
        jnp.stack([gain_one, shift_one, gain_two]),
        feed_sums,
        tokens,
    )
    expand_out, contract_out, merged_out, output_out = widen(
        feed_all, attn_all, swap, part, ff_part
    )
    own_hidden = hidden_states[0].astype(jnp.float32)
    own_mean = jnp.mean(own_hidden, axis=1, keepdims=True)
    own_centred = own_hidden - own_mean
    own_rstd = lax.rsqrt(jnp.mean(own_centred * own_centred, axis=1, keepdims=True) + EPS)
    own_xhat = own_centred * own_rstd
    output = (own_hidden + out_sum + bias_out + bias_contract).astype(jnp.bfloat16)
    upstream = out_cotangent[0].astype(jnp.float32)
    input_gradient = upstream + own_rstd * (
        term_sum
        - jnp.mean(term_sum, axis=1, keepdims=True)
        - own_xhat * jnp.mean(term_sum * own_xhat, axis=1, keepdims=True)
    )

    sums = attn_all[:, :, half : half + lines, : 2 * swap].astype(jnp.float32)
    sums = sums.reshape(2, 2, lines, 2, swap).transpose(3, 1, 0, 2, 4).reshape(GROUP, lines, swap)
    per = -(-width // swap)
    shared = jnp.sum(sums[:, : 4 * per], axis=0).reshape(4, per * swap)[:, :width]
    row_total = sums[0, 4 * per : 5 * per].reshape(-1)[:width]
    merged_sums = sums[:, 5 * per].reshape(GROUP, 3, part).transpose(1, 0, 2).reshape(-1)
    expand_sums = sums[:, 5 * per + 1 : 5 * per + 1 - (-ff_part // swap)]
    expand_sums = expand_sums.reshape(GROUP, -1)[:, :ff_part].reshape(-1)

    def own_half(vector):
        size = vector.shape[0] // 2
        return lax.dynamic_slice_in_dim(vector, y * size, size, 0)

    row_total = own_half(row_total)
    return (
        output[None],
        input_gradient[None],
        own_half(shared[0]),
        own_half(shared[1]),
        own_half(shared[2]),
        own_half(shared[3]),
        merged_out,
        own_half(merged_sums),
        output_out,
        row_total,
        expand_out,
        own_half(expand_sums),
        contract_out,
        row_total,
    )


def fits_groups(mesh, args):
    hidden, order = args[0], args[1]
    count = mesh.shape["seq"]
    tokens = hidden.shape[1] // count
    return (
        mesh.shape["rep"] == 2
        and mesh.shape["fsdp"] == 2
        and count == 2 * LINE
        and hidden.shape[0] == LINE
        and hidden.shape[2] == GROUP * 2 * HEAD
        and tokens % UNIT == 0
        and hidden.shape[1] % SPAN == 0
        and order.shape[1] + args[2].shape[1] <= 128
    )


def solution(mesh):
    in_specs = (
        P(("rep", "fsdp"), "seq", None),
        P(("rep", "fsdp"), None),
        P(("rep", "fsdp"), None),
        P("fsdp"),
        P("fsdp"),
        P("fsdp"),
        P("fsdp"),
        P("fsdp", None),
        P("fsdp"),
        P("fsdp", None),
        P("fsdp"),
        P("fsdp", None),
        P("fsdp"),
        P("fsdp", None),
        P("fsdp"),
        P(("rep", "fsdp"), "seq", None),
    )
    out_specs = (
        P(("rep", "fsdp"), "seq", None),
        P(("rep", "fsdp"), "seq", None),
        P("fsdp"),
        P("fsdp"),
        P("fsdp"),
        P("fsdp"),
        P("fsdp", None),
        P("fsdp"),
        P("fsdp", None),
        P("fsdp"),
        P("fsdp", None),
        P("fsdp"),
        P("fsdp", None),
        P("fsdp"),
    )

    def run(*args):
        chosen = group_body if fits_groups(mesh, args) else body
        mapped = jax.shard_map(
            chosen, mesh=mesh, in_specs=in_specs, out_specs=out_specs, check_vma=False
        )
        return mapped(*args)

    return run
```

```python
import functools
import math

import jax
import jax.numpy as jnp
from jax import lax
from jax.experimental import pallas as pl
from jax.experimental.pallas import tpu as pltpu
from jax.sharding import PartitionSpec as P

HEAD = 64
ROT = 16
UNIT = 128
PIECE = 256


EPS = 1e-05
NEGATIVE = -1e30


def norm_rows(values, gain, shift):
    mean = jnp.mean(values, axis=-1, keepdims=True)
    centred = values - mean
    spread = jnp.mean(centred * centred, axis=-1, keepdims=True)
    return centred * lax.rsqrt(spread + EPS) * gain + shift


def gelu_exact(values):
    return jax.nn.gelu(values, approximate=False)


def rotary_tables(positions):
    index = jnp.arange(ROT // 2, dtype=jnp.float32)
    inverse = jnp.exp(index * (-2.0 * math.log(10000.0) / ROT))
    angles = positions.astype(jnp.float32)[:, None] * inverse[None, :]
    angles = jnp.concatenate([angles, angles], axis=1)
    return (jnp.cos(angles), jnp.sin(angles))


def rotate(values, cosine, sine):
    part = values[..., :ROT]
    turned = jnp.concatenate([-part[..., ROT // 2 :], part[..., : ROT // 2]], axis=-1)
    moved = part * cosine[:, None, :] + turned * sine[:, None, :]
    return jnp.concatenate([moved, values[..., ROT:]], axis=-1)


def unit_positions(order):
    offsets = jnp.arange(UNIT, dtype=jnp.int32)
    return (order[:, None] * UNIT + offsets[None, :]).reshape(-1)


def piece_labels(positions, starts):
    inside = (positions[:, None] >= starts[None, :]) & (
        positions[:, None] < starts[None, :] + PIECE
    )
    labels = jnp.arange(1, starts.shape[0] + 1, dtype=jnp.int32)
    return jnp.sum(jnp.where(inside, labels[None, :], 0), axis=1) - 1


def visible(row_pos, row_lab, col_pos, col_lab):
    earlier = col_pos[None, :] <= row_pos[:, None]
    same = (row_lab[:, None] == col_lab[None, :]) & (row_lab[:, None] >= 0)
    return earlier | same


def merged_parts(first, merged_weight, merged_bias, cosine, sine):
    tokens = first.shape[0]
    width = first.shape[1]
    heads = width // HEAD
    merged = jnp.dot(first, merged_weight, preferred_element_type=jnp.float32) + merged_bias.astype(
        jnp.float32
    )
    queries = rotate(merged[:, :width].reshape(tokens, heads, HEAD), cosine, sine).astype(
        jnp.bfloat16
    )
    keys = rotate(merged[:, width : 2 * width].reshape(tokens, heads, HEAD), cosine, sine)
    keys = keys.reshape(tokens, width).astype(jnp.bfloat16)
    values = merged[:, 2 * width :].astype(jnp.bfloat16)
    return (queries, keys, values)


def block_view(queries, keys_all, values_all, row_pos, row_lab, col_pos, col_lab, span):
    heads = queries.shape[1]
    scale = 1.0 / math.sqrt(HEAD)

    def view(index):
        start = index * span
        key_rows = lax.dynamic_slice_in_dim(keys_all, start, span, 0).reshape(span, heads, HEAD)
        value_rows = lax.dynamic_slice_in_dim(values_all, start, span, 0).reshape(span, heads, HEAD)
        scores = (
            jnp.einsum("thd,khd->htk", queries, key_rows, preferred_element_type=jnp.float32)
            * scale
        )
        allowed = visible(
            row_pos,
            row_lab,
            lax.dynamic_slice_in_dim(col_pos, start, span, 0),
            lax.dynamic_slice_in_dim(col_lab, start, span, 0),
        )[None]
        return (scores, allowed, key_rows, value_rows)

    return view


def log_sums(view, count, heads, tokens):

    def log_step(carry, index):
        top, total = carry
        scores, allowed, key_rows, value_rows = view(index)
        masked = jnp.where(allowed, scores, NEGATIVE)
        newer = jnp.maximum(top, jnp.max(masked, axis=-1))
        terms = jnp.where(allowed, jnp.exp(masked - newer[..., None]), 0.0)
        total = total * jnp.exp(top - newer) + jnp.sum(terms, axis=-1)
        return ((newer, total), None)

    begin = (
        jnp.full((heads, tokens), NEGATIVE, jnp.float32),
        jnp.zeros((heads, tokens), jnp.float32),
    )
    (top, total), unused = lax.scan(log_step, begin, jnp.arange(count, dtype=jnp.int32))
    return top + jnp.log(total)


def mix_values(view, count, logsum, heads, tokens, grad_rows):

    def mix_step(carry, index):
        mixed, delta = carry
        scores, allowed, key_rows, value_rows = view(index)
        weights = jnp.where(allowed, jnp.exp(scores - logsum[..., None]), 0.0)
        mixed = mixed + jnp.einsum(
            "htk,khd->thd",
            weights.astype(jnp.bfloat16),
            value_rows,
            preferred_element_type=jnp.float32,
        )
        if grad_rows is not None:
            slopes = jnp.einsum(
                "thd,khd->htk", grad_rows, value_rows, preferred_element_type=jnp.float32
            )
            delta = delta + jnp.sum(weights * slopes, axis=-1)
        return ((mixed, delta), None)

    begin = (jnp.zeros((tokens, heads, HEAD), jnp.float32), jnp.zeros((heads, tokens), jnp.float32))
    (mixed, delta), unused = lax.scan(mix_step, begin, jnp.arange(count, dtype=jnp.int32))
    return (mixed, delta)


def attend_back(view, count, logsum, delta, grad_rows, queries):
    scale = 1.0 / math.sqrt(HEAD)

    def attend_step(carry, index):
        scores, allowed, key_rows, value_rows = view(index)
        weights = jnp.where(allowed, jnp.exp(scores - logsum[..., None]), 0.0)
        slopes = jnp.einsum(
            "thd,khd->htk", grad_rows, value_rows, preferred_element_type=jnp.float32
        )
        grad_scores = (weights * (slopes - delta[..., None])).astype(jnp.bfloat16)
        carry = carry + jnp.einsum(
            "htk,khd->thd", grad_scores, key_rows, preferred_element_type=jnp.float32
        )
        key_grad = jnp.einsum(
            "htk,thd->khd", grad_scores, queries, preferred_element_type=jnp.float32
        )
        value_grad = jnp.einsum(
            "htk,thd->khd",
            weights.astype(jnp.bfloat16),
            grad_rows,
            preferred_element_type=jnp.float32,
        )
        span = key_rows.shape[0]
        joined = jnp.concatenate(
            [key_grad.reshape(span, -1) * scale, value_grad.reshape(span, -1)], axis=1
        )
        return (carry, joined)

    begin = jnp.zeros(queries.shape, jnp.float32)
    grad_query, parts = lax.scan(attend_step, begin, jnp.arange(count, dtype=jnp.int32))
    return (grad_query * scale, parts)


def body(
    hidden_states,
    unit_order,
    piece_starts,
    first_gain,
    first_shift,
    second_gain,
    second_shift,
    merged_weight,
    merged_bias,
    output_weight,
    output_bias,
    expand_weight,
    expand_bias,
    contract_weight,
    contract_bias,
    out_cotangent,
):
    shards = (
        first_gain,
        first_shift,
        second_gain,
        second_shift,
        merged_weight,
        merged_bias,
        output_weight,
        output_bias,
        expand_weight,
        expand_bias,
        contract_weight,
        contract_bias,
    )
    gathered = (
        lax.all_gather(shards[0], "fsdp", axis=0, tiled=True),
        lax.all_gather(shards[1], "fsdp", axis=0, tiled=True),
        lax.all_gather(shards[2], "fsdp", axis=0, tiled=True),
        lax.all_gather(shards[3], "fsdp", axis=0, tiled=True),
        lax.all_gather(shards[4], "fsdp", axis=0, tiled=True),
        lax.all_gather(shards[5], "fsdp", axis=0, tiled=True),
        lax.all_gather(shards[6], "fsdp", axis=0, tiled=True),
        lax.all_gather(shards[7], "fsdp", axis=0, tiled=True),
        lax.all_gather(shards[8], "fsdp", axis=0, tiled=True),
        lax.all_gather(shards[9], "fsdp", axis=0, tiled=True),
        lax.all_gather(shards[10], "fsdp", axis=0, tiled=True),
        lax.all_gather(shards[11], "fsdp", axis=0, tiled=True),
    )
    hidden = hidden_states[0].astype(jnp.float32)
    tokens = hidden.shape[0]
    width = hidden.shape[1]
    heads = width // HEAD
    length = tokens * lax.axis_size("seq")
    span = min(length, 512)
    count = length // span
    col_pos = unit_positions(unit_order[0])
    col_lab = piece_labels(col_pos, piece_starts[0])
    offset = lax.axis_index("seq") * tokens
    row_pos = lax.dynamic_slice_in_dim(col_pos, offset, tokens, 0)
    row_lab = lax.dynamic_slice_in_dim(col_lab, offset, tokens, 0)
    cosine, sine = rotary_tables(row_pos)
    first = norm_rows(
        hidden, gathered[0].astype(jnp.float32), gathered[1].astype(jnp.float32)
    ).astype(jnp.bfloat16)
    queries, keys, values = merged_parts(first, gathered[4], gathered[5], cosine, sine)
    keys_all, values_all = (
        lax.all_gather(keys, "seq", axis=0, tiled=True),
        lax.all_gather(values, "seq", axis=0, tiled=True),
    )
    view = block_view(queries, keys_all, values_all, row_pos, row_lab, col_pos, col_lab, span)
    logsum = log_sums(view, count, heads, tokens)
    mixed, unused = mix_values(view, count, logsum, heads, tokens, None)
    mixed = mixed.reshape(tokens, width).astype(jnp.bfloat16)
    attention = jnp.dot(mixed, gathered[6], preferred_element_type=jnp.float32) + gathered[
        7
    ].astype(jnp.float32)
    second = norm_rows(
        hidden, gathered[2].astype(jnp.float32), gathered[3].astype(jnp.float32)
    ).astype(jnp.bfloat16)
    expanded = jnp.dot(second, gathered[8], preferred_element_type=jnp.float32) + gathered[
        9
    ].astype(jnp.float32)
    active = gelu_exact(expanded).astype(jnp.bfloat16)
    feed = jnp.dot(active, gathered[10], preferred_element_type=jnp.float32) + gathered[11].astype(
        jnp.float32
    )
    output = (hidden + attention + feed).astype(jnp.bfloat16)
    weights = (
        lax.all_gather(shards[0], "fsdp", axis=0, tiled=True),
        lax.all_gather(shards[1], "fsdp", axis=0, tiled=True),
        lax.all_gather(shards[2], "fsdp", axis=0, tiled=True),
        lax.all_gather(shards[3], "fsdp", axis=0, tiled=True),
        lax.all_gather(shards[4], "fsdp", axis=0, tiled=True),
        lax.all_gather(shards[5], "fsdp", axis=0, tiled=True),
        lax.all_gather(shards[6], "fsdp", axis=0, tiled=True),
        lax.all_gather(shards[7], "fsdp", axis=0, tiled=True),
        lax.all_gather(shards[8], "fsdp", axis=0, tiled=True),
        lax.all_gather(shards[9], "fsdp", axis=0, tiled=True),
        lax.all_gather(shards[10], "fsdp", axis=0, tiled=True),
        lax.all_gather(shards[11], "fsdp", axis=0, tiled=True),
    )
    cotangent = out_cotangent[0]
    upstream = cotangent.astype(jnp.float32)
    normed_one, first_pull = jax.vjp(
        norm_rows, hidden, weights[0].astype(jnp.float32), weights[1].astype(jnp.float32)
    )
    first = normed_one.astype(jnp.bfloat16)
    queries, keys, values = merged_parts(first, weights[4], weights[5], cosine, sine)
    keys_back, values_back = (
        lax.all_gather(keys, "seq", axis=0, tiled=True),
        lax.all_gather(values, "seq", axis=0, tiled=True),
    )
    view = block_view(queries, keys_back, values_back, row_pos, row_lab, col_pos, col_lab, span)
    grad_mixed = jnp.einsum(
        "te,de->td", cotangent, weights[6], preferred_element_type=jnp.float32
    ).astype(jnp.bfloat16)
    grad_rows = grad_mixed.reshape(tokens, heads, HEAD)
    mixed, delta = mix_values(view, count, logsum, heads, tokens, grad_rows)
    mixed = mixed.reshape(tokens, width).astype(jnp.bfloat16)
    grad_query, parts = attend_back(view, count, logsum, delta, grad_rows, queries)
    term = parts.reshape(length, 2 * width)
    own_grads = lax.psum_scatter(
        term.astype(jnp.bfloat16), "seq", scatter_dimension=0, tiled=True
    ).astype(jnp.float32)
    normed_two, second_pull = jax.vjp(
        norm_rows, hidden, weights[2].astype(jnp.float32), weights[3].astype(jnp.float32)
    )
    second = normed_two.astype(jnp.bfloat16)
    expanded = jnp.dot(second, weights[8], preferred_element_type=jnp.float32) + weights[9].astype(
        jnp.float32
    )
    activated, gelu_pull = jax.vjp(gelu_exact, expanded)
    active = activated.astype(jnp.bfloat16)
    grad_active = jnp.einsum(
        "te,fe->tf", cotangent, weights[10], preferred_element_type=jnp.float32
    )
    grad_expanded = gelu_pull(grad_active)[0].astype(jnp.bfloat16)
    grad_second = jnp.einsum(
        "tf,df->td", grad_expanded, weights[8], preferred_element_type=jnp.float32
    )
    unused, turn_pull = jax.vjp(rotate, grad_query, cosine, sine)
    query_back = turn_pull(grad_query)[0].reshape(tokens, width)
    key_back = turn_pull(own_grads[:, :width].reshape(tokens, heads, HEAD))[0].reshape(
        tokens, width
    )
    grad_merged = jnp.concatenate([query_back, key_back, own_grads[:, width:]], axis=1).astype(
        jnp.bfloat16
    )
    grad_first = jnp.einsum(
        "tc,dc->td", grad_merged, weights[4], preferred_element_type=jnp.float32
    )
    first_term, first_gain_grad, first_shift_grad = first_pull(grad_first)
    second_term, second_gain_grad, second_shift_grad = second_pull(grad_second)
    input_gradient = upstream + first_term + second_term
    row_total = jnp.sum(upstream, axis=0)
    local_grads = (
        first_gain_grad,
        first_shift_grad,
        second_gain_grad,
        second_shift_grad,
        jnp.einsum("td,tc->dc", first, grad_merged, preferred_element_type=jnp.float32),
        jnp.sum(grad_merged.astype(jnp.float32), axis=0),
        jnp.einsum("td,te->de", mixed, cotangent, preferred_element_type=jnp.float32),
        row_total,
        jnp.einsum("td,tf->df", second, grad_expanded, preferred_element_type=jnp.float32),
        jnp.sum(grad_expanded.astype(jnp.float32), axis=0),
        jnp.einsum("tf,te->fe", active, cotangent, preferred_element_type=jnp.float32),
        row_total,
    )
    owned = (
        lax.psum_scatter(
            local_grads[0].astype(jnp.bfloat16), "fsdp", scatter_dimension=0, tiled=True
        ).astype(jnp.float32),
        lax.psum_scatter(
            local_grads[1].astype(jnp.bfloat16), "fsdp", scatter_dimension=0, tiled=True
        ).astype(jnp.float32),
        lax.psum_scatter(
            local_grads[2].astype(jnp.bfloat16), "fsdp", scatter_dimension=0, tiled=True
        ).astype(jnp.float32),
        lax.psum_scatter(
            local_grads[3].astype(jnp.bfloat16), "fsdp", scatter_dimension=0, tiled=True
        ).astype(jnp.float32),
        lax.psum_scatter(
            local_grads[4].astype(jnp.bfloat16), "fsdp", scatter_dimension=0, tiled=True
        ).astype(jnp.float32),
        lax.psum_scatter(
            local_grads[5].astype(jnp.bfloat16), "fsdp", scatter_dimension=0, tiled=True
        ).astype(jnp.float32),
        lax.psum_scatter(
            local_grads[6].astype(jnp.bfloat16), "fsdp", scatter_dimension=0, tiled=True
        ).astype(jnp.float32),
        lax.psum_scatter(
            local_grads[7].astype(jnp.bfloat16), "fsdp", scatter_dimension=0, tiled=True
        ).astype(jnp.float32),
        lax.psum_scatter(
            local_grads[8].astype(jnp.bfloat16), "fsdp", scatter_dimension=0, tiled=True
        ).astype(jnp.float32),
        lax.psum_scatter(
            local_grads[9].astype(jnp.bfloat16), "fsdp", scatter_dimension=0, tiled=True
        ).astype(jnp.float32),
        lax.psum_scatter(
            local_grads[10].astype(jnp.bfloat16), "fsdp", scatter_dimension=0, tiled=True
        ).astype(jnp.float32),
        lax.psum_scatter(
            local_grads[11].astype(jnp.bfloat16), "fsdp", scatter_dimension=0, tiled=True
        ).astype(jnp.float32),
    )
    summed = lax.psum(
        (
            owned[0],
            owned[1],
            owned[2],
            owned[3],
            owned[4],
            owned[5],
            owned[6],
            owned[7],
            owned[8],
            owned[9],
            owned[10],
            owned[11],
        ),
        ("rep", "seq"),
    )
    return (
        output[None],
        input_gradient[None],
        summed[0],
        summed[1],
        summed[2],
        summed[3],
        summed[4],
        summed[5],
        summed[6],
        summed[7],
        summed[8],
        summed[9],
        summed[10],
        summed[11],
    )


MESH = pl.DeviceIdType.MESH
GROUP = 8
LINE = 4
HALF = ROT // 2
SPAN = 512
CHUNK = 32
FEED_CHUNK = 16
EVERY = 4


def place_here():
    c, y, s = (lax.axis_index("rep"), lax.axis_index("fsdp"), lax.axis_index("seq"))
    x = lax.rem(s, 2)
    return (c, y, x, s // 2)


def device_at(c, y, x, z):
    return (c, y, 2 * z + x)


def greet(partners):
    barrier = pltpu.get_barrier_semaphore()
    for partner in partners:
        pl.semaphore_signal(barrier, inc=1, device_id=partner, device_id_type=MESH)
    pl.semaphore_wait(barrier, len(partners))


def remote(src, dst, send, recv, target):
    return pltpu.make_async_remote_copy(
        src_ref=src,
        dst_ref=dst,
        send_sem=send,
        recv_sem=recv,
        device_id=target,
        device_id_type=MESH,
    )


def dot_rows(a, b):
    return lax.dot_general(a, b, (((1,), (1,)), ((), ())), preferred_element_type=jnp.float32)


def dot_tokens(a, b):
    return lax.dot_general(a, b, (((0,), (0,)), ((), ())), preferred_element_type=jnp.float32)


def dot_plain(a, b):
    return jnp.dot(a, b, preferred_element_type=jnp.float32)


class TokenExchange:
    def __init__(self, place, send, recv):
        self.place, self.send, self.recv = place, send, recv
        self.count = 0
        self.sends = []

    def go(self, src, dst, target):
        copy = remote(src, dst, self.send.at[self.count], self.recv.at[self.count], target)
        self.count += 1
        copy.start()
        self.sends.append(copy)
        return copy

    def blocks(self, cc):
        c, y, x, z = self.place

        def block(yy, xx):
            return (2 * cc + yy) * 2 + xx

        return (block(y, x), block(y, 1 - x), block(1 - y, x), block(1 - y, 1 - x))

    def start(self, src, full):
        c, y, x, z = self.place
        self.full = full
        me = self.blocks(c)[0]
        self.from_x = self.go(src, full.at[me], device_at(c, y, 1 - x, z))
        self.from_y = self.go(src, full.at[me], device_at(c, 1 - y, x, z))
        self.from_core = [self.go(src, full.at[me], device_at(1 - c, y, x, z))]

    def relay(self):
        c, y, x, z = self.place
        full = self.full
        me, near_x, near_y, far = self.blocks(c)
        half = full.shape[1] // 2
        core = device_at(1 - c, y, x, z)
        upper, lower = pl.ds(0, half), pl.ds(half, half)
        self.from_x.wait_recv()
        second = self.go(
            full.at[near_x, lower], full.at[near_x, lower], device_at(c, 1 - y, x, z)
        )
        self.from_core.append(self.go(full.at[near_x], full.at[near_x], core))
        self.from_y.wait_recv()
        first = self.go(full.at[near_y, upper], full.at[near_y, upper], device_at(c, y, 1 - x, z))
        self.from_core.append(self.go(full.at[near_y], full.at[near_y], core))
        self.corner = (first, second)

    def relay_corner(self):
        c, y, x, z = self.place
        far = self.blocks(c)[3]
        for copy in self.corner:
            copy.wait_recv()
        self.from_core.append(
            self.go(self.full.at[far], self.full.at[far], device_at(1 - c, y, x, z))
        )

    def wait_core(self, index):
        self.from_core[index].wait_recv()

    def finish(self):
        for copy in self.sends:
            copy.wait_send()


def column_block(part, at):
    return pl.ds(pl.multiple_of(at, part), part)


def enter_kernel(
    hid,
    ints,
    vec,
    wm,
    unit_cos,
    unit_sin,
    row_cos,
    row_sin,
    hid_all,
    ints_all,
    vec_all,
    wm_all,
    heads,
    second,
    units,
    rotated,
    send,
    recv,
    local,
):
    place = place_here()
    c, y, x, z = place
    core = device_at(1 - c, y, x, z)
    over_x = device_at(c, y, 1 - x, z)
    over_y = device_at(c, 1 - y, x, z)
    lanes = wm_all.shape[2] // 3
    width = wm.shape[1] // 3
    tokens = hid.shape[0]
    own = 4 * y + 2 * x + c
    other = 4 * (1 - y) + 2 * x + c
    moved = []

    def keep(src, dst):
        copy = pltpu.make_async_copy(src, dst, local.at[len(moved)])
        copy.start()
        moved.append(copy)
        return copy

    me = (2 * c + y) * 2 + x
    own_block = keep(hid, hid_all.at[me])
    keep(ints, ints_all.at[2 * c + y])
    keep(vec, vec_all.at[y])
    for j in range(3):
        keep(
            wm.at[:, column_block(lanes, j * width + own * lanes)],
            wm_all.at[y, :, pl.ds(j * lanes, lanes)],
        )
    greet((core, over_x, over_y))
    tokens_move = TokenExchange(place, send, recv)
    go = tokens_move.go
    ints_y = go(ints, ints_all.at[2 * c + y], over_y)
    vec_y = go(vec, vec_all.at[y], over_y)
    ints_core = [go(ints, ints_all.at[2 * c + y], core)]
    tokens_move.start(hid, hid_all)
    weights = [
        go(
            wm.at[:, column_block(lanes, j * width + other * lanes)],
            wm_all.at[y, :, pl.ds(j * lanes, lanes)],
            over_y,
        )
        for j in range(3)
    ]
    ints_y.wait_recv()
    ints_core.append(go(ints_all.at[2 * c + 1 - y], ints_all.at[2 * c + 1 - y], core))
    vec_y.wait_recv()
    for copy in moved:
        copy.wait()
    for copy in ints_core:
        copy.wait_recv()
    to_units = pltpu.make_async_copy(ints_all, units, local.at[0])
    to_units.start()
    to_units.wait()

    def vector(row):
        return jnp.concatenate(
            [vec_all[h, row + i : row + i + 1, :] for h in range(2) for i in range(4)], axis=1
        )

    gain_one, shift_one, gain_two, shift_two = [vector(4 * i) for i in range(4)]
    bias = []
    for j in range(3):
        at = j * GROUP + own
        bias.append(vec_all[at // 12, pl.ds(16 + lax.rem(at, 12), 1), :])
    bias = jnp.concatenate(bias, axis=1)

    def normal(block):
        raw = hid_all[block].astype(jnp.float32)
        mean = jnp.mean(raw, axis=1, keepdims=True)
        centred = raw - mean
        rstd = lax.rsqrt(jnp.mean(centred * centred, axis=1, keepdims=True) + EPS)
        xhat = centred * rstd
        rows = pl.ds(pl.multiple_of(block * tokens, tokens), tokens)
        second[rows, :] = (xhat * gain_two + shift_two).astype(jnp.bfloat16)
        return (xhat * gain_one + shift_one).astype(jnp.bfloat16)

    unit_index = lax.broadcasted_iota(jnp.int32, unit_cos.shape, 0)
    lane = lax.rem(lax.broadcasted_iota(jnp.int32, row_cos.shape, 1), HEAD)

    def project(block):
        rows = pl.ds(pl.multiple_of(block * tokens, tokens), tokens)
        sequence, side = block // 2, lax.rem(block, 2)
        normed = normal(block)
        half = wm.shape[0]
        merged = (
            dot_plain(normed[:, :half], wm_all[0])
            + dot_plain(normed[:, half:], wm_all[1])
            + bias
        )
        count = tokens // UNIT
        for u in range(count):
            unit = units[sequence, 0, (2 * z + side) * count + u]
            here = pl.ds(u * UNIT, UNIT)
            chosen = unit_index == unit
            base_cos = jnp.sum(jnp.where(chosen, unit_cos[...], 0.0), axis=0, keepdims=True)
            base_sin = jnp.sum(jnp.where(chosen, unit_sin[...], 0.0), axis=0, keepdims=True)
            sine = base_sin * row_cos[...] + base_cos * row_sin[...]
            rotated[0, here, :] = base_cos * row_cos[...] - base_sin * row_sin[...]
            rotated[1, here, :] = jnp.where(lane < HALF, sine, 0.0)
            rotated[2, here, :] = jnp.where(lane < HALF, 0.0, sine)
        for j in range(2):
            values = merged[:, j * lanes : (j + 1) * lanes]
            turned = (
                values * rotated[0]
                - pltpu.roll(values, lanes - HALF, 1) * rotated[1]
                + pltpu.roll(values, HALF, 1) * rotated[2]
            )
            heads[j, rows, :] = turned.astype(jnp.bfloat16)
        heads[2, rows, :] = merged[:, 2 * lanes :].astype(jnp.bfloat16)

    tokens_move.relay()
    for copy in weights:
        copy.wait_recv()
    mine, theirs = tokens_move.blocks(c), tokens_move.blocks(1 - c)
    for index in range(3):
        project(mine[index])
    tokens_move.relay_corner()
    for index in range(3):
        tokens_move.wait_core(index)
        project(theirs[index])
    project(mine[3])
    tokens_move.wait_core(3)
    project(theirs[3])
    tokens_move.finish()


def enter(hid, ints, vec, wm, tables):
    tokens, width = hid.shape
    rows = wm.shape[0]
    lanes = width // GROUP
    vmem = pl.BlockSpec(memory_space=pltpu.VMEM)
    any_spec = pl.BlockSpec(memory_space=pl.ANY)
    return pl.pallas_call(
        enter_kernel,
        out_shape=(
            jax.ShapeDtypeStruct((GROUP,) + hid.shape, hid.dtype),
            jax.ShapeDtypeStruct((4,) + ints.shape, ints.dtype),
            jax.ShapeDtypeStruct((2,) + vec.shape, vec.dtype),
            jax.ShapeDtypeStruct((2, rows, 3 * lanes), wm.dtype),
            jax.ShapeDtypeStruct((3, GROUP * tokens, lanes), jnp.bfloat16),
            jax.ShapeDtypeStruct((GROUP * tokens, width), jnp.bfloat16),
        ),
        in_specs=[any_spec] * 4 + [vmem] * 4,
        out_specs=[vmem, any_spec, vmem, vmem, vmem, vmem],
        scratch_shapes=[
            pltpu.SMEM((4,) + ints.shape, jnp.int32),
            pltpu.VMEM((3, tokens, lanes), jnp.float32),
            pltpu.SemaphoreType.DMA((20,)),
            pltpu.SemaphoreType.DMA((20,)),
            pltpu.SemaphoreType.DMA((8,)),
        ],
        compiler_params=pltpu.CompilerParams(
            collective_id=0, has_side_effects=True, vmem_limit_bytes=48 << 20
        ),
        name="enter",
    )(hid, ints, vec, wm, *tables)


def greet_line(place, more=()):
    c, y, x, z = place
    barrier = pltpu.get_barrier_semaphore()
    partners = (device_at(1 - c, y, x, z), device_at(c, y, 1 - x, z), device_at(c, 1 - y, x, z))
    for partner in partners:
        pl.semaphore_signal(barrier, inc=1, device_id=partner, device_id_type=MESH)

    @pl.when(z > 0)
    def _():
        pl.semaphore_signal(barrier, inc=1, device_id=device_at(c, y, x, z - 1), device_id_type=MESH)

    @pl.when(z < LINE - 1)
    def _():
        pl.semaphore_signal(barrier, inc=1, device_id=device_at(c, y, x, z + 1), device_id_type=MESH)

    @pl.when((z > 0) & (z < LINE - 1))
    def _():
        pl.semaphore_wait(barrier, 5)

    @pl.when((z == 0) | (z == LINE - 1))
    def _():
        pl.semaphore_wait(barrier, 4)


TILE = 256


def feed_kernel(
    heads,
    second,
    cot,
    we,
    wo_src,
    wc_src,
    bias,
    got,
    cot_all,
    we_all,
    active,
    grad_expanded,
    feed_grad,
    sums,
    slope,
    grad_heads,
    wo,
    wc,
    send,
    recv,
    token_send,
    token_recv,
    local,
):
    place = place_here()
    c, y, x, z = place
    rows = got.shape[2]
    tokens = cot.shape[0]
    ff = we_all.shape[2]
    half = we.shape[0]
    own = 4 * y + 2 * x + c
    other = 4 * (1 - y) + 2 * x + c
    core = device_at(1 - c, y, x, z)
    over_x = device_at(c, y, 1 - x, z)
    over_y = device_at(c, 1 - y, x, z)
    peers = [lax.rem(z + d, LINE) for d in range(1, LINE)]
    mine = pl.ds(pl.multiple_of(z * rows, rows), rows)
    me = (2 * c + y) * 2 + x
    inner = 2 * x + c

    def rows_of(src, dst):
        count = dst.shape[0]
        return src.at[pl.ds(pl.multiple_of(inner * count, count), count)]

    keeps = [
        pltpu.make_async_copy(we.at[:, column_block(ff, own * ff)], we_all.at[y], local.at[0]),
        pltpu.make_async_copy(cot, cot_all.at[me], local.at[1]),
        pltpu.make_async_copy(rows_of(wo_src, wo), wo, local.at[2]),
        pltpu.make_async_copy(rows_of(wc_src, wc), wc, local.at[3]),
        pltpu.make_async_copy(heads.at[:, mine], got.at[pl.ds(0, 3), z], local.at[4]),
    ]
    for copy in keeps:
        copy.start()
    greet([device_at(c, y, x, peer) for peer in peers] + [core, over_x, over_y])
    tokens_move = TokenExchange(place, token_send, token_recv)
    weight = tokens_move.go(we.at[:, column_block(ff, other * ff)], we_all.at[y], over_y)
    tokens_move.start(cot, cot_all)
    copies = []
    for index, peer in enumerate(peers):
        copy = remote(
            heads.at[:, pl.ds(pl.multiple_of(peer * rows, rows), rows)],
            got.at[pl.ds(0, 3), z],
            send.at[0, index],
            recv.at[0, index],
            device_at(c, y, x, peer),
        )
        copy.start()
        copies.append(copy)
    for copy in keeps[:4]:
        copy.wait()
    weight.wait_recv()
    sums[...] = jnp.zeros_like(sums)

    def forward(index, carry):
        at = pl.ds(pl.multiple_of(index * TILE, TILE), TILE)
        normed = second[at, :]
        expanded = (
            dot_plain(normed[:, :half], we_all[0])
            + dot_plain(normed[:, half:], we_all[1])
            + bias[...]
        )
        below = 0.5 * (1.0 + lax.erf(expanded * math.sqrt(0.5)))
        density = jnp.exp(expanded * expanded * -0.5) * (1.0 / math.sqrt(2.0 * math.pi))
        active[at, :] = (expanded * below).astype(jnp.bfloat16)
        slope[at, :] = below + expanded * density
        return carry

    tiles = second.shape[0] // TILE
    lax.fori_loop(0, tiles // 2, forward, 0)
    tokens_move.relay()
    lax.fori_loop(tiles // 2, tiles, forward, 0)
    tokens_move.relay_corner()

    def backward(block):
        at = pl.ds(pl.multiple_of(block * tokens, tokens), tokens)
        cots = cot_all[block]
        grad_heads[at, :] = dot_rows(cots, wo[...]).astype(jnp.bfloat16)
        grad = (dot_rows(cots, wc[...]) * slope[at, :]).astype(jnp.bfloat16)
        grad_expanded[at, :] = grad
        sums[...] += jnp.sum(grad.astype(jnp.float32), axis=0, keepdims=True)

    ours, theirs = tokens_move.blocks(c), tokens_move.blocks(1 - c)
    for index in range(4):
        backward(ours[index])
    for index in range(4):
        tokens_move.wait_core(index)
        backward(theirs[index])
    for index, peer in enumerate(peers):
        copy = remote(
            grad_heads.at[pl.ds(pl.multiple_of(peer * rows, rows), rows)],
            got.at[3, z],
            send.at[1, index],
            recv.at[1, index],
            device_at(c, y, x, peer),
        )
        copy.start()
        copies.append(copy)
    last = pltpu.make_async_copy(grad_heads.at[mine], got.at[3, z], local.at[0])
    last.start()
    for index in range(2 * half // TILE):
        block = dot_tokens(second[:, pl.ds(index * TILE, TILE)], grad_expanded[...])
        side, row = divmod(index * TILE, half)
        feed_grad[pl.ds(row, TILE), pl.ds(side * ff, ff)] = block.astype(jnp.bfloat16)
    cots = cot_all[...].reshape(GROUP * tokens, 2 * half)
    for index in range(ff // TILE):
        block = dot_tokens(active[:, pl.ds(index * TILE, TILE)], cots)
        feed_grad[pl.ds(index * TILE, TILE), pl.ds(2 * ff, 2 * half)] = block.astype(jnp.bfloat16)
    keeps[4].wait()
    last.wait()
    for copy in copies:
        copy.wait()
    tokens_move.finish()


def feed_forward(heads, second, cot, we, wo, wc, bias):
    rows, width = second.shape
    ff = we.shape[1] // GROUP
    lanes = heads.shape[2]
    vmem = pl.BlockSpec(memory_space=pltpu.VMEM)
    any_spec = pl.BlockSpec(memory_space=pl.ANY)
    return pl.pallas_call(
        feed_kernel,
        out_shape=(
            jax.ShapeDtypeStruct((4, LINE, rows // LINE, lanes), heads.dtype),
            jax.ShapeDtypeStruct((GROUP,) + cot.shape, cot.dtype),
            jax.ShapeDtypeStruct((2, we.shape[0], ff), we.dtype),
            jax.ShapeDtypeStruct((rows, ff), jnp.bfloat16),
            jax.ShapeDtypeStruct((rows, ff), jnp.bfloat16),
            jax.ShapeDtypeStruct((width // 2, 2 * ff + width), jnp.bfloat16),
            jax.ShapeDtypeStruct((1, ff), jnp.float32),
        ),
        in_specs=[any_spec, vmem] + [any_spec] * 4 + [vmem],
        out_specs=[any_spec] + [vmem] * 6,
        scratch_shapes=[
            pltpu.VMEM((rows, ff), jnp.float32),
            pltpu.VMEM((rows, lanes), jnp.bfloat16),
            pltpu.VMEM((lanes, width), jnp.bfloat16),
            pltpu.VMEM((ff, width), jnp.bfloat16),
            pltpu.SemaphoreType.DMA((2, LINE - 1)),
            pltpu.SemaphoreType.DMA((2, LINE - 1)),
            pltpu.SemaphoreType.DMA((12,)),
            pltpu.SemaphoreType.DMA((12,)),
            pltpu.SemaphoreType.DMA((5,)),
        ],
        compiler_params=pltpu.CompilerParams(
            collective_id=1, has_side_effects=True, vmem_limit_bytes=56 << 20
        ),
        name="feed_forward",
    )(heads, second, cot, we, wo, wc, bias)


class LineSum:
    KINDS = 9

    def __init__(self, grad, result, inbox, sems, swap, size, lag, place):
        self.grad, self.result, self.inbox, self.sems, self.swap = grad, result, inbox, sems, swap
        self.c, self.y, self.x, self.z = place
        self.size = size
        self.count = grad.shape[0] // size
        self.split = (self.count + 1) // 2
        self.lag = lag
        self.slots = self.split + 6 * lag

    def rows(self, chunk):
        return pl.ds(pl.multiple_of(chunk * self.size, self.size), self.size)

    def moves(self, chunk, half):
        c, y, x, z = self.c, self.y, self.x, self.z
        up = 1 if half == 0 else -1
        rows = self.rows(chunk)
        grad, result, swap = self.grad, self.result, self.swap
        mine = result.at[c, x, rows]
        beside = result.at[c, 1 - x, rows]
        lower, upper = device_at(c, y, x, z - up), device_at(c, y, x, z + up)

        def lanes(which):
            return pl.ds(pl.multiple_of(which * swap, swap), swap)

        makers = {
            "near": (0, lambda: (grad.at[rows], self.inbox.at[0, rows], upper)),
            "far": (1, lambda: (grad.at[rows], self.inbox.at[1, rows], lower)),
            "swap": (
                2,
                lambda: (
                    grad.at[rows, lanes(1 - y)],
                    result.at[c, x, rows, lanes(y)],
                    device_at(c, 1 - y, x, z),
                ),
            ),
            "down": (3, lambda: (mine, mine, lower)),
            "out": (4, lambda: (mine, mine, upper)),
            "side": (5, lambda: (mine, mine, device_at(c, y, 1 - x, z))),
            "core": (6, lambda: (mine, mine, device_at(1 - c, y, x, z))),
            "late": (7, lambda: (beside, beside, device_at(1 - c, y, x, z))),
        }

        def make(name):
            kind, parts = makers[name]
            src, dst, target = parts()
            return remote(
                src, dst, self.sems.at[2 * kind, chunk], self.sems.at[2 * kind + 1, chunk], target
            )

        return make

    def keeps(self, chunk):
        rows, swap = self.rows(chunk), self.swap
        own = pl.ds(pl.multiple_of(self.y * swap, swap), swap)
        plain = pl.ds(2 * swap, self.grad.shape[1] - 2 * swap)
        return [
            pltpu.make_async_copy(
                self.grad.at[rows, lanes],
                self.result.at[self.c, self.x, rows, lanes],
                self.sems.at[2 * self.KINDS - 2 + index, chunk],
            )
            for index, lanes in enumerate((own, plain))
        ]

    def slot(self, t):
        for half in range(2):
            self.half_slot(t, half)

    def extent(self, half):
        size = self.split if half == 0 else self.count - self.split
        base = 0 if half == 0 else self.split
        at = self.z if half == 0 else LINE - 1 - self.z
        return (size, base, at)

    def half_slot(self, t, half):
        size, base, at = self.extent(half)
        lag = self.lag
        swap = self.swap
        owner = at == 1

        def event(delay, run):
            chunk = t - delay
            index = jnp.clip(chunk, 0, size - 1) + base

            @pl.when((chunk >= 0) & (chunk < size))
            def _():
                run(index, self.moves(index, half))

        def reduce(index, moves):
            rows = self.rows(index)

            @pl.when(at == 0)
            def _():
                moves("near").start()

            @pl.when(at == 2)
            def _():
                moves("far").wait_recv()
                total = self.grad[rows].astype(jnp.float32) + self.inbox[1, rows].astype(
                    jnp.float32
                )
                self.grad[rows] = total.astype(jnp.bfloat16)

            @pl.when(at >= 2)
            def _():
                moves("far").start()

            @pl.when(owner)
            def _():
                moves("near").wait_recv()
                moves("far").wait_recv()
                total = (
                    self.grad[rows].astype(jnp.float32)
                    + self.inbox[0, rows].astype(jnp.float32)
                    + self.inbox[1, rows].astype(jnp.float32)
                )
                self.grad[rows] = total.astype(jnp.bfloat16)
                moves("swap").start()
                for copy in self.keeps(index):
                    copy.start()

        event(jnp.where(owner, 2 * lag, jnp.where(at == 2, lag, 0)), reduce)

        def spread(index, moves):
            @pl.when(owner)
            def _():
                moves("swap").wait_recv()
                for copy in self.keeps(index):
                    copy.wait()
                moves("down").start()

            @pl.when(at == 0)
            def _():
                moves("down").wait_recv()

            @pl.when(at >= 2)
            def _():
                moves("out").wait_recv()

            @pl.when((at == 1) | (at == 2))
            def _():
                moves("out").start()

            moves("side").start()
            moves("core").start()

        wait = jnp.where(owner, 3 * lag, jnp.where(at == 3, 5 * lag, 4 * lag))
        event(wait, spread)

        def late(index, moves):
            moves("side").wait_recv()
            moves("late").start()

        event(wait + lag, late)

    def drain(self):
        for half in range(2):
            size, base, at = self.extent(half)

            def finish(chunk, carry):
                moves = self.moves(chunk + base, half)

                @pl.when(at == 0)
                def _():
                    moves("near").wait_send()

                @pl.when(at >= 2)
                def _():
                    moves("far").wait_send()

                @pl.when(at == 1)
                def _():
                    moves("swap").wait_send()
                    moves("down").wait_send()

                @pl.when((at == 1) | (at == 2))
                def _():
                    moves("out").wait_send()

                moves("side").wait_send()
                moves("core").wait()
                moves("late").wait()
                return carry

            lax.fori_loop(0, size, finish, 0)


def sort_kernel(order, src, dst, *, units):
    for unit in range(units):
        dst[:, order[0, unit]] = src[:, unit]


def sort_units(order, array, units):
    shape = array.shape
    vmem = pl.BlockSpec(memory_space=pltpu.VMEM)
    view = (shape[0], units, UNIT, shape[-1])
    return pl.pallas_call(
        functools.partial(sort_kernel, units=units),
        out_shape=jax.ShapeDtypeStruct(view, array.dtype),
        in_specs=[pl.BlockSpec(memory_space=pltpu.SMEM), vmem],
        out_specs=vmem,
        compiler_params=pltpu.CompilerParams(vmem_limit_bytes=16 << 20),
        name="sort_units",
    )(order, array.reshape(view))


def middle_kernel(
    ints,
    sorted_parts,
    unit_cos,
    unit_sin,
    row_cos,
    row_sin,
    feed_grad,
    active_src,
    grad_expanded_src,
    we_src,
    wc_src,
    wm_src,
    wo_src,
    hidden_src,
    cots_src,
    vectors,
    feed_sums,
    feed_all,
    attn_all,
    out_sum,
    term_sum,
    done,
    feed_own,
    feed_inbox,
    parts,
    attn_own,
    attn_inbox,
    near,
    beside,
    far,
    totals,
    send,
    recv,
    feed_sems,
    attn_sems,
    near_sems,
    beside_sems,
    far_sems,
    local,
    loads,
    *,
    units,
    pieces,
    feed_swap,
    swap,
):
    place = place_here()
    c, y, x, z = place
    core = device_at(1 - c, y, x, z)
    over_x = device_at(c, y, 1 - x, z)
    over_y = device_at(c, 1 - y, x, z)
    inner = 2 * x + c

    def rows_of(src, dst):
        count = dst.shape[0]
        return src.at[pl.ds(pl.multiple_of(inner * count, count), count)]

    first_load = pltpu.make_async_copy(feed_grad, feed_own, loads.at[8])
    first_load.start()
    peers = [lax.rem(z + d, LINE) for d in range(1, LINE)]
    greet([device_at(c, y, x, peer) for peer in peers] + [core, over_x, over_y])
    first_load.wait()
    line = LineSum(feed_own, feed_all, feed_inbox, feed_sems, feed_swap, FEED_CHUNK, 2, place)
    lanes = done.shape[2]
    rows = done.shape[1] // LINE
    mine = pl.ds(pl.multiple_of(z * rows, rows), rows)

    def gather(index, which):
        peer = peers[index]
        return remote(
            done.at[which, pl.ds(pl.multiple_of(peer * rows, rows), rows)],
            parts.at[mine, pl.ds(which * lanes, lanes)],
            send.at[index, which],
            recv.at[index, which],
            device_at(c, y, x, peer),
        )

    def gather_own(which):
        return pltpu.make_async_copy(
            done.at[which, mine], parts.at[mine, pl.ds(which * lanes, lanes)], local.at[which]
        )

    def attention_phase(
        masked, flat, scores, slopes, key_sum, value_sum, mixed_sum, query_sum
    ):
        length = sorted_parts.shape[1]
        scale = 1.0 / math.sqrt(HEAD)
        blocks = length // SPAN
        lanes = lax.broadcasted_iota(jnp.int32, (UNIT, 2 * HEAD), 1)
        lower = lanes < HEAD

        def arrange(index, carry):
            @pl.when(lax.rem(index, 8) == 0)
            def _():
                line.slot(lax.div(index, 8))

            at = pl.ds(pl.multiple_of(index * UNIT, UNIT), UNIT)
            for which in range(4):
                rows = sorted_parts[which, at, :].astype(jnp.float32)
                if which == 0:
                    rows = rows * scale
                masked[which, 0, at, :] = jnp.where(lower, rows, 0.0).astype(jnp.bfloat16)
                masked[which, 1, at, :] = jnp.where(lower, 0.0, rows).astype(jnp.bfloat16)
                flat[which, :, at] = rows.T.astype(jnp.bfloat16)
            return carry

        lax.fori_loop(0, units, arrange, 0)
        early = -(-units // 8)
        key_sum[...] = jnp.zeros_like(key_sum)
        value_sum[...] = jnp.zeros_like(value_sum)

        def labels(positions):
            found = jnp.full(positions.shape, -1, jnp.int32)
            for piece in range(pieces):
                start = ints[0, units + piece]
                found = jnp.where(
                    (positions >= start) & (positions < start + PIECE), piece, found
                )
            return found

        def dot(a, b):
            return jnp.dot(a, b, preferred_element_type=jnp.float32)

        for block in range(blocks):
            begin = block * SPAN
            last = SPAN + (UNIT if block + 1 < blocks else 0)
            columns = pl.ds(begin, SPAN)
            row_at = begin + lax.broadcasted_iota(jnp.int32, (1, SPAN), 1)
            col_at = begin + lax.broadcasted_iota(jnp.int32, (last, 1), 0)
            row_lab = labels(row_at)
            col_lab = labels(col_at)
            allowed = (col_at <= row_at) | (
                (col_lab == row_lab) & (row_lab >= 0)
            )

            def one_head(head, carry):
                start_tick = 3 * block * (block + 1) + head * 3 * (block + 1)

                def tick(index):
                    at = start_tick + index

                    @pl.when(lax.rem(at, EVERY) == 0)
                    def _():
                        line.slot(early + lax.div(at, EVERY))

                queries = flat[0, :, columns]
                grads = flat[3, :, columns]
                side = pl.ds(pl.multiple_of(head * HEAD, HEAD), HEAD)

                def score_tile(start, size, top, mask=None):
                    rows = pl.ds(start, size)
                    tile = dot(masked[1, head, rows, :], queries)
                    if mask is not None:
                        tile = jnp.where(mask, tile, NEGATIVE)
                    scores[rows, :] = tile
                    return jnp.maximum(top, jnp.max(tile, axis=0, keepdims=True))

                def tile_step(step, run, j, carry):
                    tick(step * (block + 1) + j)
                    start = pl.multiple_of(j * SPAN, SPAN)
                    return run(start, SPAN, carry)

                top = lax.fori_loop(
                    0,
                    block,
                    functools.partial(tile_step, 0, score_tile),
                    jnp.full((1, SPAN), NEGATIVE, jnp.float32),
                )
                tick(block)
                top = score_tile(begin, last, top, allowed)

                def weight_tile(start, size, sums):
                    total, delta = sums
                    rows = pl.ds(start, size)
                    weights = jnp.exp(scores[rows, :] - top)
                    slope = dot(masked[2, head, rows, :], grads)
                    scores[rows, :] = weights
                    slopes[rows, :] = slope
                    return (
                        total + jnp.sum(weights, axis=0, keepdims=True),
                        delta + jnp.sum(weights * slope, axis=0, keepdims=True),
                    )

                zero = jnp.zeros((1, SPAN), jnp.float32)
                sums = lax.fori_loop(
                    0,
                    block,
                    functools.partial(tile_step, 1, weight_tile),
                    (zero, zero),
                )
                tick(2 * block + 1)
                total, delta = weight_tile(begin, last, sums)
                inverse = 1.0 / total
                delta = delta * inverse

                def grad_tile(start, size, sums):
                    mixed, query = sums
                    rows = pl.ds(start, size)
                    probs = scores[rows, :] * inverse
                    grad = (probs * (slopes[rows, :] - delta)).astype(jnp.bfloat16)
                    probs = probs.astype(jnp.bfloat16)
                    value_sum[rows, :] += dot(probs, masked[3, head, columns, :])
                    key_sum[rows, :] += dot(grad, masked[0, head, columns, :])
                    mixed = mixed + dot(flat[2, side, rows], probs)
                    query = query + dot(flat[1, side, rows], grad)
                    return (mixed, query)

                none = jnp.zeros((HEAD, SPAN), jnp.float32)
                sums = lax.fori_loop(
                    0,
                    block,
                    functools.partial(tile_step, 2, grad_tile),
                    (none, none),
                )
                tick(3 * block + 2)
                mixed, query = grad_tile(begin, last, sums)
                mixed_sum[side, columns] = mixed
                query_sum[side, columns] = query * scale
                return carry

            lax.fori_loop(0, 2, one_head, 0)

        lane = lax.rem(lax.broadcasted_iota(jnp.int32, row_cos.shape, 1), HEAD)
        ticked = early - (-3 * blocks * (blocks + 1) // EVERY)

        def finish(index, carry):
            @pl.when(lax.rem(index, 8) == 0)
            def _():
                line.slot(ticked + lax.div(index, 8))

            at = pl.ds(pl.multiple_of(index * UNIT, UNIT), UNIT)
            base_cos, base_sin = unit_cos[pl.ds(index, 1), :], unit_sin[pl.ds(index, 1), :]
            cosine = base_cos * row_cos[...] - base_sin * row_sin[...]
            sine = base_sin * row_cos[...] + base_cos * row_sin[...]
            sine_up = jnp.where(lane < HALF, sine, 0.0)
            sine_down = jnp.where(lane < HALF, 0.0, sine)

            def turn_back(rows):
                up = pltpu.roll(rows, 2 * HEAD - HALF, 1)
                down = pltpu.roll(rows, HALF, 1)
                return rows * cosine + up * sine_up - down * sine_down

            masked[0, 0, at, :] = mixed_sum[:, at].T.astype(jnp.bfloat16)
            masked[1, 0, at, :] = turn_back(query_sum[:, at].T).astype(jnp.bfloat16)
            masked[2, 0, at, :] = turn_back(key_sum[at, :]).astype(jnp.bfloat16)
            masked[3, 0, at, :] = value_sum[at, :].astype(jnp.bfloat16)
            return carry

        lax.fori_loop(0, units, finish, 0)
        ticked += -(-units // 8)

        def restore(owner):
            for index in range(units // LINE):
                unit = owner * (units // LINE) + index
                here = pl.ds(pl.multiple_of(unit * UNIT, UNIT), UNIT)
                place = ints[0, unit]
                for which in range(4):
                    rows = masked[which, 0, pl.ds(0, UNIT), :]
                    for other in range(1, units):
                        rows = jnp.where(
                            place == other, masked[which, 0, pl.ds(other * UNIT, UNIT), :], rows
                        )
                    done[which, here, :] = rows

        for index, peer in enumerate(peers):
            restore(peer)
            for which in (1, 2, 3, 0):
                gather(index, which).start()
        restore(z)
        for which in range(4):
            gather_own(which).start()


    length = sorted_parts.shape[1]
    ticked = (
        2 * -(-units // 8) - (-3 * (length // SPAN) * (length // SPAN + 1) // EVERY)
    )
    pl.run_scoped(
        attention_phase,
        pltpu.VMEM((4, 2, length, 2 * HEAD), jnp.bfloat16),
        pltpu.VMEM((4, 2 * HEAD, length), jnp.bfloat16),
        pltpu.VMEM((length, SPAN), jnp.float32),
        pltpu.VMEM((length, SPAN), jnp.float32),
        pltpu.VMEM((length, 2 * HEAD), jnp.float32),
        pltpu.VMEM((length, 2 * HEAD), jnp.float32),
        pltpu.VMEM((2 * HEAD, length), jnp.float32),
        pltpu.VMEM((2 * HEAD, length), jnp.float32),
    )

    def close_phase(
        stats, outs, terms, single, active, grad_expanded, we, wc, wm, wo, hidden, cots
    ):
        sources = (
            (hidden_src, hidden),
            (grad_expanded_src, grad_expanded),
            (we_src, we),
            (active_src, active),
            (rows_of(wc_src, wc), wc),
            (cots_src, cots),
            (wm_src, wm),
            (rows_of(wo_src, wo), wo),
        )
        fetched = []
        for index, (src, dst) in enumerate(sources):
            copy = pltpu.make_async_copy(src, dst, loads.at[index])
            copy.start()
            fetched.append(copy)
        gain_one, shift_one, gain_two = vectors[0:1, :], vectors[1:2, :], vectors[2:3, :]
        width = hidden.shape[1]
        half = width // 2
        totals[...] = jnp.zeros_like(totals)
        for copy in fetched:
            copy.wait()

        def before(index, carry):
            at = pl.ds(pl.multiple_of(index * TILE, TILE), TILE)
            raw = hidden[at, :].astype(jnp.float32)
            mean = jnp.mean(raw, axis=1, keepdims=True)
            centred = raw - mean
            rstd = lax.rsqrt(jnp.mean(centred * centred, axis=1, keepdims=True) + EPS)
            stats[0, at, :] = jnp.broadcast_to(mean, (TILE, stats.shape[2]))
            stats[1, at, :] = jnp.broadcast_to(rstd, (TILE, stats.shape[2]))
            xhat = centred * rstd
            grad_second = dot_rows(grad_expanded[at, :], we[...])
            terms[index] = (grad_second * gain_two).astype(jnp.bfloat16)
            outs[index] = dot_plain(active[at, :], wc[...]).astype(jnp.bfloat16)
            totals[2:3, :] += jnp.sum(grad_second * xhat, axis=0, keepdims=True)
            totals[3:4, :] += jnp.sum(grad_second, axis=0, keepdims=True)
            totals[4:5, :] += jnp.sum(cots[at, :].astype(jnp.float32), axis=0, keepdims=True)
            return carry

        tiles = hidden.shape[0] // TILE
        lax.fori_loop(0, tiles, before, 0)

        for which in range(4):
            gather_own(which).wait()
        for index in range(len(peers)):
            for which in range(4):
                gather(index, which).wait()

        arrays = (outs, terms)

        def block_at(cc, yy, xx):
            return (2 * cc + yy) * 2 + xx

        def to_core(a, yy, xx):
            block = block_at(1 - c, yy, xx)
            return remote(
                arrays[a].at[block],
                near.at[a, yy, xx],
                near_sems.at[0, a, yy, xx],
                near_sems.at[1, a, yy, xx],
                core,
            )

        ways = ((y, x, over_y, over_x), (x, y, over_x, over_y))

        def own_block(a, near_at, far_at):
            yy, xx = (near_at, far_at) if a == 0 else (far_at, near_at)
            return block_at(c, yy, xx)

        def hop_one(a, index):
            near_axis, far_axis, target, beyond = ways[a]
            return remote(
                arrays[a].at[own_block(a, 1 - near_axis, index)],
                beside.at[a, index],
                beside_sems.at[0, a, index],
                beside_sems.at[1, a, index],
                target,
            )

        def hop_two(a):
            return remote(
                single.at[a], far.at[a], far_sems.at[0, a], far_sems.at[1, a], ways[a][3]
            )

        def after(index):
            at = pl.ds(pl.multiple_of(index * TILE, TILE), TILE)
            grads = parts[at, pl.ds(lanes, 3 * lanes)]
            grad_first = dot_rows(grads, wm[...])
            xhat = (hidden[at, :].astype(jnp.float32) - stats[0, at, 0:1]) * stats[1, at, 0:1]
            hidden[at, :] = (xhat * gain_one + shift_one).astype(jnp.bfloat16)
            terms[index] = (terms[index].astype(jnp.float32) + grad_first * gain_one).astype(
                jnp.bfloat16
            )
            outs[index] = (
                outs[index].astype(jnp.float32) + dot_plain(parts[at, pl.ds(0, lanes)], wo[...])
            ).astype(jnp.bfloat16)
            totals[0:1, :] += jnp.sum(grad_first * xhat, axis=0, keepdims=True)
            totals[1:2, :] += jnp.sum(grad_first, axis=0, keepdims=True)
            totals[5:6, pl.ds(0, 3 * lanes)] += jnp.sum(
                grads.astype(jnp.float32), axis=0, keepdims=True
            )

        def others(step, carry):
            line.slot(ticked + step)
            yy, xx = lax.rem(1 - y + step // 2, 2), lax.rem(step, 2)
            after(block_at(1 - c, yy, xx))
            for a in range(2):
                to_core(a, yy, xx).start()
            return carry

        lax.fori_loop(0, 4, others, 0)

        def ours(step, carry):
            line.slot(ticked + 4 + step)
            yy, xx = lax.rem(1 - y + step // 2, 2), lax.rem(step, 2)
            after(block_at(c, yy, xx))
            for a in range(2):
                to_core(a, yy, xx).wait_recv()
                block = block_at(c, yy, xx)
                total = arrays[a][block].astype(jnp.float32) + near[a, yy, xx].astype(jnp.float32)
                arrays[a][block] = total.astype(jnp.bfloat16)
                near_at, far_at = (yy, xx) if a == 0 else (xx, yy)

                @pl.when(near_at != ways[a][0])
                def _():
                    hop_one(a, far_at).start()

            return carry

        lax.fori_loop(0, 4, ours, 0)
        later = ticked + 8
        for index in range(width // TILE):
            line.slot(later + index)
            block = dot_tokens(hidden[:, pl.ds(index * TILE, TILE)], parts[:, pl.ds(lanes, 3 * lanes)])
            side, row = divmod(index * TILE, half)
            attn_own[pl.ds(row, TILE), pl.ds(side * swap, swap)] = block.astype(jnp.bfloat16)
        block = dot_tokens(parts[:, pl.ds(0, lanes)], cots[...]).astype(jnp.bfloat16)
        wide = 2 * lanes
        for index in range(width // wide):
            attn_own[pl.ds(index * lanes, lanes), pl.ds(2 * swap, wide)] = block[
                :, index * wide : (index + 1) * wide
            ]
        lines = []
        fill = jnp.zeros((1, swap), jnp.float32)
        for index in range(5):
            for begin in range(0, width, swap):
                stop = min(begin + swap, width)
                entry = totals[index : index + 1, begin:stop]
                if stop - begin < swap:
                    entry = jnp.concatenate([entry, fill[:, : swap - (stop - begin)]], axis=1)
                lines.append(entry)
        lines.append(totals[5:6, 0:swap])
        ff = feed_sums.shape[1]
        for begin in range(0, ff, swap):
            stop = min(begin + swap, ff)
            entry = feed_sums[:, begin:stop]
            if stop - begin < swap:
                entry = jnp.concatenate([entry, fill[:, : swap - (stop - begin)]], axis=1)
            lines.append(entry)
        lines += [fill] * (attn_own.shape[0] - half - len(lines))
        small = jnp.concatenate(lines, axis=0).astype(jnp.bfloat16)
        tail = pl.ds(half, attn_own.shape[0] - half)
        attn_own[tail, pl.ds(0, swap)] = small
        attn_own[tail, pl.ds(swap, swap)] = small
        attn_own[tail, pl.ds(2 * swap, wide)] = jnp.zeros((small.shape[0], wide), jnp.bfloat16)

        attn = LineSum(attn_own, attn_all, attn_inbox, attn_sems, swap, CHUNK, 1, place)

        later += width // TILE

        def step(t, carry):
            attn.slot(t)
            line.slot(later + t)
            return carry

        def pass_on(a):
            near_axis, far_axis = ways[a][:2]
            for index in range(2):
                hop_one(a, index).wait()
            single[a] = (
                arrays[a][own_block(a, near_axis, 1 - far_axis)].astype(jnp.float32)
                + beside[a, 1 - far_axis].astype(jnp.float32)
            ).astype(jnp.bfloat16)
            hop_two(a).start()

        middle = attn.slots - 6
        lax.fori_loop(0, middle, step, 0)
        pass_on(0)
        pass_on(1)
        lax.fori_loop(middle, attn.slots, step, 0)
        for a, dst in enumerate((out_sum, term_sum)):
            hop_two(a).wait()
            near_axis, far_axis = ways[a][:2]
            dst[...] = (
                arrays[a][own_block(a, near_axis, far_axis)].astype(jnp.float32)
                + beside[a, far_axis].astype(jnp.float32)
                + far[a].astype(jnp.float32)
            )

        def sent(step, carry):
            for a in range(2):
                to_core(a, step // 2, lax.rem(step, 2)).wait_send()
            return carry

        lax.fori_loop(0, 4, sent, 0)
        attn.drain()
        line.drain()

    token_rows, width = hidden_src.shape
    ff = active_src.shape[1]
    block = (token_rows // GROUP, width)
    pl.run_scoped(
        close_phase,
        pltpu.VMEM((2, token_rows, 128), jnp.float32),
        pltpu.VMEM((GROUP,) + block, jnp.bfloat16),
        pltpu.VMEM((GROUP,) + block, jnp.bfloat16),
        pltpu.VMEM((2,) + block, jnp.bfloat16),
        pltpu.VMEM((token_rows, ff), jnp.bfloat16),
        pltpu.VMEM((token_rows, ff), jnp.bfloat16),
        pltpu.VMEM((width, ff), jnp.bfloat16),
        pltpu.VMEM((ff, width), jnp.bfloat16),
        pltpu.VMEM((width, 3 * lanes), jnp.bfloat16),
        pltpu.VMEM((lanes, width), jnp.bfloat16),
        pltpu.VMEM((token_rows, width), jnp.bfloat16),
        pltpu.VMEM((token_rows, width), jnp.bfloat16),
    )


def middle(
    ints,
    sorted_parts,
    tables,
    feed_grad,
    active,
    grad_expanded,
    we,
    wc,
    wm,
    wo,
    hidden,
    cots,
    vectors,
    feed_sums,
    tokens,
    units,
    pieces,
    feed_swap,
):
    rows, width = hidden.shape
    lanes = sorted_parts.shape[2]
    swap = 3 * lanes
    block = (tokens, width)
    vmem = pl.BlockSpec(memory_space=pltpu.VMEM)
    any_spec = pl.BlockSpec(memory_space=pl.ANY)
    grad_shape = (width // 2 + CHUNK, 2 * swap + 2 * lanes)
    scratch = [
        pltpu.VMEM(sorted_parts.shape, jnp.bfloat16),
        pltpu.VMEM(feed_grad.shape, jnp.bfloat16),
        pltpu.VMEM((2,) + feed_grad.shape, jnp.bfloat16),
        pltpu.VMEM((rows, 4 * lanes), jnp.bfloat16),
        pltpu.VMEM(grad_shape, jnp.bfloat16),
        pltpu.VMEM((2,) + grad_shape, jnp.bfloat16),
        pltpu.VMEM((2, 2, 2) + block, jnp.bfloat16),
        pltpu.VMEM((2, 2) + block, jnp.bfloat16),
        pltpu.VMEM((2,) + block, jnp.bfloat16),
        pltpu.VMEM((8, width), jnp.float32),
        pltpu.SemaphoreType.DMA((LINE - 1, 4)),
        pltpu.SemaphoreType.DMA((LINE - 1, 4)),
        pltpu.SemaphoreType.DMA((2 * LineSum.KINDS, feed_grad.shape[0] // FEED_CHUNK)),
        pltpu.SemaphoreType.DMA((2 * LineSum.KINDS, grad_shape[0] // CHUNK)),
        pltpu.SemaphoreType.DMA((2, 2, 2, 2)),
        pltpu.SemaphoreType.DMA((2, 2, 2)),
        pltpu.SemaphoreType.DMA((2, 2)),
        pltpu.SemaphoreType.DMA((4,)),
        pltpu.SemaphoreType.DMA((9,)),
    ]
    return pl.pallas_call(
        functools.partial(
            middle_kernel, units=units, pieces=pieces, feed_swap=feed_swap, swap=swap
        ),
        out_shape=(
            jax.ShapeDtypeStruct((2, 2) + feed_grad.shape, jnp.bfloat16),
            jax.ShapeDtypeStruct((2, 2) + grad_shape, jnp.bfloat16),
            jax.ShapeDtypeStruct(block, jnp.float32),
            jax.ShapeDtypeStruct(block, jnp.float32),
        ),
        in_specs=[pl.BlockSpec(memory_space=pltpu.SMEM)]
        + [vmem] * 5
        + [any_spec] * 9
        + [vmem] * 2,
        out_specs=[any_spec] + [vmem] * 3,
        scratch_shapes=scratch,
        compiler_params=pltpu.CompilerParams(
            collective_id=3, has_side_effects=True, vmem_limit_bytes=60 << 20
        ),
        name="middle",
    )(
        ints,
        sorted_parts,
        *tables,
        feed_grad,
        active,
        grad_expanded,
        we,
        wc,
        wm,
        wo,
        hidden,
        cots,
        vectors,
        feed_sums,
    )


def widen_kernel(
    feed_all,
    attn_all,
    expand,
    contract,
    merged,
    output,
    feed,
    attn,
    expand_wide,
    contract_wide,
    merged_wide,
    output_wide,
    loads,
    stores,
    *,
    swap,
    lanes,
    ff,
):
    half = feed.shape[2]
    gets = []
    for index, (src, dst) in enumerate(((feed_all, feed), (attn_all, attn))):
        for part in range(4):
            copy = pltpu.make_async_copy(
                src.at[part // 2, part % 2], dst.at[part // 2, part % 2], loads.at[index, part]
            )
            copy.start()
            gets.append(copy)
    puts = []

    def put(src, dst):
        copy = pltpu.make_async_copy(src, dst, stores.at[len(puts)])
        copy.start()
        puts.append(copy)

    for part in range(4):
        c, x = part // 2, part % 2
        gets[part].wait()
        for y in range(2):
            at = pl.ds((4 * y + 2 * x + c) * ff, ff)
            expand_wide[:, at] = feed[c, x, :, pl.ds(y * ff, ff)].astype(jnp.float32)
            put(expand_wide.at[:, at], expand.at[:, at])
        at = pl.ds((2 * x + c) * ff, ff)
        contract_wide[at, :] = feed[c, x, :, pl.ds(2 * ff, 2 * half)].astype(jnp.float32)
        put(contract_wide.at[at], contract.at[at])
    for copy in gets[4:]:
        copy.wait()
    width = 2 * half
    for j in range(3):
        for octant in range(GROUP):
            c, x, y = octant % 2, octant // 2 % 2, octant // 4
            at = pl.ds(j * width + octant * lanes, lanes)
            merged_wide[:, at] = attn[
                c, x, pl.ds(0, half), pl.ds(y * swap + j * lanes, lanes)
            ].astype(jnp.float32)
        at = pl.ds(j * width, width)
        put(merged_wide.at[:, at], merged.at[:, at])
    for part in range(4):
        c, x = part % 2, part // 2
        for index in range(half // lanes):
            output_wide[pl.ds(part * lanes, lanes), pl.ds(2 * lanes * index, 2 * lanes)] = attn[
                c, x, pl.ds(index * lanes, lanes), pl.ds(2 * swap, 2 * lanes)
            ].astype(jnp.float32)
    put(output_wide, output)
    for copy in puts:
        copy.wait()


def widen(feed_all, attn_all, swap, lanes, ff):
    half = feed_all.shape[2]
    width = 2 * half
    shapes = ((half, GROUP * ff), (4 * ff, width), (half, 3 * width), (4 * lanes, width))
    any_spec = pl.BlockSpec(memory_space=pl.ANY)
    return pl.pallas_call(
        functools.partial(widen_kernel, swap=swap, lanes=lanes, ff=ff),
        out_shape=tuple(jax.ShapeDtypeStruct(shape, jnp.float32) for shape in shapes),
        in_specs=[any_spec] * 2,
        out_specs=[any_spec] * 4,
        scratch_shapes=[
            pltpu.VMEM(feed_all.shape, jnp.bfloat16),
            pltpu.VMEM(attn_all.shape, jnp.bfloat16),
        ]
        + [pltpu.VMEM(shape, jnp.float32) for shape in shapes]
        + [pltpu.SemaphoreType.DMA((2, 4)), pltpu.SemaphoreType.DMA((16,))],
        compiler_params=pltpu.CompilerParams(vmem_limit_bytes=48 << 20),
        name="widen",
    )(feed_all, attn_all)


def turn_tables(positions, lanes):
    lane = jnp.arange(lanes, dtype=jnp.int32) % HEAD
    inverse = jnp.exp((lane % HALF).astype(jnp.float32) * (-2.0 * math.log(10000.0) / ROT))
    angles = positions.astype(jnp.float32)[:, None] * inverse[None, :]
    turned = lane[None, :] < ROT
    return (jnp.where(turned, jnp.cos(angles), 1.0), jnp.where(turned, jnp.sin(angles), 0.0))


def group_body(
    hidden_states,
    unit_order,
    piece_starts,
    first_gain,
    first_shift,
    second_gain,
    second_shift,
    merged_weight,
    merged_bias,
    output_weight,
    output_bias,
    expand_weight,
    expand_bias,
    contract_weight,
    contract_bias,
    out_cotangent,
):
    c, y, x, z = place_here()
    tokens, width = hidden_states.shape[1:]
    length = tokens * 2 * LINE
    units = unit_order.shape[1]
    pieces = piece_starts.shape[1]
    rows = GROUP * tokens
    part = width // GROUP
    ff_part = expand_weight.shape[1] // GROUP
    half = width // 2
    vectors = (
        first_gain,
        first_shift,
        second_gain,
        second_shift,
        merged_bias,
        output_bias,
        expand_bias,
        contract_bias,
    )
    sizes = [v.shape[0] for v in vectors]
    packed = jnp.concatenate([v.astype(jnp.float32).reshape(-1, 128) for v in vectors])
    ints = jnp.concatenate([unit_order[0], piece_starts[0]])
    ints = jnp.broadcast_to(jnp.pad(ints, (0, 128 - ints.shape[0]))[None], (8, 128))
    tables = turn_tables(jnp.arange(units, dtype=jnp.int32) * UNIT, part) + turn_tables(
        jnp.arange(UNIT, dtype=jnp.int32), part
    )
    hid_all, ints_all, vec_all, wm_all, heads, second = enter(
        hidden_states[0], ints, packed, merged_weight, tables
    )
    inner = 2 * x + c
    own_expand = lax.dynamic_slice_in_dim(expand_bias, inner * ff_part, ff_part, 0)
    got, cot_all, we_all, active, grad_expanded, feed_grad, feed_sums = feed_forward(
        heads,
        second,
        out_cotangent[0],
        expand_weight,
        output_weight,
        contract_weight,
        own_expand.astype(jnp.float32)[None],
    )
    vec_all = vec_all.reshape(2, -1)
    whole = []
    at = 0
    for size in sizes:
        whole.append(vec_all[:, at : at + size].reshape(-1))
        at += size
    gain_one, shift_one, gain_two, shift_two, bias_merged, bias_out, bias_expand, bias_contract = whole
    wm = wm_all.reshape(width, 3 * part)
    we = we_all.reshape(width, ff_part)
    cots = cot_all.reshape(rows, width)
    own_ints = lax.dynamic_index_in_dim(ints_all[:, 0], z, 0, keepdims=True)
    sorted_parts = sort_units(own_ints, got, units)
    swap = 3 * part
    lines = CHUNK
    feed_all, attn_all, out_sum, term_sum = middle(
        own_ints,
        sorted_parts.reshape(4, length, part),
        tables,
        feed_grad,
        active,
        grad_expanded,
        we,
        contract_weight,
        wm,
        output_weight,
        hid_all.reshape(rows, width),
        cots,
        jnp.stack([gain_one, shift_one, gain_two]),
        feed_sums,
        tokens,
        units,
        pieces,
        ff_part,
    )
    expand_out, contract_out, merged_out, output_out = widen(
        feed_all, attn_all, swap, part, ff_part
    )
    own_hidden = hidden_states[0].astype(jnp.float32)
    own_mean = jnp.mean(own_hidden, axis=1, keepdims=True)
    own_centred = own_hidden - own_mean
    own_rstd = lax.rsqrt(jnp.mean(own_centred * own_centred, axis=1, keepdims=True) + EPS)
    own_xhat = own_centred * own_rstd
    output = (own_hidden + out_sum + bias_out + bias_contract).astype(jnp.bfloat16)
    upstream = out_cotangent[0].astype(jnp.float32)
    input_gradient = upstream + own_rstd * (
        term_sum
        - jnp.mean(term_sum, axis=1, keepdims=True)
        - own_xhat * jnp.mean(term_sum * own_xhat, axis=1, keepdims=True)
    )

    sums = attn_all[:, :, half : half + lines, : 2 * swap].astype(jnp.float32)
    sums = sums.reshape(2, 2, lines, 2, swap).transpose(3, 1, 0, 2, 4).reshape(GROUP, lines, swap)
    per = -(-width // swap)
    shared = jnp.sum(sums[:, : 4 * per], axis=0).reshape(4, per * swap)[:, :width]
    row_total = sums[0, 4 * per : 5 * per].reshape(-1)[:width]
    merged_sums = sums[:, 5 * per].reshape(GROUP, 3, part).transpose(1, 0, 2).reshape(-1)
    expand_sums = sums[:, 5 * per + 1 : 5 * per + 1 - (-ff_part // swap)]
    expand_sums = expand_sums.reshape(GROUP, -1)[:, :ff_part].reshape(-1)

    def own_half(vector):
        size = vector.shape[0] // 2
        return lax.dynamic_slice_in_dim(vector, y * size, size, 0)

    row_total = own_half(row_total)
    return (
        output[None],
        input_gradient[None],
        own_half(shared[0]),
        own_half(shared[1]),
        own_half(shared[2]),
        own_half(shared[3]),
        merged_out,
        own_half(merged_sums),
        output_out,
        row_total,
        expand_out,
        own_half(expand_sums),
        contract_out,
        row_total,
    )


def fits_groups(mesh, args):
    hidden, order = args[0], args[1]
    count = mesh.shape["seq"]
    tokens = hidden.shape[1] // count
    return (
        mesh.shape["rep"] == 2
        and mesh.shape["fsdp"] == 2
        and count == 2 * LINE
        and hidden.shape[0] == LINE
        and hidden.shape[2] == GROUP * 2 * HEAD
        and tokens % UNIT == 0
        and hidden.shape[1] % SPAN == 0
        and order.shape[1] + args[2].shape[1] <= 128
    )


def solution(mesh):
    in_specs = (
        P(("rep", "fsdp"), "seq", None),
        P(("rep", "fsdp"), None),
        P(("rep", "fsdp"), None),
        P("fsdp"),
        P("fsdp"),
        P("fsdp"),
        P("fsdp"),
        P("fsdp", None),
        P("fsdp"),
        P("fsdp", None),
        P("fsdp"),
        P("fsdp", None),
        P("fsdp"),
        P("fsdp", None),
        P("fsdp"),
        P(("rep", "fsdp"), "seq", None),
    )
    out_specs = (
        P(("rep", "fsdp"), "seq", None),
        P(("rep", "fsdp"), "seq", None),
        P("fsdp"),
        P("fsdp"),
        P("fsdp"),
        P("fsdp"),
        P("fsdp", None),
        P("fsdp"),
        P("fsdp", None),
        P("fsdp"),
        P("fsdp", None),
        P("fsdp"),
        P("fsdp", None),
        P("fsdp"),
    )

    def run(*args):
        chosen = group_body if fits_groups(mesh, args) else body
        mapped = jax.shard_map(
            chosen, mesh=mesh, in_specs=in_specs, out_specs=out_specs, check_vma=False
        )
        return mapped(*args)

    return run
```

```python
import functools
import math

import jax
import jax.numpy as jnp
from jax import lax
from jax.experimental import pallas as pl
from jax.experimental.pallas import tpu as pltpu
from jax.sharding import PartitionSpec as P

HEAD = 64
ROT = 16
UNIT = 128
PIECE = 256


EPS = 1e-05
NEGATIVE = -1e30


def norm_rows(values, gain, shift):
    mean = jnp.mean(values, axis=-1, keepdims=True)
    centred = values - mean
    spread = jnp.mean(centred * centred, axis=-1, keepdims=True)
    return centred * lax.rsqrt(spread + EPS) * gain + shift


def gelu_exact(values):
    return jax.nn.gelu(values, approximate=False)


def rotary_tables(positions):
    index = jnp.arange(ROT // 2, dtype=jnp.float32)
    inverse = jnp.exp(index * (-2.0 * math.log(10000.0) / ROT))
    angles = positions.astype(jnp.float32)[:, None] * inverse[None, :]
    angles = jnp.concatenate([angles, angles], axis=1)
    return (jnp.cos(angles), jnp.sin(angles))


def rotate(values, cosine, sine):
    part = values[..., :ROT]
    turned = jnp.concatenate([-part[..., ROT // 2 :], part[..., : ROT // 2]], axis=-1)
    moved = part * cosine[:, None, :] + turned * sine[:, None, :]
    return jnp.concatenate([moved, values[..., ROT:]], axis=-1)


def unit_positions(order):
    offsets = jnp.arange(UNIT, dtype=jnp.int32)
    return (order[:, None] * UNIT + offsets[None, :]).reshape(-1)


def piece_labels(positions, starts):
    inside = (positions[:, None] >= starts[None, :]) & (
        positions[:, None] < starts[None, :] + PIECE
    )
    labels = jnp.arange(1, starts.shape[0] + 1, dtype=jnp.int32)
    return jnp.sum(jnp.where(inside, labels[None, :], 0), axis=1) - 1


def visible(row_pos, row_lab, col_pos, col_lab):
    earlier = col_pos[None, :] <= row_pos[:, None]
    same = (row_lab[:, None] == col_lab[None, :]) & (row_lab[:, None] >= 0)
    return earlier | same


def merged_parts(first, merged_weight, merged_bias, cosine, sine):
    tokens = first.shape[0]
    width = first.shape[1]
    heads = width // HEAD
    merged = jnp.dot(first, merged_weight, preferred_element_type=jnp.float32) + merged_bias.astype(
        jnp.float32
    )
    queries = rotate(merged[:, :width].reshape(tokens, heads, HEAD), cosine, sine).astype(
        jnp.bfloat16
    )
    keys = rotate(merged[:, width : 2 * width].reshape(tokens, heads, HEAD), cosine, sine)
    keys = keys.reshape(tokens, width).astype(jnp.bfloat16)
    values = merged[:, 2 * width :].astype(jnp.bfloat16)
    return (queries, keys, values)


def block_view(queries, keys_all, values_all, row_pos, row_lab, col_pos, col_lab, span):
    heads = queries.shape[1]
    scale = 1.0 / math.sqrt(HEAD)

    def view(index):
        start = index * span
        key_rows = lax.dynamic_slice_in_dim(keys_all, start, span, 0).reshape(span, heads, HEAD)
        value_rows = lax.dynamic_slice_in_dim(values_all, start, span, 0).reshape(span, heads, HEAD)
        scores = (
            jnp.einsum("thd,khd->htk", queries, key_rows, preferred_element_type=jnp.float32)
            * scale
        )
        allowed = visible(
            row_pos,
            row_lab,
            lax.dynamic_slice_in_dim(col_pos, start, span, 0),
            lax.dynamic_slice_in_dim(col_lab, start, span, 0),
        )[None]
        return (scores, allowed, key_rows, value_rows)

    return view


def log_sums(view, count, heads, tokens):

    def log_step(carry, index):
        top, total = carry
        scores, allowed, key_rows, value_rows = view(index)
        masked = jnp.where(allowed, scores, NEGATIVE)
        newer = jnp.maximum(top, jnp.max(masked, axis=-1))
        terms = jnp.where(allowed, jnp.exp(masked - newer[..., None]), 0.0)
        total = total * jnp.exp(top - newer) + jnp.sum(terms, axis=-1)
        return ((newer, total), None)

    begin = (
        jnp.full((heads, tokens), NEGATIVE, jnp.float32),
        jnp.zeros((heads, tokens), jnp.float32),
    )
    (top, total), unused = lax.scan(log_step, begin, jnp.arange(count, dtype=jnp.int32))
    return top + jnp.log(total)


def mix_values(view, count, logsum, heads, tokens, grad_rows):

    def mix_step(carry, index):
        mixed, delta = carry
        scores, allowed, key_rows, value_rows = view(index)
        weights = jnp.where(allowed, jnp.exp(scores - logsum[..., None]), 0.0)
        mixed = mixed + jnp.einsum(
            "htk,khd->thd",
            weights.astype(jnp.bfloat16),
            value_rows,
            preferred_element_type=jnp.float32,
        )
        if grad_rows is not None:
            slopes = jnp.einsum(
                "thd,khd->htk", grad_rows, value_rows, preferred_element_type=jnp.float32
            )
            delta = delta + jnp.sum(weights * slopes, axis=-1)
        return ((mixed, delta), None)

    begin = (jnp.zeros((tokens, heads, HEAD), jnp.float32), jnp.zeros((heads, tokens), jnp.float32))
    (mixed, delta), unused = lax.scan(mix_step, begin, jnp.arange(count, dtype=jnp.int32))
    return (mixed, delta)


def attend_back(view, count, logsum, delta, grad_rows, queries):
    scale = 1.0 / math.sqrt(HEAD)

    def attend_step(carry, index):
        scores, allowed, key_rows, value_rows = view(index)
        weights = jnp.where(allowed, jnp.exp(scores - logsum[..., None]), 0.0)
        slopes = jnp.einsum(
            "thd,khd->htk", grad_rows, value_rows, preferred_element_type=jnp.float32
        )
        grad_scores = (weights * (slopes - delta[..., None])).astype(jnp.bfloat16)
        carry = carry + jnp.einsum(
            "htk,khd->thd", grad_scores, key_rows, preferred_element_type=jnp.float32
        )
        key_grad = jnp.einsum(
            "htk,thd->khd", grad_scores, queries, preferred_element_type=jnp.float32
        )
        value_grad = jnp.einsum(
            "htk,thd->khd",
            weights.astype(jnp.bfloat16),
            grad_rows,
            preferred_element_type=jnp.float32,
        )
        span = key_rows.shape[0]
        joined = jnp.concatenate(
            [key_grad.reshape(span, -1) * scale, value_grad.reshape(span, -1)], axis=1
        )
        return (carry, joined)

    begin = jnp.zeros(queries.shape, jnp.float32)
    grad_query, parts = lax.scan(attend_step, begin, jnp.arange(count, dtype=jnp.int32))
    return (grad_query * scale, parts)


def body(
    hidden_states,
    unit_order,
    piece_starts,
    first_gain,
    first_shift,
    second_gain,
    second_shift,
    merged_weight,
    merged_bias,
    output_weight,
    output_bias,
    expand_weight,
    expand_bias,
    contract_weight,
    contract_bias,
    out_cotangent,
):
    shards = (
        first_gain,
        first_shift,
        second_gain,
        second_shift,
        merged_weight,
        merged_bias,
        output_weight,
        output_bias,
        expand_weight,
        expand_bias,
        contract_weight,
        contract_bias,
    )
    gathered = (
        lax.all_gather(shards[0], "fsdp", axis=0, tiled=True),
        lax.all_gather(shards[1], "fsdp", axis=0, tiled=True),
        lax.all_gather(shards[2], "fsdp", axis=0, tiled=True),
        lax.all_gather(shards[3], "fsdp", axis=0, tiled=True),
        lax.all_gather(shards[4], "fsdp", axis=0, tiled=True),
        lax.all_gather(shards[5], "fsdp", axis=0, tiled=True),
        lax.all_gather(shards[6], "fsdp", axis=0, tiled=True),
        lax.all_gather(shards[7], "fsdp", axis=0, tiled=True),
        lax.all_gather(shards[8], "fsdp", axis=0, tiled=True),
        lax.all_gather(shards[9], "fsdp", axis=0, tiled=True),
        lax.all_gather(shards[10], "fsdp", axis=0, tiled=True),
        lax.all_gather(shards[11], "fsdp", axis=0, tiled=True),
    )
    hidden = hidden_states[0].astype(jnp.float32)
    tokens = hidden.shape[0]
    width = hidden.shape[1]
    heads = width // HEAD
    length = tokens * lax.axis_size("seq")
    span = min(length, 512)
    count = length // span
    col_pos = unit_positions(unit_order[0])
    col_lab = piece_labels(col_pos, piece_starts[0])
    offset = lax.axis_index("seq") * tokens
    row_pos = lax.dynamic_slice_in_dim(col_pos, offset, tokens, 0)
    row_lab = lax.dynamic_slice_in_dim(col_lab, offset, tokens, 0)
    cosine, sine = rotary_tables(row_pos)
    first = norm_rows(
        hidden, gathered[0].astype(jnp.float32), gathered[1].astype(jnp.float32)
    ).astype(jnp.bfloat16)
    queries, keys, values = merged_parts(first, gathered[4], gathered[5], cosine, sine)
    keys_all, values_all = (
        lax.all_gather(keys, "seq", axis=0, tiled=True),
        lax.all_gather(values, "seq", axis=0, tiled=True),
    )
    view = block_view(queries, keys_all, values_all, row_pos, row_lab, col_pos, col_lab, span)
    logsum = log_sums(view, count, heads, tokens)
    mixed, unused = mix_values(view, count, logsum, heads, tokens, None)
    mixed = mixed.reshape(tokens, width).astype(jnp.bfloat16)
    attention = jnp.dot(mixed, gathered[6], preferred_element_type=jnp.float32) + gathered[
        7
    ].astype(jnp.float32)
    second = norm_rows(
        hidden, gathered[2].astype(jnp.float32), gathered[3].astype(jnp.float32)
    ).astype(jnp.bfloat16)
    expanded = jnp.dot(second, gathered[8], preferred_element_type=jnp.float32) + gathered[
        9
    ].astype(jnp.float32)
    active = gelu_exact(expanded).astype(jnp.bfloat16)
    feed = jnp.dot(active, gathered[10], preferred_element_type=jnp.float32) + gathered[11].astype(
        jnp.float32
    )
    output = (hidden + attention + feed).astype(jnp.bfloat16)
    weights = (
        lax.all_gather(shards[0], "fsdp", axis=0, tiled=True),
        lax.all_gather(shards[1], "fsdp", axis=0, tiled=True),
        lax.all_gather(shards[2], "fsdp", axis=0, tiled=True),
        lax.all_gather(shards[3], "fsdp", axis=0, tiled=True),
        lax.all_gather(shards[4], "fsdp", axis=0, tiled=True),
        lax.all_gather(shards[5], "fsdp", axis=0, tiled=True),
        lax.all_gather(shards[6], "fsdp", axis=0, tiled=True),
        lax.all_gather(shards[7], "fsdp", axis=0, tiled=True),
        lax.all_gather(shards[8], "fsdp", axis=0, tiled=True),
        lax.all_gather(shards[9], "fsdp", axis=0, tiled=True),
        lax.all_gather(shards[10], "fsdp", axis=0, tiled=True),
        lax.all_gather(shards[11], "fsdp", axis=0, tiled=True),
    )
    cotangent = out_cotangent[0]
    upstream = cotangent.astype(jnp.float32)
    normed_one, first_pull = jax.vjp(
        norm_rows, hidden, weights[0].astype(jnp.float32), weights[1].astype(jnp.float32)
    )
    first = normed_one.astype(jnp.bfloat16)
    queries, keys, values = merged_parts(first, weights[4], weights[5], cosine, sine)
    keys_back, values_back = (
        lax.all_gather(keys, "seq", axis=0, tiled=True),
        lax.all_gather(values, "seq", axis=0, tiled=True),
    )
    view = block_view(queries, keys_back, values_back, row_pos, row_lab, col_pos, col_lab, span)
    grad_mixed = jnp.einsum(
        "te,de->td", cotangent, weights[6], preferred_element_type=jnp.float32
    ).astype(jnp.bfloat16)
    grad_rows = grad_mixed.reshape(tokens, heads, HEAD)
    mixed, delta = mix_values(view, count, logsum, heads, tokens, grad_rows)
    mixed = mixed.reshape(tokens, width).astype(jnp.bfloat16)
    grad_query, parts = attend_back(view, count, logsum, delta, grad_rows, queries)
    term = parts.reshape(length, 2 * width)
    own_grads = lax.psum_scatter(
        term.astype(jnp.bfloat16), "seq", scatter_dimension=0, tiled=True
    ).astype(jnp.float32)
    normed_two, second_pull = jax.vjp(
        norm_rows, hidden, weights[2].astype(jnp.float32), weights[3].astype(jnp.float32)
    )
    second = normed_two.astype(jnp.bfloat16)
    expanded = jnp.dot(second, weights[8], preferred_element_type=jnp.float32) + weights[9].astype(
        jnp.float32
    )
    activated, gelu_pull = jax.vjp(gelu_exact, expanded)
    active = activated.astype(jnp.bfloat16)
    grad_active = jnp.einsum(
        "te,fe->tf", cotangent, weights[10], preferred_element_type=jnp.float32
    )
    grad_expanded = gelu_pull(grad_active)[0].astype(jnp.bfloat16)
    grad_second = jnp.einsum(
        "tf,df->td", grad_expanded, weights[8], preferred_element_type=jnp.float32
    )
    unused, turn_pull = jax.vjp(rotate, grad_query, cosine, sine)
    query_back = turn_pull(grad_query)[0].reshape(tokens, width)
    key_back = turn_pull(own_grads[:, :width].reshape(tokens, heads, HEAD))[0].reshape(
        tokens, width
    )
    grad_merged = jnp.concatenate([query_back, key_back, own_grads[:, width:]], axis=1).astype(
        jnp.bfloat16
    )
    grad_first = jnp.einsum(
        "tc,dc->td", grad_merged, weights[4], preferred_element_type=jnp.float32
    )
    first_term, first_gain_grad, first_shift_grad = first_pull(grad_first)
    second_term, second_gain_grad, second_shift_grad = second_pull(grad_second)
    input_gradient = upstream + first_term + second_term
    row_total = jnp.sum(upstream, axis=0)
    local_grads = (
        first_gain_grad,
        first_shift_grad,
        second_gain_grad,
        second_shift_grad,
        jnp.einsum("td,tc->dc", first, grad_merged, preferred_element_type=jnp.float32),
        jnp.sum(grad_merged.astype(jnp.float32), axis=0),
        jnp.einsum("td,te->de", mixed, cotangent, preferred_element_type=jnp.float32),
        row_total,
        jnp.einsum("td,tf->df", second, grad_expanded, preferred_element_type=jnp.float32),
        jnp.sum(grad_expanded.astype(jnp.float32), axis=0),
        jnp.einsum("tf,te->fe", active, cotangent, preferred_element_type=jnp.float32),
        row_total,
    )
    owned = (
        lax.psum_scatter(
            local_grads[0].astype(jnp.bfloat16), "fsdp", scatter_dimension=0, tiled=True
        ).astype(jnp.float32),
        lax.psum_scatter(
            local_grads[1].astype(jnp.bfloat16), "fsdp", scatter_dimension=0, tiled=True
        ).astype(jnp.float32),
        lax.psum_scatter(
            local_grads[2].astype(jnp.bfloat16), "fsdp", scatter_dimension=0, tiled=True
        ).astype(jnp.float32),
        lax.psum_scatter(
            local_grads[3].astype(jnp.bfloat16), "fsdp", scatter_dimension=0, tiled=True
        ).astype(jnp.float32),
        lax.psum_scatter(
            local_grads[4].astype(jnp.bfloat16), "fsdp", scatter_dimension=0, tiled=True
        ).astype(jnp.float32),
        lax.psum_scatter(
            local_grads[5].astype(jnp.bfloat16), "fsdp", scatter_dimension=0, tiled=True
        ).astype(jnp.float32),
        lax.psum_scatter(
            local_grads[6].astype(jnp.bfloat16), "fsdp", scatter_dimension=0, tiled=True
        ).astype(jnp.float32),
        lax.psum_scatter(
            local_grads[7].astype(jnp.bfloat16), "fsdp", scatter_dimension=0, tiled=True
        ).astype(jnp.float32),
        lax.psum_scatter(
            local_grads[8].astype(jnp.bfloat16), "fsdp", scatter_dimension=0, tiled=True
        ).astype(jnp.float32),
        lax.psum_scatter(
            local_grads[9].astype(jnp.bfloat16), "fsdp", scatter_dimension=0, tiled=True
        ).astype(jnp.float32),
        lax.psum_scatter(
            local_grads[10].astype(jnp.bfloat16), "fsdp", scatter_dimension=0, tiled=True
        ).astype(jnp.float32),
        lax.psum_scatter(
            local_grads[11].astype(jnp.bfloat16), "fsdp", scatter_dimension=0, tiled=True
        ).astype(jnp.float32),
    )
    summed = lax.psum(
        (
            owned[0],
            owned[1],
            owned[2],
            owned[3],
            owned[4],
            owned[5],
            owned[6],
            owned[7],
            owned[8],
            owned[9],
            owned[10],
            owned[11],
        ),
        ("rep", "seq"),
    )
    return (
        output[None],
        input_gradient[None],
        summed[0],
        summed[1],
        summed[2],
        summed[3],
        summed[4],
        summed[5],
        summed[6],
        summed[7],
        summed[8],
        summed[9],
        summed[10],
        summed[11],
    )


MESH = pl.DeviceIdType.MESH
GROUP = 8
LINE = 4
HALF = ROT // 2
SPAN = 512
CHUNK = 32
FEED_CHUNK = 16
EVERY = 4


def place_here():
    c, y, s = (lax.axis_index("rep"), lax.axis_index("fsdp"), lax.axis_index("seq"))
    x = lax.rem(s, 2)
    return (c, y, x, s // 2)


def device_at(c, y, x, z):
    return (c, y, 2 * z + x)


def greet(partners):
    barrier = pltpu.get_barrier_semaphore()
    for partner in partners:
        pl.semaphore_signal(barrier, inc=1, device_id=partner, device_id_type=MESH)
    pl.semaphore_wait(barrier, len(partners))


def remote(src, dst, send, recv, target):
    return pltpu.make_async_remote_copy(
        src_ref=src,
        dst_ref=dst,
        send_sem=send,
        recv_sem=recv,
        device_id=target,
        device_id_type=MESH,
    )


def dot_rows(a, b):
    return lax.dot_general(a, b, (((1,), (1,)), ((), ())), preferred_element_type=jnp.float32)


def dot_tokens(a, b):
    return lax.dot_general(a, b, (((0,), (0,)), ((), ())), preferred_element_type=jnp.float32)


def dot_plain(a, b):
    return jnp.dot(a, b, preferred_element_type=jnp.float32)


class TokenExchange:
    def __init__(self, place, send, recv):
        self.place, self.send, self.recv = place, send, recv
        self.count = 0
        self.sends = []

    def go(self, src, dst, target):
        copy = remote(src, dst, self.send.at[self.count], self.recv.at[self.count], target)
        self.count += 1
        copy.start()
        self.sends.append(copy)
        return copy

    def blocks(self, cc):
        c, y, x, z = self.place

        def block(yy, xx):
            return (2 * cc + yy) * 2 + xx

        return (block(y, x), block(y, 1 - x), block(1 - y, x), block(1 - y, 1 - x))

    def start_near(self, src, full):
        c, y, x, z = self.place
        self.full = full
        me = self.blocks(c)[0]
        self.from_x = self.go(src, full.at[me], device_at(c, y, 1 - x, z))
        self.from_core = [self.go(src, full.at[me], device_at(1 - c, y, x, z))]

    def start_far(self, src):
        c, y, x, z = self.place
        self.from_y = self.go(src, self.full.at[self.blocks(c)[0]], device_at(c, 1 - y, x, z))

    def relay_x(self):
        c, y, x, z = self.place
        full = self.full
        near_x = self.blocks(c)[1]
        lower = pl.ds(full.shape[1] - full.shape[1] // 4, full.shape[1] // 4)
        self.from_x.wait_recv()
        self.second = self.go(
            full.at[near_x, lower], full.at[near_x, lower], device_at(c, 1 - y, x, z)
        )
        self.from_core.append(
            self.go(full.at[near_x], full.at[near_x], device_at(1 - c, y, x, z))
        )

    def relay_y(self):
        c, y, x, z = self.place
        full = self.full
        near_y = self.blocks(c)[2]
        upper = pl.ds(0, full.shape[1] - full.shape[1] // 4)
        self.from_y.wait_recv()
        first = self.go(full.at[near_y, upper], full.at[near_y, upper], device_at(c, y, 1 - x, z))
        self.from_core.append(
            self.go(full.at[near_y], full.at[near_y], device_at(1 - c, y, x, z))
        )
        self.corner = (first, self.second)

    def relay_corner(self):
        c, y, x, z = self.place
        far = self.blocks(c)[3]
        for copy in self.corner:
            copy.wait_recv()
        self.from_core.append(
            self.go(self.full.at[far], self.full.at[far], device_at(1 - c, y, x, z))
        )

    def wait_core(self, index):
        self.from_core[index].wait_recv()

    def finish(self):
        for copy in self.sends:
            copy.wait_send()


def column_block(part, at):
    return pl.ds(pl.multiple_of(at, part), part)


TILE = 256


def front_kernel(
    hid,
    ints,
    vec,
    wm,
    unit_cos,
    unit_sin,
    row_cos,
    row_sin,
    cot,
    we,
    wo_src,
    wc_src,
    hid_all,
    ints_all,
    vec_all,
    wm_all,
    cot_all,
    we_all,
    got,
    active,
    grad_expanded,
    feed_grad,
    sums,
    second,
    heads,
    grad_heads,
    wo,
    wc,
    units,
    rotated,
    send,
    recv,
    cot_send,
    cot_recv,
    head_send,
    head_recv,
    local,
    head_local,
):
    place = place_here()
    c, y, x, z = place
    core = device_at(1 - c, y, x, z)
    over_x = device_at(c, y, 1 - x, z)
    over_y = device_at(c, 1 - y, x, z)
    lanes = wm_all.shape[2] // 3
    width = wm.shape[1] // 3
    half = wm.shape[0]
    ff = we_all.shape[2]
    tokens = hid.shape[0]
    inner = 2 * x + c
    own = 4 * y + inner
    other = 4 * (1 - y) + inner
    me = (2 * c + y) * 2 + x
    moved = []

    def keep(src, dst):
        copy = pltpu.make_async_copy(src, dst, local.at[len(moved)])
        copy.start()
        moved.append(copy)

    def rows_of(src, dst):
        count = dst.shape[0]
        return src.at[pl.ds(pl.multiple_of(inner * count, count), count)]

    keep(hid, hid_all.at[me])
    keep(ints, ints_all.at[2 * c + y])
    keep(vec, vec_all.at[y])
    for j in range(3):
        keep(
            wm.at[:, column_block(lanes, j * width + own * lanes)],
            wm_all.at[y, :, pl.ds(j * lanes, lanes)],
        )
    early = len(moved)
    keep(we.at[:, column_block(ff, own * ff)], we_all.at[y])
    keep(cot, cot_all.at[me])
    keep(rows_of(wo_src, wo), wo)
    keep(rows_of(wc_src, wc), wc)
    peers = [lax.rem(z + d, LINE) for d in range(1, LINE)]
    greet([device_at(c, y, x, peer) for peer in peers] + [core, over_x, over_y])
    tokens_move = TokenExchange(place, send, recv)
    go = tokens_move.go
    ints_y = go(ints, ints_all.at[2 * c + y], over_y)
    vec_y = go(vec, vec_all.at[y], over_y)
    ints_core = [go(ints, ints_all.at[2 * c + y], core)]
    tokens_move.start_near(hid, hid_all)
    tokens_move.start_far(hid)
    weights = [
        go(
            wm.at[:, column_block(lanes, j * width + other * lanes)],
            wm_all.at[y, :, pl.ds(j * lanes, lanes)],
            over_y,
        )
        for j in range(3)
    ]
    ints_y.wait_recv()
    ints_core.append(go(ints_all.at[2 * c + 1 - y], ints_all.at[2 * c + 1 - y], core))
    vec_y.wait_recv()
    for copy in moved[:early]:
        copy.wait()
    for copy in ints_core:
        copy.wait_recv()
    to_units = pltpu.make_async_copy(ints_all, units, local.at[0])
    to_units.start()
    to_units.wait()

    def vector(row):
        return jnp.concatenate(
            [vec_all[h, row + i : row + i + 1, :] for h in range(2) for i in range(4)], axis=1
        )

    gain_one, shift_one, gain_two, shift_two = [vector(4 * i) for i in range(4)]
    bias = []
    for j in range(3):
        at = j * GROUP + own
        bias.append(vec_all[at // 12, pl.ds(16 + lax.rem(at, 12), 1), :])
    bias = jnp.concatenate(bias, axis=1)
    expand_bias = jnp.concatenate(
        [vec_all[y, pl.ds(32 + 4 * inner + i, 1), :] for i in range(4)], axis=1
    )
    unit_index = lax.broadcasted_iota(jnp.int32, unit_cos.shape, 0)
    lane = lax.rem(lax.broadcasted_iota(jnp.int32, row_cos.shape, 1), HEAD)

    def project(block):
        rows = pl.ds(pl.multiple_of(block * tokens, tokens), tokens)
        sequence, side = block // 2, lax.rem(block, 2)
        raw = hid_all[block].astype(jnp.float32)
        mean = jnp.mean(raw, axis=1, keepdims=True)
        centred = raw - mean
        rstd = lax.rsqrt(jnp.mean(centred * centred, axis=1, keepdims=True) + EPS)
        xhat = centred * rstd
        second[rows, :] = (xhat * gain_two + shift_two).astype(jnp.bfloat16)
        normed = (xhat * gain_one + shift_one).astype(jnp.bfloat16)
        merged = (
            dot_plain(normed[:, :half], wm_all[0])
            + dot_plain(normed[:, half:], wm_all[1])
            + bias
        )
        count = tokens // UNIT
        for u in range(count):
            unit = units[sequence, 0, (2 * z + side) * count + u]
            here = pl.ds(u * UNIT, UNIT)
            chosen = unit_index == unit
            base_cos = jnp.sum(jnp.where(chosen, unit_cos[...], 0.0), axis=0, keepdims=True)
            base_sin = jnp.sum(jnp.where(chosen, unit_sin[...], 0.0), axis=0, keepdims=True)
            sine = base_sin * row_cos[...] + base_cos * row_sin[...]
            rotated[0, here, :] = base_cos * row_cos[...] - base_sin * row_sin[...]
            rotated[1, here, :] = jnp.where(lane < HALF, sine, 0.0)
            rotated[2, here, :] = jnp.where(lane < HALF, 0.0, sine)
        for j in range(2):
            values = merged[:, j * lanes : (j + 1) * lanes]
            turned = (
                values * rotated[0]
                - pltpu.roll(values, lanes - HALF, 1) * rotated[1]
                + pltpu.roll(values, HALF, 1) * rotated[2]
            )
            heads[j, rows, :] = turned.astype(jnp.bfloat16)
        heads[2, rows, :] = merged[:, 2 * lanes :].astype(jnp.bfloat16)

    span = got.shape[2]

    def rows_at(sequence):
        return pl.ds(pl.multiple_of(sequence * span, span), span)

    def head_copy(kind, sequence, sender):
        if kind == 0:
            src, dst = heads.at[:, rows_at(sequence)], got.at[pl.ds(0, 3), sender]
        else:
            src, dst = grad_heads.at[rows_at(sequence)], got.at[3, sender]
        return remote(
            src,
            dst,
            head_send.at[kind, sequence],
            head_recv.at[kind, sender],
            device_at(c, y, x, sequence),
        )

    def head_keep(kind):
        if kind == 0:
            src, dst = heads.at[:, rows_at(z)], got.at[pl.ds(0, 3), z]
        else:
            src, dst = grad_heads.at[rows_at(z)], got.at[3, z]
        return pltpu.make_async_copy(src, dst, head_local.at[kind])

    def send_heads(kind, sequence):
        @pl.when(sequence == z)
        def _():
            head_keep(kind).start()

        @pl.when(sequence != z)
        def _():
            head_copy(kind, sequence, z).start()

    tokens_move.relay_x()
    tokens_move.relay_y()
    cots_move = TokenExchange(place, cot_send, cot_recv)
    cots_move.start_near(cot, cot_all)
    cots_move.start_far(cot)
    weight = cots_move.go(we.at[:, column_block(ff, other * ff)], we_all.at[y], over_y)
    for copy in weights:
        copy.wait_recv()
    mine, theirs = tokens_move.blocks(c), tokens_move.blocks(1 - c)
    project(mine[0])
    project(mine[1])
    send_heads(0, mine[0] // 2)
    for index in range(2):
        tokens_move.wait_core(index)
        project(theirs[index])
    send_heads(0, theirs[0] // 2)
    project(mine[2])
    tokens_move.relay_corner()
    tokens_move.wait_core(2)
    project(theirs[2])
    project(mine[3])
    send_heads(0, mine[2] // 2)
    cots_move.relay_x()
    cots_move.relay_y()
    tokens_move.wait_core(3)
    project(theirs[3])
    send_heads(0, theirs[2] // 2)
    for copy in moved[early:]:
        copy.wait()
    sums[...] = jnp.zeros_like(sums)

    def project_back(block):
        at = pl.ds(pl.multiple_of(block * tokens, tokens), tokens)
        grad_heads[at, :] = dot_rows(cot_all[block], wo[...]).astype(jnp.bfloat16)

    def feed(block):
        at = pl.ds(pl.multiple_of(block * tokens, tokens), tokens)
        normed = second[at, :]
        expanded = (
            dot_plain(normed[:, :half], we_all[0])
            + dot_plain(normed[:, half:], we_all[1])
            + expand_bias
        )
        below = 0.5 * (1.0 + lax.erf(expanded * math.sqrt(0.5)))
        density = jnp.exp(expanded * expanded * -0.5) * (1.0 / math.sqrt(2.0 * math.pi))
        active[at, :] = (expanded * below).astype(jnp.bfloat16)
        grad_active = dot_rows(cot_all[block], wc[...])
        grad = (grad_active * (below + expanded * density)).astype(jnp.bfloat16)
        grad_expanded[at, :] = grad
        sums[...] += jnp.sum(grad.astype(jnp.float32), axis=0, keepdims=True)

    def feed_two(one, two):
        def body(index, carry):
            feed(one + index * (two - one))
            return carry

        lax.fori_loop(0, 2, body, 0)

    project_back(mine[0])
    project_back(mine[1])
    send_heads(1, mine[0] // 2)
    for index in range(2):
        cots_move.wait_core(index)
        project_back(theirs[index])
    send_heads(1, theirs[0] // 2)
    weight.wait_recv()
    feed_two(mine[0], mine[1])
    cots_move.relay_corner()
    project_back(mine[2])
    project_back(mine[3])
    send_heads(1, mine[2] // 2)
    cots_move.wait_core(2)
    project_back(theirs[2])
    cots_move.wait_core(3)
    project_back(theirs[3])
    send_heads(1, theirs[2] // 2)
    feed_two(theirs[0], theirs[1])
    feed_two(mine[2], theirs[2])
    feed_two(mine[3], theirs[3])
    for index in range(2 * half // TILE):
        block = dot_tokens(second[:, pl.ds(index * TILE, TILE)], grad_expanded[...])
        side, row = divmod(index * TILE, half)
        feed_grad[pl.ds(row, TILE), pl.ds(side * ff, ff)] = block.astype(jnp.bfloat16)
    cots = cot_all[...].reshape(GROUP * tokens, 2 * half)
    for index in range(ff // TILE):
        block = dot_tokens(active[:, pl.ds(index * TILE, TILE)], cots)
        feed_grad[pl.ds(index * TILE, TILE), pl.ds(2 * ff, 2 * half)] = block.astype(jnp.bfloat16)
    tokens_move.finish()
    cots_move.finish()
    for kind in range(2):
        head_keep(kind).wait()
        for peer in peers:
            head_copy(kind, peer, z).wait_send()
            head_copy(kind, peer, peer).wait_recv()


def front(hid, ints, vec, wm, tables, cot, we, wo, wc):
    tokens, width = hid.shape
    rows = wm.shape[0]
    lanes = width // GROUP
    ff = we.shape[1] // GROUP
    total = GROUP * tokens
    vmem = pl.BlockSpec(memory_space=pltpu.VMEM)
    any_spec = pl.BlockSpec(memory_space=pl.ANY)
    return pl.pallas_call(
        front_kernel,
        out_shape=(
            jax.ShapeDtypeStruct((GROUP,) + hid.shape, hid.dtype),
            jax.ShapeDtypeStruct((4,) + ints.shape, ints.dtype),
            jax.ShapeDtypeStruct((2,) + vec.shape, vec.dtype),
            jax.ShapeDtypeStruct((2, rows, 3 * lanes), wm.dtype),
            jax.ShapeDtypeStruct((GROUP,) + cot.shape, cot.dtype),
            jax.ShapeDtypeStruct((2, rows, ff), we.dtype),
            jax.ShapeDtypeStruct((4, LINE, total // LINE, lanes), jnp.bfloat16),
            jax.ShapeDtypeStruct((total, ff), jnp.bfloat16),
            jax.ShapeDtypeStruct((total, ff), jnp.bfloat16),
            jax.ShapeDtypeStruct((width // 2, 2 * ff + width), jnp.bfloat16),
            jax.ShapeDtypeStruct((1, ff), jnp.float32),
        ),
        in_specs=[any_spec] * 4 + [vmem] * 4 + [any_spec] * 4,
        out_specs=[vmem, any_spec, vmem, vmem, vmem, vmem, any_spec] + [vmem] * 4,
        scratch_shapes=[
            pltpu.VMEM((total, width), jnp.bfloat16),
            pltpu.VMEM((3, total, lanes), jnp.bfloat16),
            pltpu.VMEM((total, lanes), jnp.bfloat16),
            pltpu.VMEM((lanes, width), jnp.bfloat16),
            pltpu.VMEM((ff, width), jnp.bfloat16),
            pltpu.SMEM((4,) + ints.shape, jnp.int32),
            pltpu.VMEM((3, tokens, lanes), jnp.float32),
            pltpu.SemaphoreType.DMA((20,)),
            pltpu.SemaphoreType.DMA((20,)),
            pltpu.SemaphoreType.DMA((12,)),
            pltpu.SemaphoreType.DMA((12,)),
            pltpu.SemaphoreType.DMA((2, LINE)),
            pltpu.SemaphoreType.DMA((2, LINE)),
            pltpu.SemaphoreType.DMA((10,)),
            pltpu.SemaphoreType.DMA((2,)),
        ],
        compiler_params=pltpu.CompilerParams(
            collective_id=0, has_side_effects=True, vmem_limit_bytes=56 << 20
        ),
        name="front",
    )(hid, ints, vec, wm, *tables, cot, we, wo, wc)


class LineSum:
    KINDS = 9

    def __init__(self, grad, result, inbox, sems, swap, size, lag, place):
        self.grad, self.result, self.inbox, self.sems, self.swap = grad, result, inbox, sems, swap
        self.c, self.y, self.x, self.z = place
        self.size = size
        self.count = grad.shape[0] // size
        self.split = (self.count + 1) // 2
        self.lag = lag
        self.slots = self.split + 6 * lag

    def rows(self, chunk):
        return pl.ds(pl.multiple_of(chunk * self.size, self.size), self.size)

    def moves(self, chunk, half):
        c, y, x, z = self.c, self.y, self.x, self.z
        up = 1 if half == 0 else -1
        rows = self.rows(chunk)
        grad, result, swap = self.grad, self.result, self.swap
        mine = result.at[c, x, rows]
        beside = result.at[c, 1 - x, rows]
        lower, upper = device_at(c, y, x, z - up), device_at(c, y, x, z + up)

        def lanes(which):
            return pl.ds(pl.multiple_of(which * swap, swap), swap)

        makers = {
            "near": (0, lambda: (grad.at[rows], self.inbox.at[0, rows], upper)),
            "far": (1, lambda: (grad.at[rows], self.inbox.at[1, rows], lower)),
            "swap": (
                2,
                lambda: (
                    grad.at[rows, lanes(1 - y)],
                    result.at[c, x, rows, lanes(y)],
                    device_at(c, 1 - y, x, z),
                ),
            ),
            "down": (3, lambda: (mine, mine, lower)),
            "out": (4, lambda: (mine, mine, upper)),
            "side": (5, lambda: (mine, mine, device_at(c, y, 1 - x, z))),
            "core": (6, lambda: (mine, mine, device_at(1 - c, y, x, z))),
            "late": (7, lambda: (beside, beside, device_at(1 - c, y, x, z))),
        }

        def make(name):
            kind, parts = makers[name]
            src, dst, target = parts()
            return remote(
                src, dst, self.sems.at[2 * kind, chunk], self.sems.at[2 * kind + 1, chunk], target
            )

        return make

    def keeps(self, chunk):
        rows, swap = self.rows(chunk), self.swap
        own = pl.ds(pl.multiple_of(self.y * swap, swap), swap)
        plain = pl.ds(2 * swap, self.grad.shape[1] - 2 * swap)
        return [
            pltpu.make_async_copy(
                self.grad.at[rows, lanes],
                self.result.at[self.c, self.x, rows, lanes],
                self.sems.at[2 * self.KINDS - 2 + index, chunk],
            )
            for index, lanes in enumerate((own, plain))
        ]

    def slot(self, t):
        for half in range(2):
            self.half_slot(t, half)

    def extent(self, half):
        size = self.split if half == 0 else self.count - self.split
        base = 0 if half == 0 else self.split
        at = self.z if half == 0 else LINE - 1 - self.z
        return (size, base, at)

    def half_slot(self, t, half):
        size, base, at = self.extent(half)
        lag = self.lag
        swap = self.swap
        owner = at == 1

        def event(delay, run):
            chunk = t - delay
            index = jnp.clip(chunk, 0, size - 1) + base

            @pl.when((chunk >= 0) & (chunk < size))
            def _():
                run(index, self.moves(index, half))

        def reduce(index, moves):
            rows = self.rows(index)

            @pl.when(at == 0)
            def _():
                moves("near").start()

            @pl.when(at == 2)
            def _():
                moves("far").wait_recv()
                total = self.grad[rows].astype(jnp.float32) + self.inbox[1, rows].astype(
                    jnp.float32
                )
                self.grad[rows] = total.astype(jnp.bfloat16)

            @pl.when(at >= 2)
            def _():
                moves("far").start()

            @pl.when(owner)
            def _():
                moves("near").wait_recv()
                moves("far").wait_recv()
                total = (
                    self.grad[rows].astype(jnp.float32)
                    + self.inbox[0, rows].astype(jnp.float32)
                    + self.inbox[1, rows].astype(jnp.float32)
                )
                self.grad[rows] = total.astype(jnp.bfloat16)
                moves("swap").start()
                for copy in self.keeps(index):
                    copy.start()

        event(jnp.where(owner, 2 * lag, jnp.where(at == 2, lag, 0)), reduce)

        def spread(index, moves):
            @pl.when(owner)
            def _():
                moves("swap").wait_recv()
                for copy in self.keeps(index):
                    copy.wait()
                moves("down").start()

            @pl.when(at == 0)
            def _():
                moves("down").wait_recv()

            @pl.when(at >= 2)
            def _():
                moves("out").wait_recv()

            @pl.when((at == 1) | (at == 2))
            def _():
                moves("out").start()

            moves("side").start()
            moves("core").start()

        wait = jnp.where(owner, 3 * lag, jnp.where(at == 3, 5 * lag, 4 * lag))
        event(wait, spread)

        def late(index, moves):
            moves("side").wait_recv()
            moves("late").start()

        event(wait + lag, late)

    def drain(self):
        for half in range(2):
            size, base, at = self.extent(half)

            def finish(chunk, carry):
                moves = self.moves(chunk + base, half)

                @pl.when(at == 0)
                def _():
                    moves("near").wait_send()

                @pl.when(at >= 2)
                def _():
                    moves("far").wait_send()

                @pl.when(at == 1)
                def _():
                    moves("swap").wait_send()
                    moves("down").wait_send()

                @pl.when((at == 1) | (at == 2))
                def _():
                    moves("out").wait_send()

                moves("side").wait_send()
                moves("core").wait()
                moves("late").wait()
                return carry

            lax.fori_loop(0, size, finish, 0)


def sort_kernel(order, src, dst, *, units):
    for unit in range(units):
        dst[:, order[0, unit]] = src[:, unit]


def sort_units(order, array, units):
    shape = array.shape
    vmem = pl.BlockSpec(memory_space=pltpu.VMEM)
    view = (shape[0], units, UNIT, shape[-1])
    return pl.pallas_call(
        functools.partial(sort_kernel, units=units),
        out_shape=jax.ShapeDtypeStruct(view, array.dtype),
        in_specs=[pl.BlockSpec(memory_space=pltpu.SMEM), vmem],
        out_specs=vmem,
        compiler_params=pltpu.CompilerParams(vmem_limit_bytes=16 << 20),
        name="sort_units",
    )(order, array.reshape(view))


def middle_kernel(
    ints,
    sorted_parts,
    unit_cos,
    unit_sin,
    row_cos,
    row_sin,
    feed_grad,
    active_src,
    grad_expanded_src,
    we_src,
    wc_src,
    wm_src,
    wo_src,
    hidden_src,
    cots_src,
    vectors,
    feed_sums,
    feed_all,
    attn_all,
    out_sum,
    term_sum,
    done,
    feed_own,
    feed_inbox,
    parts,
    attn_own,
    attn_inbox,
    near,
    beside,
    far,
    totals,
    send,
    recv,
    feed_sems,
    attn_sems,
    near_sems,
    beside_sems,
    far_sems,
    local,
    loads,
    *,
    units,
    pieces,
    feed_swap,
    swap,
):
    place = place_here()
    c, y, x, z = place
    core = device_at(1 - c, y, x, z)
    over_x = device_at(c, y, 1 - x, z)
    over_y = device_at(c, 1 - y, x, z)
    inner = 2 * x + c

    def rows_of(src, dst):
        count = dst.shape[0]
        return src.at[pl.ds(pl.multiple_of(inner * count, count), count)]

    first_load = pltpu.make_async_copy(feed_grad, feed_own, loads.at[8])
    first_load.start()
    peers = [lax.rem(z + d, LINE) for d in range(1, LINE)]
    greet([device_at(c, y, x, peer) for peer in peers] + [core, over_x, over_y])
    first_load.wait()
    line = LineSum(feed_own, feed_all, feed_inbox, feed_sems, feed_swap, FEED_CHUNK, 2, place)
    lanes = done.shape[2]
    rows = done.shape[1] // LINE
    mine = pl.ds(pl.multiple_of(z * rows, rows), rows)

    def gather(index, which):
        peer = peers[index]
        return remote(
            done.at[which, pl.ds(pl.multiple_of(peer * rows, rows), rows)],
            parts.at[mine, pl.ds(which * lanes, lanes)],
            send.at[index, which],
            recv.at[index, which],
            device_at(c, y, x, peer),
        )

    def gather_own(which):
        return pltpu.make_async_copy(
            done.at[which, mine], parts.at[mine, pl.ds(which * lanes, lanes)], local.at[which]
        )

    def attention_phase(
        masked, flat, scores, slopes, key_sum, value_sum, mixed_sum, query_sum
    ):
        length = sorted_parts.shape[1]
        scale = 1.0 / math.sqrt(HEAD)
        blocks = length // SPAN
        lanes = lax.broadcasted_iota(jnp.int32, (UNIT, 2 * HEAD), 1)
        lower = lanes < HEAD

        def arrange(index, carry):
            @pl.when(lax.rem(index, 8) == 0)
            def _():
                line.slot(lax.div(index, 8))

            at = pl.ds(pl.multiple_of(index * UNIT, UNIT), UNIT)
            for which in range(4):
                rows = sorted_parts[which, at, :].astype(jnp.float32)
                if which == 0:
                    rows = rows * scale
                masked[which, 0, at, :] = jnp.where(lower, rows, 0.0).astype(jnp.bfloat16)
                masked[which, 1, at, :] = jnp.where(lower, 0.0, rows).astype(jnp.bfloat16)
                flat[which, :, at] = rows.T.astype(jnp.bfloat16)
            return carry

        lax.fori_loop(0, units, arrange, 0)
        early = -(-units // 8)
        key_sum[...] = jnp.zeros_like(key_sum)
        value_sum[...] = jnp.zeros_like(value_sum)

        def labels(positions):
            found = jnp.full(positions.shape, -1, jnp.int32)
            for piece in range(pieces):
                start = ints[0, units + piece]
                found = jnp.where(
                    (positions >= start) & (positions < start + PIECE), piece, found
                )
            return found

        def dot(a, b):
            return jnp.dot(a, b, preferred_element_type=jnp.float32)

        for block in range(blocks):
            begin = block * SPAN
            last = SPAN + (UNIT if block + 1 < blocks else 0)
            columns = pl.ds(begin, SPAN)
            row_at = begin + lax.broadcasted_iota(jnp.int32, (1, SPAN), 1)
            col_at = begin + lax.broadcasted_iota(jnp.int32, (last, 1), 0)
            row_lab = labels(row_at)
            col_lab = labels(col_at)
            allowed = (col_at <= row_at) | (
                (col_lab == row_lab) & (row_lab >= 0)
            )

            def one_head(head, carry):
                start_tick = 3 * block * (block + 1) + head * 3 * (block + 1)

                def tick(index):
                    at = start_tick + index

                    @pl.when(lax.rem(at, EVERY) == 0)
                    def _():
                        line.slot(early + lax.div(at, EVERY))

                queries = flat[0, :, columns]
                grads = flat[3, :, columns]
                side = pl.ds(pl.multiple_of(head * HEAD, HEAD), HEAD)

                def score_tile(start, size, top, mask=None):
                    rows = pl.ds(start, size)
                    tile = dot(masked[1, head, rows, :], queries)
                    if mask is not None:
                        tile = jnp.where(mask, tile, NEGATIVE)
                    scores[rows, :] = tile
                    return jnp.maximum(top, jnp.max(tile, axis=0, keepdims=True))

                def tile_step(step, run, j, carry):
                    tick(step * (block + 1) + j)
                    start = pl.multiple_of(j * SPAN, SPAN)
                    return run(start, SPAN, carry)

                top = lax.fori_loop(
                    0,
                    block,
                    functools.partial(tile_step, 0, score_tile),
                    jnp.full((1, SPAN), NEGATIVE, jnp.float32),
                )
                tick(block)
                top = score_tile(begin, last, top, allowed)

                def weight_tile(start, size, sums):
                    total, delta = sums
                    rows = pl.ds(start, size)
                    weights = jnp.exp(scores[rows, :] - top)
                    slope = dot(masked[2, head, rows, :], grads)
                    scores[rows, :] = weights
                    slopes[rows, :] = slope
                    return (
                        total + jnp.sum(weights, axis=0, keepdims=True),
                        delta + jnp.sum(weights * slope, axis=0, keepdims=True),
                    )

                zero = jnp.zeros((1, SPAN), jnp.float32)
                sums = lax.fori_loop(
                    0,
                    block,
                    functools.partial(tile_step, 1, weight_tile),
                    (zero, zero),
                )
                tick(2 * block + 1)
                total, delta = weight_tile(begin, last, sums)
                inverse = 1.0 / total
                delta = delta * inverse

                def grad_tile(start, size, sums):
                    mixed, query = sums
                    rows = pl.ds(start, size)
                    probs = scores[rows, :] * inverse
                    grad = (probs * (slopes[rows, :] - delta)).astype(jnp.bfloat16)
                    probs = probs.astype(jnp.bfloat16)
                    value_sum[rows, :] += dot(probs, masked[3, head, columns, :])
                    key_sum[rows, :] += dot(grad, masked[0, head, columns, :])
                    mixed = mixed + dot(flat[2, side, rows], probs)
                    query = query + dot(flat[1, side, rows], grad)
                    return (mixed, query)

                none = jnp.zeros((HEAD, SPAN), jnp.float32)
                sums = lax.fori_loop(
                    0,
                    block,
                    functools.partial(tile_step, 2, grad_tile),
                    (none, none),
                )
                tick(3 * block + 2)
                mixed, query = grad_tile(begin, last, sums)
                mixed_sum[side, columns] = mixed
                query_sum[side, columns] = query * scale
                return carry

            lax.fori_loop(0, 2, one_head, 0)

        lane = lax.rem(lax.broadcasted_iota(jnp.int32, row_cos.shape, 1), HEAD)
        ticked = early - (-3 * blocks * (blocks + 1) // EVERY)

        def finish(index, carry):
            @pl.when(lax.rem(index, 8) == 0)
            def _():
                line.slot(ticked + lax.div(index, 8))

            at = pl.ds(pl.multiple_of(index * UNIT, UNIT), UNIT)
            base_cos, base_sin = unit_cos[pl.ds(index, 1), :], unit_sin[pl.ds(index, 1), :]
            cosine = base_cos * row_cos[...] - base_sin * row_sin[...]
            sine = base_sin * row_cos[...] + base_cos * row_sin[...]
            sine_up = jnp.where(lane < HALF, sine, 0.0)
            sine_down = jnp.where(lane < HALF, 0.0, sine)

            def turn_back(rows):
                up = pltpu.roll(rows, 2 * HEAD - HALF, 1)
                down = pltpu.roll(rows, HALF, 1)
                return rows * cosine + up * sine_up - down * sine_down

            masked[0, 0, at, :] = mixed_sum[:, at].T.astype(jnp.bfloat16)
            masked[1, 0, at, :] = turn_back(query_sum[:, at].T).astype(jnp.bfloat16)
            masked[2, 0, at, :] = turn_back(key_sum[at, :]).astype(jnp.bfloat16)
            masked[3, 0, at, :] = value_sum[at, :].astype(jnp.bfloat16)
            return carry

        lax.fori_loop(0, units, finish, 0)
        ticked += -(-units // 8)

        def restore(owner):
            for index in range(units // LINE):
                unit = owner * (units // LINE) + index
                here = pl.ds(pl.multiple_of(unit * UNIT, UNIT), UNIT)
                place = ints[0, unit]
                for which in range(4):
                    rows = masked[which, 0, pl.ds(0, UNIT), :]
                    for other in range(1, units):
                        rows = jnp.where(
                            place == other, masked[which, 0, pl.ds(other * UNIT, UNIT), :], rows
                        )
                    done[which, here, :] = rows

        for index, peer in enumerate(peers):
            restore(peer)
            for which in (1, 2, 3, 0):
                gather(index, which).start()
        restore(z)
        for which in range(4):
            gather_own(which).start()


    length = sorted_parts.shape[1]
    ticked = (
        2 * -(-units // 8) - (-3 * (length // SPAN) * (length // SPAN + 1) // EVERY)
    )
    pl.run_scoped(
        attention_phase,
        pltpu.VMEM((4, 2, length, 2 * HEAD), jnp.bfloat16),
        pltpu.VMEM((4, 2 * HEAD, length), jnp.bfloat16),
        pltpu.VMEM((length, SPAN), jnp.float32),
        pltpu.VMEM((length, SPAN), jnp.float32),
        pltpu.VMEM((length, 2 * HEAD), jnp.float32),
        pltpu.VMEM((length, 2 * HEAD), jnp.float32),
        pltpu.VMEM((2 * HEAD, length), jnp.float32),
        pltpu.VMEM((2 * HEAD, length), jnp.float32),
    )

    def close_phase(
        stats, outs, terms, single, active, grad_expanded, we, wc, wm, wo, hidden, cots
    ):
        sources = (
            (hidden_src, hidden),
            (grad_expanded_src, grad_expanded),
            (we_src, we),
            (active_src, active),
            (rows_of(wc_src, wc), wc),
            (cots_src, cots),
            (wm_src, wm),
            (rows_of(wo_src, wo), wo),
        )
        fetched = []
        for index, (src, dst) in enumerate(sources):
            copy = pltpu.make_async_copy(src, dst, loads.at[index])
            copy.start()
            fetched.append(copy)
        gain_one, shift_one, gain_two = vectors[0:1, :], vectors[1:2, :], vectors[2:3, :]
        width = hidden.shape[1]
        half = width // 2
        totals[...] = jnp.zeros_like(totals)
        for copy in fetched:
            copy.wait()

        def before(index, carry):
            at = pl.ds(pl.multiple_of(index * TILE, TILE), TILE)
            raw = hidden[at, :].astype(jnp.float32)
            mean = jnp.mean(raw, axis=1, keepdims=True)
            centred = raw - mean
            rstd = lax.rsqrt(jnp.mean(centred * centred, axis=1, keepdims=True) + EPS)
            stats[0, at, :] = jnp.broadcast_to(mean, (TILE, stats.shape[2]))
            stats[1, at, :] = jnp.broadcast_to(rstd, (TILE, stats.shape[2]))
            xhat = centred * rstd
            grad_second = dot_rows(grad_expanded[at, :], we[...])
            terms[index] = (grad_second * gain_two).astype(jnp.bfloat16)
            outs[index] = dot_plain(active[at, :], wc[...]).astype(jnp.bfloat16)
            totals[2:3, :] += jnp.sum(grad_second * xhat, axis=0, keepdims=True)
            totals[3:4, :] += jnp.sum(grad_second, axis=0, keepdims=True)
            totals[4:5, :] += jnp.sum(cots[at, :].astype(jnp.float32), axis=0, keepdims=True)
            return carry

        tiles = hidden.shape[0] // TILE
        lax.fori_loop(0, tiles, before, 0)

        for which in range(4):
            gather_own(which).wait()
        for index in range(len(peers)):
            for which in range(4):
                gather(index, which).wait()

        arrays = (outs, terms)

        def block_at(cc, yy, xx):
            return (2 * cc + yy) * 2 + xx

        def to_core(a, yy, xx):
            block = block_at(1 - c, yy, xx)
            return remote(
                arrays[a].at[block],
                near.at[a, yy, xx],
                near_sems.at[0, a, yy, xx],
                near_sems.at[1, a, yy, xx],
                core,
            )

        ways = ((y, x, over_y, over_x), (x, y, over_x, over_y))

        def own_block(a, near_at, far_at):
            yy, xx = (near_at, far_at) if a == 0 else (far_at, near_at)
            return block_at(c, yy, xx)

        def hop_one(a, index):
            near_axis, far_axis, target, beyond = ways[a]
            return remote(
                arrays[a].at[own_block(a, 1 - near_axis, index)],
                beside.at[a, index],
                beside_sems.at[0, a, index],
                beside_sems.at[1, a, index],
                target,
            )

        def hop_two(a):
            return remote(
                single.at[a], far.at[a], far_sems.at[0, a], far_sems.at[1, a], ways[a][3]
            )

        def after(index):
            at = pl.ds(pl.multiple_of(index * TILE, TILE), TILE)
            grads = parts[at, pl.ds(lanes, 3 * lanes)]
            grad_first = dot_rows(grads, wm[...])
            xhat = (hidden[at, :].astype(jnp.float32) - stats[0, at, 0:1]) * stats[1, at, 0:1]
            hidden[at, :] = (xhat * gain_one + shift_one).astype(jnp.bfloat16)
            terms[index] = (terms[index].astype(jnp.float32) + grad_first * gain_one).astype(
                jnp.bfloat16
            )
            outs[index] = (
                outs[index].astype(jnp.float32) + dot_plain(parts[at, pl.ds(0, lanes)], wo[...])
            ).astype(jnp.bfloat16)
            totals[0:1, :] += jnp.sum(grad_first * xhat, axis=0, keepdims=True)
            totals[1:2, :] += jnp.sum(grad_first, axis=0, keepdims=True)
            totals[5:6, pl.ds(0, 3 * lanes)] += jnp.sum(
                grads.astype(jnp.float32), axis=0, keepdims=True
            )

        def others(step, carry):
            line.slot(ticked + step)
            yy, xx = lax.rem(1 - y + step // 2, 2), lax.rem(step, 2)
            after(block_at(1 - c, yy, xx))
            for a in range(2):
                to_core(a, yy, xx).start()
            return carry

        lax.fori_loop(0, 4, others, 0)

        def ours(step, carry):
            line.slot(ticked + 4 + step)
            yy, xx = lax.rem(1 - y + step // 2, 2), lax.rem(step, 2)
            after(block_at(c, yy, xx))
            for a in range(2):
                to_core(a, yy, xx).wait_recv()
                block = block_at(c, yy, xx)
                total = arrays[a][block].astype(jnp.float32) + near[a, yy, xx].astype(jnp.float32)
                arrays[a][block] = total.astype(jnp.bfloat16)
                near_at, far_at = (yy, xx) if a == 0 else (xx, yy)

                @pl.when(near_at != ways[a][0])
                def _():
                    hop_one(a, far_at).start()

            return carry

        lax.fori_loop(0, 4, ours, 0)
        later = ticked + 8
        for index in range(width // TILE):
            line.slot(later + index)
            block = dot_tokens(hidden[:, pl.ds(index * TILE, TILE)], parts[:, pl.ds(lanes, 3 * lanes)])
            side, row = divmod(index * TILE, half)
            attn_own[pl.ds(row, TILE), pl.ds(side * swap, swap)] = block.astype(jnp.bfloat16)
        block = dot_tokens(parts[:, pl.ds(0, lanes)], cots[...]).astype(jnp.bfloat16)
        wide = 2 * lanes
        for index in range(width // wide):
            attn_own[pl.ds(index * lanes, lanes), pl.ds(2 * swap, wide)] = block[
                :, index * wide : (index + 1) * wide
            ]
        lines = []
        fill = jnp.zeros((1, swap), jnp.float32)
        for index in range(5):
            for begin in range(0, width, swap):
                stop = min(begin + swap, width)
                entry = totals[index : index + 1, begin:stop]
                if stop - begin < swap:
                    entry = jnp.concatenate([entry, fill[:, : swap - (stop - begin)]], axis=1)
                lines.append(entry)
        lines.append(totals[5:6, 0:swap])
        ff = feed_sums.shape[1]
        for begin in range(0, ff, swap):
            stop = min(begin + swap, ff)
            entry = feed_sums[:, begin:stop]
            if stop - begin < swap:
                entry = jnp.concatenate([entry, fill[:, : swap - (stop - begin)]], axis=1)
            lines.append(entry)
        lines += [fill] * (attn_own.shape[0] - half - len(lines))
        small = jnp.concatenate(lines, axis=0).astype(jnp.bfloat16)
        tail = pl.ds(half, attn_own.shape[0] - half)
        attn_own[tail, pl.ds(0, swap)] = small
        attn_own[tail, pl.ds(swap, swap)] = small
        attn_own[tail, pl.ds(2 * swap, wide)] = jnp.zeros((small.shape[0], wide), jnp.bfloat16)

        attn = LineSum(attn_own, attn_all, attn_inbox, attn_sems, swap, CHUNK, 1, place)

        later += width // TILE

        def step(t, carry):
            attn.slot(t)
            line.slot(later + t)
            return carry

        def pass_on(a):
            near_axis, far_axis = ways[a][:2]
            for index in range(2):
                hop_one(a, index).wait()
            single[a] = (
                arrays[a][own_block(a, near_axis, 1 - far_axis)].astype(jnp.float32)
                + beside[a, 1 - far_axis].astype(jnp.float32)
            ).astype(jnp.bfloat16)
            hop_two(a).start()

        middle = attn.slots - 6
        lax.fori_loop(0, middle, step, 0)
        pass_on(0)
        pass_on(1)
        lax.fori_loop(middle, attn.slots, step, 0)
        for a, dst in enumerate((out_sum, term_sum)):
            hop_two(a).wait()
            near_axis, far_axis = ways[a][:2]
            dst[...] = (
                arrays[a][own_block(a, near_axis, far_axis)].astype(jnp.float32)
                + beside[a, far_axis].astype(jnp.float32)
                + far[a].astype(jnp.float32)
            )

        def sent(step, carry):
            for a in range(2):
                to_core(a, step // 2, lax.rem(step, 2)).wait_send()
            return carry

        lax.fori_loop(0, 4, sent, 0)
        attn.drain()
        line.drain()

    token_rows, width = hidden_src.shape
    ff = active_src.shape[1]
    block = (token_rows // GROUP, width)
    pl.run_scoped(
        close_phase,
        pltpu.VMEM((2, token_rows, 128), jnp.float32),
        pltpu.VMEM((GROUP,) + block, jnp.bfloat16),
        pltpu.VMEM((GROUP,) + block, jnp.bfloat16),
        pltpu.VMEM((2,) + block, jnp.bfloat16),
        pltpu.VMEM((token_rows, ff), jnp.bfloat16),
        pltpu.VMEM((token_rows, ff), jnp.bfloat16),
        pltpu.VMEM((width, ff), jnp.bfloat16),
        pltpu.VMEM((ff, width), jnp.bfloat16),
        pltpu.VMEM((width, 3 * lanes), jnp.bfloat16),
        pltpu.VMEM((lanes, width), jnp.bfloat16),
        pltpu.VMEM((token_rows, width), jnp.bfloat16),
        pltpu.VMEM((token_rows, width), jnp.bfloat16),
    )


def middle(
    ints,
    sorted_parts,
    tables,
    feed_grad,
    active,
    grad_expanded,
    we,
    wc,
    wm,
    wo,
    hidden,
    cots,
    vectors,
    feed_sums,
    tokens,
    units,
    pieces,
    feed_swap,
):
    rows, width = hidden.shape
    lanes = sorted_parts.shape[2]
    swap = 3 * lanes
    block = (tokens, width)
    vmem = pl.BlockSpec(memory_space=pltpu.VMEM)
    any_spec = pl.BlockSpec(memory_space=pl.ANY)
    grad_shape = (width // 2 + CHUNK, 2 * swap + 2 * lanes)
    scratch = [
        pltpu.VMEM(sorted_parts.shape, jnp.bfloat16),
        pltpu.VMEM(feed_grad.shape, jnp.bfloat16),
        pltpu.VMEM((2,) + feed_grad.shape, jnp.bfloat16),
        pltpu.VMEM((rows, 4 * lanes), jnp.bfloat16),
        pltpu.VMEM(grad_shape, jnp.bfloat16),
        pltpu.VMEM((2,) + grad_shape, jnp.bfloat16),
        pltpu.VMEM((2, 2, 2) + block, jnp.bfloat16),
        pltpu.VMEM((2, 2) + block, jnp.bfloat16),
        pltpu.VMEM((2,) + block, jnp.bfloat16),
        pltpu.VMEM((8, width), jnp.float32),
        pltpu.SemaphoreType.DMA((LINE - 1, 4)),
        pltpu.SemaphoreType.DMA((LINE - 1, 4)),
        pltpu.SemaphoreType.DMA((2 * LineSum.KINDS, feed_grad.shape[0] // FEED_CHUNK)),
        pltpu.SemaphoreType.DMA((2 * LineSum.KINDS, grad_shape[0] // CHUNK)),
        pltpu.SemaphoreType.DMA((2, 2, 2, 2)),
        pltpu.SemaphoreType.DMA((2, 2, 2)),
        pltpu.SemaphoreType.DMA((2, 2)),
        pltpu.SemaphoreType.DMA((4,)),
        pltpu.SemaphoreType.DMA((9,)),
    ]
    return pl.pallas_call(
        functools.partial(
            middle_kernel, units=units, pieces=pieces, feed_swap=feed_swap, swap=swap
        ),
        out_shape=(
            jax.ShapeDtypeStruct((2, 2) + feed_grad.shape, jnp.bfloat16),
            jax.ShapeDtypeStruct((2, 2) + grad_shape, jnp.bfloat16),
            jax.ShapeDtypeStruct(block, jnp.float32),
            jax.ShapeDtypeStruct(block, jnp.float32),
        ),
        in_specs=[pl.BlockSpec(memory_space=pltpu.SMEM)]
        + [vmem] * 5
        + [any_spec] * 9
        + [vmem] * 2,
        out_specs=[any_spec] + [vmem] * 3,
        scratch_shapes=scratch,
        compiler_params=pltpu.CompilerParams(
            collective_id=3, has_side_effects=True, vmem_limit_bytes=60 << 20
        ),
        name="middle",
    )(
        ints,
        sorted_parts,
        *tables,
        feed_grad,
        active,
        grad_expanded,
        we,
        wc,
        wm,
        wo,
        hidden,
        cots,
        vectors,
        feed_sums,
    )


def widen_kernel(
    feed_all,
    attn_all,
    expand,
    contract,
    merged,
    output,
    shared_out,
    merged_sums,
    expand_sums,
    feed,
    attn,
    expand_wide,
    contract_wide,
    merged_wide,
    output_wide,
    loads,
    stores,
    *,
    swap,
    lanes,
    ff,
):
    half = feed.shape[2]
    gets = []
    for index, (src, dst) in enumerate(((feed_all, feed), (attn_all, attn))):
        for part in range(4):
            copy = pltpu.make_async_copy(
                src.at[part // 2, part % 2], dst.at[part // 2, part % 2], loads.at[index, part]
            )
            copy.start()
            gets.append(copy)
    puts = []

    def put(src, dst):
        copy = pltpu.make_async_copy(src, dst, stores.at[len(puts)])
        copy.start()
        puts.append(copy)

    for part in range(4):
        c, x = part // 2, part % 2
        gets[part].wait()
        for y in range(2):
            at = pl.ds((4 * y + 2 * x + c) * ff, ff)
            expand_wide[:, at] = feed[c, x, :, pl.ds(y * ff, ff)].astype(jnp.float32)
            put(expand_wide.at[:, at], expand.at[:, at])
        at = pl.ds((2 * x + c) * ff, ff)
        contract_wide[at, :] = feed[c, x, :, pl.ds(2 * ff, 2 * half)].astype(jnp.float32)
        put(contract_wide.at[at], contract.at[at])
    for copy in gets[4:]:
        copy.wait()
    width = 2 * half
    for j in range(3):
        for octant in range(GROUP):
            c, x, y = octant % 2, octant // 2 % 2, octant // 4
            at = pl.ds(j * width + octant * lanes, lanes)
            merged_wide[:, at] = attn[
                c, x, pl.ds(0, half), pl.ds(y * swap + j * lanes, lanes)
            ].astype(jnp.float32)
        at = pl.ds(j * width, width)
        put(merged_wide.at[:, at], merged.at[:, at])
    for part in range(4):
        c, x = part % 2, part // 2
        for index in range(half // lanes):
            output_wide[pl.ds(part * lanes, lanes), pl.ds(2 * lanes * index, 2 * lanes)] = attn[
                c, x, pl.ds(index * lanes, lanes), pl.ds(2 * swap, 2 * lanes)
            ].astype(jnp.float32)
    put(output_wide, output)
    tail = pl.ds(half, attn.shape[2] - half)
    y = lax.axis_index("fsdp")
    per = -(-width // swap)

    def entry(octant):
        c, x, side = octant % 2, octant // 2 % 2, octant // 4
        return attn[c, x, tail, pl.ds(side * swap, swap)].astype(jnp.float32)

    entries = [entry(octant) for octant in range(GROUP)]
    total = entries[0]
    for item in entries[1:]:
        total = total + item

    def vector(source, row, size):
        count = -(-size // swap)
        rows = [source[row + index : row + index + 1] for index in range(count)]
        return jnp.concatenate(rows, axis=1)[:, :size]

    whole = [vector(total, per * index, width) for index in range(4)]
    whole.append(vector(entries[0], per * 4, width))
    heads = [vector(item, per * 5, swap) for item in entries]
    heads = jnp.concatenate(
        [item[:, j * lanes : (j + 1) * lanes] for j in range(3) for item in heads], axis=1
    )
    hidden = jnp.concatenate([vector(item, per * 5 + 1, ff) for item in entries], axis=1)
    for side in range(2):

        @pl.when(y == side)
        def _():
            for index, item in enumerate(whole):
                shared_out[index : index + 1, :] = item[:, side * half : (side + 1) * half]
            for src, dst in ((heads, merged_sums), (hidden, expand_sums)):
                size = dst.shape[1]
                dst[...] = src[:, side * size : (side + 1) * size]

    for copy in puts:
        copy.wait()


def widen(feed_all, attn_all, swap, lanes, ff):
    half = feed_all.shape[2]
    width = 2 * half
    shapes = ((half, GROUP * ff), (4 * ff, width), (half, 3 * width), (4 * lanes, width))
    small = ((5, half), (1, 3 * half), (1, 4 * ff))
    any_spec = pl.BlockSpec(memory_space=pl.ANY)
    return pl.pallas_call(
        functools.partial(widen_kernel, swap=swap, lanes=lanes, ff=ff),
        out_shape=tuple(jax.ShapeDtypeStruct(shape, jnp.float32) for shape in shapes + small),
        in_specs=[any_spec] * 2,
        out_specs=[any_spec] * 4 + [pl.BlockSpec(memory_space=pltpu.VMEM)] * 3,
        scratch_shapes=[
            pltpu.VMEM(feed_all.shape, jnp.bfloat16),
            pltpu.VMEM(attn_all.shape, jnp.bfloat16),
        ]
        + [pltpu.VMEM(shape, jnp.float32) for shape in shapes]
        + [pltpu.SemaphoreType.DMA((2, 4)), pltpu.SemaphoreType.DMA((16,))],
        compiler_params=pltpu.CompilerParams(vmem_limit_bytes=48 << 20),
        name="widen",
    )(feed_all, attn_all)


def turn_tables(positions, lanes):
    lane = jnp.arange(lanes, dtype=jnp.int32) % HEAD
    inverse = jnp.exp((lane % HALF).astype(jnp.float32) * (-2.0 * math.log(10000.0) / ROT))
    angles = positions.astype(jnp.float32)[:, None] * inverse[None, :]
    turned = lane[None, :] < ROT
    return (jnp.where(turned, jnp.cos(angles), 1.0), jnp.where(turned, jnp.sin(angles), 0.0))


def group_body(
    hidden_states,
    unit_order,
    piece_starts,
    first_gain,
    first_shift,
    second_gain,
    second_shift,
    merged_weight,
    merged_bias,
    output_weight,
    output_bias,
    expand_weight,
    expand_bias,
    contract_weight,
    contract_bias,
    out_cotangent,
):
    c, y, x, z = place_here()
    tokens, width = hidden_states.shape[1:]
    length = tokens * 2 * LINE
    units = unit_order.shape[1]
    pieces = piece_starts.shape[1]
    rows = GROUP * tokens
    part = width // GROUP
    ff_part = expand_weight.shape[1] // GROUP
    half = width // 2
    vectors = (
        first_gain,
        first_shift,
        second_gain,
        second_shift,
        merged_bias,
        output_bias,
        expand_bias,
        contract_bias,
    )
    sizes = [v.shape[0] for v in vectors]
    total = sum(sizes)
    packed = jnp.zeros((total,), jnp.float32)
    at = 0
    for vector in vectors:
        size = vector.shape[0]
        packed = packed + jnp.pad(vector.astype(jnp.float32), (at, total - at - size))
        at += size
    packed = packed.reshape(-1, 128)
    ints = jnp.concatenate([unit_order[0], piece_starts[0]])
    ints = jnp.broadcast_to(jnp.pad(ints, (0, 128 - ints.shape[0]))[None], (8, 128))
    tables = turn_tables(jnp.arange(units, dtype=jnp.int32) * UNIT, part) + turn_tables(
        jnp.arange(UNIT, dtype=jnp.int32), part
    )
    (
        hid_all,
        ints_all,
        vec_all,
        wm_all,
        cot_all,
        we_all,
        got,
        active,
        grad_expanded,
        feed_grad,
        feed_sums,
    ) = front(
        hidden_states[0],
        ints,
        packed,
        merged_weight,
        tables,
        out_cotangent[0],
        expand_weight,
        output_weight,
        contract_weight,
    )
    vec_all = vec_all.reshape(2, -1)
    whole = []
    at = 0
    for size in sizes:
        whole.append(vec_all[:, at : at + size].reshape(-1))
        at += size
    gain_one, shift_one, gain_two, shift_two, bias_merged, bias_out, bias_expand, bias_contract = whole
    wm = wm_all.reshape(width, 3 * part)
    we = we_all.reshape(width, ff_part)
    cots = cot_all.reshape(rows, width)
    own_ints = lax.dynamic_index_in_dim(ints_all[:, 0], z, 0, keepdims=True)
    sorted_parts = sort_units(own_ints, got, units)
    swap = 3 * part
    feed_all, attn_all, out_sum, term_sum = middle(
        own_ints,
        sorted_parts.reshape(4, length, part),
        tables,
        feed_grad,
        active,
        grad_expanded,
        we,
        contract_weight,
        wm,
        output_weight,
        hid_all.reshape(rows, width),
        cots,
        jnp.stack([gain_one, shift_one, gain_two]),
        feed_sums,
        tokens,
        units,
        pieces,
        ff_part,
    )
    expand_out, contract_out, merged_out, output_out, shared, merged_sums, expand_sums = widen(
        feed_all, attn_all, swap, part, ff_part
    )
    own_hidden = hidden_states[0].astype(jnp.float32)
    own_mean = jnp.mean(own_hidden, axis=1, keepdims=True)
    own_centred = own_hidden - own_mean
    own_rstd = lax.rsqrt(jnp.mean(own_centred * own_centred, axis=1, keepdims=True) + EPS)
    own_xhat = own_centred * own_rstd
    output = (own_hidden + out_sum + bias_out + bias_contract).astype(jnp.bfloat16)
    upstream = out_cotangent[0].astype(jnp.float32)
    input_gradient = upstream + own_rstd * (
        term_sum
        - jnp.mean(term_sum, axis=1, keepdims=True)
        - own_xhat * jnp.mean(term_sum * own_xhat, axis=1, keepdims=True)
    )

    return (
        output[None],
        input_gradient[None],
        shared[0],
        shared[1],
        shared[2],
        shared[3],
        merged_out,
        merged_sums[0],
        output_out,
        shared[4],
        expand_out,
        expand_sums[0],
        contract_out,
        shared[4],
    )


def fits_groups(mesh, args):
    hidden, order = args[0], args[1]
    count = mesh.shape["seq"]
    tokens = hidden.shape[1] // count
    return (
        mesh.shape["rep"] == 2
        and mesh.shape["fsdp"] == 2
        and count == 2 * LINE
        and hidden.shape[0] == LINE
        and hidden.shape[2] == GROUP * 2 * HEAD
        and tokens % UNIT == 0
        and hidden.shape[1] % SPAN == 0
        and order.shape[1] + args[2].shape[1] <= 128
    )


def solution(mesh):
    in_specs = (
        P(("rep", "fsdp"), "seq", None),
        P(("rep", "fsdp"), None),
        P(("rep", "fsdp"), None),
        P("fsdp"),
        P("fsdp"),
        P("fsdp"),
        P("fsdp"),
        P("fsdp", None),
        P("fsdp"),
        P("fsdp", None),
        P("fsdp"),
        P("fsdp", None),
        P("fsdp"),
        P("fsdp", None),
        P("fsdp"),
        P(("rep", "fsdp"), "seq", None),
    )
    out_specs = (
        P(("rep", "fsdp"), "seq", None),
        P(("rep", "fsdp"), "seq", None),
        P("fsdp"),
        P("fsdp"),
        P("fsdp"),
        P("fsdp"),
        P("fsdp", None),
        P("fsdp"),
        P("fsdp", None),
        P("fsdp"),
        P("fsdp", None),
        P("fsdp"),
        P("fsdp", None),
        P("fsdp"),
    )

    def run(*args):
        chosen = group_body if fits_groups(mesh, args) else body
        mapped = jax.shard_map(
            chosen, mesh=mesh, in_specs=in_specs, out_specs=out_specs, check_vma=False
        )
        return mapped(*args)

    return run
```

```python
import functools
import math

import jax
import jax.numpy as jnp
from jax import lax
from jax.experimental import pallas as pl
from jax.experimental.pallas import tpu as pltpu
from jax.sharding import PartitionSpec as P

HEAD = 64
ROT = 16
UNIT = 128
PIECE = 256


EPS = 1e-05
NEGATIVE = -1e30


def norm_rows(values, gain, shift):
    mean = jnp.mean(values, axis=-1, keepdims=True)
    centred = values - mean
    spread = jnp.mean(centred * centred, axis=-1, keepdims=True)
    return centred * lax.rsqrt(spread + EPS) * gain + shift


def gelu_exact(values):
    return jax.nn.gelu(values, approximate=False)


def rotary_tables(positions):
    index = jnp.arange(ROT // 2, dtype=jnp.float32)
    inverse = jnp.exp(index * (-2.0 * math.log(10000.0) / ROT))
    angles = positions.astype(jnp.float32)[:, None] * inverse[None, :]
    angles = jnp.concatenate([angles, angles], axis=1)
    return (jnp.cos(angles), jnp.sin(angles))


def rotate(values, cosine, sine):
    part = values[..., :ROT]
    turned = jnp.concatenate([-part[..., ROT // 2 :], part[..., : ROT // 2]], axis=-1)
    moved = part * cosine[:, None, :] + turned * sine[:, None, :]
    return jnp.concatenate([moved, values[..., ROT:]], axis=-1)


def unit_positions(order):
    offsets = jnp.arange(UNIT, dtype=jnp.int32)
    return (order[:, None] * UNIT + offsets[None, :]).reshape(-1)


def piece_labels(positions, starts):
    inside = (positions[:, None] >= starts[None, :]) & (
        positions[:, None] < starts[None, :] + PIECE
    )
    labels = jnp.arange(1, starts.shape[0] + 1, dtype=jnp.int32)
    return jnp.sum(jnp.where(inside, labels[None, :], 0), axis=1) - 1


def visible(row_pos, row_lab, col_pos, col_lab):
    earlier = col_pos[None, :] <= row_pos[:, None]
    same = (row_lab[:, None] == col_lab[None, :]) & (row_lab[:, None] >= 0)
    return earlier | same


def merged_parts(first, merged_weight, merged_bias, cosine, sine):
    tokens = first.shape[0]
    width = first.shape[1]
    heads = width // HEAD
    merged = jnp.dot(first, merged_weight, preferred_element_type=jnp.float32) + merged_bias.astype(
        jnp.float32
    )
    queries = rotate(merged[:, :width].reshape(tokens, heads, HEAD), cosine, sine).astype(
        jnp.bfloat16
    )
    keys = rotate(merged[:, width : 2 * width].reshape(tokens, heads, HEAD), cosine, sine)
    keys = keys.reshape(tokens, width).astype(jnp.bfloat16)
    values = merged[:, 2 * width :].astype(jnp.bfloat16)
    return (queries, keys, values)


def block_view(queries, keys_all, values_all, row_pos, row_lab, col_pos, col_lab, span):
    heads = queries.shape[1]
    scale = 1.0 / math.sqrt(HEAD)

    def view(index):
        start = index * span
        key_rows = lax.dynamic_slice_in_dim(keys_all, start, span, 0).reshape(span, heads, HEAD)
        value_rows = lax.dynamic_slice_in_dim(values_all, start, span, 0).reshape(span, heads, HEAD)
        scores = (
            jnp.einsum("thd,khd->htk", queries, key_rows, preferred_element_type=jnp.float32)
            * scale
        )
        allowed = visible(
            row_pos,
            row_lab,
            lax.dynamic_slice_in_dim(col_pos, start, span, 0),
            lax.dynamic_slice_in_dim(col_lab, start, span, 0),
        )[None]
        return (scores, allowed, key_rows, value_rows)

    return view


def log_sums(view, count, heads, tokens):

    def log_step(carry, index):
        top, total = carry
        scores, allowed, key_rows, value_rows = view(index)
        masked = jnp.where(allowed, scores, NEGATIVE)
        newer = jnp.maximum(top, jnp.max(masked, axis=-1))
        terms = jnp.where(allowed, jnp.exp(masked - newer[..., None]), 0.0)
        total = total * jnp.exp(top - newer) + jnp.sum(terms, axis=-1)
        return ((newer, total), None)

    begin = (
        jnp.full((heads, tokens), NEGATIVE, jnp.float32),
        jnp.zeros((heads, tokens), jnp.float32),
    )
    (top, total), unused = lax.scan(log_step, begin, jnp.arange(count, dtype=jnp.int32))
    return top + jnp.log(total)


def mix_values(view, count, logsum, heads, tokens, grad_rows):

    def mix_step(carry, index):
        mixed, delta = carry
        scores, allowed, key_rows, value_rows = view(index)
        weights = jnp.where(allowed, jnp.exp(scores - logsum[..., None]), 0.0)
        mixed = mixed + jnp.einsum(
            "htk,khd->thd",
            weights.astype(jnp.bfloat16),
            value_rows,
            preferred_element_type=jnp.float32,
        )
        if grad_rows is not None:
            slopes = jnp.einsum(
                "thd,khd->htk", grad_rows, value_rows, preferred_element_type=jnp.float32
            )
            delta = delta + jnp.sum(weights * slopes, axis=-1)
        return ((mixed, delta), None)

    begin = (jnp.zeros((tokens, heads, HEAD), jnp.float32), jnp.zeros((heads, tokens), jnp.float32))
    (mixed, delta), unused = lax.scan(mix_step, begin, jnp.arange(count, dtype=jnp.int32))
    return (mixed, delta)


def attend_back(view, count, logsum, delta, grad_rows, queries):
    scale = 1.0 / math.sqrt(HEAD)

    def attend_step(carry, index):
        scores, allowed, key_rows, value_rows = view(index)
        weights = jnp.where(allowed, jnp.exp(scores - logsum[..., None]), 0.0)
        slopes = jnp.einsum(
            "thd,khd->htk", grad_rows, value_rows, preferred_element_type=jnp.float32
        )
        grad_scores = (weights * (slopes - delta[..., None])).astype(jnp.bfloat16)
        carry = carry + jnp.einsum(
            "htk,khd->thd", grad_scores, key_rows, preferred_element_type=jnp.float32
        )
        key_grad = jnp.einsum(
            "htk,thd->khd", grad_scores, queries, preferred_element_type=jnp.float32
        )
        value_grad = jnp.einsum(
            "htk,thd->khd",
            weights.astype(jnp.bfloat16),
            grad_rows,
            preferred_element_type=jnp.float32,
        )
        span = key_rows.shape[0]
        joined = jnp.concatenate(
            [key_grad.reshape(span, -1) * scale, value_grad.reshape(span, -1)], axis=1
        )
        return (carry, joined)

    begin = jnp.zeros(queries.shape, jnp.float32)
    grad_query, parts = lax.scan(attend_step, begin, jnp.arange(count, dtype=jnp.int32))
    return (grad_query * scale, parts)


def body(
    hidden_states,
    unit_order,
    piece_starts,
    first_gain,
    first_shift,
    second_gain,
    second_shift,
    merged_weight,
    merged_bias,
    output_weight,
    output_bias,
    expand_weight,
    expand_bias,
    contract_weight,
    contract_bias,
    out_cotangent,
):
    shards = (
        first_gain,
        first_shift,
        second_gain,
        second_shift,
        merged_weight,
        merged_bias,
        output_weight,
        output_bias,
        expand_weight,
        expand_bias,
        contract_weight,
        contract_bias,
    )
    gathered = (
        lax.all_gather(shards[0], "fsdp", axis=0, tiled=True),
        lax.all_gather(shards[1], "fsdp", axis=0, tiled=True),
        lax.all_gather(shards[2], "fsdp", axis=0, tiled=True),
        lax.all_gather(shards[3], "fsdp", axis=0, tiled=True),
        lax.all_gather(shards[4], "fsdp", axis=0, tiled=True),
        lax.all_gather(shards[5], "fsdp", axis=0, tiled=True),
        lax.all_gather(shards[6], "fsdp", axis=0, tiled=True),
        lax.all_gather(shards[7], "fsdp", axis=0, tiled=True),
        lax.all_gather(shards[8], "fsdp", axis=0, tiled=True),
        lax.all_gather(shards[9], "fsdp", axis=0, tiled=True),
        lax.all_gather(shards[10], "fsdp", axis=0, tiled=True),
        lax.all_gather(shards[11], "fsdp", axis=0, tiled=True),
    )
    hidden = hidden_states[0].astype(jnp.float32)
    tokens = hidden.shape[0]
    width = hidden.shape[1]
    heads = width // HEAD
    length = tokens * lax.axis_size("seq")
    span = min(length, 512)
    count = length // span
    col_pos = unit_positions(unit_order[0])
    col_lab = piece_labels(col_pos, piece_starts[0])
    offset = lax.axis_index("seq") * tokens
    row_pos = lax.dynamic_slice_in_dim(col_pos, offset, tokens, 0)
    row_lab = lax.dynamic_slice_in_dim(col_lab, offset, tokens, 0)
    cosine, sine = rotary_tables(row_pos)
    first = norm_rows(
        hidden, gathered[0].astype(jnp.float32), gathered[1].astype(jnp.float32)
    ).astype(jnp.bfloat16)
    queries, keys, values = merged_parts(first, gathered[4], gathered[5], cosine, sine)
    keys_all, values_all = (
        lax.all_gather(keys, "seq", axis=0, tiled=True),
        lax.all_gather(values, "seq", axis=0, tiled=True),
    )
    view = block_view(queries, keys_all, values_all, row_pos, row_lab, col_pos, col_lab, span)
    logsum = log_sums(view, count, heads, tokens)
    mixed, unused = mix_values(view, count, logsum, heads, tokens, None)
    mixed = mixed.reshape(tokens, width).astype(jnp.bfloat16)
    attention = jnp.dot(mixed, gathered[6], preferred_element_type=jnp.float32) + gathered[
        7
    ].astype(jnp.float32)
    second = norm_rows(
        hidden, gathered[2].astype(jnp.float32), gathered[3].astype(jnp.float32)
    ).astype(jnp.bfloat16)
    expanded = jnp.dot(second, gathered[8], preferred_element_type=jnp.float32) + gathered[
        9
    ].astype(jnp.float32)
    active = gelu_exact(expanded).astype(jnp.bfloat16)
    feed = jnp.dot(active, gathered[10], preferred_element_type=jnp.float32) + gathered[11].astype(
        jnp.float32
    )
    output = (hidden + attention + feed).astype(jnp.bfloat16)
    weights = (
        lax.all_gather(shards[0], "fsdp", axis=0, tiled=True),
        lax.all_gather(shards[1], "fsdp", axis=0, tiled=True),
        lax.all_gather(shards[2], "fsdp", axis=0, tiled=True),
        lax.all_gather(shards[3], "fsdp", axis=0, tiled=True),
        lax.all_gather(shards[4], "fsdp", axis=0, tiled=True),
        lax.all_gather(shards[5], "fsdp", axis=0, tiled=True),
        lax.all_gather(shards[6], "fsdp", axis=0, tiled=True),
        lax.all_gather(shards[7], "fsdp", axis=0, tiled=True),
        lax.all_gather(shards[8], "fsdp", axis=0, tiled=True),
        lax.all_gather(shards[9], "fsdp", axis=0, tiled=True),
        lax.all_gather(shards[10], "fsdp", axis=0, tiled=True),
        lax.all_gather(shards[11], "fsdp", axis=0, tiled=True),
    )
    cotangent = out_cotangent[0]
    upstream = cotangent.astype(jnp.float32)
    normed_one, first_pull = jax.vjp(
        norm_rows, hidden, weights[0].astype(jnp.float32), weights[1].astype(jnp.float32)
    )
    first = normed_one.astype(jnp.bfloat16)
    queries, keys, values = merged_parts(first, weights[4], weights[5], cosine, sine)
    keys_back, values_back = (
        lax.all_gather(keys, "seq", axis=0, tiled=True),
        lax.all_gather(values, "seq", axis=0, tiled=True),
    )
    view = block_view(queries, keys_back, values_back, row_pos, row_lab, col_pos, col_lab, span)
    grad_mixed = jnp.einsum(
        "te,de->td", cotangent, weights[6], preferred_element_type=jnp.float32
    ).astype(jnp.bfloat16)
    grad_rows = grad_mixed.reshape(tokens, heads, HEAD)
    mixed, delta = mix_values(view, count, logsum, heads, tokens, grad_rows)
    mixed = mixed.reshape(tokens, width).astype(jnp.bfloat16)
    grad_query, parts = attend_back(view, count, logsum, delta, grad_rows, queries)
    term = parts.reshape(length, 2 * width)
    own_grads = lax.psum_scatter(
        term.astype(jnp.bfloat16), "seq", scatter_dimension=0, tiled=True
    ).astype(jnp.float32)
    normed_two, second_pull = jax.vjp(
        norm_rows, hidden, weights[2].astype(jnp.float32), weights[3].astype(jnp.float32)
    )
    second = normed_two.astype(jnp.bfloat16)
    expanded = jnp.dot(second, weights[8], preferred_element_type=jnp.float32) + weights[9].astype(
        jnp.float32
    )
    activated, gelu_pull = jax.vjp(gelu_exact, expanded)
    active = activated.astype(jnp.bfloat16)
    grad_active = jnp.einsum(
        "te,fe->tf", cotangent, weights[10], preferred_element_type=jnp.float32
    )
    grad_expanded = gelu_pull(grad_active)[0].astype(jnp.bfloat16)
    grad_second = jnp.einsum(
        "tf,df->td", grad_expanded, weights[8], preferred_element_type=jnp.float32
    )
    unused, turn_pull = jax.vjp(rotate, grad_query, cosine, sine)
    query_back = turn_pull(grad_query)[0].reshape(tokens, width)
    key_back = turn_pull(own_grads[:, :width].reshape(tokens, heads, HEAD))[0].reshape(
        tokens, width
    )
    grad_merged = jnp.concatenate([query_back, key_back, own_grads[:, width:]], axis=1).astype(
        jnp.bfloat16
    )
    grad_first = jnp.einsum(
        "tc,dc->td", grad_merged, weights[4], preferred_element_type=jnp.float32
    )
    first_term, first_gain_grad, first_shift_grad = first_pull(grad_first)
    second_term, second_gain_grad, second_shift_grad = second_pull(grad_second)
    input_gradient = upstream + first_term + second_term
    row_total = jnp.sum(upstream, axis=0)
    local_grads = (
        first_gain_grad,
        first_shift_grad,
        second_gain_grad,
        second_shift_grad,
        jnp.einsum("td,tc->dc", first, grad_merged, preferred_element_type=jnp.float32),
        jnp.sum(grad_merged.astype(jnp.float32), axis=0),
        jnp.einsum("td,te->de", mixed, cotangent, preferred_element_type=jnp.float32),
        row_total,
        jnp.einsum("td,tf->df", second, grad_expanded, preferred_element_type=jnp.float32),
        jnp.sum(grad_expanded.astype(jnp.float32), axis=0),
        jnp.einsum("tf,te->fe", active, cotangent, preferred_element_type=jnp.float32),
        row_total,
    )
    owned = (
        lax.psum_scatter(
            local_grads[0].astype(jnp.bfloat16), "fsdp", scatter_dimension=0, tiled=True
        ).astype(jnp.float32),
        lax.psum_scatter(
            local_grads[1].astype(jnp.bfloat16), "fsdp", scatter_dimension=0, tiled=True
        ).astype(jnp.float32),
        lax.psum_scatter(
            local_grads[2].astype(jnp.bfloat16), "fsdp", scatter_dimension=0, tiled=True
        ).astype(jnp.float32),
        lax.psum_scatter(
            local_grads[3].astype(jnp.bfloat16), "fsdp", scatter_dimension=0, tiled=True
        ).astype(jnp.float32),
        lax.psum_scatter(
            local_grads[4].astype(jnp.bfloat16), "fsdp", scatter_dimension=0, tiled=True
        ).astype(jnp.float32),
        lax.psum_scatter(
            local_grads[5].astype(jnp.bfloat16), "fsdp", scatter_dimension=0, tiled=True
        ).astype(jnp.float32),
        lax.psum_scatter(
            local_grads[6].astype(jnp.bfloat16), "fsdp", scatter_dimension=0, tiled=True
        ).astype(jnp.float32),
        lax.psum_scatter(
            local_grads[7].astype(jnp.bfloat16), "fsdp", scatter_dimension=0, tiled=True
        ).astype(jnp.float32),
        lax.psum_scatter(
            local_grads[8].astype(jnp.bfloat16), "fsdp", scatter_dimension=0, tiled=True
        ).astype(jnp.float32),
        lax.psum_scatter(
            local_grads[9].astype(jnp.bfloat16), "fsdp", scatter_dimension=0, tiled=True
        ).astype(jnp.float32),
        lax.psum_scatter(
            local_grads[10].astype(jnp.bfloat16), "fsdp", scatter_dimension=0, tiled=True
        ).astype(jnp.float32),
        lax.psum_scatter(
            local_grads[11].astype(jnp.bfloat16), "fsdp", scatter_dimension=0, tiled=True
        ).astype(jnp.float32),
    )
    summed = lax.psum(
        (
            owned[0],
            owned[1],
            owned[2],
            owned[3],
            owned[4],
            owned[5],
            owned[6],
            owned[7],
            owned[8],
            owned[9],
            owned[10],
            owned[11],
        ),
        ("rep", "seq"),
    )
    return (
        output[None],
        input_gradient[None],
        summed[0],
        summed[1],
        summed[2],
        summed[3],
        summed[4],
        summed[5],
        summed[6],
        summed[7],
        summed[8],
        summed[9],
        summed[10],
        summed[11],
    )


MESH = pl.DeviceIdType.MESH
GROUP = 8
LINE = 4
HALF = ROT // 2
SPAN = 512
CHUNK = 32
FEED_CHUNK = 16
EVERY = 4


def place_here():
    c, y, s = (lax.axis_index("rep"), lax.axis_index("fsdp"), lax.axis_index("seq"))
    x = lax.rem(s, 2)
    return (c, y, x, s // 2)


def device_at(c, y, x, z):
    return (c, y, 2 * z + x)


def greet(partners):
    barrier = pltpu.get_barrier_semaphore()
    for partner in partners:
        pl.semaphore_signal(barrier, inc=1, device_id=partner, device_id_type=MESH)
    pl.semaphore_wait(barrier, len(partners))


def remote(src, dst, send, recv, target):
    return pltpu.make_async_remote_copy(
        src_ref=src,
        dst_ref=dst,
        send_sem=send,
        recv_sem=recv,
        device_id=target,
        device_id_type=MESH,
    )


def dot_rows(a, b):
    return lax.dot_general(a, b, (((1,), (1,)), ((), ())), preferred_element_type=jnp.float32)


def dot_tokens(a, b):
    return lax.dot_general(a, b, (((0,), (0,)), ((), ())), preferred_element_type=jnp.float32)


def dot_plain(a, b):
    return jnp.dot(a, b, preferred_element_type=jnp.float32)


class TokenExchange:
    def __init__(self, place, send, recv):
        self.place, self.send, self.recv = place, send, recv
        self.count = 0
        self.sends = []

    def go(self, src, dst, target):
        copy = remote(src, dst, self.send.at[self.count], self.recv.at[self.count], target)
        self.count += 1
        copy.start()
        self.sends.append(copy)
        return copy

    def blocks(self, cc):
        c, y, x, z = self.place

        def block(yy, xx):
            return (2 * cc + yy) * 2 + xx

        return (block(y, x), block(y, 1 - x), block(1 - y, x), block(1 - y, 1 - x))

    def start_near(self, src, full):
        c, y, x, z = self.place
        self.full = full
        me = self.blocks(c)[0]
        self.from_x = self.go(src, full.at[me], device_at(c, y, 1 - x, z))
        self.from_core = [self.go(src, full.at[me], device_at(1 - c, y, x, z))]

    def start_far(self, src):
        c, y, x, z = self.place
        self.from_y = self.go(src, self.full.at[self.blocks(c)[0]], device_at(c, 1 - y, x, z))

    def relay_x(self):
        c, y, x, z = self.place
        full = self.full
        near_x = self.blocks(c)[1]
        lower = pl.ds(full.shape[1] - full.shape[1] // 4, full.shape[1] // 4)
        self.from_x.wait_recv()
        self.second = self.go(
            full.at[near_x, lower], full.at[near_x, lower], device_at(c, 1 - y, x, z)
        )
        self.from_core.append(
            self.go(full.at[near_x], full.at[near_x], device_at(1 - c, y, x, z))
        )

    def relay_y(self):
        c, y, x, z = self.place
        full = self.full
        near_y = self.blocks(c)[2]
        upper = pl.ds(0, full.shape[1] - full.shape[1] // 4)
        self.from_y.wait_recv()
        first = self.go(full.at[near_y, upper], full.at[near_y, upper], device_at(c, y, 1 - x, z))
        self.from_core.append(
            self.go(full.at[near_y], full.at[near_y], device_at(1 - c, y, x, z))
        )
        self.corner = (first, self.second)

    def relay_corner(self):
        c, y, x, z = self.place
        far = self.blocks(c)[3]
        for copy in self.corner:
            copy.wait_recv()
        self.from_core.append(
            self.go(self.full.at[far], self.full.at[far], device_at(1 - c, y, x, z))
        )

    def wait_core(self, index):
        self.from_core[index].wait_recv()

    def finish(self):
        for copy in self.sends:
            copy.wait_send()


def column_block(part, at):
    return pl.ds(pl.multiple_of(at, part), part)


TILE = 256


def front_kernel(
    hid,
    ints,
    vec,
    wm,
    unit_cos,
    unit_sin,
    row_cos,
    row_sin,
    cot,
    we,
    wo_src,
    wc_src,
    hid_all,
    ints_all,
    vec_all,
    wm_all,
    cot_all,
    we_all,
    got,
    active,
    grad_expanded,
    feed_grad,
    sums,
    second,
    slope,
    heads,
    grad_heads,
    wo,
    wc,
    units,
    rotated,
    send,
    recv,
    cot_send,
    cot_recv,
    head_send,
    head_recv,
    local,
    head_local,
):
    place = place_here()
    c, y, x, z = place
    core = device_at(1 - c, y, x, z)
    over_x = device_at(c, y, 1 - x, z)
    over_y = device_at(c, 1 - y, x, z)
    lanes = wm_all.shape[2] // 3
    width = wm.shape[1] // 3
    half = wm.shape[0]
    ff = we_all.shape[2]
    tokens = hid.shape[0]
    inner = 2 * x + c
    own = 4 * y + inner
    other = 4 * (1 - y) + inner
    me = (2 * c + y) * 2 + x
    moved = []

    def keep(src, dst):
        copy = pltpu.make_async_copy(src, dst, local.at[len(moved)])
        copy.start()
        moved.append(copy)

    def rows_of(src, dst):
        count = dst.shape[0]
        return src.at[pl.ds(pl.multiple_of(inner * count, count), count)]

    keep(hid, hid_all.at[me])
    keep(ints, ints_all.at[2 * c + y])
    keep(vec, vec_all.at[y])
    for j in range(3):
        keep(
            wm.at[:, column_block(lanes, j * width + own * lanes)],
            wm_all.at[y, :, pl.ds(j * lanes, lanes)],
        )
    early = len(moved)
    keep(we.at[:, column_block(ff, own * ff)], we_all.at[y])
    keep(cot, cot_all.at[me])
    keep(rows_of(wo_src, wo), wo)
    keep(rows_of(wc_src, wc), wc)
    peers = [lax.rem(z + d, LINE) for d in range(1, LINE)]
    greet([device_at(c, y, x, peer) for peer in peers] + [core, over_x, over_y])
    tokens_move = TokenExchange(place, send, recv)
    go = tokens_move.go
    ints_y = go(ints, ints_all.at[2 * c + y], over_y)
    vec_y = go(vec, vec_all.at[y], over_y)
    ints_core = [go(ints, ints_all.at[2 * c + y], core)]
    tokens_move.start_near(hid, hid_all)
    tokens_move.start_far(hid)
    weights = [
        go(
            wm.at[:, column_block(lanes, j * width + other * lanes)],
            wm_all.at[y, :, pl.ds(j * lanes, lanes)],
            over_y,
        )
        for j in range(3)
    ]
    ints_y.wait_recv()
    ints_core.append(go(ints_all.at[2 * c + 1 - y], ints_all.at[2 * c + 1 - y], core))
    vec_y.wait_recv()
    for copy in moved[:early]:
        copy.wait()
    for copy in ints_core:
        copy.wait_recv()
    to_units = pltpu.make_async_copy(ints_all, units, local.at[0])
    to_units.start()
    to_units.wait()

    def vector(row):
        return jnp.concatenate(
            [vec_all[h, row + i : row + i + 1, :] for h in range(2) for i in range(4)], axis=1
        )

    gain_one, shift_one, gain_two, shift_two = [vector(4 * i) for i in range(4)]
    bias = []
    for j in range(3):
        at = j * GROUP + own
        bias.append(vec_all[at // 12, pl.ds(16 + lax.rem(at, 12), 1), :])
    bias = jnp.concatenate(bias, axis=1)
    expand_bias = jnp.concatenate(
        [vec_all[y, pl.ds(32 + 4 * inner + i, 1), :] for i in range(4)], axis=1
    )
    unit_index = lax.broadcasted_iota(jnp.int32, unit_cos.shape, 0)
    lane = lax.rem(lax.broadcasted_iota(jnp.int32, row_cos.shape, 1), HEAD)

    def project(block):
        rows = pl.ds(pl.multiple_of(block * tokens, tokens), tokens)
        sequence, side = block // 2, lax.rem(block, 2)
        raw = hid_all[block].astype(jnp.float32)
        mean = jnp.mean(raw, axis=1, keepdims=True)
        centred = raw - mean
        rstd = lax.rsqrt(jnp.mean(centred * centred, axis=1, keepdims=True) + EPS)
        xhat = centred * rstd
        second[rows, :] = (xhat * gain_two + shift_two).astype(jnp.bfloat16)
        normed = (xhat * gain_one + shift_one).astype(jnp.bfloat16)
        merged = (
            dot_plain(normed[:, :half], wm_all[0])
            + dot_plain(normed[:, half:], wm_all[1])
            + bias
        )
        count = tokens // UNIT
        for u in range(count):
            unit = units[sequence, 0, (2 * z + side) * count + u]
            here = pl.ds(u * UNIT, UNIT)
            chosen = unit_index == unit
            base_cos = jnp.sum(jnp.where(chosen, unit_cos[...], 0.0), axis=0, keepdims=True)
            base_sin = jnp.sum(jnp.where(chosen, unit_sin[...], 0.0), axis=0, keepdims=True)
            sine = base_sin * row_cos[...] + base_cos * row_sin[...]
            rotated[0, here, :] = base_cos * row_cos[...] - base_sin * row_sin[...]
            rotated[1, here, :] = jnp.where(lane < HALF, sine, 0.0)
            rotated[2, here, :] = jnp.where(lane < HALF, 0.0, sine)
        for j in range(2):
            values = merged[:, j * lanes : (j + 1) * lanes]
            turned = (
                values * rotated[0]
                - pltpu.roll(values, lanes - HALF, 1) * rotated[1]
                + pltpu.roll(values, HALF, 1) * rotated[2]
            )
            heads[j, rows, :] = turned.astype(jnp.bfloat16)
        heads[2, rows, :] = merged[:, 2 * lanes :].astype(jnp.bfloat16)

    span = got.shape[2]

    def rows_at(sequence):
        return pl.ds(pl.multiple_of(sequence * span, span), span)

    def head_copy(kind, sequence, sender):
        if kind == 0:
            src, dst = heads.at[:, rows_at(sequence)], got.at[pl.ds(0, 3), sender]
        else:
            src, dst = grad_heads.at[rows_at(sequence)], got.at[3, sender]
        return remote(
            src,
            dst,
            head_send.at[kind, sequence],
            head_recv.at[kind, sender],
            device_at(c, y, x, sequence),
        )

    def head_keep(kind):
        if kind == 0:
            src, dst = heads.at[:, rows_at(z)], got.at[pl.ds(0, 3), z]
        else:
            src, dst = grad_heads.at[rows_at(z)], got.at[3, z]
        return pltpu.make_async_copy(src, dst, head_local.at[kind])

    def send_heads(kind, sequence):
        @pl.when(sequence == z)
        def _():
            head_keep(kind).start()

        @pl.when(sequence != z)
        def _():
            head_copy(kind, sequence, z).start()

    tokens_move.relay_x()
    tokens_move.relay_y()
    cots_move = TokenExchange(place, cot_send, cot_recv)
    weight = cots_move.go(we.at[:, column_block(ff, other * ff)], we_all.at[y], over_y)
    cots_move.start_near(cot, cot_all)
    for copy in weights:
        copy.wait_recv()
    mine, theirs = tokens_move.blocks(c), tokens_move.blocks(1 - c)
    project(mine[0])
    project(mine[1])
    send_heads(0, mine[0] // 2)
    for index in range(2):
        tokens_move.wait_core(index)
        project(theirs[index])
    send_heads(0, theirs[0] // 2)
    project(mine[2])
    tokens_move.relay_corner()
    tokens_move.wait_core(2)
    project(theirs[2])
    project(mine[3])
    send_heads(0, mine[2] // 2)
    cots_move.relay_x()
    tokens_move.wait_core(3)
    project(theirs[3])
    send_heads(0, theirs[2] // 2)
    weight.wait_send()
    cots_move.sends = cots_move.sends[1:]
    cots_move.start_far(cot)
    for copy in moved[early:]:
        copy.wait()
    sums[...] = jnp.zeros_like(sums)

    def project_back(block):
        at = pl.ds(pl.multiple_of(block * tokens, tokens), tokens)
        grad_heads[at, :] = dot_rows(cot_all[block], wo[...]).astype(jnp.bfloat16)

    def forward(block, carry):
        at = pl.ds(pl.multiple_of(block * tokens, tokens), tokens)
        normed = second[at, :]
        expanded = (
            dot_plain(normed[:, :half], we_all[0])
            + dot_plain(normed[:, half:], we_all[1])
            + expand_bias
        )
        below = 0.5 * (1.0 + lax.erf(expanded * math.sqrt(0.5)))
        density = jnp.exp(expanded * expanded * -0.5) * (1.0 / math.sqrt(2.0 * math.pi))
        active[at, :] = (expanded * below).astype(jnp.bfloat16)
        slope[at, :] = below + expanded * density
        return carry

    def backward(block):
        at = pl.ds(pl.multiple_of(block * tokens, tokens), tokens)
        grad = (dot_rows(cot_all[block], wc[...]) * slope[at, :]).astype(jnp.bfloat16)
        grad_expanded[at, :] = grad
        sums[...] += jnp.sum(grad.astype(jnp.float32), axis=0, keepdims=True)

    project_back(mine[0])
    project_back(mine[1])
    send_heads(1, mine[0] // 2)
    for index in range(2):
        cots_move.wait_core(index)
        project_back(theirs[index])
    send_heads(1, theirs[0] // 2)
    weight.wait_recv()
    lax.fori_loop(0, GROUP, forward, 0)
    backward(mine[0])
    backward(mine[1])
    cots_move.relay_y()
    backward(theirs[0])
    backward(theirs[1])
    project_back(mine[2])
    cots_move.wait_core(2)
    project_back(theirs[2])
    backward(mine[2])
    backward(theirs[2])
    cots_move.relay_corner()
    project_back(mine[3])
    send_heads(1, mine[2] // 2)
    cots_move.wait_core(3)
    project_back(theirs[3])
    send_heads(1, theirs[2] // 2)
    backward(mine[3])
    backward(theirs[3])
    for index in range(2 * half // TILE):
        block = dot_tokens(second[:, pl.ds(index * TILE, TILE)], grad_expanded[...])
        side, row = divmod(index * TILE, half)
        feed_grad[pl.ds(row, TILE), pl.ds(side * ff, ff)] = block.astype(jnp.bfloat16)
    cots = cot_all[...].reshape(GROUP * tokens, 2 * half)
    for index in range(ff // TILE):
        block = dot_tokens(active[:, pl.ds(index * TILE, TILE)], cots)
        feed_grad[pl.ds(index * TILE, TILE), pl.ds(2 * ff, 2 * half)] = block.astype(jnp.bfloat16)
    tokens_move.finish()
    cots_move.finish()
    for kind in range(2):
        head_keep(kind).wait()
        for peer in peers:
            head_copy(kind, peer, z).wait_send()
            head_copy(kind, peer, peer).wait_recv()


def front(hid, ints, vec, wm, tables, cot, we, wo, wc):
    tokens, width = hid.shape
    rows = wm.shape[0]
    lanes = width // GROUP
    ff = we.shape[1] // GROUP
    total = GROUP * tokens
    vmem = pl.BlockSpec(memory_space=pltpu.VMEM)
    any_spec = pl.BlockSpec(memory_space=pl.ANY)
    return pl.pallas_call(
        front_kernel,
        out_shape=(
            jax.ShapeDtypeStruct((GROUP,) + hid.shape, hid.dtype),
            jax.ShapeDtypeStruct((4,) + ints.shape, ints.dtype),
            jax.ShapeDtypeStruct((2,) + vec.shape, vec.dtype),
            jax.ShapeDtypeStruct((2, rows, 3 * lanes), wm.dtype),
            jax.ShapeDtypeStruct((GROUP,) + cot.shape, cot.dtype),
            jax.ShapeDtypeStruct((2, rows, ff), we.dtype),
            jax.ShapeDtypeStruct((4, LINE, total // LINE, lanes), jnp.bfloat16),
            jax.ShapeDtypeStruct((total, ff), jnp.bfloat16),
            jax.ShapeDtypeStruct((total, ff), jnp.bfloat16),
            jax.ShapeDtypeStruct((width // 2, 2 * ff + width), jnp.bfloat16),
            jax.ShapeDtypeStruct((1, ff), jnp.float32),
        ),
        in_specs=[any_spec] * 4 + [vmem] * 4 + [any_spec] * 4,
        out_specs=[vmem, any_spec, vmem, vmem, vmem, vmem, any_spec] + [vmem] * 4,
        scratch_shapes=[
            pltpu.VMEM((total, width), jnp.bfloat16),
            pltpu.VMEM((total, ff), jnp.float32),
            pltpu.VMEM((3, total, lanes), jnp.bfloat16),
            pltpu.VMEM((total, lanes), jnp.bfloat16),
            pltpu.VMEM((lanes, width), jnp.bfloat16),
            pltpu.VMEM((ff, width), jnp.bfloat16),
            pltpu.SMEM((4,) + ints.shape, jnp.int32),
            pltpu.VMEM((3, tokens, lanes), jnp.float32),
            pltpu.SemaphoreType.DMA((20,)),
            pltpu.SemaphoreType.DMA((20,)),
            pltpu.SemaphoreType.DMA((12,)),
            pltpu.SemaphoreType.DMA((12,)),
            pltpu.SemaphoreType.DMA((2, LINE)),
            pltpu.SemaphoreType.DMA((2, LINE)),
            pltpu.SemaphoreType.DMA((10,)),
            pltpu.SemaphoreType.DMA((2,)),
        ],
        compiler_params=pltpu.CompilerParams(
            collective_id=0, has_side_effects=True, vmem_limit_bytes=56 << 20
        ),
        name="front",
    )(hid, ints, vec, wm, *tables, cot, we, wo, wc)


class LineSum:
    KINDS = 9

    def __init__(self, grad, result, inbox, sems, swap, size, lag, place):
        self.grad, self.result, self.inbox, self.sems, self.swap = grad, result, inbox, sems, swap
        self.c, self.y, self.x, self.z = place
        self.size = size
        self.count = grad.shape[0] // size
        self.split = (self.count + 1) // 2
        self.lag = lag
        self.slots = self.split + 6 * lag

    def rows(self, chunk):
        return pl.ds(pl.multiple_of(chunk * self.size, self.size), self.size)

    def moves(self, chunk, half):
        c, y, x, z = self.c, self.y, self.x, self.z
        up = 1 if half == 0 else -1
        rows = self.rows(chunk)
        grad, result, swap = self.grad, self.result, self.swap
        mine = result.at[c, x, rows]
        beside = result.at[c, 1 - x, rows]
        lower, upper = device_at(c, y, x, z - up), device_at(c, y, x, z + up)

        def lanes(which):
            return pl.ds(pl.multiple_of(which * swap, swap), swap)

        makers = {
            "near": (0, lambda: (grad.at[rows], self.inbox.at[0, rows], upper)),
            "far": (1, lambda: (grad.at[rows], self.inbox.at[1, rows], lower)),
            "swap": (
                2,
                lambda: (
                    grad.at[rows, lanes(1 - y)],
                    result.at[c, x, rows, lanes(y)],
                    device_at(c, 1 - y, x, z),
                ),
            ),
            "down": (3, lambda: (mine, mine, lower)),
            "out": (4, lambda: (mine, mine, upper)),
            "side": (5, lambda: (mine, mine, device_at(c, y, 1 - x, z))),
            "core": (6, lambda: (mine, mine, device_at(1 - c, y, x, z))),
            "late": (7, lambda: (beside, beside, device_at(1 - c, y, x, z))),
        }

        def make(name):
            kind, parts = makers[name]
            src, dst, target = parts()
            return remote(
                src, dst, self.sems.at[2 * kind, chunk], self.sems.at[2 * kind + 1, chunk], target
            )

        return make

    def keeps(self, chunk):
        rows, swap = self.rows(chunk), self.swap
        own = pl.ds(pl.multiple_of(self.y * swap, swap), swap)
        plain = pl.ds(2 * swap, self.grad.shape[1] - 2 * swap)
        return [
            pltpu.make_async_copy(
                self.grad.at[rows, lanes],
                self.result.at[self.c, self.x, rows, lanes],
                self.sems.at[2 * self.KINDS - 2 + index, chunk],
            )
            for index, lanes in enumerate((own, plain))
        ]

    def slot(self, t):
        for half in range(2):
            self.half_slot(t, half)

    def extent(self, half):
        size = self.split if half == 0 else self.count - self.split
        base = 0 if half == 0 else self.split
        at = self.z if half == 0 else LINE - 1 - self.z
        return (size, base, at)

    def half_slot(self, t, half):
        size, base, at = self.extent(half)
        lag = self.lag
        swap = self.swap
        owner = at == 1

        def event(delay, run):
            chunk = t - delay
            index = jnp.clip(chunk, 0, size - 1) + base

            @pl.when((chunk >= 0) & (chunk < size))
            def _():
                run(index, self.moves(index, half))

        def reduce(index, moves):
            rows = self.rows(index)

            @pl.when(at == 0)
            def _():
                moves("near").start()

            @pl.when(at == 2)
            def _():
                moves("far").wait_recv()
                total = self.grad[rows].astype(jnp.float32) + self.inbox[1, rows].astype(
                    jnp.float32
                )
                self.grad[rows] = total.astype(jnp.bfloat16)

            @pl.when(at >= 2)
            def _():
                moves("far").start()

            @pl.when(owner)
            def _():
                moves("near").wait_recv()
                moves("far").wait_recv()
                total = (
                    self.grad[rows].astype(jnp.float32)
                    + self.inbox[0, rows].astype(jnp.float32)
                    + self.inbox[1, rows].astype(jnp.float32)
                )
                self.grad[rows] = total.astype(jnp.bfloat16)
                moves("swap").start()
                for copy in self.keeps(index):
                    copy.start()

        event(jnp.where(owner, 2 * lag, jnp.where(at == 2, lag, 0)), reduce)

        def spread(index, moves):
            @pl.when(owner)
            def _():
                moves("swap").wait_recv()
                for copy in self.keeps(index):
                    copy.wait()
                moves("down").start()

            @pl.when(at == 0)
            def _():
                moves("down").wait_recv()

            @pl.when(at >= 2)
            def _():
                moves("out").wait_recv()

            @pl.when((at == 1) | (at == 2))
            def _():
                moves("out").start()

            moves("side").start()
            moves("core").start()

        wait = jnp.where(owner, 3 * lag, jnp.where(at == 3, 5 * lag, 4 * lag))
        event(wait, spread)

        def late(index, moves):
            moves("side").wait_recv()
            moves("late").start()

        event(wait + lag, late)

    def drain(self):
        for half in range(2):
            size, base, at = self.extent(half)

            def finish(chunk, carry):
                moves = self.moves(chunk + base, half)

                @pl.when(at == 0)
                def _():
                    moves("near").wait_send()

                @pl.when(at >= 2)
                def _():
                    moves("far").wait_send()

                @pl.when(at == 1)
                def _():
                    moves("swap").wait_send()
                    moves("down").wait_send()

                @pl.when((at == 1) | (at == 2))
                def _():
                    moves("out").wait_send()

                moves("side").wait_send()
                moves("core").wait()
                moves("late").wait()
                return carry

            lax.fori_loop(0, size, finish, 0)


def sort_kernel(order, src, dst, *, units):
    for unit in range(units):
        dst[:, order[0, unit]] = src[:, unit]


def sort_units(order, array, units):
    shape = array.shape
    vmem = pl.BlockSpec(memory_space=pltpu.VMEM)
    view = (shape[0], units, UNIT, shape[-1])
    return pl.pallas_call(
        functools.partial(sort_kernel, units=units),
        out_shape=jax.ShapeDtypeStruct(view, array.dtype),
        in_specs=[pl.BlockSpec(memory_space=pltpu.SMEM), vmem],
        out_specs=vmem,
        compiler_params=pltpu.CompilerParams(vmem_limit_bytes=16 << 20),
        name="sort_units",
    )(order, array.reshape(view))


def middle_kernel(
    ints,
    sorted_parts,
    unit_cos,
    unit_sin,
    row_cos,
    row_sin,
    feed_grad,
    active_src,
    grad_expanded_src,
    we_src,
    wc_src,
    wm_src,
    wo_src,
    hidden_src,
    cots_src,
    vectors,
    feed_sums,
    feed_all,
    attn_all,
    output,
    input_gradient,
    done,
    feed_own,
    feed_inbox,
    parts,
    attn_own,
    attn_inbox,
    near,
    beside,
    far,
    totals,
    send,
    recv,
    feed_sems,
    attn_sems,
    near_sems,
    beside_sems,
    far_sems,
    local,
    loads,
    *,
    units,
    pieces,
    feed_swap,
    swap,
):
    place = place_here()
    c, y, x, z = place
    core = device_at(1 - c, y, x, z)
    over_x = device_at(c, y, 1 - x, z)
    over_y = device_at(c, 1 - y, x, z)
    inner = 2 * x + c

    def rows_of(src, dst):
        count = dst.shape[0]
        return src.at[pl.ds(pl.multiple_of(inner * count, count), count)]

    first_load = pltpu.make_async_copy(feed_grad, feed_own, loads.at[8])
    first_load.start()
    peers = [lax.rem(z + d, LINE) for d in range(1, LINE)]
    greet([device_at(c, y, x, peer) for peer in peers] + [core, over_x, over_y])
    first_load.wait()
    line = LineSum(feed_own, feed_all, feed_inbox, feed_sems, feed_swap, FEED_CHUNK, 2, place)
    lanes = done.shape[2]
    rows = done.shape[1] // LINE
    mine = pl.ds(pl.multiple_of(z * rows, rows), rows)

    def gather(index, which):
        peer = peers[index]
        return remote(
            done.at[which, pl.ds(pl.multiple_of(peer * rows, rows), rows)],
            parts.at[mine, pl.ds(which * lanes, lanes)],
            send.at[index, which],
            recv.at[index, which],
            device_at(c, y, x, peer),
        )

    def gather_own(which):
        return pltpu.make_async_copy(
            done.at[which, mine], parts.at[mine, pl.ds(which * lanes, lanes)], local.at[which]
        )

    def attention_phase(
        masked, flat, scores, slopes, key_sum, value_sum, mixed_sum, query_sum
    ):
        length = sorted_parts.shape[1]
        scale = 1.0 / math.sqrt(HEAD)
        blocks = length // SPAN
        lanes = lax.broadcasted_iota(jnp.int32, (UNIT, 2 * HEAD), 1)
        lower = lanes < HEAD

        def arrange(index, carry):
            @pl.when(lax.rem(index, 8) == 0)
            def _():
                line.slot(lax.div(index, 8))

            at = pl.ds(pl.multiple_of(index * UNIT, UNIT), UNIT)
            for which in range(4):
                rows = sorted_parts[which, at, :].astype(jnp.float32)
                if which == 0:
                    rows = rows * scale
                masked[which, 0, at, :] = jnp.where(lower, rows, 0.0).astype(jnp.bfloat16)
                masked[which, 1, at, :] = jnp.where(lower, 0.0, rows).astype(jnp.bfloat16)
                flat[which, :, at] = rows.T.astype(jnp.bfloat16)
            return carry

        lax.fori_loop(0, units, arrange, 0)
        early = -(-units // 8)
        key_sum[...] = jnp.zeros_like(key_sum)
        value_sum[...] = jnp.zeros_like(value_sum)

        def labels(positions):
            found = jnp.full(positions.shape, -1, jnp.int32)
            for piece in range(pieces):
                start = ints[0, units + piece]
                found = jnp.where(
                    (positions >= start) & (positions < start + PIECE), piece, found
                )
            return found

        def dot(a, b):
            return jnp.dot(a, b, preferred_element_type=jnp.float32)

        for block in range(blocks):
            begin = block * SPAN
            last = SPAN + (UNIT if block + 1 < blocks else 0)
            columns = pl.ds(begin, SPAN)
            row_at = begin + lax.broadcasted_iota(jnp.int32, (1, SPAN), 1)
            col_at = begin + lax.broadcasted_iota(jnp.int32, (last, 1), 0)
            row_lab = labels(row_at)
            col_lab = labels(col_at)
            allowed = (col_at <= row_at) | (
                (col_lab == row_lab) & (row_lab >= 0)
            )

            def one_head(head, carry):
                start_tick = 3 * block * (block + 1) + head * 3 * (block + 1)

                def tick(index):
                    at = start_tick + index

                    @pl.when(lax.rem(at, EVERY) == 0)
                    def _():
                        line.slot(early + lax.div(at, EVERY))

                queries = flat[0, :, columns]
                grads = flat[3, :, columns]
                side = pl.ds(pl.multiple_of(head * HEAD, HEAD), HEAD)

                def score_tile(start, size, top, mask=None):
                    rows = pl.ds(start, size)
                    tile = dot(masked[1, head, rows, :], queries)
                    if mask is not None:
                        tile = jnp.where(mask, tile, NEGATIVE)
                    scores[rows, :] = tile
                    return jnp.maximum(top, jnp.max(tile, axis=0, keepdims=True))

                def tile_step(step, run, j, carry):
                    tick(step * (block + 1) + j)
                    start = pl.multiple_of(j * SPAN, SPAN)
                    return run(start, SPAN, carry)

                top = lax.fori_loop(
                    0,
                    block,
                    functools.partial(tile_step, 0, score_tile),
                    jnp.full((1, SPAN), NEGATIVE, jnp.float32),
                )
                tick(block)
                top = score_tile(begin, last, top, allowed)

                def weight_tile(start, size, sums):
                    total, delta = sums
                    rows = pl.ds(start, size)
                    weights = jnp.exp(scores[rows, :] - top)
                    slope = dot(masked[2, head, rows, :], grads)
                    scores[rows, :] = weights
                    slopes[rows, :] = slope
                    return (
                        total + jnp.sum(weights, axis=0, keepdims=True),
                        delta + jnp.sum(weights * slope, axis=0, keepdims=True),
                    )

                zero = jnp.zeros((1, SPAN), jnp.float32)
                sums = lax.fori_loop(
                    0,
                    block,
                    functools.partial(tile_step, 1, weight_tile),
                    (zero, zero),
                )
                tick(2 * block + 1)
                total, delta = weight_tile(begin, last, sums)
                inverse = 1.0 / total
                delta = delta * inverse

                def grad_tile(start, size, sums):
                    mixed, query = sums
                    rows = pl.ds(start, size)
                    probs = scores[rows, :] * inverse
                    grad = (probs * (slopes[rows, :] - delta)).astype(jnp.bfloat16)
                    probs = probs.astype(jnp.bfloat16)
                    value_sum[rows, :] += dot(probs, masked[3, head, columns, :])
                    key_sum[rows, :] += dot(grad, masked[0, head, columns, :])
                    mixed = mixed + dot(flat[2, side, rows], probs)
                    query = query + dot(flat[1, side, rows], grad)
                    return (mixed, query)

                none = jnp.zeros((HEAD, SPAN), jnp.float32)
                sums = lax.fori_loop(
                    0,
                    block,
                    functools.partial(tile_step, 2, grad_tile),
                    (none, none),
                )
                tick(3 * block + 2)
                mixed, query = grad_tile(begin, last, sums)
                mixed_sum[side, columns] = mixed
                query_sum[side, columns] = query * scale
                return carry

            lax.fori_loop(0, 2, one_head, 0)

        lane = lax.rem(lax.broadcasted_iota(jnp.int32, row_cos.shape, 1), HEAD)
        ticked = early - (-3 * blocks * (blocks + 1) // EVERY)

        def finish(index, carry):
            @pl.when(lax.rem(index, 8) == 0)
            def _():
                line.slot(ticked + lax.div(index, 8))

            at = pl.ds(pl.multiple_of(index * UNIT, UNIT), UNIT)
            base_cos, base_sin = unit_cos[pl.ds(index, 1), :], unit_sin[pl.ds(index, 1), :]
            cosine = base_cos * row_cos[...] - base_sin * row_sin[...]
            sine = base_sin * row_cos[...] + base_cos * row_sin[...]
            sine_up = jnp.where(lane < HALF, sine, 0.0)
            sine_down = jnp.where(lane < HALF, 0.0, sine)

            def turn_back(rows):
                up = pltpu.roll(rows, 2 * HEAD - HALF, 1)
                down = pltpu.roll(rows, HALF, 1)
                return rows * cosine + up * sine_up - down * sine_down

            masked[0, 0, at, :] = mixed_sum[:, at].T.astype(jnp.bfloat16)
            masked[1, 0, at, :] = turn_back(query_sum[:, at].T).astype(jnp.bfloat16)
            masked[2, 0, at, :] = turn_back(key_sum[at, :]).astype(jnp.bfloat16)
            masked[3, 0, at, :] = value_sum[at, :].astype(jnp.bfloat16)
            return carry

        lax.fori_loop(0, units, finish, 0)
        ticked += -(-units // 8)

        def restore(owner):
            for index in range(units // LINE):
                unit = owner * (units // LINE) + index
                here = pl.ds(pl.multiple_of(unit * UNIT, UNIT), UNIT)
                place = ints[0, unit]
                for which in range(4):
                    rows = masked[which, 0, pl.ds(0, UNIT), :]
                    for other in range(1, units):
                        rows = jnp.where(
                            place == other, masked[which, 0, pl.ds(other * UNIT, UNIT), :], rows
                        )
                    done[which, here, :] = rows

        for index, peer in enumerate(peers):
            restore(peer)
            for which in (1, 2, 3, 0):
                gather(index, which).start()
        restore(z)
        for which in range(4):
            gather_own(which).start()


    length = sorted_parts.shape[1]
    ticked = (
        2 * -(-units // 8) - (-3 * (length // SPAN) * (length // SPAN + 1) // EVERY)
    )
    pl.run_scoped(
        attention_phase,
        pltpu.VMEM((4, 2, length, 2 * HEAD), jnp.bfloat16),
        pltpu.VMEM((4, 2 * HEAD, length), jnp.bfloat16),
        pltpu.VMEM((length, SPAN), jnp.float32),
        pltpu.VMEM((length, SPAN), jnp.float32),
        pltpu.VMEM((length, 2 * HEAD), jnp.float32),
        pltpu.VMEM((length, 2 * HEAD), jnp.float32),
        pltpu.VMEM((2 * HEAD, length), jnp.float32),
        pltpu.VMEM((2 * HEAD, length), jnp.float32),
    )

    def close_phase(
        stats,
        outs,
        terms,
        single,
        active,
        grad_expanded,
        we,
        wc,
        wm,
        wo,
        hidden,
        cots,
        own_hidden,
    ):
        sources = (
            (hidden_src, hidden),
            (grad_expanded_src, grad_expanded),
            (we_src, we),
            (active_src, active),
            (rows_of(wc_src, wc), wc),
            (cots_src, cots),
            (wm_src, wm),
            (rows_of(wo_src, wo), wo),
        )
        fetched = []
        for index, (src, dst) in enumerate(sources):
            copy = pltpu.make_async_copy(src, dst, loads.at[index])
            copy.start()
            fetched.append(copy)
        gain_one, shift_one, gain_two = vectors[0:1, :], vectors[1:2, :], vectors[2:3, :]
        width = hidden.shape[1]
        half = width // 2
        totals[...] = jnp.zeros_like(totals)
        for copy in fetched:
            copy.wait()

        def before(index, carry):
            at = pl.ds(pl.multiple_of(index * TILE, TILE), TILE)
            raw = hidden[at, :].astype(jnp.float32)
            mean = jnp.mean(raw, axis=1, keepdims=True)
            centred = raw - mean
            rstd = lax.rsqrt(jnp.mean(centred * centred, axis=1, keepdims=True) + EPS)
            stats[at, 0:1] = mean
            stats[at, 1:2] = rstd
            xhat = centred * rstd
            grad_second = dot_rows(grad_expanded[at, :], we[...])
            terms[index] = (grad_second * gain_two).astype(jnp.bfloat16)
            outs[index] = dot_plain(active[at, :], wc[...]).astype(jnp.bfloat16)
            totals[2:3, :] += jnp.sum(grad_second * xhat, axis=0, keepdims=True)
            totals[3:4, :] += jnp.sum(grad_second, axis=0, keepdims=True)
            totals[4:5, :] += jnp.sum(cots[at, :].astype(jnp.float32), axis=0, keepdims=True)
            return carry

        tiles = hidden.shape[0] // TILE
        lax.fori_loop(0, tiles, before, 0)
        tokens = outs.shape[1]
        own_rows = pl.ds(pl.multiple_of(((2 * c + y) * 2 + x) * tokens, tokens), tokens)
        own_hidden[...] = hidden[own_rows, :]

        for which in range(4):
            gather_own(which).wait()
        for index in range(len(peers)):
            for which in range(4):
                gather(index, which).wait()

        arrays = (outs, terms)

        def block_at(cc, yy, xx):
            return (2 * cc + yy) * 2 + xx

        def to_core(a, yy, xx):
            block = block_at(1 - c, yy, xx)
            return remote(
                arrays[a].at[block],
                near.at[a, yy, xx],
                near_sems.at[0, a, yy, xx],
                near_sems.at[1, a, yy, xx],
                core,
            )

        ways = ((y, x, over_y, over_x), (x, y, over_x, over_y))

        def own_block(a, near_at, far_at):
            yy, xx = (near_at, far_at) if a == 0 else (far_at, near_at)
            return block_at(c, yy, xx)

        def hop_one(a, index):
            near_axis, far_axis, target, beyond = ways[a]
            return remote(
                arrays[a].at[own_block(a, 1 - near_axis, index)],
                beside.at[a, index],
                beside_sems.at[0, a, index],
                beside_sems.at[1, a, index],
                target,
            )

        def hop_two(a):
            return remote(
                single.at[a], far.at[a], far_sems.at[0, a], far_sems.at[1, a], ways[a][3]
            )

        def after(index):
            at = pl.ds(pl.multiple_of(index * TILE, TILE), TILE)
            grads = parts[at, pl.ds(lanes, 3 * lanes)]
            grad_first = dot_rows(grads, wm[...])
            xhat = (hidden[at, :].astype(jnp.float32) - stats[at, 0:1]) * stats[at, 1:2]
            hidden[at, :] = (xhat * gain_one + shift_one).astype(jnp.bfloat16)
            terms[index] = (terms[index].astype(jnp.float32) + grad_first * gain_one).astype(
                jnp.bfloat16
            )
            outs[index] = (
                outs[index].astype(jnp.float32) + dot_plain(parts[at, pl.ds(0, lanes)], wo[...])
            ).astype(jnp.bfloat16)
            totals[0:1, :] += jnp.sum(grad_first * xhat, axis=0, keepdims=True)
            totals[1:2, :] += jnp.sum(grad_first, axis=0, keepdims=True)
            totals[5:6, pl.ds(0, 3 * lanes)] += jnp.sum(
                grads.astype(jnp.float32), axis=0, keepdims=True
            )

        def others(step, carry):
            line.slot(ticked + step)
            yy, xx = lax.rem(1 - y + step // 2, 2), lax.rem(step, 2)
            after(block_at(1 - c, yy, xx))
            for a in range(2):
                to_core(a, yy, xx).start()
            return carry

        lax.fori_loop(0, 4, others, 0)

        def ours(step, carry):
            line.slot(ticked + 4 + step)
            yy, xx = lax.rem(1 - y + step // 2, 2), lax.rem(step, 2)
            after(block_at(c, yy, xx))
            for a in range(2):
                to_core(a, yy, xx).wait_recv()
                block = block_at(c, yy, xx)
                total = arrays[a][block].astype(jnp.float32) + near[a, yy, xx].astype(jnp.float32)
                arrays[a][block] = total.astype(jnp.bfloat16)
                near_at, far_at = (yy, xx) if a == 0 else (xx, yy)

                @pl.when(near_at != ways[a][0])
                def _():
                    hop_one(a, far_at).start()

            return carry

        lax.fori_loop(0, 4, ours, 0)
        later = ticked + 8
        for index in range(width // TILE):
            line.slot(later + index)
            block = dot_tokens(hidden[:, pl.ds(index * TILE, TILE)], parts[:, pl.ds(lanes, 3 * lanes)])
            side, row = divmod(index * TILE, half)
            attn_own[pl.ds(row, TILE), pl.ds(side * swap, swap)] = block.astype(jnp.bfloat16)
        block = dot_tokens(parts[:, pl.ds(0, lanes)], cots[...]).astype(jnp.bfloat16)
        wide = 2 * lanes
        for index in range(width // wide):
            attn_own[pl.ds(index * lanes, lanes), pl.ds(2 * swap, wide)] = block[
                :, index * wide : (index + 1) * wide
            ]
        lines = []
        fill = jnp.zeros((1, swap), jnp.float32)
        for index in range(5):
            for begin in range(0, width, swap):
                stop = min(begin + swap, width)
                entry = totals[index : index + 1, begin:stop]
                if stop - begin < swap:
                    entry = jnp.concatenate([entry, fill[:, : swap - (stop - begin)]], axis=1)
                lines.append(entry)
        lines.append(totals[5:6, 0:swap])
        ff = feed_sums.shape[1]
        for begin in range(0, ff, swap):
            stop = min(begin + swap, ff)
            entry = feed_sums[:, begin:stop]
            if stop - begin < swap:
                entry = jnp.concatenate([entry, fill[:, : swap - (stop - begin)]], axis=1)
            lines.append(entry)
        lines += [fill] * (attn_own.shape[0] - half - len(lines))
        small = jnp.concatenate(lines, axis=0).astype(jnp.bfloat16)
        tail = pl.ds(half, attn_own.shape[0] - half)
        attn_own[tail, pl.ds(0, swap)] = small
        attn_own[tail, pl.ds(swap, swap)] = small
        attn_own[tail, pl.ds(2 * swap, wide)] = jnp.zeros((small.shape[0], wide), jnp.bfloat16)

        attn = LineSum(attn_own, attn_all, attn_inbox, attn_sems, swap, CHUNK, 1, place)

        later += width // TILE

        def step(t, carry):
            attn.slot(t)
            line.slot(later + t)
            return carry

        def pass_on(a):
            near_axis, far_axis = ways[a][:2]
            for index in range(2):
                hop_one(a, index).wait()
            single[a] = (
                arrays[a][own_block(a, near_axis, 1 - far_axis)].astype(jnp.float32)
                + beside[a, 1 - far_axis].astype(jnp.float32)
            ).astype(jnp.bfloat16)
            hop_two(a).start()

        middle = attn.slots - 4
        lax.fori_loop(0, middle, step, 0)
        pass_on(0)
        pass_on(1)
        lax.fori_loop(middle, attn.slots, step, 0)
        sums = []
        for a in range(2):
            hop_two(a).wait()
            near_axis, far_axis = ways[a][:2]
            sums.append(
                arrays[a][own_block(a, near_axis, far_axis)].astype(jnp.float32)
                + beside[a, far_axis].astype(jnp.float32)
                + far[a].astype(jnp.float32)
            )
        raw = own_hidden[...].astype(jnp.float32)
        output[...] = (raw + sums[0] + vectors[3:4, :]).astype(jnp.bfloat16)
        rstd = stats[own_rows, 1:2]
        xhat = (raw - stats[own_rows, 0:1]) * rstd
        term = sums[1]
        input_gradient[...] = cots[own_rows, :].astype(jnp.float32) + rstd * (
            term
            - jnp.mean(term, axis=1, keepdims=True)
            - xhat * jnp.mean(term * xhat, axis=1, keepdims=True)
        )

        def sent(step, carry):
            for a in range(2):
                to_core(a, step // 2, lax.rem(step, 2)).wait_send()
            return carry

        lax.fori_loop(0, 4, sent, 0)
        attn.drain()
        line.drain()

    token_rows, width = hidden_src.shape
    ff = active_src.shape[1]
    block = (token_rows // GROUP, width)
    pl.run_scoped(
        close_phase,
        pltpu.VMEM((token_rows, 128), jnp.float32),
        pltpu.VMEM((GROUP,) + block, jnp.bfloat16),
        pltpu.VMEM((GROUP,) + block, jnp.bfloat16),
        pltpu.VMEM((2,) + block, jnp.bfloat16),
        pltpu.VMEM((token_rows, ff), jnp.bfloat16),
        pltpu.VMEM((token_rows, ff), jnp.bfloat16),
        pltpu.VMEM((width, ff), jnp.bfloat16),
        pltpu.VMEM((ff, width), jnp.bfloat16),
        pltpu.VMEM((width, 3 * lanes), jnp.bfloat16),
        pltpu.VMEM((lanes, width), jnp.bfloat16),
        pltpu.VMEM((token_rows, width), jnp.bfloat16),
        pltpu.VMEM((token_rows, width), jnp.bfloat16),
        pltpu.VMEM(block, jnp.bfloat16),
    )


def middle(
    ints,
    sorted_parts,
    tables,
    feed_grad,
    active,
    grad_expanded,
    we,
    wc,
    wm,
    wo,
    hidden,
    cots,
    vectors,
    feed_sums,
    tokens,
    units,
    pieces,
    feed_swap,
):
    rows, width = hidden.shape
    lanes = sorted_parts.shape[2]
    swap = 3 * lanes
    block = (tokens, width)
    vmem = pl.BlockSpec(memory_space=pltpu.VMEM)
    any_spec = pl.BlockSpec(memory_space=pl.ANY)
    grad_shape = (width // 2 + CHUNK, 2 * swap + 2 * lanes)
    scratch = [
        pltpu.VMEM(sorted_parts.shape, jnp.bfloat16),
        pltpu.VMEM(feed_grad.shape, jnp.bfloat16),
        pltpu.VMEM((2,) + feed_grad.shape, jnp.bfloat16),
        pltpu.VMEM((rows, 4 * lanes), jnp.bfloat16),
        pltpu.VMEM(grad_shape, jnp.bfloat16),
        pltpu.VMEM((2,) + grad_shape, jnp.bfloat16),
        pltpu.VMEM((2, 2, 2) + block, jnp.bfloat16),
        pltpu.VMEM((2, 2) + block, jnp.bfloat16),
        pltpu.VMEM((2,) + block, jnp.bfloat16),
        pltpu.VMEM((8, width), jnp.float32),
        pltpu.SemaphoreType.DMA((LINE - 1, 4)),
        pltpu.SemaphoreType.DMA((LINE - 1, 4)),
        pltpu.SemaphoreType.DMA((2 * LineSum.KINDS, feed_grad.shape[0] // FEED_CHUNK)),
        pltpu.SemaphoreType.DMA((2 * LineSum.KINDS, grad_shape[0] // CHUNK)),
        pltpu.SemaphoreType.DMA((2, 2, 2, 2)),
        pltpu.SemaphoreType.DMA((2, 2, 2)),
        pltpu.SemaphoreType.DMA((2, 2)),
        pltpu.SemaphoreType.DMA((4,)),
        pltpu.SemaphoreType.DMA((9,)),
    ]
    return pl.pallas_call(
        functools.partial(
            middle_kernel, units=units, pieces=pieces, feed_swap=feed_swap, swap=swap
        ),
        out_shape=(
            jax.ShapeDtypeStruct((2, 2) + feed_grad.shape, jnp.bfloat16),
            jax.ShapeDtypeStruct((2, 2) + grad_shape, jnp.bfloat16),
            jax.ShapeDtypeStruct(block, jnp.bfloat16),
            jax.ShapeDtypeStruct(block, jnp.float32),
        ),
        in_specs=[pl.BlockSpec(memory_space=pltpu.SMEM)]
        + [vmem] * 5
        + [any_spec] * 9
        + [vmem] * 2,
        out_specs=[any_spec] + [vmem] * 3,
        scratch_shapes=scratch,
        compiler_params=pltpu.CompilerParams(
            collective_id=3, has_side_effects=True, vmem_limit_bytes=61 << 20
        ),
        name="middle",
    )(
        ints,
        sorted_parts,
        *tables,
        feed_grad,
        active,
        grad_expanded,
        we,
        wc,
        wm,
        wo,
        hidden,
        cots,
        vectors,
        feed_sums,
    )


def widen_kernel(
    feed_all,
    attn_all,
    expand,
    contract,
    merged,
    output,
    shared_out,
    merged_sums,
    expand_sums,
    feed,
    attn,
    expand_wide,
    contract_wide,
    merged_wide,
    output_wide,
    loads,
    stores,
    *,
    swap,
    lanes,
    ff,
):
    half = feed.shape[2]
    gets = []
    for index, (src, dst) in enumerate(((feed_all, feed), (attn_all, attn))):
        for part in range(4):
            copy = pltpu.make_async_copy(
                src.at[part // 2, part % 2], dst.at[part // 2, part % 2], loads.at[index, part]
            )
            copy.start()
            gets.append(copy)
    puts = []

    def put(src, dst):
        copy = pltpu.make_async_copy(src, dst, stores.at[len(puts)])
        copy.start()
        puts.append(copy)

    for part in range(4):
        c, x = part // 2, part % 2
        gets[part].wait()
        for y in range(2):
            at = pl.ds((4 * y + 2 * x + c) * ff, ff)
            expand_wide[:, at] = feed[c, x, :, pl.ds(y * ff, ff)].astype(jnp.float32)
            put(expand_wide.at[:, at], expand.at[:, at])
        at = pl.ds((2 * x + c) * ff, ff)
        contract_wide[at, :] = feed[c, x, :, pl.ds(2 * ff, 2 * half)].astype(jnp.float32)
        put(contract_wide.at[at], contract.at[at])
    for copy in gets[4:]:
        copy.wait()
    width = 2 * half
    for j in range(3):
        for octant in range(GROUP):
            c, x, y = octant % 2, octant // 2 % 2, octant // 4
            at = pl.ds(j * width + octant * lanes, lanes)
            merged_wide[:, at] = attn[
                c, x, pl.ds(0, half), pl.ds(y * swap + j * lanes, lanes)
            ].astype(jnp.float32)
        at = pl.ds(j * width, width)
        put(merged_wide.at[:, at], merged.at[:, at])
    for part in range(4):
        c, x = part % 2, part // 2
        for index in range(half // lanes):
            output_wide[pl.ds(part * lanes, lanes), pl.ds(2 * lanes * index, 2 * lanes)] = attn[
                c, x, pl.ds(index * lanes, lanes), pl.ds(2 * swap, 2 * lanes)
            ].astype(jnp.float32)
    put(output_wide, output)
    tail = pl.ds(half, attn.shape[2] - half)
    y = lax.axis_index("fsdp")
    per = -(-width // swap)

    def entry(octant):
        c, x, side = octant % 2, octant // 2 % 2, octant // 4
        return attn[c, x, tail, pl.ds(side * swap, swap)].astype(jnp.float32)

    entries = [entry(octant) for octant in range(GROUP)]
    total = entries[0]
    for item in entries[1:]:
        total = total + item

    def vector(source, row, size):
        count = -(-size // swap)
        rows = [source[row + index : row + index + 1] for index in range(count)]
        return jnp.concatenate(rows, axis=1)[:, :size]

    whole = [vector(total, per * index, width) for index in range(4)]
    whole.append(vector(entries[0], per * 4, width))
    heads = [vector(item, per * 5, swap) for item in entries]
    heads = jnp.concatenate(
        [item[:, j * lanes : (j + 1) * lanes] for j in range(3) for item in heads], axis=1
    )
    hidden = jnp.concatenate([vector(item, per * 5 + 1, ff) for item in entries], axis=1)
    for side in range(2):

        @pl.when(y == side)
        def _():
            for index, item in enumerate(whole):
                shared_out[index : index + 1, :] = item[:, side * half : (side + 1) * half]
            for src, dst in ((heads, merged_sums), (hidden, expand_sums)):
                size = dst.shape[1]
                dst[...] = src[:, side * size : (side + 1) * size]

    for copy in puts:
        copy.wait()


def widen(feed_all, attn_all, swap, lanes, ff):
    half = feed_all.shape[2]
    width = 2 * half
    shapes = ((half, GROUP * ff), (4 * ff, width), (half, 3 * width), (4 * lanes, width))
    small = ((5, half), (1, 3 * half), (1, 4 * ff))
    any_spec = pl.BlockSpec(memory_space=pl.ANY)
    return pl.pallas_call(
        functools.partial(widen_kernel, swap=swap, lanes=lanes, ff=ff),
        out_shape=tuple(jax.ShapeDtypeStruct(shape, jnp.float32) for shape in shapes + small),
        in_specs=[any_spec] * 2,
        out_specs=[any_spec] * 4 + [pl.BlockSpec(memory_space=pltpu.VMEM)] * 3,
        scratch_shapes=[
            pltpu.VMEM(feed_all.shape, jnp.bfloat16),
            pltpu.VMEM(attn_all.shape, jnp.bfloat16),
        ]
        + [pltpu.VMEM(shape, jnp.float32) for shape in shapes]
        + [pltpu.SemaphoreType.DMA((2, 4)), pltpu.SemaphoreType.DMA((16,))],
        compiler_params=pltpu.CompilerParams(vmem_limit_bytes=48 << 20),
        name="widen",
    )(feed_all, attn_all)


def turn_tables(positions, lanes):
    lane = jnp.arange(lanes, dtype=jnp.int32) % HEAD
    inverse = jnp.exp((lane % HALF).astype(jnp.float32) * (-2.0 * math.log(10000.0) / ROT))
    angles = positions.astype(jnp.float32)[:, None] * inverse[None, :]
    turned = lane[None, :] < ROT
    return (jnp.where(turned, jnp.cos(angles), 1.0), jnp.where(turned, jnp.sin(angles), 0.0))


def group_body(
    hidden_states,
    unit_order,
    piece_starts,
    first_gain,
    first_shift,
    second_gain,
    second_shift,
    merged_weight,
    merged_bias,
    output_weight,
    output_bias,
    expand_weight,
    expand_bias,
    contract_weight,
    contract_bias,
    out_cotangent,
):
    c, y, x, z = place_here()
    tokens, width = hidden_states.shape[1:]
    length = tokens * 2 * LINE
    units = unit_order.shape[1]
    pieces = piece_starts.shape[1]
    rows = GROUP * tokens
    part = width // GROUP
    ff_part = expand_weight.shape[1] // GROUP
    half = width // 2
    vectors = (
        first_gain,
        first_shift,
        second_gain,
        second_shift,
        merged_bias,
        output_bias,
        expand_bias,
        contract_bias,
    )
    sizes = [v.shape[0] for v in vectors]
    total = sum(sizes)
    packed = jnp.zeros((total,), jnp.float32)
    at = 0
    for vector in vectors:
        size = vector.shape[0]
        packed = packed + jnp.pad(vector.astype(jnp.float32), (at, total - at - size))
        at += size
    packed = packed.reshape(-1, 128)
    ints = jnp.concatenate([unit_order[0], piece_starts[0]])
    ints = jnp.broadcast_to(jnp.pad(ints, (0, 128 - ints.shape[0]))[None], (8, 128))
    tables = turn_tables(jnp.arange(units, dtype=jnp.int32) * UNIT, part) + turn_tables(
        jnp.arange(UNIT, dtype=jnp.int32), part
    )
    (
        hid_all,
        ints_all,
        vec_all,
        wm_all,
        cot_all,
        we_all,
        got,
        active,
        grad_expanded,
        feed_grad,
        feed_sums,
    ) = front(
        hidden_states[0],
        ints,
        packed,
        merged_weight,
        tables,
        out_cotangent[0],
        expand_weight,
        output_weight,
        contract_weight,
    )
    vec_all = vec_all.reshape(2, -1)
    whole = []
    at = 0
    for size in sizes:
        whole.append(vec_all[:, at : at + size].reshape(-1))
        at += size
    gain_one, shift_one, gain_two, shift_two, bias_merged, bias_out, bias_expand, bias_contract = whole
    wm = wm_all.reshape(width, 3 * part)
    we = we_all.reshape(width, ff_part)
    cots = cot_all.reshape(rows, width)
    own_ints = lax.dynamic_index_in_dim(ints_all[:, 0], z, 0, keepdims=True)
    sorted_parts = sort_units(own_ints, got, units)
    swap = 3 * part
    feed_all, attn_all, output, input_gradient = middle(
        own_ints,
        sorted_parts.reshape(4, length, part),
        tables,
        feed_grad,
        active,
        grad_expanded,
        we,
        contract_weight,
        wm,
        output_weight,
        hid_all.reshape(rows, width),
        cots,
        jnp.stack([gain_one, shift_one, gain_two, bias_out + bias_contract]),
        feed_sums,
        tokens,
        units,
        pieces,
        ff_part,
    )
    expand_out, contract_out, merged_out, output_out, shared, merged_sums, expand_sums = widen(
        feed_all, attn_all, swap, part, ff_part
    )
    return (
        output[None],
        input_gradient[None],
        shared[0],
        shared[1],
        shared[2],
        shared[3],
        merged_out,
        merged_sums[0],
        output_out,
        shared[4],
        expand_out,
        expand_sums[0],
        contract_out,
        shared[4],
    )


def fits_groups(mesh, args):
    hidden, order = args[0], args[1]
    count = mesh.shape["seq"]
    tokens = hidden.shape[1] // count
    return (
        mesh.shape["rep"] == 2
        and mesh.shape["fsdp"] == 2
        and count == 2 * LINE
        and hidden.shape[0] == LINE
        and hidden.shape[2] == GROUP * 2 * HEAD
        and tokens % UNIT == 0
        and hidden.shape[1] % SPAN == 0
        and order.shape[1] + args[2].shape[1] <= 128
    )


def solution(mesh):
    in_specs = (
        P(("rep", "fsdp"), "seq", None),
        P(("rep", "fsdp"), None),
        P(("rep", "fsdp"), None),
        P("fsdp"),
        P("fsdp"),
        P("fsdp"),
        P("fsdp"),
        P("fsdp", None),
        P("fsdp"),
        P("fsdp", None),
        P("fsdp"),
        P("fsdp", None),
        P("fsdp"),
        P("fsdp", None),
        P("fsdp"),
        P(("rep", "fsdp"), "seq", None),
    )
    out_specs = (
        P(("rep", "fsdp"), "seq", None),
        P(("rep", "fsdp"), "seq", None),
        P("fsdp"),
        P("fsdp"),
        P("fsdp"),
        P("fsdp"),
        P("fsdp", None),
        P("fsdp"),
        P("fsdp", None),
        P("fsdp"),
        P("fsdp", None),
        P("fsdp"),
        P("fsdp", None),
        P("fsdp"),
    )

    def run(*args):
        chosen = group_body if fits_groups(mesh, args) else body
        mapped = jax.shard_map(
            chosen, mesh=mesh, in_specs=in_specs, out_specs=out_specs, check_vma=False
        )
        return mapped(*args)

    return run
```
